32 devices in a mesh: rep: 4 (over x, core), fsdp: 8 (over z, y).
Axes of the slice: x: 2, y: 2, z: 4, core: 2. Of those that a mesh axis runs over, the one named last changes fastest.
Arguments:
- tokens: bfloat16 [4, 16384, 1024], P(None, ('rep', 'fsdp')), may hold values from -6 to 6
- cotangent: bfloat16 [4, 16384, 1024], P(None, ('rep', 'fsdp')), may hold values from -6 to 6
- path: int32 [4, 16384, 3], P(None, ('rep', 'fsdp')), may hold values from 0 to 12, as said below
- chosen: int32 [4, 2048], P(None, ('rep', 'fsdp')), may hold values from 0 to 511, as said below
- router: bfloat16 [1024], P('fsdp'), may hold values from -0.1875 to 0.1875
- gains: bfloat16 [1024, 2], P('fsdp'), may hold values from 0.25 to 1.75
- w_qkv: bfloat16 [1024, 3072], P('fsdp'), may hold values from -0.1875 to 0.1875
- w_out: bfloat16 [1024, 1024], P('fsdp'), may hold values from -1 to 1
- w_up: bfloat16 [1024, 4096], P('fsdp'), may hold values from -0.1875 to 0.1875
- w_down: bfloat16 [4096, 1024], P('fsdp'), may hold values from -0.09375 to 0.09375
Outputs:
- mixed: bfloat16 [4, 16384, 1024], P(None, ('rep', 'fsdp'))
- grad_tokens: float32 [4, 16384, 1024], P(None, ('rep', 'fsdp'))
- grad_router: float32 [1024], P('fsdp')
- grad_gains: float32 [1024, 2], P('fsdp')
- grad_qkv: float32 [1024, 3072], P('fsdp')
- grad_out: float32 [1024, 1024], P('fsdp')
- grad_up: float32 [1024, 4096], P('fsdp')
- grad_down: float32 [4096, 1024], P('fsdp')
The draws below stay inside these ranges and needn't reach their ends.
Inputs may be any that keep to these rules, and one draw needn't show every extreme that they name: `path`: each tree's 4096 rows hold 13 segments with 13 distinct numbers, each of one token or more, laid out as the trunk and then, for each of 4 branches, the branch followed by its 2 leaves. Column 0 is a token's segment, column 1 its parent's (the trunk's own for the trunk), column 2 the trunk's. `chosen`: for each micro-batch and device, its 64 entries are distinct numbers of that device's tokens, in increasing order.
All inputs are finite; a program needn't handle non-finite values.
Results may differ from the reference program's by a relative error of at most 0.011.
Values may be sent and summed in bfloat16 or wider, within the bound.
A program may use at most 384 MiB of HBM per device.

```python
import jax
import jax.numpy as jnp
import numpy as np
from jax import lax

D = 1024
HEADS = 16
HEAD_DIM = 64
FF = 4096
TOK_DEV = 512
MB = 4
CAP = 64
GROUPS = 4
GROUP_TOK = 4096
GROUP_KEYS = 512
TOKENS = 16384
ROUTED = 2048


PARENT_TABLE = np.array([0, 0, 1, 1, 0, 4, 4, 0, 7, 7, 0, 10, 10], np.int32)


def tree_layout(tree_key):
    length_key, name_key = jax.random.split(tree_key)
    shares = jax.random.randint(length_key, (13,), 1, 9)
    seg_lengths = 1 + (GROUP_TOK - 13) * shares // jnp.sum(shares)
    seg_lengths = seg_lengths.at[0].add(GROUP_TOK - jnp.sum(seg_lengths))
    seg_ends = jnp.cumsum(seg_lengths)
    positions = jnp.arange(GROUP_TOK, dtype=jnp.int32)
    segment = jnp.sum((positions[:, None] >= seg_ends[None, :]).astype(jnp.int32), axis=1)
    seg_names = jax.random.permutation(name_key, 13).astype(jnp.int32)
    parent = jnp.asarray(PARENT_TABLE)[segment]
    trunk_name = jnp.zeros_like(segment) + seg_names[0]
    return jnp.stack([seg_names[segment], seg_names[parent], trunk_name], axis=1).astype(jnp.int32)


def draw_path(key, part):
    tree_keys = jax.random.split(jax.random.fold_in(key, 11), MB * GROUPS)
    trees = jax.vmap(tree_layout)(tree_keys)
    return trees.reshape(MB, TOKENS, 3)


def draw_chosen(key, part):
    device_count = MB * ROUTED // CAP
    device_keys = jax.random.split(jax.random.fold_in(key, 23), device_count)

    def one_device(sub_key):
        return jnp.sort(jax.random.permutation(sub_key, TOK_DEV)[:CAP]).astype(jnp.int32)
    return jax.vmap(one_device)(device_keys).reshape(MB, ROUTED)


def with_spikes(values, key, source, target, parts, factor):
    def block_of(axis_at):
        return (jnp.arange(values.shape[axis_at]) // (values.shape[axis_at] // parts)).reshape((-1,) + (1,) * (values.ndim - 1 - axis_at))

    first = jax.random.permutation(key, parts)[block_of(target)]
    far = (block_of(target) + parts // 2) % parts
    return jnp.where((block_of(source) == first) | (block_of(source) == far), factor * values, values)


def block_scale(rng, shape, cuts, smallest, largest):
    gain = 1.0
    for position, blocks in cuts:
        heights = jax.random.uniform(jax.random.fold_in(jax.random.fold_in(rng, 6), position), (blocks,), jnp.float32, smallest / len(cuts), largest / len(cuts))
        gain = gain * jnp.repeat(jnp.exp(heights), shape[position] // blocks).reshape((-1,) + (1,) * (len(shape) - 1 - position))
    return gain


def centred(stream_key, shape, deviation, most, cuts=(), kind=jnp.bfloat16):
    entries = jax.random.normal(stream_key, shape, jnp.float32) * deviation
    if len(cuts) > 0:
        entries = block_scale(stream_key, shape, cuts, -0.22, 0.18) * entries
    return jnp.clip(entries, min=-most, max=most).astype(kind)


def bell_draw_with(own_key, extent, width, bound, shards, heavy, kind=jnp.bfloat16):
    values = width * jax.random.normal(own_key, extent, jnp.float32)
    if shards:
        values = values * block_scale(own_key, extent, shards, -0.22, 0.18)
    return jnp.clip(with_spikes(values, jax.random.fold_in(own_key, 3), *heavy), -bound, bound).astype(kind)


def setup_inputs(seed: int = 0) -> dict:
    key_list = jax.random.split(jax.random.key(seed), 11)
    return {
        "tokens": bell_draw_with(key_list[0], (MB, TOKENS, D), 1.0, 6.0, ((1, 32),), (1, 2, 32, 2.75)),
        "cotangent": centred(key_list[1], (MB, TOKENS, D), 1.0, 6.0, ((1, 32),)),
        "path": draw_path(jax.random.fold_in(key_list[10], 71), 0),
        "chosen": draw_chosen(jax.random.fold_in(key_list[10], 71), 0),
        "router": centred(key_list[4], (D,), D ** -0.5, 0.1875, ((0, 8),)),
        "gains": jnp.clip(1.0 + 0.15 * jax.random.normal(key_list[5], (D, 2), jnp.float32), 0.25, 1.75).astype(jnp.bfloat16),
        "w_qkv": centred(key_list[6], (D, 3 * D), D ** -0.5, 0.1875, ((0, 8),)),
        "w_out": centred(key_list[7], (D, D), (D // 32) ** -0.5, 1.0, ((0, 8),)),
        "w_up": centred(key_list[8], (D, FF), D ** -0.5, 0.1875, ((0, 8),)),
        "w_down": centred(key_list[9], (FF, D), FF ** -0.5, 0.09375, ((0, 8),)),
    }


eps = 1e-05
HI = lax.Precision.HIGHEST

@jax.custom_vjp
def low(v):
    return lax.optimization_barrier(v.astype(jnp.bfloat16)).astype(jnp.float32)

@jax.custom_vjp
def low_back(v):
    return v

def low_keep(v):
    return (low(v), None)

def low_pass(kept, grad):
    return (grad,)

def back_keep(v):
    return (v, None)

def back_low(kept, grad):
    return (low(grad),)
low.defvjp(low_keep, low_pass)
low_back.defvjp(back_keep, back_low)

def rms_scale(matrix, gain_row):
    return matrix * lax.rsqrt(lax.optimization_barrier(jnp.mean(matrix * matrix, axis=-1, keepdims=True)) + eps) * gain_row

def reference(tokens, cotangent, path, chosen, router, gains, w_qkv, w_out, w_up, w_down):
    score_scale = HEAD_DIM ** (-0.5)
    qblock = min(512, GROUP_KEYS)
    block_count = GROUP_KEYS // qblock
    tree_paths = path.reshape(MB * GROUPS, GROUP_TOK, 3)
    tree_picks = chosen.reshape(MB * GROUPS, GROUP_KEYS)

    def forward(source, router_w, gain_w, qkv_w, out_w, up_w, down_w):
        tree_rows = source.reshape(MB * GROUPS, GROUP_TOK, D)

        def one_tree(inputs):
            tree_tokens, picks, tree_path = inputs
            slot_ids = jnp.arange(GROUP_KEYS, dtype=jnp.int32)
            global_row = slot_ids // CAP * TOK_DEV + picks
            hidden = tree_tokens[global_row]
            gate_rate = jax.nn.sigmoid(jnp.dot(hidden, router_w, precision=HI))
            normed = low(rms_scale(hidden, gain_w[:, 0]))
            projected = low_back(low(jnp.dot(normed, qkv_w, precision=HI)))
            queries = projected[:, :D].reshape(GROUP_KEYS, HEADS, HEAD_DIM)
            key_rows = projected[:, D:2 * D].reshape(GROUP_KEYS, HEADS, HEAD_DIM)
            value_rows = projected[:, 2 * D:].reshape(GROUP_KEYS, HEADS, HEAD_DIM)
            own_path = tree_path[global_row]
            key_seg = own_path[:, 0]

            def query_block(pieces):
                query_part, path_part, place_part = pieces
                scores = jnp.einsum('qhd,khd->hqk', query_part, key_rows, precision=HI) * score_scale
                visible = ((key_seg[None, :] == path_part[:, 0:1]) | (key_seg[None, :] == path_part[:, 1:2]) | (key_seg[None, :] == path_part[:, 2:3])) & (global_row[None, :] <= place_part[:, None])
                scores = low_back(jnp.where(visible[None], scores, -1e+30))
                row_max = lax.optimization_barrier(jnp.max(scores, axis=-1, keepdims=True))
                exponent = jnp.where(visible[None], jnp.exp(scores - row_max), 0.0)
                probs = low(exponent / lax.optimization_barrier(jnp.sum(exponent, axis=-1, keepdims=True)))
                mixed_heads = jnp.einsum('hqk,khd->qhd', probs, value_rows, precision=HI)
                return mixed_heads.reshape(query_part.shape[0], D)
            attention = lax.map(jax.checkpoint(query_block), (queries.reshape(block_count, qblock, HEADS, HEAD_DIM), own_path.reshape(block_count, qblock, 3), global_row.reshape(block_count, qblock)))
            attention = low_back(low(attention.reshape(GROUP_KEYS, D)))
            branch = low_back(jnp.dot(attention, out_w, precision=HI))
            middle = hidden + branch
            normed_two = low(rms_scale(middle, gain_w[:, 1]))
            up_proj = low_back(jnp.dot(normed_two, up_w, precision=HI))
            activated = low(jax.nn.gelu(up_proj))
            mlp_out = low_back(jnp.dot(activated, down_w, precision=HI))
            change = branch + mlp_out
            return tree_tokens.at[global_row].set(hidden + gate_rate[:, None] * change)
        result = lax.map(jax.checkpoint(one_tree), (tree_rows, tree_picks, tree_paths))
        return result.reshape(MB, TOKENS, D)
    primal = (tokens.astype(jnp.float32), router.astype(jnp.float32), gains.astype(jnp.float32), w_qkv.astype(jnp.float32), w_out.astype(jnp.float32), w_up.astype(jnp.float32), w_down.astype(jnp.float32))
    output, pullback = jax.vjp(forward, *primal)
    gradients = pullback(cotangent.astype(jnp.float32))
    return (output.astype(jnp.bfloat16), gradients[0], gradients[1], gradients[2], gradients[3], gradients[4], gradients[5], gradients[6])
```

```python
import jax
import jax.numpy as jnp
from jax import lax
from jax.sharding import PartitionSpec as P

HEADS = 16


eps = 1e-05


def rms_scale(matrix, gain_row):
    return matrix * lax.rsqrt(jnp.mean(matrix * matrix, axis=-1, keepdims=True) + eps) * gain_row


def inner(left, right):
    return lax.dot_general(
        left, right, (((0,), (0,)), ((), ())), preferred_element_type=jnp.float32
    )


def by_rows(left, right):
    return lax.dot_general(
        left, right, (((1,), (1,)), ((), ())), preferred_element_type=jnp.float32
    )


def gather_rows(arrays):
    return lax.all_gather(arrays, "fsdp", axis=0, tiled=True)


def scatter_sum(array):
    return lax.psum_scatter(
        array.astype(jnp.bfloat16), "fsdp", scatter_dimension=0, tiled=True
    ).astype(jnp.float32)


def shards(tokens, cotangent, path, chosen, router, gains, w_qkv, w_out, w_up, w_down):
    micro_count, tok_count, model_width = tokens.shape
    slot_count = chosen.shape[1]
    row_count = micro_count * slot_count
    head_dim = model_width // HEADS
    score_scale = head_dim ** (-0.5)
    offset = lax.axis_index("fsdp") * tok_count
    fsdp = lax.axis_size("fsdp")

    def pick(array):
        return jax.vmap(lambda rows, at: rows[at])(array, chosen)

    small = jnp.concatenate([router[:, None], gains], axis=1)
    small_all = gather_rows(small)
    qkv_all = gather_rows(w_qkv)
    out_all = gather_rows(w_out)
    up_all = gather_rows(w_up)
    down_all = gather_rows(w_down)
    router_float = small_all[:, 0].astype(jnp.float32)
    gain_one = small_all[:, 1].astype(jnp.float32)
    gain_two = small_all[:, 2].astype(jnp.float32)

    routed = pick(tokens).reshape(row_count, model_width)
    hidden = routed.astype(jnp.float32)
    gate_rate = jax.nn.sigmoid(
        jnp.dot(routed, small_all[:, 0], preferred_element_type=jnp.float32)
    )
    normed = rms_scale(hidden, gain_one).astype(jnp.bfloat16)
    projected = jnp.dot(normed, qkv_all, preferred_element_type=jnp.float32).astype(jnp.bfloat16)
    queries = projected[:, :model_width].reshape(micro_count, slot_count, HEADS, head_dim)
    own_path = pick(path)
    own_place = offset + chosen
    key_info = jnp.concatenate([own_path[:, :, :1], own_place[:, :, None]], axis=2)
    gathered = lax.all_gather(
        projected[:, model_width:].reshape(micro_count, slot_count, 2 * model_width), "fsdp"
    )
    info_all = lax.all_gather(key_info, "fsdp")
    key_count = fsdp * slot_count
    gathered = jnp.swapaxes(gathered, 0, 1).reshape(micro_count, key_count, 2, HEADS, head_dim)
    info_all = jnp.swapaxes(info_all, 0, 1).reshape(micro_count, key_count, 2)
    key_rows = gathered[:, :, 0]
    value_rows = gathered[:, :, 1]
    key_seg = info_all[:, None, :, 0]
    visible = (
        (key_seg == own_path[:, :, 0:1])
        | (key_seg == own_path[:, :, 1:2])
        | (key_seg == own_path[:, :, 2:3])
    ) & (info_all[:, None, :, 1] <= own_place[:, :, None])
    visible = visible[:, None]

    def product(form, left, right):
        return jnp.einsum(form, left, right, preferred_element_type=jnp.float32)

    scores = product("mqhd,mkhd->mhqk", queries, key_rows) * score_scale
    scores = jnp.where(visible, scores, -1e30)
    row_max = jnp.max(scores, axis=-1, keepdims=True)
    exponent = jnp.where(visible, jnp.exp(scores - row_max), 0.0)
    row_total = jnp.sum(exponent, axis=-1, keepdims=True)
    soft_prob = exponent / row_total
    probs = soft_prob.astype(jnp.bfloat16)
    attention = product("mhqk,mkhd->mqhd", probs, value_rows)
    attention = attention.reshape(row_count, model_width).astype(jnp.bfloat16)
    branch = jnp.dot(attention, out_all, preferred_element_type=jnp.float32)
    middle = hidden + branch
    normed_two = rms_scale(middle, gain_two).astype(jnp.bfloat16)
    up_proj = jnp.dot(normed_two, up_all, preferred_element_type=jnp.float32)
    activated = jax.nn.gelu(up_proj).astype(jnp.bfloat16)
    change = branch + jnp.dot(activated, down_all, preferred_element_type=jnp.float32)
    new_rows = hidden + gate_rate[:, None] * change

    def put(array, rows):
        rows = rows.reshape(micro_count, slot_count, model_width).astype(array.dtype)
        return jax.vmap(lambda whole, at, new: whole.at[at].set(new))(array, chosen, rows)

    mixed = put(tokens, new_rows)

    grad_rows = pick(cotangent).reshape(row_count, model_width).astype(jnp.float32)
    grad_change = gate_rate[:, None] * grad_rows
    grad_logit = jnp.sum(grad_rows * change, axis=-1) * gate_rate * (1.0 - gate_rate)
    grad_mlp = grad_change.astype(jnp.bfloat16)
    grad_down = scatter_sum(inner(activated, grad_mlp))
    grad_act = by_rows(grad_mlp, down_all)
    gelu_value, gelu_back = jax.vjp(jax.nn.gelu, up_proj)
    grad_up_proj = gelu_back(grad_act)[0].astype(jnp.bfloat16)
    grad_up = scatter_sum(inner(normed_two, grad_up_proj))
    grad_normed_two = by_rows(grad_up_proj, up_all)
    norm_value, norm_back_two = jax.vjp(rms_scale, middle, gain_two)
    grad_middle, grad_gain_two = norm_back_two(grad_normed_two)
    grad_branch = (grad_change + grad_middle).astype(jnp.bfloat16)
    grad_outw = scatter_sum(inner(attention, grad_branch))
    grad_attention = by_rows(grad_branch, out_all).astype(jnp.bfloat16)
    grad_heads = grad_attention.reshape(micro_count, slot_count, HEADS, head_dim)
    prob_grad = product("mqhd,mkhd->mhqk", grad_heads, value_rows)
    delta = jnp.sum(soft_prob * prob_grad, axis=-1, keepdims=True)
    grad_scores = (soft_prob * (prob_grad - delta)).astype(jnp.bfloat16)
    grad_query = product("mhqk,mkhd->mqhd", grad_scores, key_rows) * score_scale
    grad_key = product("mhqk,mqhd->mkhd", grad_scores, queries) * score_scale
    grad_value = product("mhqk,mqhd->mkhd", probs, grad_heads)
    grad_kv = jnp.stack([grad_key, grad_value], axis=2).reshape(
        micro_count, fsdp, slot_count, 2 * model_width
    )
    grad_kv = lax.psum_scatter(
        jnp.swapaxes(grad_kv, 0, 1).astype(jnp.bfloat16).reshape(-1, 2 * model_width),
        "fsdp",
        scatter_dimension=0,
        tiled=True,
    )
    grad_projected = jnp.concatenate(
        [
            grad_query.reshape(row_count, model_width).astype(jnp.bfloat16),
            grad_kv.reshape(row_count, 2 * model_width),
        ],
        axis=1,
    )
    grad_qkvw = scatter_sum(inner(normed, grad_projected))
    grad_normed = by_rows(grad_projected, qkv_all)
    norm_value_one, norm_back_one = jax.vjp(rms_scale, hidden, gain_one)
    grad_hidden_norm, grad_gain_one = norm_back_one(grad_normed)
    grad_hidden = (
        grad_rows + grad_middle + grad_hidden_norm + grad_logit[:, None] * router_float[None, :]
    )
    grad_tokens = put(cotangent.astype(jnp.float32), grad_hidden)
    grad_routerw = jnp.sum(grad_logit[:, None] * hidden, axis=0)
    grad_small = jnp.stack([grad_routerw, grad_gain_one, grad_gain_two], axis=1)
    grad_small = lax.psum_scatter(grad_small, "fsdp", scatter_dimension=0, tiled=True)
    summed = lax.psum((grad_small, grad_qkvw, grad_outw, grad_up, grad_down), "rep")
    return (mixed, grad_tokens, summed[0][:, 0], summed[0][:, 1:]) + tuple(summed[1:])


def solution(mesh):
    rows = P(None, ("rep", "fsdp"), None)
    weight = P("fsdp", None)
    return jax.shard_map(
        shards,
        mesh=mesh,
        in_specs=(
            rows,
            rows,
            rows,
            P(None, ("rep", "fsdp")),
            P("fsdp"),
            weight,
            weight,
            weight,
            weight,
            weight,
        ),
        out_specs=(rows, rows, P("fsdp"), weight, weight, weight, weight, weight),
        check_vma=False,
    )
```

```python
import functools
import math
import types

import jax
import jax.numpy as jnp
from jax import lax
from jax.experimental import pallas as pl
from jax.experimental.pallas import tpu as pltpu
from jax.sharding import PartitionSpec as P

HEADS = 16


eps = 1e-05
MESH = pl.DeviceIdType.MESH
BF = jnp.bfloat16
F32 = jnp.float32
GELU_A = math.sqrt(2.0 / math.pi)
GELU_B = 0.044715


def dot(left, right, contract):
    return lax.dot_general(
        left, right, (((contract[0],), (contract[1],)), ((), ())), preferred_element_type=F32
    )


def aligned(index, size):
    return pl.ds(pl.multiple_of(index * size, size), size)


def loop(count, body):
    def step(index, carry):
        body(index)
        return carry

    lax.fori_loop(0, count, step, 0)


def fits(mesh, tokens, chosen, w_up):
    rep, fsdp = mesh.shape["rep"], mesh.shape["fsdp"]
    micro, width, hidden = tokens.shape[0], tokens.shape[2], w_up.shape[1]
    if fsdp % micro or rep % 2:
        return False
    inner_count = fsdp // micro
    return (
        rep % inner_count == 0
        and rep == micro
        and fsdp == rep * inner_count
        and width == fsdp * 128
        and hidden == fsdp * rep * 128
        and HEADS % (2 * rep) == 0
        and width // HEADS == 64
        and chosen.shape[1] // (rep * fsdp) == 64
    )


def scratch_shapes(g):
    own, rows, d = g.own, g.rows, g.d
    vmem = {
        "hid": ((own, d), BF),
        "ct": ((own, d), BF),
        "infos": ((g.R * g.MB * 8, 128), F32),
        "sm": ((g.F * 8, 128), F32),
        "vec": ((8, d), F32),
        "wqa": ((d, g.qc), BF),
        "woa": ((g.ac, d), BF),
        "wua": ((d, g.fc), BF),
        "wda": ((g.fc, d), BF),
        "normed": ((rows, d), BF),
        "norm2": ((rows, d), BF),
        "gmlp": ((rows, d), BF),
        "gbr": ((rows, d), BF),
        "proj": ((rows, g.qc), BF),
        "att": ((rows, g.ac), BF),
        "gatt": ((rows, g.ac), BF),
        "gproj": ((rows, g.qc), BF),
        "lse": ((rows, 128), F32),
        "bias": ((g.tree, g.tree), F32),
        "act": ((rows, g.fc), BF),
        "dact": ((rows, g.fc), F32),
        "gup": ((rows, g.fc), BF),
        "gate": ((own, 128), F32),
        "glog": ((own, 128), F32),
        "branch": ((own, d), F32),
        "acc": ((own, d), F32),
        "gmid": ((own, d), F32),
        "nrow": ((own, d), BF),
        "grow": ((own, d), BF),
        "to_sib": ((2, g.X * own, d), BF),
        "of_sib": ((2, g.X * own, d), BF),
        "to_x": ((2, (g.X - 1) * own, d), BF),
        "of_x": ((2, (g.X - 1) * own, d), BF),
        "gsum": ((8, d), F32),
        "gsp": ((g.F * 8, 128), F32),
        "gs_pair": ((2, 8, 128), F32),
        "gs_mine": ((2, 8, 128), F32),
    }
    piece = d // g.F
    for name, count, cols, kind in g.items:
        height = 8 if name == "s" else piece
        if name != "s":
            vmem["g" + name] = ((count * height, cols), kind)
        vmem["gi" + name] = (((count // g.S) * height, cols), kind)
        vmem["go" + name] = (((g.A - 1) * height, cols), kind)
        if name != "s":
            vmem["gr" + name] = (((g.R if name != "o" else 1) * height, cols), kind)
    vmem["stage"] = ((2, piece, g.fc), F32)
    sems = {
        "a2a_s": (5, g.MB),
        "a2a_r": (5, g.MB),
        "stage_sem": (2,),
    }
    for name in ("small", "wq", "wo", "wu", "wd"):
        sems[name + "_l"] = (1,)
        sems[name + "_os"] = (g.A - 1,)
        sems[name + "_or"] = (g.A - 1,)
        sems[name + "_is"] = (g.A,)
        sems[name + "_ir"] = (g.A,)
    for name in ("info", "normed", "gmlp", "norm2", "gbr", "rq", "ru", "rd", "ro"):
        sems[name + "_xs"] = (g.X - 1,)
        sems[name + "_xr"] = (g.X - 1,)
        sems[name + "_ss"] = (g.X,)
        sems[name + "_sr"] = (g.X,)
    for index in range(4):
        name = "sum%d" % index
        sems[name + "_xs"] = (g.X - 1,)
        sems[name + "_xr"] = (g.X - 1,)
        sems[name + "_ss"] = (g.X,)
        sems[name + "_sr"] = (g.X,)
    for name, count, cols, kind in g.items:
        sems["g" + name + "_is"] = (g.A,)
        sems["g" + name + "_ir"] = (g.A,)
        sems["g" + name + "_os"] = (g.A - 1,)
        sems["g" + name + "_or"] = (g.A - 1,)
    sems["pair_s"] = (2,)
    sems["pair_r"] = (2,)
    return vmem, sems


def block_kernel(g, names, *refs):
    n = types.SimpleNamespace(**dict(zip(names, refs)))
    R, F, S, A, X, MB = g.R, g.F, g.S, g.A, g.X, g.MB
    own, rows, d, cap = g.own, g.rows, g.d, g.cap
    piece = d // F
    r = lax.axis_index("rep")
    f = lax.axis_index("fsdp")
    x, c = r // 2, lax.rem(r, 2)
    a, b = f // S, lax.rem(f, S)
    other_b = lax.rem(b + 1, S)
    sib = x * 2 + 1 - c
    pending = {}

    def remote(src, dst, ss, rs, rep, fsdp):
        return pltpu.make_async_remote_copy(
            src_ref=src,
            dst_ref=dst,
            send_sem=ss,
            recv_sem=rs,
            device_id={"rep": rep, "fsdp": fsdp},
            device_id_type=MESH,
        )

    def send(src, dst, ss, rs, rep, fsdp, cond=None, tag="end"):
        def start():
            remote(src, dst, ss, rs, rep, fsdp).start()

        def done():
            remote(src, dst, ss, rs, rep, fsdp).wait_send()

        if cond is None:
            start()
            pending.setdefault(tag, []).append(done)
        else:
            pl.when(cond)(start)
            pending.setdefault(tag, []).append(lambda: pl.when(cond)(done))

    def drain(tag):
        for done in pending.pop(tag, []):
            done()

    def got(dst, rs):
        remote(dst, dst, rs, rs, sib, f).wait_recv()

    def xpeer(step):
        return lax.rem(x + 1 + step, X)

    def xfrom(step):
        return lax.rem(x + X - 1 - step, X)

    def outer(step):
        return lax.rem(a + step, A)

    def outer_from(step):
        return lax.rem(a + A - step, A)

    home_rep = (r // S) * S + b

    def home_fsdp(m):
        return m * S + lax.rem(r, S)

    barrier = pltpu.get_barrier_semaphore()

    def greet(rep, fsdp):
        pl.semaphore_signal(
            barrier, inc=1, device_id={"rep": rep, "fsdp": fsdp}, device_id_type=MESH
        )

    for step in range(1, A):
        greet(r, outer(step) * S + b)
    greet(r, a * S + other_b)
    greet(sib, f)
    for step in range(X - 1):
        greet(xpeer(step) * 2 + c, f)
    mine = [(home_fsdp(m) == f) & (home_rep == r) for m in range(MB)]
    for m in range(MB):

        @pl.when(jnp.logical_not(mine[m]))
        def _(m=m):
            greet(home_rep, home_fsdp(m))

    stays = (home_rep == r) & (lax.rem(r, S) == b)
    pl.semaphore_wait(barrier, (A - 1) + 1 + 1 + (X - 1) + MB - stays.astype(jnp.int32))

    def swap_start(which, src_of, dst_of):
        for m in range(MB):
            src, dst = src_of(m), dst_of(a)
            ss, rs = n.a2a_s.at[which, m], n.a2a_r.at[which, a]

            @pl.when(jnp.logical_not(mine[m]))
            def _():
                remote(src, dst, ss, rs, home_rep, home_fsdp(m)).start()

            @pl.when(mine[m])
            def _():
                pltpu.make_async_copy(src, dst, rs).start()

    def swap_end(which, src_of, dst_of):
        for m in range(MB):
            src, dst = src_of(m), dst_of(m)
            ss, rs = n.a2a_s.at[which, m], n.a2a_r.at[which, m]

            @pl.when(jnp.logical_not(mine[m]))
            def _():
                remote(src, dst, ss, rs, home_rep, home_fsdp(m)).wait()

            @pl.when(mine[m])
            def _():
                pltpu.make_async_copy(src, dst, rs).wait()

    def sem(name):
        return getattr(n, name)

    def gather_start(name, src, buf, height):
        at = aligned(f, height)
        pltpu.make_async_copy(src, buf.at[at], sem(name + "_l").at[0]).start()
        for step in range(1, A):
            send(
                src,
                buf.at[at],
                sem(name + "_os").at[step - 1],
                sem(name + "_or").at[step - 1],
                r,
                outer(step) * S + b,
            )
        send(src, buf.at[at], sem(name + "_is").at[0], sem(name + "_ir").at[0], r, a * S + other_b)

    def gather_forward(name, buf, height):
        for step in range(1, A):
            at = buf.at[aligned(outer_from(step) * S + b, height)]
            got(at, sem(name + "_or").at[step - 1])
            send(at, at, sem(name + "_is").at[step], sem(name + "_ir").at[step], r, a * S + other_b)

    def gather_end(name, src, buf, height):
        pltpu.make_async_copy(src, buf.at[aligned(f, height)], sem(name + "_l").at[0]).wait()
        for step in range(A):
            at = buf.at[aligned(outer_from(step) * S + other_b, height)]
            got(at, sem(name + "_ir").at[step])

    is_source = a == r

    def out_start(src, buf):
        at = buf.at[aligned(b, piece)]

        @pl.when(is_source)
        def _():
            pltpu.make_async_copy(src, at, n.wo_l.at[0]).start()

        for step in range(1, A):
            send(
                src, at, n.wo_os.at[step - 1], n.wo_or.at[0], r, outer(step) * S + b, is_source
            )
        send(src, at, n.wo_is.at[0], n.wo_ir.at[0], r, a * S + other_b, is_source)

    def out_forward(buf):
        at = buf.at[aligned(b, piece)]

        @pl.when(jnp.logical_not(is_source))
        def _():
            got(at, n.wo_or.at[0])

        send(
            at, at, n.wo_is.at[1], n.wo_ir.at[0], r, a * S + other_b, jnp.logical_not(is_source)
        )

    def out_end(src, buf):
        @pl.when(is_source)
        def _():
            pltpu.make_async_copy(src, buf.at[aligned(b, piece)], n.wo_l.at[0]).wait()

        got(buf.at[aligned(other_b, piece)], n.wo_ir.at[0])

    def share_start(name, buf, height):
        at = buf.at[aligned(r, height)]
        for step in range(X - 1):
            send(
                at,
                at,
                sem(name + "_xs").at[step],
                sem(name + "_xr").at[step],
                xpeer(step) * 2 + c,
                f,
            )
        send(at, at, sem(name + "_ss").at[0], sem(name + "_sr").at[0], sib, f)

    def share_forward(name, buf, height):
        for step in range(X - 1):
            at = buf.at[aligned(xfrom(step) * 2 + c, height)]
            got(at, sem(name + "_xr").at[step])
            send(at, at, sem(name + "_ss").at[1 + step], sem(name + "_sr").at[1 + step], sib, f)

    def share_end(name, buf, height):
        got(buf.at[aligned(sib, height)], sem(name + "_sr").at[0])
        for step in range(X - 1):
            at = buf.at[aligned(xfrom(step) * 2 + 1 - c, height)]
            got(at, sem(name + "_sr").at[1 + step])

    wide = 256

    def sum_start(index, slot, partial, acc):
        name = "sum%d" % index
        to_sib, of_sib = n.to_sib.at[slot], n.of_sib.at[slot]
        to_x, of_x = n.to_x.at[slot], n.of_x.at[slot]
        drain("slot%d" % slot)
        order = [xpeer(step) for step in range(X - 1)] + [x]
        for step, xo in enumerate(order):
            at = pl.ds(step * own, own)

            def one(tile, xo=xo, at=at):
                cols = aligned(tile, wide)
                to_sib[at, cols] = partial(xo * 2 + 1 - c, cols).astype(BF)

            loop(d // wide, one)
            send(
                to_sib.at[at],
                of_sib.at[at],
                sem(name + "_ss").at[step],
                sem(name + "_sr").at[step],
                sib,
                f,
                tag="slot%d" % slot,
            )
        for step, xo in enumerate(order):
            at = pl.ds(step * own, own)
            got(of_sib.at[at], sem(name + "_sr").at[step])
            last = step == X - 1

            def one(tile, xo=xo, at=at, last=last):
                cols = aligned(tile, wide)
                total = partial(xo * 2 + c, cols) + of_sib[at, cols].astype(F32)
                if last:
                    acc[:, cols] = total
                else:
                    to_x[at, cols] = total.astype(BF)

            loop(d // wide, one)
            if not last:
                send(
                    to_x.at[at],
                    of_x.at[at],
                    sem(name + "_xs").at[step],
                    sem(name + "_xr").at[step],
                    xo * 2 + c,
                    f,
                    tag="slot%d" % slot,
                )

    def sum_end(index, slot):
        of_x = n.of_x.at[slot]
        for step in range(X - 1):
            got(of_x.at[pl.ds(step * own, own)], sem("sum%d_xr" % index).at[step])

    def came(slot, at):
        total = None
        for step in range(X - 1):
            part = n.of_x[slot, pl.ds(step * own + at, tall), :].astype(F32)
            total = part if total is None else total + part
        return total

    tall = 32

    def by_own(body):
        def one(index):
            at = pl.multiple_of(index * tall, tall)
            body(at, pl.ds(at, tall))

        loop(own // tall, one)

    def grad_start(name, buf, height):
        out = name == "o"
        inbox = sem("gi" + name)
        for step in range(1 if out else A):
            to_a = r if out else outer(step + 1)
            src = buf.at[aligned((0 if out else to_a * S) + other_b, height)]
            send(
                src,
                inbox.at[pl.ds(step * height, height)],
                sem("g" + name + "_is").at[step],
                sem("g" + name + "_ir").at[step],
                r,
                a * S + other_b,
            )

    def add_into(dst, base, inbox, start, height):
        small = min(height, 32)

        def one(index):
            at = pl.ds(pl.multiple_of(base + index * small, small), small)
            of = pl.ds(pl.multiple_of(start + index * small, small), small)
            dst[at, :] = (dst[at, :].astype(F32) + inbox[of, :].astype(F32)).astype(dst.dtype)

        loop(height // small, one)

    def grad_forward(name, buf, height):
        out = name == "o"
        inbox, outbox = sem("gi" + name), sem("go" + name)
        for step in range(1 if out else A):
            to_a = r if out else outer(step + 1)
            base = ((0 if out else to_a * S) + b) * height
            got(inbox.at[pl.ds(step * height, height)], sem("g" + name + "_ir").at[step])
            add_into(buf, base, inbox, step * height, height)
            if out:
                slot = lax.rem(r + A - a - 1, A)
                slot = jnp.where(is_source, 0, slot)
                send(
                    buf.at[pl.ds(pl.multiple_of(base, height), height)],
                    outbox.at[aligned(slot, height)],
                    n.go_os.at[0],
                    n.go_or.at[slot],
                    r,
                    r * S + b,
                    jnp.logical_not(is_source),
                )
            elif step < A - 1:
                send(
                    buf.at[pl.ds(pl.multiple_of(base, height), height)],
                    outbox.at[pl.ds(step * height, height)],
                    sem("g" + name + "_os").at[step],
                    sem("g" + name + "_or").at[step],
                    r,
                    to_a * S + b,
                )

    def grad_wait(name, height):
        for step in range(A - 1):
            got(
                sem("go" + name).at[pl.ds(step * height, height)],
                sem("g" + name + "_or").at[step],
            )

    def grad_total(name, buf, base, height, target, target_base):
        outbox = sem("go" + name)
        small = min(height, 32)

        def one(index):
            off = index * small
            total = buf[pl.ds(pl.multiple_of(base + off, small), small), :].astype(F32)
            for step in range(A - 1):
                at = pl.ds(pl.multiple_of(step * height + off, small), small)
                total = total + outbox[at, :].astype(F32)
            at = pl.ds(pl.multiple_of(target_base + off, small), small)
            target[at, :] = total.astype(target.dtype)

        loop(height // small, one)

    def grad_own(name, buf, height):
        grad_wait(name, height)
        grad_total(name, buf, f * height, height, sem("gr" + name), r * height)
        share_start("r" + name, sem("gr" + name), height)

    def hid_at(i):
        return n.hid.at[aligned(i, cap)]

    def ct_at(i):
        return n.ct.at[aligned(i, cap)]

    def info_src(i):
        return n.info.at[i]

    def info_own(i):
        return n.infos.at[aligned(r * MB + i, 8)]

    def info_home(i):
        return n.infos.at[aligned(home_rep * MB + i, 8)]

    swap_start(0, lambda m: n.tok.at[m], hid_at)
    for m in range(MB):
        ss, rs = n.a2a_s.at[1, m], n.a2a_r.at[1, a]

        @pl.when(jnp.logical_not(mine[m]))
        def _():
            remote(info_src(m), info_home(a), ss, rs, home_rep, home_fsdp(m)).start()

        @pl.when(mine[m])
        def _():
            pltpu.make_async_copy(info_src(m), info_own(a), rs).start()

    gather_start("small", n.small, n.sm, 8)
    gather_start("wq", n.wq, n.wqa, piece)
    gather_forward("small", n.sm, 8)
    gather_end("small", n.small, n.sm, 8)
    for index in range(F):
        n.vec[:, index * 128 : (index + 1) * 128] = n.sm[index * 8 : (index + 1) * 8, :]
    swap_end(0, lambda m: n.tok.at[m], hid_at)
    swap_end(1, info_src, info_own)
    swap_start(2, lambda m: n.cot.at[m], ct_at)

    def first_norm(at, rows_at):
        h = n.hid[rows_at, :].astype(F32)
        scale = lax.rsqrt(jnp.mean(h * h, axis=-1, keepdims=True) + eps)
        n.normed[pl.ds(pl.multiple_of(r * own + at, tall), tall), :] = (
            h * scale * n.vec[1:2, :]
        ).astype(BF)
        logit = jnp.sum(h * n.vec[0:1, :], axis=-1, keepdims=True)
        n.gate[rows_at, :] = jnp.broadcast_to(1.0 / (1.0 + jnp.exp(-logit)), (tall, 128))

    by_own(first_norm)
    share_start("normed", n.normed, own)
    share_start("info", n.infos, MB * 8)
    out_start(n.wo, n.woa)
    gather_start("wu", n.wu, n.wua, piece)
    gather_start("wd", n.wd, n.wda, piece)
    gather_forward("wq", n.wqa, piece)
    share_forward("info", n.infos, MB * 8)
    share_forward("normed", n.normed, own)
    share_end("info", n.infos, MB * 8)
    share_end("normed", n.normed, own)
    gather_end("wq", n.wq, n.wqa, piece)

    def project(index):
        at = aligned(index, own)
        n.proj[at, :] = dot(n.normed[at, :], n.wqa[...], (1, 0)).astype(BF)

    loop(R, project)

    swap_end(2, lambda m: n.cot.at[m], ct_at)

    def mlp_cotangent(at, rows_at):
        gc = n.gate[rows_at, 0:1] * n.ct[rows_at, :].astype(F32)
        n.gmlp[pl.ds(pl.multiple_of(r * own + at, tall), tall), :] = gc.astype(BF)

    by_own(mlp_cotangent)
    out_forward(n.woa)

    tree, pairs = g.tree, g.heads // 2
    scale = 64 ** (-0.5)
    low_lane = lax.broadcasted_iota(jnp.int32, (tree, 128), 1) < 64

    def half_of(value, half):
        keep = low_lane if half == 0 else jnp.logical_not(low_lane)
        return jnp.where(keep, value, jnp.zeros_like(value))

    def join(first, second):
        return jnp.where(low_lane, first, second)

    def make_bias(t):
        blocks = []
        for index in range(S * MB // 2):
            at = pl.multiple_of((t * S * MB + index * 2) * 8, 8)
            blocks.append(n.infos[pl.ds(at, 8), :] + n.infos[pl.ds(at + 8, 8), :])
        keys = jnp.concatenate(blocks, axis=1)
        asked = jnp.transpose(keys)
        near = keys[0:1, :] == asked[:, 0:1]
        near = near | (keys[0:1, :] == asked[:, 1:2])
        near = near | (keys[0:1, :] == asked[:, 2:3])
        near = near & (keys[3:4, :] <= asked[:, 3:4])
        n.bias[...] = jnp.where(near, 0.0, -1e30)

    def columns(part, pair):
        return pl.ds(part * g.ac + pair * 128, 128)

    def attend(t):
        make_bias(t)
        at = aligned(t, tree)
        for pair in range(pairs):
            q = n.proj[at, columns(0, pair)]
            k = n.proj[at, columns(1, pair)]
            v = n.proj[at, columns(2, pair)]
            made = []
            for half in range(2):
                s = dot(half_of(q, half), k, (1, 1)) * scale + n.bias[...]
                top = jnp.max(s, axis=-1, keepdims=True)
                e = jnp.exp(s - top)
                total = jnp.sum(e, axis=-1, keepdims=True)
                made.append(dot((e * (1.0 / total)).astype(BF), v, (1, 0)))
                head = pair * 2 + half
                n.lse[at, head : head + 1] = top + jnp.log(total)
            n.att[at, pl.ds(pair * 128, 128)] = join(*made).astype(BF)

    loop(g.trees, attend)
    out_end(n.wo, n.woa)

    def branch_part(owner, cols):
        return dot(n.att[aligned(owner, own), :], n.woa[:, cols], (1, 0))

    sum_start(0, 0, branch_part, n.branch)
    share_start("gmlp", n.gmlp, own)
    gather_forward("wu", n.wua, piece)
    sum_end(0, 0)

    def second_norm(at, rows_at):
        br = n.branch[rows_at, :] + came(0, at)
        n.branch[rows_at, :] = br
        mid = n.hid[rows_at, :].astype(F32) + br
        inv = lax.rsqrt(jnp.mean(mid * mid, axis=-1, keepdims=True) + eps)
        n.norm2[pl.ds(pl.multiple_of(r * own + at, tall), tall), :] = (
            mid * inv * n.vec[2:3, :]
        ).astype(BF)

    by_own(second_norm)
    share_start("norm2", n.norm2, own)
    gather_forward("wd", n.wda, piece)
    share_forward("gmlp", n.gmlp, own)
    share_end("gmlp", n.gmlp, own)
    gather_end("wu", n.wu, n.wua, piece)
    share_forward("norm2", n.norm2, own)
    share_end("norm2", n.norm2, own)

    tiles = g.fc // wide

    def mlp_up(index):
        at = aligned(index // tiles, own)
        cols = aligned(lax.rem(index, tiles), wide)
        u = dot(n.norm2[at, :], n.wua[:, cols], (1, 0))
        square = u * u
        t = jnp.tanh(GELU_A * (u + GELU_B * square * u))
        n.act[at, cols] = (0.5 * u * (1.0 + t)).astype(BF)
        n.dact[at, cols] = 0.5 * (1.0 + t) + (0.5 * GELU_A) * u * (1.0 - t * t) * (
            1.0 + (3.0 * GELU_B) * square
        )

    loop(R * tiles, mlp_up)
    gather_end("wd", n.wd, n.wda, piece)

    def mlp_back(index):
        at = aligned(index // tiles, own)
        cols = aligned(lax.rem(index, tiles), wide)
        ga = dot(n.gmlp[at, :], n.wda[cols, :], (1, 1))
        n.gup[at, cols] = (ga * n.dact[at, cols]).astype(BF)

    loop(R * tiles, mlp_back)

    def norm2_part(owner, cols):
        return dot(n.gup[aligned(owner, own), :], n.wua[cols, :], (1, 1))

    sum_start(1, 1, norm2_part, n.gmid)

    def weight_grad(left, right, target, count):
        def one(index):
            cols = aligned(index, 256)
            target[cols, :] = dot(left[:, cols], right[...], (0, 0)).astype(BF)

        loop(count // 256, one)

    weight_grad(n.act, n.gmlp, n.gd, g.fc)
    grad_start("d", n.gd, piece)
    weight_grad(n.norm2, n.gup, n.gu, d)
    grad_start("u", n.gu, piece)
    sum_end(1, 1)
    n.gsum[...] = jnp.zeros_like(n.gsum)

    def second_back(at, rows_at):
        dy = n.gmid[rows_at, :] + came(1, at)
        mid = n.hid[rows_at, :].astype(F32) + n.branch[rows_at, :]
        inv = lax.rsqrt(jnp.mean(mid * mid, axis=-1, keepdims=True) + eps)
        n.gsum[2:3, :] = n.gsum[2:3, :] + jnp.sum(dy * mid * inv, axis=0, keepdims=True)
        t = dy * n.vec[2:3, :]
        along = jnp.sum(mid * t, axis=-1, keepdims=True) * (inv * inv * inv * (1.0 / d))
        gm = inv * t - mid * along
        n.gmid[rows_at, :] = gm
        gc = n.gate[rows_at, 0:1] * n.ct[rows_at, :].astype(F32)
        n.gbr[pl.ds(pl.multiple_of(r * own + at, tall), tall), :] = (gc + gm).astype(BF)

    by_own(second_back)
    share_start("gbr", n.gbr, own)

    def change_part(owner, cols):
        return dot(n.act[aligned(owner, own), :], n.wda[:, cols], (1, 0))

    sum_start(2, 0, change_part, n.acc)
    grad_forward("d", n.gd, piece)
    share_forward("gbr", n.gbr, own)
    share_end("gbr", n.gbr, own)

    def attention_cotangent(index):
        at = aligned(index, own)
        n.gatt[at, :] = dot(n.gbr[at, :], n.woa[...], (1, 1)).astype(BF)

    loop(R, attention_cotangent)
    weight_grad(n.att, n.gbr, n.go, g.ac)
    grad_start("o", n.go, piece)

    def attend_back(t):
        make_bias(t)
        at = aligned(t, tree)
        for pair in range(pairs):
            q = n.proj[at, columns(0, pair)]
            k = n.proj[at, columns(1, pair)]
            v = n.proj[at, columns(2, pair)]
            da = n.gatt[at, pl.ds(pair * 128, 128)]
            dq, dk, dv = [], [], []
            for half in range(2):
                head = pair * 2 + half
                s = dot(half_of(q, half), k, (1, 1)) * scale + n.bias[...]
                p = jnp.exp(s - n.lse[at, head : head + 1])
                dp = dot(half_of(da, half), v, (1, 1))
                delta = jnp.sum(p * dp, axis=-1, keepdims=True)
                ds = (p * (dp - delta)).astype(BF)
                dq.append(dot(ds, k, (1, 0)))
                dk.append(dot(ds, q, (0, 0)))
                dv.append(dot(p.astype(BF), da, (0, 0)))
            n.gproj[at, columns(0, pair)] = (join(*dq) * scale).astype(BF)
            n.gproj[at, columns(1, pair)] = (join(*dk) * scale).astype(BF)
            n.gproj[at, columns(2, pair)] = join(*dv).astype(BF)

    loop(g.trees, attend_back)

    sum_end(2, 0)

    def new_rows(at, rows_at):
        change = n.branch[rows_at, :] + n.acc[rows_at, :] + came(0, at)
        h = n.hid[rows_at, :].astype(F32)
        gate = n.gate[rows_at, 0:1]
        n.nrow[rows_at, :] = (h + gate * change).astype(BF)
        logit = jnp.sum(n.ct[rows_at, :].astype(F32) * change, axis=-1, keepdims=True)
        logit = logit * gate * (1.0 - gate)
        n.glog[rows_at, :] = jnp.broadcast_to(logit, (tall, 128))
        n.gsum[0:1, :] = n.gsum[0:1, :] + jnp.sum(logit * h, axis=0, keepdims=True)

    by_own(new_rows)

    def normed_part(owner, cols):
        return dot(n.gproj[aligned(owner, own), :], n.wqa[cols, :], (1, 1))

    sum_start(3, 1, normed_part, n.acc)
    weight_grad(n.normed, n.gproj, n.gq, d)
    grad_start("q", n.gq, piece)
    grad_forward("u", n.gu, piece)
    grad_forward("o", n.go, piece)
    grad_own("d", n.gd, piece)

    def new_at(i):
        return n.nrow.at[aligned(i, cap)]

    swap_start(4, new_at, lambda m: n.new_out.at[m])
    sum_end(3, 1)

    def first_back(at, rows_at):
        dy = n.acc[rows_at, :] + came(1, at)
        h = n.hid[rows_at, :].astype(F32)
        inv = lax.rsqrt(jnp.mean(h * h, axis=-1, keepdims=True) + eps)
        n.gsum[1:2, :] = n.gsum[1:2, :] + jnp.sum(dy * h * inv, axis=0, keepdims=True)
        t = dy * n.vec[1:2, :]
        along = jnp.sum(h * t, axis=-1, keepdims=True) * (inv * inv * inv * (1.0 / d))
        total = n.ct[rows_at, :].astype(F32) + n.gmid[rows_at, :] + (inv * t - h * along)
        total = total + n.glog[rows_at, 0:1] * n.vec[0:1, :]
        n.grow[rows_at, :] = total.astype(BF)

    by_own(first_back)

    def grow_at(i):
        return n.grow.at[aligned(i, cap)]

    swap_start(3, grow_at, lambda m: n.grad_out.at[m])
    for index in range(F):
        n.gsp[index * 8 : (index + 1) * 8, :] = n.gsum[:, index * 128 : (index + 1) * 128]
    grad_start("s", n.gsp, 8)
    grad_forward("q", n.gq, piece)
    grad_forward("s", n.gsp, 8)
    grad_own("u", n.gu, piece)

    @pl.when(is_source)
    def _():
        grad_wait("o", piece)
        grad_total("o", n.go, b * piece, piece, n.gro, 0)

    ax, ac = a // 2, lax.rem(a, 2)
    for step in range(X - 1):
        send(n.gro, n.gro, n.ro_xs.at[step], n.ro_xr.at[0], xpeer(step) * 2 + c, f, is_source)
    send(n.gro, n.gro, n.ro_ss.at[0], n.ro_sr.at[0], sib, f, is_source)
    grad_own("q", n.gq, piece)
    grad_wait("s", 8)
    grad_total("s", n.gsp, f * 8, 8, n.gs_mine.at[0], 0)
    send(n.gs_mine.at[0], n.gs_pair.at[0], n.pair_s.at[0], n.pair_r.at[0], sib, f)

    off_x = (c == ac) & (x != ax)

    @pl.when(off_x)
    def _():
        got(n.gro, n.ro_xr.at[0])

    send(n.gro, n.gro, n.ro_ss.at[1], n.ro_sr.at[0], sib, f, off_x)
    share_forward("rd", n.grd, piece)
    share_end("rd", n.grd, piece)

    used = [None, None]
    turn = [0]

    def emit(src, base, target, cols):
        slot = turn[0] % 2
        turn[0] += 1
        if used[slot] is not None:
            used[slot]()

        def one(index):
            at = pl.ds(pl.multiple_of(index * 32, 32), 32)
            of = pl.ds(base + index * 32, 32)
            n.stage[slot, at, 0:cols] = src[of, :].astype(F32)

        loop(piece // 32, one)
        copy = pltpu.make_async_copy(
            n.stage.at[slot, :, pl.ds(0, cols)], target, n.stage_sem.at[slot]
        )
        copy.start()
        used[slot] = copy.wait

    for index in range(R):
        emit(n.grd, index * piece, n.gd_out.at[index], d)
    share_forward("ru", n.gru, piece)
    share_end("ru", n.gru, piece)
    for index in range(R):
        emit(n.gru, index * piece, n.gu_out.at[index], g.fc)

    @pl.when((c != ac))
    def _():
        got(n.gro, n.ro_sr.at[0])

    emit(n.gro, 0, n.go_out, d)
    got(n.gs_pair.at[0], n.pair_r.at[0])
    n.gs_mine[1] = n.gs_mine[0] + n.gs_pair[0]
    send(n.gs_mine.at[1], n.gs_pair.at[1], n.pair_s.at[1], n.pair_r.at[1], xpeer(0) * 2 + c, f)
    share_forward("rq", n.grq, piece)
    share_end("rq", n.grq, piece)
    for index in range(R):
        emit(n.grq, index * piece, n.gq_out.at[index], g.qc)
    got(n.gs_pair.at[1], n.pair_r.at[1])
    n.gs_out[...] = n.gs_mine[1] + n.gs_pair[1]
    swap_end(4, new_at, lambda m: n.new_out.at[m])
    swap_end(3, grow_at, lambda m: n.grad_out.at[m])
    for slot in range(2):
        used[slot]()
    for tag in list(pending):
        drain(tag)


def group_shards(tokens, cotangent, path, chosen, router, gains, w_qkv, w_out, w_up, w_down):
    R, F = lax.axis_size("rep"), lax.axis_size("fsdp")
    MB, tok_count, d = tokens.shape
    cap = chosen.shape[1]
    S = F // MB
    hidden = w_up.shape[1]
    g = types.SimpleNamespace(
        R=R,
        F=F,
        S=S,
        A=MB,
        X=R // 2,
        MB=MB,
        cap=cap,
        d=d,
        own=MB * cap,
        rows=R * MB * cap,
        tree=S * MB * cap,
        trees=R // S,
        heads=HEADS // R,
        qc=3 * d // R,
        ac=d // R,
        fc=hidden // R,
    )
    g.items = (
        ("q", F, g.qc, BF),
        ("u", F, g.fc, BF),
        ("d", F, d, BF),
        ("o", S, d, BF),
        ("s", F, 128, F32),
    )
    piece = d // F
    r, f = lax.axis_index("rep"), lax.axis_index("fsdp")

    def pick(array):
        return jax.vmap(lambda rows, at: rows[at])(array, chosen)

    def slice_of(array, axis):
        return lax.dynamic_index_in_dim(array, r, axis, keepdims=False)

    wq = slice_of(w_qkv.reshape(piece, 3, R, g.ac), 2).reshape(piece, g.qc)
    wu = slice_of(w_up.reshape(piece, F, R, piece), 2).reshape(piece, g.fc)
    wd = slice_of(w_down.reshape(R, piece, d), 0)
    own_path = jnp.swapaxes(pick(path), 1, 2)
    place = (f * tok_count + chosen)[:, None, :]
    info = jnp.concatenate([own_path, place, jnp.zeros((MB, 4, cap), jnp.int32)], axis=1)
    info = info.astype(F32)
    blank = jnp.zeros_like(info)
    info = jnp.where(
        lax.rem(f // S, 2) == 1,
        jnp.concatenate([blank, info], axis=2),
        jnp.concatenate([info, blank], axis=2),
    )
    small = jnp.concatenate([router[None], gains.T, jnp.zeros((5, piece), BF)], axis=0)
    operands = {
        "tok": pick(tokens),
        "cot": pick(cotangent),
        "info": info,
        "small": small.astype(F32),
        "wq": wq,
        "wo": w_out,
        "wu": wu,
        "wd": wd,
    }
    results = {
        "new_out": ((MB, cap, d), BF),
        "grad_out": ((MB, cap, d), BF),
        "gq_out": ((R, piece, g.qc), F32),
        "gu_out": ((R, piece, g.fc), F32),
        "gd_out": ((R, piece, d), F32),
        "go_out": ((piece, d), F32),
        "gs_out": ((8, 128), F32),
    }
    vmem, sems = scratch_shapes(g)
    names = list(operands) + list(results) + list(vmem) + list(sems)
    made = pl.pallas_call(
        functools.partial(block_kernel, g, names),
        out_shape=[jax.ShapeDtypeStruct(*kind) for kind in results.values()],
        in_specs=[pl.BlockSpec(memory_space=pl.ANY)] * len(operands),
        out_specs=[
            pl.BlockSpec(memory_space=pltpu.VMEM if name == "gs_out" else pl.ANY)
            for name in results
        ],
        scratch_shapes=[pltpu.VMEM(*kind) for kind in vmem.values()]
        + [pltpu.SemaphoreType.DMA(shape) for shape in sems.values()],
        compiler_params=pltpu.CompilerParams(
            collective_id=0, has_side_effects=True, vmem_limit_bytes=60 * 1024 * 1024
        ),
        name="routed_block",
    )(*operands.values())
    new_rows, grad_rows, gq, gu, gd, go, gs = made

    def put(array, rows):
        return jax.vmap(lambda whole, at, new: whole.at[at].set(new))(
            array, chosen, rows.astype(array.dtype)
        )

    mixed = put(tokens, new_rows)
    grad_tokens = put(cotangent.astype(F32), grad_rows)
    grad_qkv = gq.reshape(R, piece, 3, g.ac).transpose(1, 2, 0, 3).reshape(piece, 3 * d)
    grad_up = gu.reshape(R, piece, F, piece).transpose(1, 2, 0, 3).reshape(piece, hidden)
    return (
        mixed,
        grad_tokens,
        gs[0, :piece],
        gs[1:3, :piece].T,
        grad_qkv,
        go,
        grad_up,
        gd.reshape(R * piece, d),
    )


def plain_norm(matrix, gain_row):
    return matrix * lax.rsqrt(jnp.mean(matrix * matrix, axis=-1, keepdims=True) + eps) * gain_row


def inner(left, right):
    return lax.dot_general(
        left, right, (((0,), (0,)), ((), ())), preferred_element_type=jnp.float32
    )


def by_rows(left, right):
    return lax.dot_general(
        left, right, (((1,), (1,)), ((), ())), preferred_element_type=jnp.float32
    )


def gather_rows(arrays):
    return lax.all_gather(arrays, "fsdp", axis=0, tiled=True)


def scatter_sum(array):
    return lax.psum_scatter(
        array.astype(jnp.bfloat16), "fsdp", scatter_dimension=0, tiled=True
    ).astype(jnp.float32)


def plain_shards(tokens, cotangent, path, chosen, router, gains, w_qkv, w_out, w_up, w_down):
    micro_count, tok_count, model_width = tokens.shape
    slot_count = chosen.shape[1]
    row_count = micro_count * slot_count
    head_dim = model_width // HEADS
    score_scale = head_dim ** (-0.5)
    offset = lax.axis_index("fsdp") * tok_count
    fsdp = lax.axis_size("fsdp")

    def pick(array):
        return jax.vmap(lambda rows, at: rows[at])(array, chosen)

    small = jnp.concatenate([router[:, None], gains], axis=1)
    small_all = gather_rows(small)
    qkv_all = gather_rows(w_qkv)
    out_all = gather_rows(w_out)
    up_all = gather_rows(w_up)
    down_all = gather_rows(w_down)
    router_float = small_all[:, 0].astype(jnp.float32)
    gain_one = small_all[:, 1].astype(jnp.float32)
    gain_two = small_all[:, 2].astype(jnp.float32)

    routed = pick(tokens).reshape(row_count, model_width)
    hidden = routed.astype(jnp.float32)
    gate_rate = jax.nn.sigmoid(
        jnp.dot(routed, small_all[:, 0], preferred_element_type=jnp.float32)
    )
    normed = plain_norm(hidden, gain_one).astype(jnp.bfloat16)
    projected = jnp.dot(normed, qkv_all, preferred_element_type=jnp.float32).astype(jnp.bfloat16)
    queries = projected[:, :model_width].reshape(micro_count, slot_count, HEADS, head_dim)
    own_path = pick(path)
    own_place = offset + chosen
    key_info = jnp.concatenate([own_path[:, :, :1], own_place[:, :, None]], axis=2)
    gathered = lax.all_gather(
        projected[:, model_width:].reshape(micro_count, slot_count, 2 * model_width), "fsdp"
    )
    info_all = lax.all_gather(key_info, "fsdp")
    key_count = fsdp * slot_count
    gathered = jnp.swapaxes(gathered, 0, 1).reshape(micro_count, key_count, 2, HEADS, head_dim)
    info_all = jnp.swapaxes(info_all, 0, 1).reshape(micro_count, key_count, 2)
    key_rows = gathered[:, :, 0]
    value_rows = gathered[:, :, 1]
    key_seg = info_all[:, None, :, 0]
    visible = (
        (key_seg == own_path[:, :, 0:1])
        | (key_seg == own_path[:, :, 1:2])
        | (key_seg == own_path[:, :, 2:3])
    ) & (info_all[:, None, :, 1] <= own_place[:, :, None])
    visible = visible[:, None]

    def product(form, left, right):
        return jnp.einsum(form, left, right, preferred_element_type=jnp.float32)

    scores = product("mqhd,mkhd->mhqk", queries, key_rows) * score_scale
    scores = jnp.where(visible, scores, -1e30)
    row_max = jnp.max(scores, axis=-1, keepdims=True)
    exponent = jnp.where(visible, jnp.exp(scores - row_max), 0.0)
    row_total = jnp.sum(exponent, axis=-1, keepdims=True)
    soft_prob = exponent / row_total
    probs = soft_prob.astype(jnp.bfloat16)
    attention = product("mhqk,mkhd->mqhd", probs, value_rows)
    attention = attention.reshape(row_count, model_width).astype(jnp.bfloat16)
    branch = jnp.dot(attention, out_all, preferred_element_type=jnp.float32)
    middle = hidden + branch
    normed_two = plain_norm(middle, gain_two).astype(jnp.bfloat16)
    up_proj = jnp.dot(normed_two, up_all, preferred_element_type=jnp.float32)
    activated = jax.nn.gelu(up_proj).astype(jnp.bfloat16)
    change = branch + jnp.dot(activated, down_all, preferred_element_type=jnp.float32)
    new_rows = hidden + gate_rate[:, None] * change

    def put(array, rows):
        rows = rows.reshape(micro_count, slot_count, model_width).astype(array.dtype)
        return jax.vmap(lambda whole, at, new: whole.at[at].set(new))(array, chosen, rows)

    mixed = put(tokens, new_rows)

    grad_rows = pick(cotangent).reshape(row_count, model_width).astype(jnp.float32)
    grad_change = gate_rate[:, None] * grad_rows
    grad_logit = jnp.sum(grad_rows * change, axis=-1) * gate_rate * (1.0 - gate_rate)
    grad_mlp = grad_change.astype(jnp.bfloat16)
    grad_down = scatter_sum(inner(activated, grad_mlp))
    grad_act = by_rows(grad_mlp, down_all)
    gelu_value, gelu_back = jax.vjp(jax.nn.gelu, up_proj)
    grad_up_proj = gelu_back(grad_act)[0].astype(jnp.bfloat16)
    grad_up = scatter_sum(inner(normed_two, grad_up_proj))
    grad_normed_two = by_rows(grad_up_proj, up_all)
    norm_value, norm_back_two = jax.vjp(plain_norm, middle, gain_two)
    grad_middle, grad_gain_two = norm_back_two(grad_normed_two)
    grad_branch = (grad_change + grad_middle).astype(jnp.bfloat16)
    grad_outw = scatter_sum(inner(attention, grad_branch))
    grad_attention = by_rows(grad_branch, out_all).astype(jnp.bfloat16)
    grad_heads = grad_attention.reshape(micro_count, slot_count, HEADS, head_dim)
    prob_grad = product("mqhd,mkhd->mhqk", grad_heads, value_rows)
    delta = jnp.sum(soft_prob * prob_grad, axis=-1, keepdims=True)
    grad_scores = (soft_prob * (prob_grad - delta)).astype(jnp.bfloat16)
    grad_query = product("mhqk,mkhd->mqhd", grad_scores, key_rows) * score_scale
    grad_key = product("mhqk,mqhd->mkhd", grad_scores, queries) * score_scale
    grad_value = product("mhqk,mqhd->mkhd", probs, grad_heads)
    grad_kv = jnp.stack([grad_key, grad_value], axis=2).reshape(
        micro_count, fsdp, slot_count, 2 * model_width
    )
    grad_kv = lax.psum_scatter(
        jnp.swapaxes(grad_kv, 0, 1).astype(jnp.bfloat16).reshape(-1, 2 * model_width),
        "fsdp",
        scatter_dimension=0,
        tiled=True,
    )
    grad_projected = jnp.concatenate(
        [
            grad_query.reshape(row_count, model_width).astype(jnp.bfloat16),
            grad_kv.reshape(row_count, 2 * model_width),
        ],
        axis=1,
    )
    grad_qkvw = scatter_sum(inner(normed, grad_projected))
    grad_normed = by_rows(grad_projected, qkv_all)
    norm_value_one, norm_back_one = jax.vjp(plain_norm, hidden, gain_one)
    grad_hidden_norm, grad_gain_one = norm_back_one(grad_normed)
    grad_hidden = (
        grad_rows + grad_middle + grad_hidden_norm + grad_logit[:, None] * router_float[None, :]
    )
    grad_tokens = put(cotangent.astype(jnp.float32), grad_hidden)
    grad_routerw = jnp.sum(grad_logit[:, None] * hidden, axis=0)
    grad_small = jnp.stack([grad_routerw, grad_gain_one, grad_gain_two], axis=1)
    grad_small = lax.psum_scatter(grad_small, "fsdp", scatter_dimension=0, tiled=True)
    summed = lax.psum((grad_small, grad_qkvw, grad_outw, grad_up, grad_down), "rep")
    return (mixed, grad_tokens, summed[0][:, 0], summed[0][:, 1:]) + tuple(summed[1:])


def solution(mesh):
    rows = P(None, ("rep", "fsdp"), None)
    weight = P("fsdp", None)

    def whole(*args):
        grouped = fits(mesh, args[0], args[3], args[8])
        return jax.shard_map(
            group_shards if grouped else plain_shards,
            mesh=mesh,
            in_specs=(
                rows,
                rows,
                rows,
                P(None, ("rep", "fsdp")),
                P("fsdp"),
                weight,
                weight,
                weight,
                weight,
                weight,
            ),
            out_specs=(rows, rows, P("fsdp"), weight, weight, weight, weight, weight),
            check_vma=False,
        )(*args)

    return whole
```

```python
import functools
import math
import types

import jax
import jax.numpy as jnp
from jax import lax
from jax.experimental import pallas as pl
from jax.experimental.pallas import tpu as pltpu
from jax.sharding import PartitionSpec as P

HEADS = 16


eps = 1e-05
MESH = pl.DeviceIdType.MESH
BF = jnp.bfloat16
F32 = jnp.float32
GELU_A = math.sqrt(2.0 / math.pi)
GELU_B = 0.044715


def dot(left, right, contract):
    return lax.dot_general(
        left, right, (((contract[0],), (contract[1],)), ((), ())), preferred_element_type=F32
    )


def aligned(index, size):
    return pl.ds(pl.multiple_of(index * size, size), size)


def loop(count, body):
    def step(index, carry):
        body(index)
        return carry

    lax.fori_loop(0, count, step, 0)


def fits(mesh, tokens, chosen, w_up):
    rep, fsdp = mesh.shape["rep"], mesh.shape["fsdp"]
    micro, width, hidden = tokens.shape[0], tokens.shape[2], w_up.shape[1]
    if fsdp % micro or rep % 2:
        return False
    inner_count = fsdp // micro
    return (
        rep % inner_count == 0
        and rep == micro
        and fsdp == rep * inner_count
        and width == fsdp * 128
        and hidden == fsdp * rep * 128
        and HEADS % (2 * rep) == 0
        and width // HEADS == 64
        and chosen.shape[1] // (rep * fsdp) == 64
        and tokens.shape[1] * micro // (rep * fsdp) == 2 * rep * micro * 64
    )


def scratch_shapes(g):
    own, rows, d = g.own, g.rows, g.d
    vmem = {
        "hid": ((own, d), BF),
        "ct": ((own, d), BF),
        "infos": ((g.R * g.MB * 8, 128), F32),
        "sm": ((g.F * 8, 128), F32),
        "info": ((g.MB, 8, 128), F32),
        "vec": ((8, d), F32),
        "wqa": ((d, g.qc), BF),
        "woa": ((g.ac, d), BF),
        "wua": ((d, g.fc), BF),
        "wda": ((g.fc, d), BF),
        "normed": ((rows, d), BF),
        "norm2": ((rows, d), BF),
        "proj": ((rows, g.qc), BF),
        "att": ((rows, g.ac), BF),
        "gatt": ((rows, g.ac), BF),
        "gproj": ((rows, g.qc), BF),
        "lse": ((rows, 128), F32),
        "bias": ((g.tree, g.tree), F32),
        "pair_a": ((2 * rows, g.fc), BF),
        "pair_b": ((2 * rows, d), BF),
        "dact": ((rows, g.fc), F32),
        "gate": ((own, 128), F32),
        "glog": ((own, 128), F32),
        "branch": ((own, d), F32),
        "acc": ((own, d), F32),
        "gmid": ((own, d), F32),
        "ends": ((2 * own, d), BF),
        "to_sib": ((2, g.X * own, d), BF),
        "of_sib": ((2, g.X * own, d), BF),
        "to_x": ((2, (g.X - 1) * own, d), BF),
        "of_x": ((2, (g.X - 1) * own, d), BF),
        "gsum": ((8, d), F32),
        "gsp": ((g.F * 8, 128), F32),
        "gs_pair": ((2, 8, 128), F32),
        "gs_mine": ((2, 8, 128), F32),
    }
    piece = d // g.F
    for name, count, cols, kind in g.items:
        height = 8 if name == "s" else piece
        if name != "s":
            vmem["g" + name] = ((count * height, cols), kind)
        vmem["gi" + name] = (((count // g.S) * height, cols), kind)
        vmem["go" + name] = (((g.A - 1) * height, cols), kind)
        if name != "s":
            vmem["gr" + name] = (((g.R if name != "o" else 1) * height, cols), kind)
    sems = {
        "a2a_s": (5, g.MB),
        "a2a_r": (5, g.MB),
        "tok_l": (2, g.MB),
        "out_l": (4, g.R),
    }
    for name in ("small", "wq", "wo", "wu", "wd"):
        sems[name + "_l"] = (g.F,)
        sems[name + "_os"] = (g.A - 1,)
        sems[name + "_or"] = (g.A - 1,)
        sems[name + "_is"] = (g.A,)
        sems[name + "_ir"] = (g.A,)
    for name in ("info", "normed", "gmlp", "norm2", "gbr", "rq", "ru", "rd", "ro"):
        sems[name + "_xs"] = (g.X - 1,)
        sems[name + "_xr"] = (g.X - 1,)
        sems[name + "_ss"] = (g.X,)
        sems[name + "_sr"] = (g.X,)
    for index in range(4):
        name = "sum%d" % index
        sems[name + "_xs"] = (g.X - 1,)
        sems[name + "_xr"] = (g.X - 1,)
        sems[name + "_ss"] = (g.X,)
        sems[name + "_sr"] = (g.X,)
    for name, count, cols, kind in g.items:
        sems["g" + name + "_is"] = (g.A,)
        sems["g" + name + "_ir"] = (g.A,)
        sems["g" + name + "_os"] = (g.A - 1,)
        sems["g" + name + "_or"] = (g.A - 1,)
    sems["pair_s"] = (2,)
    sems["pair_r"] = (2,)
    return vmem, sems


def block_kernel(g, names, *refs):
    n = types.SimpleNamespace(**dict(zip(names, refs)))
    R, F, S, A, X, MB = g.R, g.F, g.S, g.A, g.X, g.MB
    own, rows, d, cap = g.own, g.rows, g.d, g.cap
    piece = d // F
    r = lax.axis_index("rep")
    f = lax.axis_index("fsdp")
    x, c = r // 2, lax.rem(r, 2)
    a, b = f // S, lax.rem(f, S)
    other_b = lax.rem(b + 1, S)
    sib = x * 2 + 1 - c
    pending = {}
    n.act, n.gup = n.pair_a.at[pl.ds(0, rows)], n.pair_a.at[pl.ds(rows, rows)]
    n.gmlp, n.gbr = n.pair_b.at[pl.ds(0, rows)], n.pair_b.at[pl.ds(rows, rows)]
    n.nrow, n.grow = n.ends.at[pl.ds(0, own)], n.ends.at[pl.ds(own, own)]
    n.picked, n.picked_ct = n.ends, n.norm2
    tok_count = n.tokens.shape[1]

    def token_copy(which, m):
        source, target = (n.tokens, n.pair_a) if which == 0 else (n.cotangent, n.pair_b)
        return pltpu.make_async_copy(
            source.at[m], target.at[pl.ds(m * tok_count, tok_count)], n.tok_l.at[which, m]
        )

    for which in range(2):
        for m in range(MB):
            token_copy(which, m).start()

    def cut_copies(name):
        if name == "wq":
            return [
                pltpu.make_async_copy(
                    n.w_qkv.at[:, pl.ds(pl.multiple_of(part * d + r * g.ac, g.ac), g.ac)],
                    n.wqa.at[aligned(f, piece), pl.ds(part * g.ac, g.ac)],
                    n.wq_l.at[part],
                )
                for part in range(3)
            ]
        if name == "wu":
            return [
                pltpu.make_async_copy(
                    n.w_up.at[:, pl.ds(pl.multiple_of((block * R + r) * 128, 128), 128)],
                    n.wua.at[aligned(f, piece), pl.ds(block * 128, 128)],
                    n.wu_l.at[block],
                )
                for block in range(F)
            ]
        return [
            pltpu.make_async_copy(
                n.w_down.at[aligned(r, piece)], n.wda.at[aligned(f, piece)], n.wd_l.at[0]
            )
        ]

    for name in ("wq", "wu", "wd"):
        for copy in cut_copies(name):
            copy.start()

    def remote(src, dst, ss, rs, rep, fsdp):
        return pltpu.make_async_remote_copy(
            src_ref=src,
            dst_ref=dst,
            send_sem=ss,
            recv_sem=rs,
            device_id={"rep": rep, "fsdp": fsdp},
            device_id_type=MESH,
        )

    def send(src, dst, ss, rs, rep, fsdp, cond=None, tag="end"):
        def start():
            remote(src, dst, ss, rs, rep, fsdp).start()

        def done():
            remote(src, dst, ss, rs, rep, fsdp).wait_send()

        if cond is None:
            start()
            pending.setdefault(tag, []).append(done)
        else:
            pl.when(cond)(start)
            pending.setdefault(tag, []).append(lambda: pl.when(cond)(done))

    def drain(tag):
        for done in pending.pop(tag, []):
            done()

    def got(dst, rs):
        remote(dst, dst, rs, rs, sib, f).wait_recv()

    def xpeer(step):
        return lax.rem(x + 1 + step, X)

    def xfrom(step):
        return lax.rem(x + X - 1 - step, X)

    def outer(step):
        return lax.rem(a + step, A)

    def outer_from(step):
        return lax.rem(a + A - step, A)

    home_rep = (r // S) * S + b

    def home_fsdp(m):
        return m * S + lax.rem(r, S)

    barrier = pltpu.get_barrier_semaphore()

    def greet(rep, fsdp):
        pl.semaphore_signal(
            barrier, inc=1, device_id={"rep": rep, "fsdp": fsdp}, device_id_type=MESH
        )

    for step in range(1, A):
        greet(r, outer(step) * S + b)
    greet(r, a * S + other_b)
    greet(sib, f)
    for step in range(X - 1):
        greet(xpeer(step) * 2 + c, f)
    mine = [(home_fsdp(m) == f) & (home_rep == r) for m in range(MB)]
    for m in range(MB):

        @pl.when(jnp.logical_not(mine[m]))
        def _(m=m):
            greet(home_rep, home_fsdp(m))

    stays = (home_rep == r) & (lax.rem(r, S) == b)
    pl.semaphore_wait(barrier, (A - 1) + 1 + 1 + (X - 1) + MB - stays.astype(jnp.int32))

    def swap_start(which, src_of, dst_of):
        for m in range(MB):
            src, dst = src_of(m), dst_of(a)
            ss, rs = n.a2a_s.at[which, m], n.a2a_r.at[which, a]

            @pl.when(jnp.logical_not(mine[m]))
            def _():
                remote(src, dst, ss, rs, home_rep, home_fsdp(m)).start()

            @pl.when(mine[m])
            def _():
                pltpu.make_async_copy(src, dst, rs).start()

    def swap_end(which, src_of, dst_of):
        for m in range(MB):
            src, dst = src_of(m), dst_of(m)
            ss, rs = n.a2a_s.at[which, m], n.a2a_r.at[which, m]

            @pl.when(jnp.logical_not(mine[m]))
            def _():
                remote(src, dst, ss, rs, home_rep, home_fsdp(m)).wait()

            @pl.when(mine[m])
            def _():
                pltpu.make_async_copy(src, dst, rs).wait()

    def sem(name):
        return getattr(n, name)

    def gather_start(name, buf, height):
        at = aligned(f, height)
        src = buf.at[at]
        for step in range(1, A):
            send(
                src,
                buf.at[at],
                sem(name + "_os").at[step - 1],
                sem(name + "_or").at[step - 1],
                r,
                outer(step) * S + b,
            )
        send(src, buf.at[at], sem(name + "_is").at[0], sem(name + "_ir").at[0], r, a * S + other_b)

    def gather_forward(name, buf, height):
        for step in range(1, A):
            at = buf.at[aligned(outer_from(step) * S + b, height)]
            got(at, sem(name + "_or").at[step - 1])
            send(at, at, sem(name + "_is").at[step], sem(name + "_ir").at[step], r, a * S + other_b)

    def gather_end(name, buf, height):
        for step in range(A):
            at = buf.at[aligned(outer_from(step) * S + other_b, height)]
            got(at, sem(name + "_ir").at[step])

    is_source = a == r

    def out_start(src, buf):
        at = buf.at[aligned(b, piece)]

        @pl.when(is_source)
        def _():
            pltpu.make_async_copy(src, at, n.wo_l.at[0]).start()

        for step in range(1, A):
            send(
                src, at, n.wo_os.at[step - 1], n.wo_or.at[0], r, outer(step) * S + b, is_source
            )
        send(src, at, n.wo_is.at[0], n.wo_ir.at[0], r, a * S + other_b, is_source)

    def out_forward(buf):
        at = buf.at[aligned(b, piece)]

        @pl.when(jnp.logical_not(is_source))
        def _():
            got(at, n.wo_or.at[0])

        send(
            at, at, n.wo_is.at[1], n.wo_ir.at[0], r, a * S + other_b, jnp.logical_not(is_source)
        )

    def out_end(src, buf):
        @pl.when(is_source)
        def _():
            pltpu.make_async_copy(src, buf.at[aligned(b, piece)], n.wo_l.at[0]).wait()

        got(buf.at[aligned(other_b, piece)], n.wo_ir.at[0])

    def share_start(name, buf, height):
        at = buf.at[aligned(r, height)]
        for step in range(X - 1):
            send(
                at,
                at,
                sem(name + "_xs").at[step],
                sem(name + "_xr").at[step],
                xpeer(step) * 2 + c,
                f,
            )
        send(at, at, sem(name + "_ss").at[0], sem(name + "_sr").at[0], sib, f)

    def share_forward(name, buf, height):
        for step in range(X - 1):
            at = buf.at[aligned(xfrom(step) * 2 + c, height)]
            got(at, sem(name + "_xr").at[step])
            send(at, at, sem(name + "_ss").at[1 + step], sem(name + "_sr").at[1 + step], sib, f)

    def share_end(name, buf, height):
        got(buf.at[aligned(sib, height)], sem(name + "_sr").at[0])
        for step in range(X - 1):
            at = buf.at[aligned(xfrom(step) * 2 + 1 - c, height)]
            got(at, sem(name + "_sr").at[1 + step])

    wide = 256

    def sum_start(index, slot, partial, acc):
        name = "sum%d" % index
        to_sib, of_sib = n.to_sib.at[slot], n.of_sib.at[slot]
        to_x, of_x = n.to_x.at[slot], n.of_x.at[slot]
        drain("slot%d" % slot)
        order = [xpeer(step) for step in range(X - 1)] + [x]
        for step, xo in enumerate(order):
            at = pl.ds(step * own, own)

            def one(tile, xo=xo, at=at):
                cols = aligned(tile, wide)
                to_sib[at, cols] = partial(xo * 2 + 1 - c, cols).astype(BF)

            loop(d // wide, one)
            send(
                to_sib.at[at],
                of_sib.at[at],
                sem(name + "_ss").at[step],
                sem(name + "_sr").at[step],
                sib,
                f,
                tag="slot%d" % slot,
            )
        for step, xo in enumerate(order):
            at = pl.ds(step * own, own)
            got(of_sib.at[at], sem(name + "_sr").at[step])
            last = step == X - 1

            def one(tile, xo=xo, at=at, last=last):
                cols = aligned(tile, wide)
                total = partial(xo * 2 + c, cols) + of_sib[at, cols].astype(F32)
                if last:
                    acc[:, cols] = total
                else:
                    to_x[at, cols] = total.astype(BF)

            loop(d // wide, one)
            if not last:
                send(
                    to_x.at[at],
                    of_x.at[at],
                    sem(name + "_xs").at[step],
                    sem(name + "_xr").at[step],
                    xo * 2 + c,
                    f,
                    tag="slot%d" % slot,
                )

    def sum_end(index, slot):
        of_x = n.of_x.at[slot]
        for step in range(X - 1):
            got(of_x.at[pl.ds(step * own, own)], sem("sum%d_xr" % index).at[step])

    def came(slot, at):
        total = None
        for step in range(X - 1):
            part = n.of_x[slot, pl.ds(step * own + at, tall), :].astype(F32)
            total = part if total is None else total + part
        return total

    tall = 32

    def by_own(body):
        def one(index):
            at = pl.multiple_of(index * tall, tall)
            body(at, pl.ds(at, tall))

        loop(own // tall, one)

    def grad_start(name, buf, height):
        out = name == "o"
        inbox = sem("gi" + name)
        for step in range(1 if out else A):
            to_a = r if out else outer(step + 1)
            src = buf.at[aligned((0 if out else to_a * S) + other_b, height)]
            send(
                src,
                inbox.at[pl.ds(step * height, height)],
                sem("g" + name + "_is").at[step],
                sem("g" + name + "_ir").at[step],
                r,
                a * S + other_b,
            )

    def add_into(dst, base, inbox, start, height):
        small = min(height, 32)

        def one(index):
            at = pl.ds(pl.multiple_of(base + index * small, small), small)
            of = pl.ds(pl.multiple_of(start + index * small, small), small)
            dst[at, :] = (dst[at, :].astype(F32) + inbox[of, :].astype(F32)).astype(dst.dtype)

        loop(height // small, one)

    def grad_forward(name, buf, height):
        out = name == "o"
        inbox, outbox = sem("gi" + name), sem("go" + name)
        for step in range(1 if out else A):
            to_a = r if out else outer(step + 1)
            base = ((0 if out else to_a * S) + b) * height
            got(inbox.at[pl.ds(step * height, height)], sem("g" + name + "_ir").at[step])
            add_into(buf, base, inbox, step * height, height)
            if out:
                slot = lax.rem(r + A - a - 1, A)
                slot = jnp.where(is_source, 0, slot)
                send(
                    buf.at[pl.ds(pl.multiple_of(base, height), height)],
                    outbox.at[aligned(slot, height)],
                    n.go_os.at[0],
                    n.go_or.at[slot],
                    r,
                    r * S + b,
                    jnp.logical_not(is_source),
                )
            elif step < A - 1:
                send(
                    buf.at[pl.ds(pl.multiple_of(base, height), height)],
                    outbox.at[pl.ds(step * height, height)],
                    sem("g" + name + "_os").at[step],
                    sem("g" + name + "_or").at[step],
                    r,
                    to_a * S + b,
                )

    def grad_wait(name, height):
        for step in range(A - 1):
            got(
                sem("go" + name).at[pl.ds(step * height, height)],
                sem("g" + name + "_or").at[step],
            )

    def grad_total(name, buf, base, height, target, target_base):
        outbox = sem("go" + name)
        small = min(height, 32)

        def one(index):
            off = index * small
            total = buf[pl.ds(pl.multiple_of(base + off, small), small), :].astype(F32)
            for step in range(A - 1):
                at = pl.ds(pl.multiple_of(step * height + off, small), small)
                total = total + outbox[at, :].astype(F32)
            at = pl.ds(pl.multiple_of(target_base + off, small), small)
            target[at, :] = total.astype(target.dtype)

        loop(height // small, one)

    def grad_own(name, buf, height):
        grad_wait(name, height)
        grad_total(name, buf, f * height, height, sem("gr" + name), r * height)
        share_start("r" + name, sem("gr" + name), height)

    def hid_at(i):
        return n.hid.at[aligned(i, cap)]

    def ct_at(i):
        return n.ct.at[aligned(i, cap)]

    def info_src(i):
        return n.info.at[i]

    def info_own(i):
        return n.infos.at[aligned(r * MB + i, 8)]

    def info_home(i):
        return n.infos.at[aligned(home_rep * MB + i, 8)]

    odd = lax.rem(a, 2)
    lane_token = lax.broadcasted_iota(jnp.int32, (tok_count, 128), 0)

    def hot_of(m):
        return (lane_token == n.chosen[m]).astype(F32).astype(BF)

    def tok_at(m):
        return n.picked.at[pl.ds(pl.multiple_of(m * 128 + odd * cap, cap), cap)]

    def cot_at(m):
        return n.picked_ct.at[pl.ds(pl.multiple_of(m * 128 + odd * cap, cap), cap)]

    n.sm[aligned(f, 8), :] = n.small[...]
    gather_start("small", n.sm, 8)
    for m in range(MB):
        hot = hot_of(m)
        token_copy(0, m).wait()
        n.picked[m * 128 : (m + 1) * 128, :] = dot(
            hot, n.pair_a[m * tok_count : (m + 1) * tok_count, :], (0, 0)
        ).astype(BF)
        lines = jnp.concatenate([n.path[line, m : m + 1, :] for line in range(3)], axis=0)
        n.info[m, 0:3, :] = dot(lines.astype(F32).astype(BF), hot, (1, 0))
        at = n.chosen[m]
        n.info[m, 3:4, :] = jnp.where(at >= 0, at + f * tok_count, 0).astype(F32)
        n.info[m, 4:8, :] = jnp.zeros((4, 128), F32)
    swap_start(0, tok_at, hid_at)
    for m in range(MB):
        ss, rs = n.a2a_s.at[1, m], n.a2a_r.at[1, a]

        @pl.when(jnp.logical_not(mine[m]))
        def _():
            remote(info_src(m), info_home(a), ss, rs, home_rep, home_fsdp(m)).start()

        @pl.when(mine[m])
        def _():
            pltpu.make_async_copy(info_src(m), info_own(a), rs).start()

    for copy in cut_copies("wq"):
        copy.wait()
    gather_start("wq", n.wqa, piece)
    gather_forward("small", n.sm, 8)
    gather_end("small", n.sm, 8)
    for index in range(F):
        n.vec[:, index * 128 : (index + 1) * 128] = n.sm[index * 8 : (index + 1) * 8, :]
    for m in range(MB):
        token_copy(1, m).wait()
        n.picked_ct[m * 128 : (m + 1) * 128, :] = dot(
            hot_of(m), n.pair_b[m * tok_count : (m + 1) * tok_count, :], (0, 0)
        ).astype(BF)
    swap_end(0, tok_at, hid_at)
    swap_end(1, info_src, info_own)
    swap_start(2, cot_at, ct_at)

    def first_norm(at, rows_at):
        h = n.hid[rows_at, :].astype(F32)
        scale = lax.rsqrt(jnp.mean(h * h, axis=-1, keepdims=True) + eps)
        n.normed[pl.ds(pl.multiple_of(r * own + at, tall), tall), :] = (
            h * scale * n.vec[1:2, :]
        ).astype(BF)
        logit = jnp.sum(h * n.vec[0:1, :], axis=-1, keepdims=True)
        n.gate[rows_at, :] = jnp.broadcast_to(1.0 / (1.0 + jnp.exp(-logit)), (tall, 128))

    by_own(first_norm)
    share_start("normed", n.normed, own)
    share_start("info", n.infos, MB * 8)
    out_start(n.w_out, n.woa)
    for name, buf in (("wu", n.wua), ("wd", n.wda)):
        for copy in cut_copies(name):
            copy.wait()
        gather_start(name, buf, piece)
    gather_forward("wq", n.wqa, piece)
    share_forward("info", n.infos, MB * 8)
    share_forward("normed", n.normed, own)
    share_end("info", n.infos, MB * 8)
    share_end("normed", n.normed, own)
    gather_end("wq", n.wqa, piece)

    def project(index):
        at = aligned(index, own)
        n.proj[at, :] = dot(n.normed[at, :], n.wqa[...], (1, 0)).astype(BF)

    loop(R, project)

    swap_end(2, cot_at, ct_at)

    def mlp_cotangent(at, rows_at):
        gc = n.gate[rows_at, 0:1] * n.ct[rows_at, :].astype(F32)
        n.gmlp[pl.ds(pl.multiple_of(r * own + at, tall), tall), :] = gc.astype(BF)

    by_own(mlp_cotangent)
    out_forward(n.woa)

    tree, pairs = g.tree, g.heads // 2
    scale = 64 ** (-0.5)
    low_lane = lax.broadcasted_iota(jnp.int32, (tree, 128), 1) < 64

    def half_of(value, half):
        keep = low_lane if half == 0 else jnp.logical_not(low_lane)
        return jnp.where(keep, value, jnp.zeros_like(value))

    def join(first, second):
        return jnp.where(low_lane, first, second)

    def make_bias(t):
        blocks = []
        for index in range(S * MB // 2):
            at = pl.multiple_of((t * S * MB + index * 2) * 8, 8)
            blocks.append(n.infos[pl.ds(at, 8), :] + n.infos[pl.ds(at + 8, 8), :])
        keys = jnp.concatenate(blocks, axis=1)
        asked = jnp.transpose(keys)
        near = keys[0:1, :] == asked[:, 0:1]
        near = near | (keys[0:1, :] == asked[:, 1:2])
        near = near | (keys[0:1, :] == asked[:, 2:3])
        near = near & (keys[3:4, :] <= asked[:, 3:4])
        n.bias[...] = jnp.where(near, 0.0, -1e30)

    def columns(part, pair):
        return pl.ds(part * g.ac + pair * 128, 128)

    def attend(t):
        make_bias(t)
        at = aligned(t, tree)
        for pair in range(pairs):
            q = n.proj[at, columns(0, pair)]
            k = n.proj[at, columns(1, pair)]
            v = n.proj[at, columns(2, pair)]
            made = []
            for half in range(2):
                s = dot(half_of(q, half), k, (1, 1)) * scale + n.bias[...]
                top = jnp.max(s, axis=-1, keepdims=True)
                e = jnp.exp(s - top)
                total = jnp.sum(e, axis=-1, keepdims=True)
                made.append(dot((e * (1.0 / total)).astype(BF), v, (1, 0)))
                head = pair * 2 + half
                n.lse[at, head : head + 1] = top + jnp.log(total)
            n.att[at, pl.ds(pair * 128, 128)] = join(*made).astype(BF)

    loop(g.trees, attend)
    out_end(n.w_out, n.woa)

    def branch_part(owner, cols):
        return dot(n.att[aligned(owner, own), :], n.woa[:, cols], (1, 0))

    sum_start(0, 0, branch_part, n.branch)
    share_start("gmlp", n.gmlp, own)
    gather_forward("wu", n.wua, piece)
    sum_end(0, 0)

    def second_norm(at, rows_at):
        br = n.branch[rows_at, :] + came(0, at)
        n.branch[rows_at, :] = br
        mid = n.hid[rows_at, :].astype(F32) + br
        inv = lax.rsqrt(jnp.mean(mid * mid, axis=-1, keepdims=True) + eps)
        n.norm2[pl.ds(pl.multiple_of(r * own + at, tall), tall), :] = (
            mid * inv * n.vec[2:3, :]
        ).astype(BF)

    by_own(second_norm)
    share_start("norm2", n.norm2, own)
    gather_forward("wd", n.wda, piece)
    share_forward("gmlp", n.gmlp, own)
    share_end("gmlp", n.gmlp, own)
    gather_end("wu", n.wua, piece)
    share_forward("norm2", n.norm2, own)
    share_end("norm2", n.norm2, own)

    tiles = g.fc // wide

    def mlp_up(index):
        at = aligned(index // tiles, own)
        cols = aligned(lax.rem(index, tiles), wide)
        u = dot(n.norm2[at, :], n.wua[:, cols], (1, 0))
        square = u * u
        t = jnp.tanh(GELU_A * (u + GELU_B * square * u))
        n.act[at, cols] = (0.5 * u * (1.0 + t)).astype(BF)
        n.dact[at, cols] = 0.5 * (1.0 + t) + (0.5 * GELU_A) * u * (1.0 - t * t) * (
            1.0 + (3.0 * GELU_B) * square
        )

    loop(R * tiles, mlp_up)
    gather_end("wd", n.wda, piece)

    def mlp_back(index):
        at = aligned(index // tiles, own)
        cols = aligned(lax.rem(index, tiles), wide)
        ga = dot(n.gmlp[at, :], n.wda[cols, :], (1, 1))
        n.gup[at, cols] = (ga * n.dact[at, cols]).astype(BF)

    loop(R * tiles, mlp_back)

    def norm2_part(owner, cols):
        return dot(n.gup[aligned(owner, own), :], n.wua[cols, :], (1, 1))

    sum_start(1, 1, norm2_part, n.gmid)

    def weight_grad(left, right, target, count):
        def one(index):
            cols = aligned(index, 256)
            target[cols, :] = dot(left[:, cols], right[...], (0, 0)).astype(BF)

        loop(count // 256, one)

    weight_grad(n.act, n.gmlp, n.gd, g.fc)
    grad_start("d", n.gd, piece)
    weight_grad(n.norm2, n.gup, n.gu, d)
    grad_start("u", n.gu, piece)
    sum_end(1, 1)
    n.gsum[...] = jnp.zeros_like(n.gsum)

    def second_back(at, rows_at):
        dy = n.gmid[rows_at, :] + came(1, at)
        mid = n.hid[rows_at, :].astype(F32) + n.branch[rows_at, :]
        inv = lax.rsqrt(jnp.mean(mid * mid, axis=-1, keepdims=True) + eps)
        n.gsum[2:3, :] = n.gsum[2:3, :] + jnp.sum(dy * mid * inv, axis=0, keepdims=True)
        t = dy * n.vec[2:3, :]
        along = jnp.sum(mid * t, axis=-1, keepdims=True) * (inv * inv * inv * (1.0 / d))
        gm = inv * t - mid * along
        n.gmid[rows_at, :] = gm
        gc = n.gate[rows_at, 0:1] * n.ct[rows_at, :].astype(F32)
        n.gbr[pl.ds(pl.multiple_of(r * own + at, tall), tall), :] = (gc + gm).astype(BF)

    by_own(second_back)
    share_start("gbr", n.gbr, own)

    def change_part(owner, cols):
        return dot(n.act[aligned(owner, own), :], n.wda[:, cols], (1, 0))

    sum_start(2, 0, change_part, n.acc)
    grad_forward("d", n.gd, piece)
    share_forward("gbr", n.gbr, own)
    share_end("gbr", n.gbr, own)

    def attention_cotangent(index):
        at = aligned(index, own)
        n.gatt[at, :] = dot(n.gbr[at, :], n.woa[...], (1, 1)).astype(BF)

    loop(R, attention_cotangent)
    weight_grad(n.att, n.gbr, n.go, g.ac)
    grad_start("o", n.go, piece)

    def attend_back(t):
        make_bias(t)
        at = aligned(t, tree)
        for pair in range(pairs):
            q = n.proj[at, columns(0, pair)]
            k = n.proj[at, columns(1, pair)]
            v = n.proj[at, columns(2, pair)]
            da = n.gatt[at, pl.ds(pair * 128, 128)]
            dq, dk, dv = [], [], []
            for half in range(2):
                head = pair * 2 + half
                s = dot(half_of(q, half), k, (1, 1)) * scale + n.bias[...]
                p = jnp.exp(s - n.lse[at, head : head + 1])
                dp = dot(half_of(da, half), v, (1, 1))
                delta = jnp.sum(p * dp, axis=-1, keepdims=True)
                ds = (p * (dp - delta)).astype(BF)
                dq.append(dot(ds, k, (1, 0)))
                dk.append(dot(ds, q, (0, 0)))
                dv.append(dot(p.astype(BF), da, (0, 0)))
            n.gproj[at, columns(0, pair)] = (join(*dq) * scale).astype(BF)
            n.gproj[at, columns(1, pair)] = (join(*dk) * scale).astype(BF)
            n.gproj[at, columns(2, pair)] = join(*dv).astype(BF)

    loop(g.trees, attend_back)

    sum_end(2, 0)

    def new_rows(at, rows_at):
        change = n.branch[rows_at, :] + n.acc[rows_at, :] + came(0, at)
        h = n.hid[rows_at, :].astype(F32)
        gate = n.gate[rows_at, 0:1]
        n.nrow[rows_at, :] = (h + gate * change).astype(BF)
        logit = jnp.sum(n.ct[rows_at, :].astype(F32) * change, axis=-1, keepdims=True)
        logit = logit * gate * (1.0 - gate)
        n.glog[rows_at, :] = jnp.broadcast_to(logit, (tall, 128))
        n.gsum[0:1, :] = n.gsum[0:1, :] + jnp.sum(logit * h, axis=0, keepdims=True)

    by_own(new_rows)

    def normed_part(owner, cols):
        return dot(n.gproj[aligned(owner, own), :], n.wqa[cols, :], (1, 1))

    sum_start(3, 1, normed_part, n.acc)
    weight_grad(n.normed, n.gproj, n.gq, d)
    grad_start("q", n.gq, piece)
    grad_forward("u", n.gu, piece)
    grad_forward("o", n.go, piece)
    grad_own("d", n.gd, piece)

    def new_at(i):
        return n.nrow.at[aligned(i, cap)]

    swap_start(4, new_at, lambda m: n.new_out.at[m])
    sum_end(3, 1)

    def first_back(at, rows_at):
        dy = n.acc[rows_at, :] + came(1, at)
        h = n.hid[rows_at, :].astype(F32)
        inv = lax.rsqrt(jnp.mean(h * h, axis=-1, keepdims=True) + eps)
        n.gsum[1:2, :] = n.gsum[1:2, :] + jnp.sum(dy * h * inv, axis=0, keepdims=True)
        t = dy * n.vec[1:2, :]
        along = jnp.sum(h * t, axis=-1, keepdims=True) * (inv * inv * inv * (1.0 / d))
        total = n.ct[rows_at, :].astype(F32) + n.gmid[rows_at, :] + (inv * t - h * along)
        total = total + n.glog[rows_at, 0:1] * n.vec[0:1, :]
        n.grow[rows_at, :] = total.astype(BF)

    by_own(first_back)

    def grow_at(i):
        return n.grow.at[aligned(i, cap)]

    swap_start(3, grow_at, lambda m: n.grad_out.at[m])
    for index in range(F):
        n.gsp[index * 8 : (index + 1) * 8, :] = n.gsum[:, index * 128 : (index + 1) * 128]
    grad_start("s", n.gsp, 8)
    grad_forward("q", n.gq, piece)
    grad_forward("s", n.gsp, 8)
    grad_own("u", n.gu, piece)

    @pl.when(is_source)
    def _():
        grad_wait("o", piece)
        grad_total("o", n.go, b * piece, piece, n.gro, 0)

    ax, ac = a // 2, lax.rem(a, 2)
    for step in range(X - 1):
        send(n.gro, n.gro, n.ro_xs.at[step], n.ro_xr.at[0], xpeer(step) * 2 + c, f, is_source)
    send(n.gro, n.gro, n.ro_ss.at[0], n.ro_sr.at[0], sib, f, is_source)
    grad_own("q", n.gq, piece)
    grad_wait("s", 8)
    grad_total("s", n.gsp, f * 8, 8, n.gs_mine.at[0], 0)
    send(n.gs_mine.at[0], n.gs_pair.at[0], n.pair_s.at[0], n.pair_r.at[0], sib, f)

    off_x = (c == ac) & (x != ax)

    @pl.when(off_x)
    def _():
        got(n.gro, n.ro_xr.at[0])

    send(n.gro, n.gro, n.ro_ss.at[1], n.ro_sr.at[0], sib, f, off_x)
    share_forward("rd", n.grd, piece)
    share_end("rd", n.grd, piece)

    def out_copies(which, name, target):
        buf = sem("gr" + name)
        return [
            pltpu.make_async_copy(
                buf.at[pl.ds(index * piece, piece)], target.at[index], n.out_l.at[which, index]
            )
            for index in range(R)
        ]

    for copy in out_copies(0, "d", n.rd_out):
        copy.start()
    share_forward("ru", n.gru, piece)
    share_end("ru", n.gru, piece)
    for copy in out_copies(1, "u", n.ru_out):
        copy.start()

    @pl.when(c != ac)
    def _():
        got(n.gro, n.ro_sr.at[0])

    last = pltpu.make_async_copy(n.gro, n.ro_out, n.out_l.at[2, 0])
    last.start()
    got(n.gs_pair.at[0], n.pair_r.at[0])
    n.gs_mine[1] = n.gs_mine[0] + n.gs_pair[0]
    send(n.gs_mine.at[1], n.gs_pair.at[1], n.pair_s.at[1], n.pair_r.at[1], xpeer(0) * 2 + c, f)
    share_forward("rq", n.grq, piece)
    share_end("rq", n.grq, piece)
    for copy in out_copies(3, "q", n.rq_out):
        copy.start()
    got(n.gs_pair.at[1], n.pair_r.at[1])
    n.gs_out[...] = n.gs_mine[1] + n.gs_pair[1]
    swap_end(4, new_at, lambda m: n.new_out.at[m])
    swap_end(3, grow_at, lambda m: n.grad_out.at[m])
    for which, name, target in ((0, "d", n.rd_out), (1, "u", n.ru_out), (3, "q", n.rq_out)):
        for copy in out_copies(which, name, target):
            copy.wait()
    last.wait()
    for tag in list(pending):
        drain(tag)


def place_kernel(g, at_ref, tok_ref, cot_ref, new_ref, grad_ref, rq_ref, ru_ref, rd_ref, ro_ref, *outs):
    mixed_ref, gt_ref, gq_ref, gu_ref, gd_ref, go_ref = outs
    tall = tok_ref.shape[1]
    first = pl.program_id(1) * tall
    token = lax.broadcasted_iota(jnp.int32, (tall, g.cap), 0) + first
    hot = token == at_ref[0]
    routed = jnp.max(hot.astype(F32), axis=-1, keepdims=True) > 0.0
    hot = hot.astype(BF)
    new = dot(hot, new_ref[0], (1, 0))
    mixed_ref[0] = jnp.where(routed, new, tok_ref[0].astype(F32)).astype(BF)
    grad = dot(hot, grad_ref[0], (1, 0))
    gt_ref[0] = jnp.where(routed, grad, cot_ref[0].astype(F32))
    for index in range(g.R):
        for part in range(3):
            gq_ref[:, pl.ds(part * g.d + index * g.ac, g.ac)] = rq_ref[
                index, :, pl.ds(part * g.ac, g.ac)
            ].astype(F32)
        for block in range(g.F):
            gu_ref[:, pl.ds((block * g.R + index) * 128, 128)] = ru_ref[
                index, :, pl.ds(block * 128, 128)
            ].astype(F32)
        gd_ref[index] = rd_ref[index].astype(F32)
    go_ref[...] = ro_ref[...].astype(F32)


def place(g, chosen, tokens, cotangent, new_rows, grad_rows, rq, ru, rd, ro):
    halves = 2
    steps = g.MB * halves
    tok_count = tokens.shape[1]
    tall = tok_count // halves
    piece = g.d // g.F
    low = piece // steps
    hidden = g.F * g.R * 128

    def block(*shape):
        return pl.BlockSpec((1,) + shape, lambda m, h: (m, h, 0))

    def micro(*shape):
        return pl.BlockSpec((1,) + shape, lambda m, h: (m, 0, 0))

    def slab(*lead, cols):
        return pl.BlockSpec(
            lead + (low, cols), lambda m, h: (0,) * len(lead) + (m * halves + h, 0)
        )

    return pl.pallas_call(
        functools.partial(place_kernel, g),
        grid=(g.MB, halves),
        in_specs=[
            micro(1, g.cap),
            block(tall, g.d),
            block(tall, g.d),
            micro(g.cap, g.d),
            micro(g.cap, g.d),
            slab(g.R, cols=g.qc),
            slab(g.R, cols=g.fc),
            slab(g.R, cols=g.d),
            slab(cols=g.d),
        ],
        out_specs=[
            block(tall, g.d),
            block(tall, g.d),
            slab(cols=3 * g.d),
            slab(cols=hidden),
            slab(g.R, cols=g.d),
            slab(cols=g.d),
        ],
        out_shape=[
            jax.ShapeDtypeStruct(tokens.shape, BF),
            jax.ShapeDtypeStruct(tokens.shape, F32),
            jax.ShapeDtypeStruct((piece, 3 * g.d), F32),
            jax.ShapeDtypeStruct((piece, hidden), F32),
            jax.ShapeDtypeStruct((g.R, piece, g.d), F32),
            jax.ShapeDtypeStruct((piece, g.d), F32),
        ],
        compiler_params=pltpu.CompilerParams(vmem_limit_bytes=48 * 1024 * 1024),
        name="place_rows",
    )(chosen[:, None, :], tokens, cotangent, new_rows, grad_rows, rq, ru, rd, ro)


def group_shards(tokens, cotangent, path, chosen, router, gains, w_qkv, w_out, w_up, w_down):
    R, F = lax.axis_size("rep"), lax.axis_size("fsdp")
    MB, tok_count, d = tokens.shape
    cap = chosen.shape[1]
    S = F // MB
    hidden = w_up.shape[1]
    g = types.SimpleNamespace(
        R=R,
        F=F,
        S=S,
        A=MB,
        X=R // 2,
        MB=MB,
        cap=cap,
        d=d,
        own=MB * cap,
        rows=R * MB * cap,
        tree=S * MB * cap,
        trees=R // S,
        heads=HEADS // R,
        qc=3 * d // R,
        ac=d // R,
        fc=hidden // R,
    )
    g.items = (
        ("q", F, g.qc, BF),
        ("u", F, g.fc, BF),
        ("d", F, d, BF),
        ("o", S, d, BF),
        ("s", F, 128, F32),
    )
    piece = d // F
    f = lax.axis_index("fsdp")

    blank = jnp.full_like(chosen, -1)
    odd = lax.rem(f // S, 2) == 1
    lanes = jnp.where(
        odd,
        jnp.concatenate([blank, chosen], axis=1),
        jnp.concatenate([chosen, blank], axis=1),
    )
    small = jnp.concatenate([router[None], gains.T, jnp.zeros((5, piece), BF)], axis=0)
    operands = {
        "tokens": tokens,
        "cotangent": cotangent,
        "w_qkv": w_qkv,
        "w_out": w_out,
        "w_up": w_up,
        "w_down": w_down,
        "path": jnp.transpose(path, (2, 0, 1)),
        "chosen": lanes[:, None, :],
        "small": small.astype(F32),
    }
    results = {
        "new_out": ((MB, cap, d), BF),
        "grad_out": ((MB, cap, d), BF),
        "rq_out": ((R, piece, g.qc), BF),
        "ru_out": ((R, piece, g.fc), BF),
        "rd_out": ((R, piece, d), BF),
        "ro_out": ((piece, d), BF),
        "gs_out": ((8, 128), F32),
    }
    vmem, sems = scratch_shapes(g)
    names = list(operands) + list(results) + list(vmem) + list(sems)
    made = pl.pallas_call(
        functools.partial(block_kernel, g, names),
        out_shape=[jax.ShapeDtypeStruct(*kind) for kind in results.values()],
        in_specs=[
            pl.BlockSpec(
                memory_space=pltpu.VMEM if name in ("path", "chosen", "small") else pl.ANY
            )
            for name in operands
        ],
        out_specs=[
            pl.BlockSpec(memory_space=pltpu.VMEM if name == "gs_out" else pl.ANY)
            for name in results
        ],
        scratch_shapes=[pltpu.VMEM(*kind) for kind in vmem.values()]
        + [pltpu.SemaphoreType.DMA(shape) for shape in sems.values()],
        compiler_params=pltpu.CompilerParams(
            collective_id=0, has_side_effects=True, vmem_limit_bytes=60 * 1024 * 1024
        ),
        name="routed_block",
    )(*operands.values())
    new_rows, grad_rows, rq, ru, rd, ro, gs = made
    mixed, grad_tokens, grad_qkv, grad_up, grad_down, grad_out = place(
        g, chosen, tokens, cotangent, new_rows, grad_rows, rq, ru, rd, ro
    )
    return (
        mixed,
        grad_tokens,
        gs[0, :piece],
        gs[1:3, :piece].T,
        grad_qkv,
        grad_out,
        grad_up,
        grad_down.reshape(R * piece, d),
    )


def plain_norm(matrix, gain_row):
    return matrix * lax.rsqrt(jnp.mean(matrix * matrix, axis=-1, keepdims=True) + eps) * gain_row


def inner(left, right):
    return lax.dot_general(
        left, right, (((0,), (0,)), ((), ())), preferred_element_type=jnp.float32
    )


def by_rows(left, right):
    return lax.dot_general(
        left, right, (((1,), (1,)), ((), ())), preferred_element_type=jnp.float32
    )


def gather_rows(arrays):
    return lax.all_gather(arrays, "fsdp", axis=0, tiled=True)


def scatter_sum(array):
    return lax.psum_scatter(
        array.astype(jnp.bfloat16), "fsdp", scatter_dimension=0, tiled=True
    ).astype(jnp.float32)


def plain_shards(tokens, cotangent, path, chosen, router, gains, w_qkv, w_out, w_up, w_down):
    micro_count, tok_count, model_width = tokens.shape
    slot_count = chosen.shape[1]
    row_count = micro_count * slot_count
    head_dim = model_width // HEADS
    score_scale = head_dim ** (-0.5)
    offset = lax.axis_index("fsdp") * tok_count
    fsdp = lax.axis_size("fsdp")

    def pick(array):
        return jax.vmap(lambda rows, at: rows[at])(array, chosen)

    small = jnp.concatenate([router[:, None], gains], axis=1)
    small_all = gather_rows(small)
    qkv_all = gather_rows(w_qkv)
    out_all = gather_rows(w_out)
    up_all = gather_rows(w_up)
    down_all = gather_rows(w_down)
    router_float = small_all[:, 0].astype(jnp.float32)
    gain_one = small_all[:, 1].astype(jnp.float32)
    gain_two = small_all[:, 2].astype(jnp.float32)

    routed = pick(tokens).reshape(row_count, model_width)
    hidden = routed.astype(jnp.float32)
    gate_rate = jax.nn.sigmoid(
        jnp.dot(routed, small_all[:, 0], preferred_element_type=jnp.float32)
    )
    normed = plain_norm(hidden, gain_one).astype(jnp.bfloat16)
    projected = jnp.dot(normed, qkv_all, preferred_element_type=jnp.float32).astype(jnp.bfloat16)
    queries = projected[:, :model_width].reshape(micro_count, slot_count, HEADS, head_dim)
    own_path = pick(path)
    own_place = offset + chosen
    key_info = jnp.concatenate([own_path[:, :, :1], own_place[:, :, None]], axis=2)
    gathered = lax.all_gather(
        projected[:, model_width:].reshape(micro_count, slot_count, 2 * model_width), "fsdp"
    )
    info_all = lax.all_gather(key_info, "fsdp")
    key_count = fsdp * slot_count
    gathered = jnp.swapaxes(gathered, 0, 1).reshape(micro_count, key_count, 2, HEADS, head_dim)
    info_all = jnp.swapaxes(info_all, 0, 1).reshape(micro_count, key_count, 2)
    key_rows = gathered[:, :, 0]
    value_rows = gathered[:, :, 1]
    key_seg = info_all[:, None, :, 0]
    visible = (
        (key_seg == own_path[:, :, 0:1])
        | (key_seg == own_path[:, :, 1:2])
        | (key_seg == own_path[:, :, 2:3])
    ) & (info_all[:, None, :, 1] <= own_place[:, :, None])
    visible = visible[:, None]

    def product(form, left, right):
        return jnp.einsum(form, left, right, preferred_element_type=jnp.float32)

    scores = product("mqhd,mkhd->mhqk", queries, key_rows) * score_scale
    scores = jnp.where(visible, scores, -1e30)
    row_max = jnp.max(scores, axis=-1, keepdims=True)
    exponent = jnp.where(visible, jnp.exp(scores - row_max), 0.0)
    row_total = jnp.sum(exponent, axis=-1, keepdims=True)
    soft_prob = exponent / row_total
    probs = soft_prob.astype(jnp.bfloat16)
    attention = product("mhqk,mkhd->mqhd", probs, value_rows)
    attention = attention.reshape(row_count, model_width).astype(jnp.bfloat16)
    branch = jnp.dot(attention, out_all, preferred_element_type=jnp.float32)
    middle = hidden + branch
    normed_two = plain_norm(middle, gain_two).astype(jnp.bfloat16)
    up_proj = jnp.dot(normed_two, up_all, preferred_element_type=jnp.float32)
    activated = jax.nn.gelu(up_proj).astype(jnp.bfloat16)
    change = branch + jnp.dot(activated, down_all, preferred_element_type=jnp.float32)
    new_rows = hidden + gate_rate[:, None] * change

    def put(array, rows):
        rows = rows.reshape(micro_count, slot_count, model_width).astype(array.dtype)
        return jax.vmap(lambda whole, at, new: whole.at[at].set(new))(array, chosen, rows)

    mixed = put(tokens, new_rows)

    grad_rows = pick(cotangent).reshape(row_count, model_width).astype(jnp.float32)
    grad_change = gate_rate[:, None] * grad_rows
    grad_logit = jnp.sum(grad_rows * change, axis=-1) * gate_rate * (1.0 - gate_rate)
    grad_mlp = grad_change.astype(jnp.bfloat16)
    grad_down = scatter_sum(inner(activated, grad_mlp))
    grad_act = by_rows(grad_mlp, down_all)
    gelu_value, gelu_back = jax.vjp(jax.nn.gelu, up_proj)
    grad_up_proj = gelu_back(grad_act)[0].astype(jnp.bfloat16)
    grad_up = scatter_sum(inner(normed_two, grad_up_proj))
    grad_normed_two = by_rows(grad_up_proj, up_all)
    norm_value, norm_back_two = jax.vjp(plain_norm, middle, gain_two)
    grad_middle, grad_gain_two = norm_back_two(grad_normed_two)
    grad_branch = (grad_change + grad_middle).astype(jnp.bfloat16)
    grad_outw = scatter_sum(inner(attention, grad_branch))
    grad_attention = by_rows(grad_branch, out_all).astype(jnp.bfloat16)
    grad_heads = grad_attention.reshape(micro_count, slot_count, HEADS, head_dim)
    prob_grad = product("mqhd,mkhd->mhqk", grad_heads, value_rows)
    delta = jnp.sum(soft_prob * prob_grad, axis=-1, keepdims=True)
    grad_scores = (soft_prob * (prob_grad - delta)).astype(jnp.bfloat16)
    grad_query = product("mhqk,mkhd->mqhd", grad_scores, key_rows) * score_scale
    grad_key = product("mhqk,mqhd->mkhd", grad_scores, queries) * score_scale
    grad_value = product("mhqk,mqhd->mkhd", probs, grad_heads)
    grad_kv = jnp.stack([grad_key, grad_value], axis=2).reshape(
        micro_count, fsdp, slot_count, 2 * model_width
    )
    grad_kv = lax.psum_scatter(
        jnp.swapaxes(grad_kv, 0, 1).astype(jnp.bfloat16).reshape(-1, 2 * model_width),
        "fsdp",
        scatter_dimension=0,
        tiled=True,
    )
    grad_projected = jnp.concatenate(
        [
            grad_query.reshape(row_count, model_width).astype(jnp.bfloat16),
            grad_kv.reshape(row_count, 2 * model_width),
        ],
        axis=1,
    )
    grad_qkvw = scatter_sum(inner(normed, grad_projected))
    grad_normed = by_rows(grad_projected, qkv_all)
    norm_value_one, norm_back_one = jax.vjp(plain_norm, hidden, gain_one)
    grad_hidden_norm, grad_gain_one = norm_back_one(grad_normed)
    grad_hidden = (
        grad_rows + grad_middle + grad_hidden_norm + grad_logit[:, None] * router_float[None, :]
    )
    grad_tokens = put(cotangent.astype(jnp.float32), grad_hidden)
    grad_routerw = jnp.sum(grad_logit[:, None] * hidden, axis=0)
    grad_small = jnp.stack([grad_routerw, grad_gain_one, grad_gain_two], axis=1)
    grad_small = lax.psum_scatter(grad_small, "fsdp", scatter_dimension=0, tiled=True)
    summed = lax.psum((grad_small, grad_qkvw, grad_outw, grad_up, grad_down), "rep")
    return (mixed, grad_tokens, summed[0][:, 0], summed[0][:, 1:]) + tuple(summed[1:])


def solution(mesh):
    rows = P(None, ("rep", "fsdp"), None)
    weight = P("fsdp", None)

    def whole(*args):
        grouped = fits(mesh, args[0], args[3], args[8])
        return jax.shard_map(
            group_shards if grouped else plain_shards,
            mesh=mesh,
            in_specs=(
                rows,
                rows,
                rows,
                P(None, ("rep", "fsdp")),
                P("fsdp"),
                weight,
                weight,
                weight,
                weight,
                weight,
            ),
            out_specs=(rows, rows, P("fsdp"), weight, weight, weight, weight, weight),
            check_vma=False,
        )(*args)

    return whole
```

```python
import functools
import math
import types

import jax
import jax.numpy as jnp
from jax import lax
from jax.experimental import pallas as pl
from jax.experimental.pallas import tpu as pltpu
from jax.sharding import PartitionSpec as P

HEADS = 16


eps = 1e-05
MESH = pl.DeviceIdType.MESH
BF = jnp.bfloat16
F32 = jnp.float32
GELU_A = math.sqrt(2.0 / math.pi)
GELU_B = 0.044715


def dot(left, right, contract):
    return lax.dot_general(
        left, right, (((contract[0],), (contract[1],)), ((), ())), preferred_element_type=F32
    )


def aligned(index, size):
    return pl.ds(pl.multiple_of(index * size, size), size)


def loop(count, body):
    def step(index, carry):
        body(index)
        return carry

    lax.fori_loop(0, count, step, 0)


def fits(mesh, tokens, chosen, w_up):
    rep, fsdp = mesh.shape["rep"], mesh.shape["fsdp"]
    micro, width, hidden = tokens.shape[0], tokens.shape[2], w_up.shape[1]
    if fsdp % micro or rep % 2:
        return False
    inner_count = fsdp // micro
    return (
        rep % inner_count == 0
        and rep == micro
        and fsdp == rep * inner_count
        and width == fsdp * 128
        and hidden == fsdp * rep * 128
        and HEADS % (2 * rep) == 0
        and width // HEADS == 64
        and chosen.shape[1] // (rep * fsdp) == 64
        and rep == 4
        and hidden == rep * width
        and tokens.shape[1] * micro // (rep * fsdp) == 2 * rep * micro * 64
    )


def scratch_shapes(g):
    own, rows, d = g.own, g.rows, g.d
    vmem = {
        "hid": ((own, d), BF),
        "ct": ((own, d), BF),
        "infos": ((g.R * g.MB * 8, 128), F32),
        "sm": ((g.F * 8, 128), F32),
        "info": ((g.MB, 8, 128), F32),
        "vec": ((8, d), F32),
        "wqa": ((d, g.qc), BF),
        "woa": ((g.ac, d), BF),
        "wua": ((d, g.fc), BF),
        "wda": ((g.fc, d), BF),
        "normed": ((rows, d), BF),
        "norm2": ((rows, d), BF),
        "proj": ((rows, g.qc), BF),
        "att": ((rows, g.ac), BF),
        "gatt": ((rows, g.ac), BF),
        "gproj": ((rows, g.qc), BF),
        "lse": ((rows, 128), F32),
        "bias": ((g.tree, g.tree), F32),
        "pair_a": ((2 * rows, g.fc), BF),
        "pair_b": ((2 * rows, d), BF),
        "dact": ((rows, g.fc), F32),
        "gate": ((own, 128), F32),
        "glog": ((own, 128), F32),
        "branch": ((own, d), F32),
        "gmid": ((own, d), F32),
        "ends": ((2 * own, d), BF),
        "to_sib": ((2, g.X * own, d), BF),
        "of_sib": ((2, g.X * own, d), BF),
        "to_x": ((2, (g.X - 1) * own, d), BF),
        "of_x": ((2, (g.X - 1) * own, d), BF),
        "gsum": ((8, d), F32),
        "gsp": ((g.F * 8, 128), F32),
        "gs_pair": ((2, 8, 128), F32),
        "gs_mine": ((2, 8, 128), F32),
    }
    piece = d // g.F
    for name, count, cols, kind in g.items:
        height = 8 if name == "s" else piece
        if name != "s":
            vmem["g" + name] = ((count * height, cols), kind)
        vmem["gi" + name] = (((count // g.S) * height, cols), kind)
        vmem["go" + name] = ((g.A * height, cols), kind)
        if name != "s":
            vmem["gr" + name] = (((g.R if name != "o" else 1) * height, cols), kind)
    sems = {
        "a2a_s": (5, g.MB),
        "a2a_r": (5, g.MB),
        "tok_l": (2, g.MB),
        "out_l": (4, g.R),
    }
    for name in ("small", "wo"):
        sems[name + "_l"] = (1,)
        sems[name + "_os"] = (g.A - 1,)
        sems[name + "_or"] = (g.A - 1,)
        sems[name + "_is"] = (g.A,)
        sems[name + "_ir"] = (g.A,)
    for name in ("wq", "wu", "wd"):
        sems[name + "_l"] = (g.F,)
        for way in ("up", "dn"):
            sems[name + "_%ss" % way] = (g.A - 1,)
            sems[name + "_%sr" % way] = (g.A - 1,)
        sems[name + "_is"] = (2 * g.A - 1,)
        sems[name + "_ir"] = (2 * g.A - 1,)
    for name in ("info", "normed", "gmlp", "norm2", "gbr", "rq", "ru", "rd", "ro"):
        sems[name + "_xs"] = (g.X - 1,)
        sems[name + "_xr"] = (g.X - 1,)
        sems[name + "_ss"] = (g.X,)
        sems[name + "_sr"] = (g.X,)
    for index in range(4):
        name = "sum%d" % index
        sems[name + "_xs"] = (g.X - 1,)
        sems[name + "_xr"] = (g.X - 1,)
        sems[name + "_ss"] = (g.X,)
        sems[name + "_sr"] = (g.X,)
    for name, count, cols, kind in g.items:
        sems["g" + name + "_is"] = (g.A,)
        sems["g" + name + "_ir"] = (g.A,)
        sems["g" + name + "_os"] = (g.A,)
        sems["g" + name + "_or"] = (g.A,)
    sems["pair_s"] = (2,)
    sems["pair_r"] = (2,)
    return vmem, sems


def block_kernel(g, names, *refs):
    n = types.SimpleNamespace(**dict(zip(names, refs)))
    R, F, S, A, X, MB = g.R, g.F, g.S, g.A, g.X, g.MB
    own, rows, d, cap = g.own, g.rows, g.d, g.cap
    piece = d // F
    r = lax.axis_index("rep")
    f = lax.axis_index("fsdp")
    x, c = r // 2, lax.rem(r, 2)
    a, b = f // S, lax.rem(f, S)
    other_b = lax.rem(b + 1, S)
    sib = x * 2 + 1 - c
    pending = {}
    n.act, n.gup = n.pair_a.at[pl.ds(0, rows)], n.pair_a.at[pl.ds(rows, rows)]
    n.gmlp, n.gbr = n.pair_b.at[pl.ds(0, rows)], n.pair_b.at[pl.ds(rows, rows)]
    n.nrow, n.grow = n.ends.at[pl.ds(0, own)], n.ends.at[pl.ds(own, own)]
    n.picked, n.picked_ct = n.ends, n.norm2
    n.acc, n.gfirst = n.dact.at[pl.ds(0, own)], n.dact.at[pl.ds(own, own)]
    tok_count = n.tokens.shape[1]

    def token_copy(which, m):
        source, target = (n.tokens, n.pair_a) if which == 0 else (n.cotangent, n.pair_b)
        return pltpu.make_async_copy(
            source.at[m], target.at[pl.ds(m * tok_count, tok_count)], n.tok_l.at[which, m]
        )

    for which in range(2):
        for m in range(MB):
            token_copy(which, m).start()

    def cut_copies(name):
        if name == "wq":
            return [
                pltpu.make_async_copy(
                    n.w_qkv.at[:, pl.ds(pl.multiple_of(part * d + r * g.ac, g.ac), g.ac)],
                    n.wqa.at[aligned(f, piece), pl.ds(part * g.ac, g.ac)],
                    n.wq_l.at[part],
                )
                for part in range(3)
            ]
        if name == "wu":
            return [
                pltpu.make_async_copy(
                    n.w_up.at[:, pl.ds(pl.multiple_of((block * R + r) * 128, 128), 128)],
                    n.wua.at[aligned(f, piece), pl.ds(block * 128, 128)],
                    n.wu_l.at[block],
                )
                for block in range(F)
            ]
        return [
            pltpu.make_async_copy(
                n.w_down.at[aligned(r, piece)], n.wda.at[aligned(f, piece)], n.wd_l.at[0]
            )
        ]

    for name in ("wq", "wu", "wd"):
        for copy in cut_copies(name):
            copy.start()

    def remote(src, dst, ss, rs, rep, fsdp):
        return pltpu.make_async_remote_copy(
            src_ref=src,
            dst_ref=dst,
            send_sem=ss,
            recv_sem=rs,
            device_id={"rep": rep, "fsdp": fsdp},
            device_id_type=MESH,
        )

    def send(src, dst, ss, rs, rep, fsdp, cond=None, tag="end"):
        def start():
            remote(src, dst, ss, rs, rep, fsdp).start()

        def done():
            remote(src, dst, ss, rs, rep, fsdp).wait_send()

        if cond is None:
            start()
            pending.setdefault(tag, []).append(done)
        else:
            pl.when(cond)(start)
            pending.setdefault(tag, []).append(lambda: pl.when(cond)(done))

    def drain(tag):
        for done in pending.pop(tag, []):
            done()

    def got(dst, rs):
        remote(dst, dst, rs, rs, sib, f).wait_recv()

    def xpeer(step):
        return lax.rem(x + 1 + step, X)

    def xfrom(step):
        return lax.rem(x + X - 1 - step, X)

    def outer(step):
        return lax.rem(a + step, A)

    def outer_from(step):
        return lax.rem(a + A - step, A)

    home_rep = (r // S) * S + b

    def home_fsdp(m):
        return m * S + lax.rem(r, S)

    barrier = pltpu.get_barrier_semaphore()

    def greet(rep, fsdp):
        pl.semaphore_signal(
            barrier, inc=1, device_id={"rep": rep, "fsdp": fsdp}, device_id_type=MESH
        )

    for step in range(1, A):
        greet(r, outer(step) * S + b)
    greet(r, a * S + other_b)
    greet(sib, f)
    for step in range(X - 1):
        greet(xpeer(step) * 2 + c, f)
    mine = [(home_fsdp(m) == f) & (home_rep == r) for m in range(MB)]
    for m in range(MB):

        @pl.when(jnp.logical_not(mine[m]))
        def _(m=m):
            greet(home_rep, home_fsdp(m))

    stays = (home_rep == r) & (lax.rem(r, S) == b)
    pl.semaphore_wait(barrier, (A - 1) + 1 + 1 + (X - 1) + MB - stays.astype(jnp.int32))

    def swap_start(which, src_of, dst_of):
        for m in range(MB):
            src, dst = src_of(m), dst_of(a)
            ss, rs = n.a2a_s.at[which, m], n.a2a_r.at[which, a]

            @pl.when(jnp.logical_not(mine[m]))
            def _():
                remote(src, dst, ss, rs, home_rep, home_fsdp(m)).start()

            @pl.when(mine[m])
            def _():
                pltpu.make_async_copy(src, dst, rs).start()

    def swap_end(which, src_of, dst_of):
        for m in range(MB):
            src, dst = src_of(m), dst_of(m)
            ss, rs = n.a2a_s.at[which, m], n.a2a_r.at[which, m]

            @pl.when(jnp.logical_not(mine[m]))
            def _():
                remote(src, dst, ss, rs, home_rep, home_fsdp(m)).wait()

            @pl.when(mine[m])
            def _():
                pltpu.make_async_copy(src, dst, rs).wait()

    def sem(name):
        return getattr(n, name)

    def gather_start(name, buf, height):
        at = aligned(f, height)
        src = buf.at[at]
        for step in range(1, A):
            send(
                src,
                buf.at[at],
                sem(name + "_os").at[step - 1],
                sem(name + "_or").at[step - 1],
                r,
                outer(step) * S + b,
            )
        send(src, buf.at[at], sem(name + "_is").at[0], sem(name + "_ir").at[0], r, a * S + other_b)

    def gather_forward(name, buf, height):
        for step in range(1, A):
            at = buf.at[aligned(outer_from(step) * S + b, height)]
            got(at, sem(name + "_or").at[step - 1])
            send(at, at, sem(name + "_is").at[step], sem(name + "_ir").at[step], r, a * S + other_b)

    def gather_end(name, buf, height):
        for step in range(A):
            at = buf.at[aligned(outer_from(step) * S + other_b, height)]
            got(at, sem(name + "_ir").at[step])

    def hop(step):
        return lax.rem(a + A + step, A)

    def chain_start(name, buf, height):
        at = buf.at[aligned(f, height)]
        send(at, at, sem(name + "_ups").at[0], sem(name + "_upr").at[0], r, hop(1) * S + b, a < A - 1)
        send(at, at, sem(name + "_dns").at[0], sem(name + "_dnr").at[0], r, hop(-1) * S + b, a > 0)
        send(at, at, sem(name + "_is").at[0], sem(name + "_ir").at[0], r, a * S + other_b)

    def chain_forward(name, buf, height, step):
        for way, has, on, to in (
            ("up", a >= step, a < A - 1, 1),
            ("dn", a + step < A, a > 0, -1),
        ):
            at = buf.at[aligned(hop(-to * step) * S + b, height)]

            @pl.when(has)
            def _():
                got(at, sem(name + "_%sr" % way).at[step - 1])

            if step < A - 1:
                send(
                    at,
                    at,
                    sem(name + "_%ss" % way).at[step],
                    sem(name + "_%sr" % way).at[step],
                    r,
                    hop(to) * S + b,
                    has & on,
                )
            index = step if way == "up" else A - 1 + step
            send(
                at,
                at,
                sem(name + "_is").at[index],
                sem(name + "_ir").at[index],
                r,
                a * S + other_b,
                has,
            )

    def chain_end(name, buf, height):
        got(buf.at[aligned(a * S + other_b, height)], sem(name + "_ir").at[0])
        for step in range(1, A):
            for has, to, index in ((a >= step, 1, step), (a + step < A, -1, A - 1 + step)):
                at = buf.at[aligned(hop(-to * step) * S + other_b, height)]

                @pl.when(has)
                def _():
                    got(at, sem(name + "_ir").at[index])

    is_source = a == r

    def out_start(src, buf):
        at = buf.at[aligned(b, piece)]

        @pl.when(is_source)
        def _():
            pltpu.make_async_copy(src, at, n.wo_l.at[0]).start()

        for step in range(1, A):
            send(
                src, at, n.wo_os.at[step - 1], n.wo_or.at[0], r, outer(step) * S + b, is_source
            )
        send(src, at, n.wo_is.at[0], n.wo_ir.at[0], r, a * S + other_b, is_source)

    def out_forward(buf):
        at = buf.at[aligned(b, piece)]

        @pl.when(jnp.logical_not(is_source))
        def _():
            got(at, n.wo_or.at[0])

        send(
            at, at, n.wo_is.at[1], n.wo_ir.at[0], r, a * S + other_b, jnp.logical_not(is_source)
        )

    def out_end(src, buf):
        @pl.when(is_source)
        def _():
            pltpu.make_async_copy(src, buf.at[aligned(b, piece)], n.wo_l.at[0]).wait()

        got(buf.at[aligned(other_b, piece)], n.wo_ir.at[0])

    def share_start(name, buf, height):
        at = buf.at[aligned(r, height)]
        for step in range(X - 1):
            send(
                at,
                at,
                sem(name + "_xs").at[step],
                sem(name + "_xr").at[step],
                xpeer(step) * 2 + c,
                f,
            )
        send(at, at, sem(name + "_ss").at[0], sem(name + "_sr").at[0], sib, f)

    def share_forward(name, buf, height):
        for step in range(X - 1):
            at = buf.at[aligned(xfrom(step) * 2 + c, height)]
            got(at, sem(name + "_xr").at[step])
            send(at, at, sem(name + "_ss").at[1 + step], sem(name + "_sr").at[1 + step], sib, f)

    def share_near(name, buf, height):
        got(buf.at[aligned(sib, height)], sem(name + "_sr").at[0])

    def share_far(name, buf, height):
        for step in range(X - 1):
            at = buf.at[aligned(xfrom(step) * 2 + 1 - c, height)]
            got(at, sem(name + "_sr").at[1 + step])

    def share_end(name, buf, height):
        share_near(name, buf, height)
        share_far(name, buf, height)

    wide = 256

    def sum_owner(step):
        return xpeer(step) if step < X - 1 else x

    def sum_near(index, slot, partial, step):
        to_sib, at = n.to_sib.at[slot], pl.ds(step * own, own)
        owner = sum_owner(step) * 2 + 1 - c
        if step == 0:
            drain("slot%d" % slot)

        def one(tile):
            cols = aligned(tile, wide)
            to_sib[at, cols] = partial(owner, cols).astype(BF)

        loop(d // wide, one)
        send(
            to_sib.at[at],
            n.of_sib.at[slot, at],
            sem("sum%d_ss" % index).at[step],
            sem("sum%d_sr" % index).at[step],
            sib,
            f,
            tag="slot%d" % slot,
        )

    def sum_mine(index, slot, partial, step, acc, post=True):
        of_sib, to_x, at = n.of_sib.at[slot], n.to_x.at[slot], pl.ds(step * own, own)
        owner = sum_owner(step) * 2 + c
        last = step == X - 1
        got(of_sib.at[at], sem("sum%d_sr" % index).at[step])

        def one(tile):
            cols = aligned(tile, wide)
            total = partial(owner, cols) + of_sib[at, cols].astype(F32)
            if last:
                acc[:, cols] = total
            else:
                to_x[at, cols] = total.astype(BF)

        loop(d // wide, one)
        if not last and post:
            sum_post(index, slot, step)

    def sum_post(index, slot, step):
        at = pl.ds(step * own, own)
        send(
            n.to_x.at[slot, at],
            n.of_x.at[slot, at],
            sem("sum%d_xs" % index).at[step],
            sem("sum%d_xr" % index).at[step],
            sum_owner(step) * 2 + c,
            f,
            tag="slot%d" % slot,
        )

    def sum_end(index, slot):
        of_x = n.of_x.at[slot]
        for step in range(X - 1):
            got(of_x.at[pl.ds(step * own, own)], sem("sum%d_xr" % index).at[step])

    def came(slot, at):
        total = None
        for step in range(X - 1):
            part = n.of_x[slot, pl.ds(step * own + at, tall), :].astype(F32)
            total = part if total is None else total + part
        return total

    tall = 32

    def by_own(body):
        def one(index):
            at = pl.multiple_of(index * tall, tall)
            body(at, pl.ds(at, tall))

        loop(own // tall, one)

    def grad_start(name, buf, height):
        out = name == "o"
        inbox = sem("gi" + name)
        for step in range(1 if out else A):
            to_a = r if out else outer(step + 1)
            src = buf.at[aligned((0 if out else to_a * S) + other_b, height)]
            send(
                src,
                inbox.at[pl.ds(step * height, height)],
                sem("g" + name + "_is").at[step],
                sem("g" + name + "_ir").at[step],
                r,
                a * S + other_b,
            )

    def add_into(dst, base, inbox, start, height):
        small = min(height, 32)

        def one(index):
            at = pl.ds(pl.multiple_of(base + index * small, small), small)
            of = pl.ds(pl.multiple_of(start + index * small, small), small)
            dst[at, :] = (dst[at, :].astype(F32) + inbox[of, :].astype(F32)).astype(dst.dtype)

        loop(height // small, one)

    def grad_forward(name, buf, height):
        out = name == "o"
        inbox, outbox = sem("gi" + name), sem("go" + name)
        for step in range(1 if out else A):
            to_a = r if out else outer(step + 1)
            base = ((0 if out else to_a * S) + b) * height
            got(inbox.at[pl.ds(step * height, height)], sem("g" + name + "_ir").at[step])
            add_into(buf, base, inbox, step * height, height)
            if out:
                slot = lax.rem(r + A - a - 1, A)
                slot = jnp.where(is_source, 0, slot)
                send(
                    buf.at[pl.ds(pl.multiple_of(base, height), height)],
                    outbox.at[aligned(slot, height)],
                    n.go_os.at[0],
                    n.go_or.at[slot],
                    r,
                    r * S + b,
                    jnp.logical_not(is_source),
                )
            elif step < A - 1:
                send(
                    buf.at[pl.ds(pl.multiple_of(base, height), height)],
                    outbox.at[pl.ds(step * height, height)],
                    sem("g" + name + "_os").at[step],
                    sem("g" + name + "_or").at[step],
                    r,
                    to_a * S + b,
                )

    def grad_wait(name, height):
        for step in range(A - 1):
            got(
                sem("go" + name).at[pl.ds(step * height, height)],
                sem("g" + name + "_or").at[step],
            )

    def grad_total(name, buf, base, height, target, target_base, boxes):
        outbox = sem("go" + name)
        small = min(height, 32)

        def one(index):
            off = index * small
            total = buf[pl.ds(pl.multiple_of(base + off, small), small), :].astype(F32)
            for box in boxes:
                at = pl.ds(pl.multiple_of(box * height + off, small), small)
                total = total + outbox[at, :].astype(F32)
            at = pl.ds(pl.multiple_of(target_base + off, small), small)
            target[at, :] = total.astype(target.dtype)

        loop(height // small, one)

    side = a // 2
    mate = a + 1 - 2 * lax.rem(a, 2)
    is_end = (a == 0) | (a == A - 1)
    passes_on = jnp.logical_not(is_end)
    piece_owner = (2 - side, 3 * (1 - side), mate, a)

    def piece_start(name, step):
        height, inbox = piece, sem("gi" + name)
        send(
            sem("g" + name).at[aligned(piece_owner[step] * S + other_b, height)],
            inbox.at[pl.ds(step * height, height)],
            sem("g" + name + "_is").at[step],
            sem("g" + name + "_ir").at[step],
            r,
            a * S + other_b,
        )

    def piece_take(name, step):
        buf, inbox, outbox = sem("g" + name), sem("gi" + name), sem("go" + name)
        base = (piece_owner[step] * S + b) * piece
        got(inbox.at[pl.ds(step * piece, piece)], sem("g" + name + "_ir").at[step])
        add_into(buf, base, inbox, step * piece, piece)
        if step < 3:
            send(
                buf.at[pl.ds(pl.multiple_of(base, piece), piece)],
                outbox.at[pl.ds(step * piece, piece)],
                sem("g" + name + "_os").at[step],
                sem("g" + name + "_or").at[step],
                r,
                mate * S + b,
                is_end if step < 2 else None,
            )

    def piece_pass(name, step):
        buf, outbox = sem("g" + name), sem("go" + name)
        base = (piece_owner[step] * S + b) * piece

        @pl.when(passes_on)
        def _():
            got(outbox.at[pl.ds(step * piece, piece)], sem("g" + name + "_or").at[step])
            add_into(buf, base, outbox, step * piece, piece)

        send(
            buf.at[pl.ds(pl.multiple_of(base, piece), piece)],
            outbox.at[pl.ds(3 * piece, piece)],
            sem("g" + name + "_os").at[step],
            sem("g" + name + "_or").at[3],
            r,
            piece_owner[step] * S + b,
            passes_on,
        )

    def piece_own(name):
        for box in (2, 3):
            got(
                sem("go" + name).at[pl.ds(box * piece, piece)], sem("g" + name + "_or").at[box]
            )
        grad_total(name, sem("g" + name), f * piece, piece, sem("gr" + name), r * piece, (2, 3))
        share_start("r" + name, sem("gr" + name), piece)

    def hid_at(i):
        return n.hid.at[aligned(i, cap)]

    def ct_at(i):
        return n.ct.at[aligned(i, cap)]

    def info_src(i):
        return n.info.at[i]

    def info_own(i):
        return n.infos.at[aligned(r * MB + i, 8)]

    def info_home(i):
        return n.infos.at[aligned(home_rep * MB + i, 8)]

    odd = lax.rem(a, 2)
    lane_token = lax.broadcasted_iota(jnp.int32, (tok_count, 128), 0)
    lane = lax.broadcasted_iota(jnp.int32, (1, 128), 1)
    lane_used = (lane // cap) == odd

    def at_of(m):
        row = n.chosen[m : m + 1, :]
        return jnp.where(lane_used, jnp.concatenate([row, row], axis=1), -1)

    def hot_of(m):
        return (lane_token == at_of(m)).astype(F32).astype(BF)

    def tok_at(m):
        return n.picked.at[pl.ds(pl.multiple_of(m * 128 + odd * cap, cap), cap)]

    def cot_at(m):
        return n.picked_ct.at[pl.ds(pl.multiple_of(m * 128 + odd * cap, cap), cap)]

    mine_sm = pl.ds(pl.multiple_of(f * 8, 8), 8)
    n.sm[mine_sm, :] = jnp.concatenate(
        [n.router[...].astype(F32), n.gains[...].astype(F32), jnp.zeros((5, 128), F32)], axis=0
    )
    gather_start("small", n.sm, 8)
    for copy in cut_copies("wq"):
        copy.wait()
    for m in range(MB):
        hot = hot_of(m)
        token_copy(0, m).wait()
        n.picked[m * 128 : (m + 1) * 128, :] = dot(
            hot, n.pair_a[m * tok_count : (m + 1) * tok_count, :], (0, 0)
        ).astype(BF)
        lines = jnp.concatenate([n.path[line, m : m + 1, :] for line in range(3)], axis=0)
        n.info[m, 0:3, :] = dot(lines.astype(F32).astype(BF), hot, (1, 0))
        at = at_of(m)
        n.info[m, 3:4, :] = jnp.where(at >= 0, at + f * tok_count, 0).astype(F32)
        n.info[m, 4:8, :] = jnp.zeros((4, 128), F32)
    swap_start(0, tok_at, hid_at)
    for m in range(MB):
        ss, rs = n.a2a_s.at[1, m], n.a2a_r.at[1, a]

        @pl.when(jnp.logical_not(mine[m]))
        def _():
            remote(info_src(m), info_home(a), ss, rs, home_rep, home_fsdp(m)).start()

        @pl.when(mine[m])
        def _():
            pltpu.make_async_copy(info_src(m), info_own(a), rs).start()

    chain_start("wq", n.wqa, piece)
    for m in range(MB):
        token_copy(1, m).wait()
        n.picked_ct[m * 128 : (m + 1) * 128, :] = dot(
            hot_of(m), n.pair_b[m * tok_count : (m + 1) * tok_count, :], (0, 0)
        ).astype(BF)
    gather_forward("small", n.sm, 8)
    gather_end("small", n.sm, 8)
    for index in range(F):
        n.vec[:, index * 128 : (index + 1) * 128] = n.sm[index * 8 : (index + 1) * 8, :]
    swap_end(0, tok_at, hid_at)

    def first_norm(at, rows_at):
        h = n.hid[rows_at, :].astype(F32)
        scale = lax.rsqrt(jnp.mean(h * h, axis=-1, keepdims=True) + eps)
        n.normed[pl.ds(pl.multiple_of(r * own + at, tall), tall), :] = (
            h * scale * n.vec[1:2, :]
        ).astype(BF)
        logit = jnp.sum(h * n.vec[0:1, :], axis=-1, keepdims=True)
        n.gate[rows_at, :] = jnp.broadcast_to(1.0 / (1.0 + jnp.exp(-logit)), (tall, 128))

    by_own(first_norm)
    share_start("normed", n.normed, own)
    chain_forward("wq", n.wqa, piece, 1)
    swap_end(1, info_src, info_own)
    share_start("info", n.infos, MB * 8)
    swap_start(2, cot_at, ct_at)
    chain_forward("wq", n.wqa, piece, 2)
    out_start(n.w_out, n.woa)
    for copy in cut_copies("wu"):
        copy.wait()
    chain_start("wu", n.wua, piece)
    chain_forward("wq", n.wqa, piece, 3)
    share_forward("info", n.infos, MB * 8)
    share_forward("normed", n.normed, own)
    for copy in cut_copies("wd"):
        copy.wait()
    chain_start("wd", n.wda, piece)
    share_end("info", n.infos, MB * 8)
    share_end("normed", n.normed, own)
    swap_end(2, cot_at, ct_at)

    def mlp_cotangent(at, rows_at):
        gc = n.gate[rows_at, 0:1] * n.ct[rows_at, :].astype(F32)
        n.gmlp[pl.ds(pl.multiple_of(r * own + at, tall), tall), :] = gc.astype(BF)

    by_own(mlp_cotangent)
    share_start("gmlp", n.gmlp, own)
    chain_end("wq", n.wqa, piece)
    far = xpeer(0)
    near_blocks, far_blocks = (r, sib), (far * 2 + c, far * 2 + 1 - c)

    def project(block):
        at = aligned(block, own)
        half = g.qc // 3

        def one(part):
            cols = aligned(part, half)
            n.proj[at, cols] = dot(n.normed[at, :], n.wqa[:, cols], (1, 0)).astype(BF)

        loop(3, one)

    tree, pairs = g.tree, g.heads // 2
    scale = 64 ** (-0.5)
    low_lane = lax.broadcasted_iota(jnp.int32, (tree, 128), 1) < 64

    def half_of(value, half):
        keep = low_lane if half == 0 else jnp.logical_not(low_lane)
        return jnp.where(keep, value, jnp.zeros_like(value))

    def join(first, second):
        return jnp.where(low_lane, first, second)

    def make_bias(t):
        blocks = []
        for index in range(S * MB // 2):
            at = pl.multiple_of((t * S * MB + index * 2) * 8, 8)
            blocks.append(n.infos[pl.ds(at, 8), :] + n.infos[pl.ds(at + 8, 8), :])
        keys = jnp.concatenate(blocks, axis=1)
        asked = jnp.transpose(keys)
        near = keys[0:1, :] == asked[:, 0:1]
        near = near | (keys[0:1, :] == asked[:, 1:2])
        near = near | (keys[0:1, :] == asked[:, 2:3])
        near = near & (keys[3:4, :] <= asked[:, 3:4])
        n.bias[...] = jnp.where(near, 0.0, -1e30)

    def columns(part, pair):
        return pl.ds(part * g.ac + pair * 128, 128)

    def attend(t):
        make_bias(t)
        at = aligned(t, tree)
        for pair in range(pairs):
            q = n.proj[at, columns(0, pair)]
            k = n.proj[at, columns(1, pair)]
            v = n.proj[at, columns(2, pair)]
            made = []
            for half in range(2):
                s = dot(half_of(q, half), k, (1, 1)) * scale + n.bias[...]
                top = jnp.max(s, axis=-1, keepdims=True)
                e = jnp.exp(s - top)
                total = jnp.sum(e, axis=-1, keepdims=True)
                made.append(dot((e * (1.0 / total)).astype(BF), v, (1, 0)))
                head = pair * 2 + half
                n.lse[at, head : head + 1] = top + jnp.log(total)
            n.att[at, pl.ds(pair * 128, 128)] = join(*made).astype(BF)

    def branch_part(owner, cols):
        return dot(n.att[aligned(owner, own), :], n.woa[:, cols], (1, 0))

    for block in far_blocks:
        project(block)
    out_forward(n.woa)
    chain_forward("wu", n.wua, piece, 1)
    attend(far)
    out_end(n.w_out, n.woa)
    sum_near(0, 0, branch_part, 0)
    for block in near_blocks:
        project(block)
    sum_mine(0, 0, branch_part, 0, n.branch)
    chain_forward("wu", n.wua, piece, 2)
    chain_forward("wd", n.wda, piece, 1)
    attend(x)
    sum_near(0, 0, branch_part, 1)
    chain_forward("wu", n.wua, piece, 3)
    sum_mine(0, 0, branch_part, 1, n.branch)
    chain_forward("wd", n.wda, piece, 2)
    share_forward("gmlp", n.gmlp, own)
    sum_end(0, 0)

    def second_norm(at, rows_at):
        br = n.branch[rows_at, :] + came(0, at)
        n.branch[rows_at, :] = br
        mid = n.hid[rows_at, :].astype(F32) + br
        inv = lax.rsqrt(jnp.mean(mid * mid, axis=-1, keepdims=True) + eps)
        n.norm2[pl.ds(pl.multiple_of(r * own + at, tall), tall), :] = (
            mid * inv * n.vec[2:3, :]
        ).astype(BF)

    by_own(second_norm)
    share_start("norm2", n.norm2, own)
    chain_end("wu", n.wua, piece)
    chain_forward("wd", n.wda, piece, 3)

    tiles = g.fc // wide

    def mlp_up(block):
        at = aligned(block, own)

        def one(tile):
            cols = aligned(tile, wide)
            u = dot(n.norm2[at, :], n.wua[:, cols], (1, 0))
            square = u * u
            t = jnp.tanh(GELU_A * (u + GELU_B * square * u))
            n.act[at, cols] = (0.5 * u * (1.0 + t)).astype(BF)
            n.dact[at, cols] = 0.5 * (1.0 + t) + (0.5 * GELU_A) * u * (1.0 - t * t) * (
                1.0 + (3.0 * GELU_B) * square
            )

        loop(tiles, one)

    def mlp_back(block):
        at = aligned(block, own)

        def one(tile):
            cols = aligned(tile, wide)
            ga = dot(n.gmlp[at, :], n.wda[cols, :], (1, 1))
            n.gup[at, cols] = (ga * n.dact[at, cols]).astype(BF)

        loop(tiles, one)

    def norm2_part(owner, cols):
        return dot(n.gup[aligned(owner, own), :], n.wua[cols, :], (1, 1))

    def weight_grad(left, right, target, count):
        def one(index):
            cols = aligned(index, 256)
            target[cols, :] = dot(left[:, cols], right[...], (0, 0)).astype(BF)

        loop(count // 256, one)

    mlp_up(r)
    share_near("norm2", n.norm2, own)
    mlp_up(sib)
    share_end("gmlp", n.gmlp, own)
    share_forward("norm2", n.norm2, own)
    mlp_up(far_blocks[0])
    share_far("norm2", n.norm2, own)
    mlp_up(far_blocks[1])
    chain_end("wd", n.wda, piece)
    mlp_back(far_blocks[1])
    sum_near(1, 1, norm2_part, 0)
    mlp_back(far_blocks[0])
    sum_mine(1, 1, norm2_part, 0, n.gmid)
    weight_grad(n.act, n.gmlp, n.gd, g.fc)
    for step in range(A):
        piece_start("d", step)
    mlp_back(sib)
    sum_near(1, 1, norm2_part, 1)
    mlp_back(r)
    sum_mine(1, 1, norm2_part, 1, n.gmid)
    weight_grad(n.norm2, n.gup, n.gu, d)
    n.gsum[...] = jnp.zeros_like(n.gsum)
    sum_end(1, 1)

    def second_back(at, rows_at):
        dy = n.gmid[rows_at, :] + came(1, at)
        mid = n.hid[rows_at, :].astype(F32) + n.branch[rows_at, :]
        inv = lax.rsqrt(jnp.mean(mid * mid, axis=-1, keepdims=True) + eps)
        n.gsum[2:3, :] = n.gsum[2:3, :] + jnp.sum(dy * mid * inv, axis=0, keepdims=True)
        t = dy * n.vec[2:3, :]
        along = jnp.sum(mid * t, axis=-1, keepdims=True) * (inv * inv * inv * (1.0 / d))
        gm = inv * t - mid * along
        n.gmid[rows_at, :] = gm
        gc = n.gate[rows_at, 0:1] * n.ct[rows_at, :].astype(F32)
        n.gbr[pl.ds(pl.multiple_of(r * own + at, tall), tall), :] = (gc + gm).astype(BF)

    by_own(second_back)
    share_start("gbr", n.gbr, own)
    piece_take("d", 0)
    piece_start("u", 0)

    def attention_cotangent(block):
        at = aligned(block, own)
        n.gatt[at, :] = dot(n.gbr[at, :], n.woa[...], (1, 1)).astype(BF)

    def attend_back(t):
        make_bias(t)
        at = aligned(t, tree)
        for pair in range(pairs):
            q = n.proj[at, columns(0, pair)]
            k = n.proj[at, columns(1, pair)]
            v = n.proj[at, columns(2, pair)]
            da = n.gatt[at, pl.ds(pair * 128, 128)]
            dq, dk, dv = [], [], []
            for half in range(2):
                head = pair * 2 + half
                s = dot(half_of(q, half), k, (1, 1)) * scale + n.bias[...]
                p = jnp.exp(s - n.lse[at, head : head + 1])
                dp = dot(half_of(da, half), v, (1, 1))
                delta = jnp.sum(p * dp, axis=-1, keepdims=True)
                ds = (p * (dp - delta)).astype(BF)
                dq.append(dot(ds, k, (1, 0)))
                dk.append(dot(ds, q, (0, 0)))
                dv.append(dot(p.astype(BF), da, (0, 0)))
            n.gproj[at, columns(0, pair)] = (join(*dq) * scale).astype(BF)
            n.gproj[at, columns(1, pair)] = (join(*dk) * scale).astype(BF)
            n.gproj[at, columns(2, pair)] = join(*dv).astype(BF)

    def change_part(owner, cols):
        return dot(n.act[aligned(owner, own), :], n.wda[:, cols], (1, 0))

    attention_cotangent(r)
    share_near("gbr", n.gbr, own)
    attention_cotangent(sib)
    attend_back(x)
    piece_take("d", 1)
    piece_start("u", 1)
    sum_near(2, 0, change_part, 0)
    sum_near(2, 0, change_part, 1)
    share_forward("gbr", n.gbr, own)
    sum_mine(2, 0, change_part, 0, n.acc)
    attention_cotangent(far_blocks[0])
    share_far("gbr", n.gbr, own)
    attention_cotangent(far_blocks[1])
    attend_back(far)

    def normed_part(owner, cols):
        return dot(n.gproj[aligned(owner, own), :], n.wqa[cols, :], (1, 1))

    sum_near(3, 1, normed_part, 0)
    sum_mine(2, 0, change_part, 1, n.acc)
    sum_mine(3, 1, normed_part, 0, n.gfirst)
    sum_near(3, 1, normed_part, 1)
    piece_take("d", 2)
    piece_start("u", 2)
    sum_mine(3, 1, normed_part, 1, n.gfirst)
    weight_grad(n.normed, n.gproj, n.gq, d)
    piece_take("d", 3)
    piece_start("u", 3)
    for step in range(A):
        piece_start("q", step)
    weight_grad(n.att, n.gbr, n.go, g.ac)
    grad_start("o", n.go, piece)
    piece_pass("d", 0)
    piece_pass("d", 1)

    sum_end(2, 0)

    def new_rows(at, rows_at):
        change = n.branch[rows_at, :] + n.acc[rows_at, :] + came(0, at)
        h = n.hid[rows_at, :].astype(F32)
        gate = n.gate[rows_at, 0:1]
        n.nrow[rows_at, :] = (h + gate * change).astype(BF)
        logit = jnp.sum(n.ct[rows_at, :].astype(F32) * change, axis=-1, keepdims=True)
        logit = logit * gate * (1.0 - gate)
        n.glog[rows_at, :] = jnp.broadcast_to(logit, (tall, 128))
        n.gsum[0:1, :] = n.gsum[0:1, :] + jnp.sum(logit * h, axis=0, keepdims=True)

    by_own(new_rows)

    def new_at(i):
        return n.nrow.at[aligned(i, cap)]

    swap_start(4, new_at, lambda m: n.new_out.at[m])
    piece_take("u", 0)
    piece_take("u", 1)
    sum_end(3, 1)

    def first_back(at, rows_at):
        dy = n.gfirst[rows_at, :] + came(1, at)
        h = n.hid[rows_at, :].astype(F32)
        inv = lax.rsqrt(jnp.mean(h * h, axis=-1, keepdims=True) + eps)
        n.gsum[1:2, :] = n.gsum[1:2, :] + jnp.sum(dy * h * inv, axis=0, keepdims=True)
        t = dy * n.vec[1:2, :]
        along = jnp.sum(h * t, axis=-1, keepdims=True) * (inv * inv * inv * (1.0 / d))
        total = n.ct[rows_at, :].astype(F32) + n.gmid[rows_at, :] + (inv * t - h * along)
        total = total + n.glog[rows_at, 0:1] * n.vec[0:1, :]
        n.grow[rows_at, :] = total.astype(BF)

    by_own(first_back)

    def grow_at(i):
        return n.grow.at[aligned(i, cap)]

    swap_start(3, grow_at, lambda m: n.grad_out.at[m])
    for index in range(F):
        n.gsp[index * 8 : (index + 1) * 8, :] = n.gsum[:, index * 128 : (index + 1) * 128]
    grad_start("s", n.gsp, 8)
    piece_own("d")
    piece_take("u", 2)
    piece_take("u", 3)
    piece_take("q", 0)
    piece_pass("u", 0)
    piece_take("q", 1)
    piece_pass("u", 1)
    piece_take("q", 2)
    piece_take("q", 3)
    grad_forward("o", n.go, piece)
    grad_forward("s", n.gsp, 8)
    piece_pass("q", 0)
    piece_pass("q", 1)
    share_forward("rd", n.grd, piece)
    piece_own("u")

    @pl.when(is_source)
    def _():
        grad_wait("o", piece)
        grad_total("o", n.go, b * piece, piece, n.gro, 0, range(A - 1))

    ax, ac = a // 2, lax.rem(a, 2)
    for step in range(X - 1):
        send(n.gro, n.gro, n.ro_xs.at[step], n.ro_xr.at[0], xpeer(step) * 2 + c, f, is_source)
    send(n.gro, n.gro, n.ro_ss.at[0], n.ro_sr.at[0], sib, f, is_source)
    grad_wait("s", 8)
    grad_total("s", n.gsp, f * 8, 8, n.gs_mine.at[0], 0, range(A - 1))
    send(n.gs_mine.at[0], n.gs_pair.at[0], n.pair_s.at[0], n.pair_r.at[0], sib, f)
    piece_own("q")
    share_end("rd", n.grd, piece)

    off_x = (c == ac) & (x != ax)

    @pl.when(off_x)
    def _():
        got(n.gro, n.ro_xr.at[0])

    send(n.gro, n.gro, n.ro_ss.at[1], n.ro_sr.at[0], sib, f, off_x)

    def out_copies(which, name, target):
        buf = sem("gr" + name)
        return [
            pltpu.make_async_copy(
                buf.at[pl.ds(index * piece, piece)], target.at[index], n.out_l.at[which, index]
            )
            for index in range(R)
        ]

    for copy in out_copies(0, "d", n.rd_out):
        copy.start()
    share_forward("ru", n.gru, piece)
    share_end("ru", n.gru, piece)
    for copy in out_copies(1, "u", n.ru_out):
        copy.start()

    @pl.when(c != ac)
    def _():
        got(n.gro, n.ro_sr.at[0])

    last = pltpu.make_async_copy(n.gro, n.ro_out, n.out_l.at[2, 0])
    last.start()
    got(n.gs_pair.at[0], n.pair_r.at[0])
    n.gs_mine[1] = n.gs_mine[0] + n.gs_pair[0]
    send(n.gs_mine.at[1], n.gs_pair.at[1], n.pair_s.at[1], n.pair_r.at[1], xpeer(0) * 2 + c, f)
    share_forward("rq", n.grq, piece)
    share_end("rq", n.grq, piece)
    for copy in out_copies(3, "q", n.rq_out):
        copy.start()
    got(n.gs_pair.at[1], n.pair_r.at[1])
    n.gs_out[...] = n.gs_mine[1] + n.gs_pair[1]
    swap_end(4, new_at, lambda m: n.new_out.at[m])
    swap_end(3, grow_at, lambda m: n.grad_out.at[m])
    for which, name, target in ((0, "d", n.rd_out), (1, "u", n.ru_out), (3, "q", n.rq_out)):
        for copy in out_copies(which, name, target):
            copy.wait()
    last.wait()
    for tag in list(pending):
        drain(tag)


def place_kernel(g, at_ref, tok_ref, cot_ref, new_ref, grad_ref, rq_ref, ru_ref, rd_ref, ro_ref, gs_ref, *outs):
    mixed_ref, gt_ref, gq_ref, gu_ref, gd_ref, go_ref, grouter_ref, ggains_ref = outs
    grouter_ref[...] = gs_ref[0:1, :]
    ggains_ref[...] = gs_ref[1:3, :]
    tall = tok_ref.shape[1]
    first = pl.program_id(1) * tall
    token = lax.broadcasted_iota(jnp.int32, (tall, g.cap), 0) + first
    hot = token == at_ref[0]
    routed = jnp.max(hot.astype(F32), axis=-1, keepdims=True) > 0.0
    hot = hot.astype(BF)
    new = dot(hot, new_ref[0], (1, 0))
    mixed_ref[0] = jnp.where(routed, new, tok_ref[0].astype(F32)).astype(BF)
    grad = dot(hot, grad_ref[0], (1, 0))
    gt_ref[0] = jnp.where(routed, grad, cot_ref[0].astype(F32))
    for index in range(g.R):
        for part in range(3):
            gq_ref[:, pl.ds(part * g.d + index * g.ac, g.ac)] = rq_ref[
                index, :, pl.ds(part * g.ac, g.ac)
            ].astype(F32)
        for block in range(g.F):
            gu_ref[:, pl.ds((block * g.R + index) * 128, 128)] = ru_ref[
                index, :, pl.ds(block * 128, 128)
            ].astype(F32)
        gd_ref[index] = rd_ref[index].astype(F32)
    go_ref[...] = ro_ref[...].astype(F32)


def place(g, chosen, tokens, cotangent, new_rows, grad_rows, rq, ru, rd, ro, gs):
    halves = 2
    steps = g.MB * halves
    tok_count = tokens.shape[1]
    tall = tok_count // halves
    piece = g.d // g.F
    low = piece // steps
    hidden = g.F * g.R * 128

    def block(*shape):
        return pl.BlockSpec((1,) + shape, lambda m, h: (m, h, 0))

    def micro(*shape):
        return pl.BlockSpec((1,) + shape, lambda m, h: (m, 0, 0))

    def slab(*lead, cols):
        return pl.BlockSpec(
            lead + (low, cols), lambda m, h: (0,) * len(lead) + (m * halves + h, 0)
        )

    return pl.pallas_call(
        functools.partial(place_kernel, g),
        grid=(g.MB, halves),
        in_specs=[
            micro(1, g.cap),
            block(tall, g.d),
            block(tall, g.d),
            micro(g.cap, g.d),
            micro(g.cap, g.d),
            slab(g.R, cols=g.qc),
            slab(g.R, cols=g.fc),
            slab(g.R, cols=g.d),
            slab(cols=g.d),
            pl.BlockSpec((8, 128), lambda m, h: (0, 0)),
        ],
        out_specs=[
            block(tall, g.d),
            block(tall, g.d),
            slab(cols=3 * g.d),
            slab(cols=hidden),
            slab(g.R, cols=g.d),
            slab(cols=g.d),
            pl.BlockSpec((1, 128), lambda m, h: (0, 0)),
            pl.BlockSpec((2, 128), lambda m, h: (0, 0)),
        ],
        out_shape=[
            jax.ShapeDtypeStruct(tokens.shape, BF),
            jax.ShapeDtypeStruct(tokens.shape, F32),
            jax.ShapeDtypeStruct((piece, 3 * g.d), F32),
            jax.ShapeDtypeStruct((piece, hidden), F32),
            jax.ShapeDtypeStruct((g.R, piece, g.d), F32),
            jax.ShapeDtypeStruct((piece, g.d), F32),
            jax.ShapeDtypeStruct((1, 128), F32),
            jax.ShapeDtypeStruct((2, 128), F32),
        ],
        compiler_params=pltpu.CompilerParams(vmem_limit_bytes=60 * 1024 * 1024),
        name="place_rows",
    )(chosen[:, None, :], tokens, cotangent, new_rows, grad_rows, rq, ru, rd, ro, gs)


def group_shards(tokens, cotangent, path, chosen, router, gains, w_qkv, w_out, w_up, w_down):
    R, F = lax.axis_size("rep"), lax.axis_size("fsdp")
    MB, tok_count, d = tokens.shape
    cap = chosen.shape[1]
    S = F // MB
    hidden = w_up.shape[1]
    g = types.SimpleNamespace(
        R=R,
        F=F,
        S=S,
        A=MB,
        X=R // 2,
        MB=MB,
        cap=cap,
        d=d,
        own=MB * cap,
        rows=R * MB * cap,
        tree=S * MB * cap,
        trees=R // S,
        heads=HEADS // R,
        qc=3 * d // R,
        ac=d // R,
        fc=hidden // R,
    )
    g.items = (
        ("q", F, g.qc, BF),
        ("u", F, g.fc, BF),
        ("d", F, d, BF),
        ("o", S, d, BF),
        ("s", F, 128, F32),
    )
    piece = d // F

    operands = {
        "tokens": tokens,
        "cotangent": cotangent,
        "w_qkv": w_qkv,
        "w_out": w_out,
        "w_up": w_up,
        "w_down": w_down,
        "path": jnp.transpose(path, (2, 0, 1)),
        "chosen": chosen,
        "router": router[None],
        "gains": gains.T,
    }
    results = {
        "new_out": ((MB, cap, d), BF),
        "grad_out": ((MB, cap, d), BF),
        "rq_out": ((R, piece, g.qc), BF),
        "ru_out": ((R, piece, g.fc), BF),
        "rd_out": ((R, piece, d), BF),
        "ro_out": ((piece, d), BF),
        "gs_out": ((8, 128), F32),
    }
    vmem, sems = scratch_shapes(g)
    names = list(operands) + list(results) + list(vmem) + list(sems)
    made = pl.pallas_call(
        functools.partial(block_kernel, g, names),
        out_shape=[jax.ShapeDtypeStruct(*kind) for kind in results.values()],
        in_specs=[
            pl.BlockSpec(
                memory_space=pltpu.VMEM if name in ("path", "chosen", "router", "gains") else pl.ANY
            )
            for name in operands
        ],
        out_specs=[
            pl.BlockSpec(memory_space=pltpu.VMEM if name == "gs_out" else pl.ANY)
            for name in results
        ],
        scratch_shapes=[pltpu.VMEM(*kind) for kind in vmem.values()]
        + [pltpu.SemaphoreType.DMA(shape) for shape in sems.values()],
        compiler_params=pltpu.CompilerParams(
            collective_id=0, has_side_effects=True, vmem_limit_bytes=60 * 1024 * 1024
        ),
        name="routed_block",
    )(*operands.values())
    new_rows, grad_rows, rq, ru, rd, ro, gs = made
    mixed, grad_tokens, grad_qkv, grad_up, grad_down, grad_out, grad_router, grad_gains = place(
        g, chosen, tokens, cotangent, new_rows, grad_rows, rq, ru, rd, ro, gs
    )
    return (
        mixed,
        grad_tokens,
        grad_router[0],
        grad_gains.T,
        grad_qkv,
        grad_out,
        grad_up,
        grad_down.reshape(R * piece, d),
    )


def plain_norm(matrix, gain_row):
    return matrix * lax.rsqrt(jnp.mean(matrix * matrix, axis=-1, keepdims=True) + eps) * gain_row


def inner(left, right):
    return lax.dot_general(
        left, right, (((0,), (0,)), ((), ())), preferred_element_type=jnp.float32
    )


def by_rows(left, right):
    return lax.dot_general(
        left, right, (((1,), (1,)), ((), ())), preferred_element_type=jnp.float32
    )


def gather_rows(arrays):
    return lax.all_gather(arrays, "fsdp", axis=0, tiled=True)


def scatter_sum(array):
    return lax.psum_scatter(
        array.astype(jnp.bfloat16), "fsdp", scatter_dimension=0, tiled=True
    ).astype(jnp.float32)


def plain_shards(tokens, cotangent, path, chosen, router, gains, w_qkv, w_out, w_up, w_down):
    micro_count, tok_count, model_width = tokens.shape
    slot_count = chosen.shape[1]
    row_count = micro_count * slot_count
    head_dim = model_width // HEADS
    score_scale = head_dim ** (-0.5)
    offset = lax.axis_index("fsdp") * tok_count
    fsdp = lax.axis_size("fsdp")

    def pick(array):
        return jax.vmap(lambda rows, at: rows[at])(array, chosen)

    small = jnp.concatenate([router[:, None], gains], axis=1)
    small_all = gather_rows(small)
    qkv_all = gather_rows(w_qkv)
    out_all = gather_rows(w_out)
    up_all = gather_rows(w_up)
    down_all = gather_rows(w_down)
    router_float = small_all[:, 0].astype(jnp.float32)
    gain_one = small_all[:, 1].astype(jnp.float32)
    gain_two = small_all[:, 2].astype(jnp.float32)

    routed = pick(tokens).reshape(row_count, model_width)
    hidden = routed.astype(jnp.float32)
    gate_rate = jax.nn.sigmoid(
        jnp.dot(routed, small_all[:, 0], preferred_element_type=jnp.float32)
    )
    normed = plain_norm(hidden, gain_one).astype(jnp.bfloat16)
    projected = jnp.dot(normed, qkv_all, preferred_element_type=jnp.float32).astype(jnp.bfloat16)
    queries = projected[:, :model_width].reshape(micro_count, slot_count, HEADS, head_dim)
    own_path = pick(path)
    own_place = offset + chosen
    key_info = jnp.concatenate([own_path[:, :, :1], own_place[:, :, None]], axis=2)
    gathered = lax.all_gather(
        projected[:, model_width:].reshape(micro_count, slot_count, 2 * model_width), "fsdp"
    )
    info_all = lax.all_gather(key_info, "fsdp")
    key_count = fsdp * slot_count
    gathered = jnp.swapaxes(gathered, 0, 1).reshape(micro_count, key_count, 2, HEADS, head_dim)
    info_all = jnp.swapaxes(info_all, 0, 1).reshape(micro_count, key_count, 2)
    key_rows = gathered[:, :, 0]
    value_rows = gathered[:, :, 1]
    key_seg = info_all[:, None, :, 0]
    visible = (
        (key_seg == own_path[:, :, 0:1])
        | (key_seg == own_path[:, :, 1:2])
        | (key_seg == own_path[:, :, 2:3])
    ) & (info_all[:, None, :, 1] <= own_place[:, :, None])
    visible = visible[:, None]

    def product(form, left, right):
        return jnp.einsum(form, left, right, preferred_element_type=jnp.float32)

    scores = product("mqhd,mkhd->mhqk", queries, key_rows) * score_scale
    scores = jnp.where(visible, scores, -1e30)
    row_max = jnp.max(scores, axis=-1, keepdims=True)
    exponent = jnp.where(visible, jnp.exp(scores - row_max), 0.0)
    row_total = jnp.sum(exponent, axis=-1, keepdims=True)
    soft_prob = exponent / row_total
    probs = soft_prob.astype(jnp.bfloat16)
    attention = product("mhqk,mkhd->mqhd", probs, value_rows)
    attention = attention.reshape(row_count, model_width).astype(jnp.bfloat16)
    branch = jnp.dot(attention, out_all, preferred_element_type=jnp.float32)
    middle = hidden + branch
    normed_two = plain_norm(middle, gain_two).astype(jnp.bfloat16)
    up_proj = jnp.dot(normed_two, up_all, preferred_element_type=jnp.float32)
    activated = jax.nn.gelu(up_proj).astype(jnp.bfloat16)
    change = branch + jnp.dot(activated, down_all, preferred_element_type=jnp.float32)
    new_rows = hidden + gate_rate[:, None] * change

    def put(array, rows):
        rows = rows.reshape(micro_count, slot_count, model_width).astype(array.dtype)
        return jax.vmap(lambda whole, at, new: whole.at[at].set(new))(array, chosen, rows)

    mixed = put(tokens, new_rows)

    grad_rows = pick(cotangent).reshape(row_count, model_width).astype(jnp.float32)
    grad_change = gate_rate[:, None] * grad_rows
    grad_logit = jnp.sum(grad_rows * change, axis=-1) * gate_rate * (1.0 - gate_rate)
    grad_mlp = grad_change.astype(jnp.bfloat16)
    grad_down = scatter_sum(inner(activated, grad_mlp))
    grad_act = by_rows(grad_mlp, down_all)
    gelu_value, gelu_back = jax.vjp(jax.nn.gelu, up_proj)
    grad_up_proj = gelu_back(grad_act)[0].astype(jnp.bfloat16)
    grad_up = scatter_sum(inner(normed_two, grad_up_proj))
    grad_normed_two = by_rows(grad_up_proj, up_all)
    norm_value, norm_back_two = jax.vjp(plain_norm, middle, gain_two)
    grad_middle, grad_gain_two = norm_back_two(grad_normed_two)
    grad_branch = (grad_change + grad_middle).astype(jnp.bfloat16)
    grad_outw = scatter_sum(inner(attention, grad_branch))
    grad_attention = by_rows(grad_branch, out_all).astype(jnp.bfloat16)
    grad_heads = grad_attention.reshape(micro_count, slot_count, HEADS, head_dim)
    prob_grad = product("mqhd,mkhd->mhqk", grad_heads, value_rows)
    delta = jnp.sum(soft_prob * prob_grad, axis=-1, keepdims=True)
    grad_scores = (soft_prob * (prob_grad - delta)).astype(jnp.bfloat16)
    grad_query = product("mhqk,mkhd->mqhd", grad_scores, key_rows) * score_scale
    grad_key = product("mhqk,mqhd->mkhd", grad_scores, queries) * score_scale
    grad_value = product("mhqk,mqhd->mkhd", probs, grad_heads)
    grad_kv = jnp.stack([grad_key, grad_value], axis=2).reshape(
        micro_count, fsdp, slot_count, 2 * model_width
    )
    grad_kv = lax.psum_scatter(
        jnp.swapaxes(grad_kv, 0, 1).astype(jnp.bfloat16).reshape(-1, 2 * model_width),
        "fsdp",
        scatter_dimension=0,
        tiled=True,
    )
    grad_projected = jnp.concatenate(
        [
            grad_query.reshape(row_count, model_width).astype(jnp.bfloat16),
            grad_kv.reshape(row_count, 2 * model_width),
        ],
        axis=1,
    )
    grad_qkvw = scatter_sum(inner(normed, grad_projected))
    grad_normed = by_rows(grad_projected, qkv_all)
    norm_value_one, norm_back_one = jax.vjp(plain_norm, hidden, gain_one)
    grad_hidden_norm, grad_gain_one = norm_back_one(grad_normed)
    grad_hidden = (
        grad_rows + grad_middle + grad_hidden_norm + grad_logit[:, None] * router_float[None, :]
    )
    grad_tokens = put(cotangent.astype(jnp.float32), grad_hidden)
    grad_routerw = jnp.sum(grad_logit[:, None] * hidden, axis=0)
    grad_small = jnp.stack([grad_routerw, grad_gain_one, grad_gain_two], axis=1)
    grad_small = lax.psum_scatter(grad_small, "fsdp", scatter_dimension=0, tiled=True)
    summed = lax.psum((grad_small, grad_qkvw, grad_outw, grad_up, grad_down), "rep")
    return (mixed, grad_tokens, summed[0][:, 0], summed[0][:, 1:]) + tuple(summed[1:])


def solution(mesh):
    rows = P(None, ("rep", "fsdp"), None)
    weight = P("fsdp", None)

    def whole(*args):
        grouped = fits(mesh, args[0], args[3], args[8])
        return jax.shard_map(
            group_shards if grouped else plain_shards,
            mesh=mesh,
            in_specs=(
                rows,
                rows,
                rows,
                P(None, ("rep", "fsdp")),
                P("fsdp"),
                weight,
                weight,
                weight,
                weight,
                weight,
            ),
            out_specs=(rows, rows, P("fsdp"), weight, weight, weight, weight, weight),
            check_vma=False,
        )(*args)

    return whole
```

```python
import functools
import math
import types

import jax
import jax.numpy as jnp
from jax import lax
from jax.experimental import pallas as pl
from jax.experimental.pallas import tpu as pltpu
from jax.sharding import PartitionSpec as P

HEADS = 16


eps = 1e-05
MESH = pl.DeviceIdType.MESH
BF = jnp.bfloat16
F32 = jnp.float32
GELU_A = math.sqrt(2.0 / math.pi)
GELU_B = 0.044715


def dot(left, right, contract):
    return lax.dot_general(
        left, right, (((contract[0],), (contract[1],)), ((), ())), preferred_element_type=F32
    )


def aligned(index, size):
    return pl.ds(pl.multiple_of(index * size, size), size)


def loop(count, body):
    def step(index, carry):
        body(index)
        return carry

    lax.fori_loop(0, count, step, 0)


def fits(mesh, tokens, chosen, w_up):
    rep, fsdp = mesh.shape["rep"], mesh.shape["fsdp"]
    micro, width, hidden = tokens.shape[0], tokens.shape[2], w_up.shape[1]
    if fsdp % micro or rep % 2:
        return False
    inner_count = fsdp // micro
    return (
        rep % inner_count == 0
        and rep == micro
        and fsdp == rep * inner_count
        and width == fsdp * 128
        and hidden == fsdp * rep * 128
        and HEADS % (2 * rep) == 0
        and width // HEADS == 64
        and chosen.shape[1] // (rep * fsdp) == 64
        and rep == 4
        and hidden == rep * width
        and tokens.shape[1] * micro // (rep * fsdp) == 2 * rep * micro * 64
    )


def scratch_shapes(g):
    own, rows, d, piece = g.own, g.rows, g.d, g.d // g.F

    def vmem(height, width, kind=BF):
        return pltpu.VMEM((height, width), kind)

    def dma(*shape):
        return pltpu.SemaphoreType.DMA(shape)

    def shared():
        return dict(xs=dma(g.X - 1), xr=dma(g.X - 1), ss=dma(g.X), sr=dma(g.X))

    def halves():
        return [shared(), shared()]

    def direct():
        return dict(l=dma(1), os=dma(g.A - 1), ors=dma(g.A - 1), ins=dma(g.A), inr=dma(g.A))

    def chained():
        ends = dict(ups=dma(g.A - 1), upr=dma(g.A - 1), dns=dma(g.A - 1), dnr=dma(g.A - 1))
        return dict(l=dma(g.F), ins=dma(2 * g.A - 1), inr=dma(2 * g.A - 1), **ends)

    def pieces(count, cols, kind, height, full):
        made = dict(
            inbox=vmem(count // g.S * height, cols, kind),
            outbox=vmem(g.A * height, cols, kind),
            ins=dma(g.A),
            inr=dma(g.A),
            os=dma(g.A),
            ors=dma(g.A),
        )
        if full:
            made.update(grad=vmem(count * height, cols), share=shared(), out=dma(g.R))
            made.update(whole=vmem(full * height, cols))
        return made

    return dict(
        hid=vmem(own, d),
        ct=vmem(own, d),
        infos=vmem(g.R * g.MB * 8, 128, F32),
        sm=vmem(g.F * 8, 128, F32),
        info=pltpu.VMEM((g.MB, 8, 128), F32),
        vec=vmem(8, d, F32),
        wqa=vmem(d, g.qc),
        woa=vmem(g.ac, d),
        wua=vmem(d, g.fc),
        wda=vmem(g.fc, d),
        normed=vmem(rows, d),
        norm2=vmem(rows, d),
        proj=vmem(rows, g.qc),
        att=vmem(rows, g.ac),
        gatt=vmem(rows, g.ac),
        gproj=vmem(rows, g.qc),
        lse=vmem(rows, 128, F32),
        bias=vmem(g.tree, g.tree, F32),
        pair_a=vmem(2 * rows, g.fc),
        pair_b=vmem(2 * rows, d),
        dact=vmem(rows, g.fc, F32),
        gate=vmem(own, 128, F32),
        branch=vmem(own, d, F32),
        gmid=vmem(own, d, F32),
        ends=vmem(2 * own, d),
        to_sib=pltpu.VMEM((2, g.X * own, d), BF),
        of_sib=pltpu.VMEM((2, g.X * own, d), BF),
        to_x=pltpu.VMEM((2, (g.X - 1) * own, d), BF),
        of_x=pltpu.VMEM((2, (g.X - 1) * own, d), BF),
        gsum=vmem(8, d, F32),
        gsp=vmem(g.F * 8, 128, F32),
        gs_pair=pltpu.VMEM((2, 8, 128), F32),
        gs_mine=pltpu.VMEM((2, 8, 128), F32),
        a2a_s=dma(5, g.MB),
        a2a_r=dma(5, g.MB),
        tok_l=dma(2, g.MB),
        pair_s=dma(2),
        pair_r=dma(2),
        small_t=direct(),
        wo_t=direct(),
        wq_t=chained(),
        wu_t=chained(),
        wd_t=chained(),
        info_t=shared(),
        normed_t=halves(),
        gmlp_t=halves(),
        norm2_t=halves(),
        gbr_t=halves(),
        sums=[halves() for _ in range(4)],
        q=pieces(g.F, g.qc, BF, piece, g.R),
        u=pieces(g.F, g.fc, BF, piece, g.R),
        d=pieces(g.F, d, BF, piece, g.R),
        o=pieces(g.S, d, BF, piece, 1),
        s=pieces(g.F, 128, F32, 8, 0),
    )


def spaces(tree):
    if isinstance(tree, dict):
        return types.SimpleNamespace(**{name: spaces(value) for name, value in tree.items()})
    return [spaces(value) for value in tree] if isinstance(tree, list) else tree


def block_kernel(g, order, form, *refs):
    split = len(order)
    n = spaces(dict(zip(order, refs[:split]), **jax.tree.unflatten(form, refs[split:])))
    R, F, S, A, X, MB = g.R, g.F, g.S, g.A, g.X, g.MB
    own, rows, d, cap = g.own, g.rows, g.d, g.cap
    piece = d // F
    r = lax.axis_index("rep")
    f = lax.axis_index("fsdp")
    x, c = r // 2, lax.rem(r, 2)
    a, b = f // S, lax.rem(f, S)
    other_b = lax.rem(b + 1, S)
    sib = x * 2 + 1 - c
    pending = {}
    n.act, n.gup = n.pair_a.at[pl.ds(0, rows)], n.pair_a.at[pl.ds(rows, rows)]
    n.gmlp, n.gbr = n.pair_b.at[pl.ds(0, rows)], n.pair_b.at[pl.ds(rows, rows)]
    n.nrow, n.grow = n.ends.at[pl.ds(0, own)], n.ends.at[pl.ds(own, own)]
    n.picked, n.picked_ct = n.ends, n.norm2
    n.acc, n.gfirst = n.dact.at[pl.ds(0, own)], n.dact.at[pl.ds(own, own)]
    tok_count = n.tokens.shape[1]

    def token_copy(which, m):
        source, target = (n.tokens, n.pair_a) if which == 0 else (n.cotangent, n.pair_b)
        return pltpu.make_async_copy(
            source.at[m], target.at[pl.ds(m * tok_count, tok_count)], n.tok_l.at[which, m]
        )

    def cut_qkv():
        return [
            pltpu.make_async_copy(
                n.w_qkv.at[:, pl.ds(pl.multiple_of(part * d + r * g.ac, g.ac), g.ac)],
                n.wqa.at[aligned(f, piece), pl.ds(part * g.ac, g.ac)],
                n.wq_t.l.at[part],
            )
            for part in range(3)
        ]

    def cut_up():
        return [
            pltpu.make_async_copy(
                n.w_up.at[:, pl.ds(pl.multiple_of((block * R + r) * 128, 128), 128)],
                n.wua.at[aligned(f, piece), pl.ds(block * 128, 128)],
                n.wu_t.l.at[block],
            )
            for block in range(F)
        ]

    def cut_down():
        return [
            pltpu.make_async_copy(
                n.w_down.at[aligned(r, piece)], n.wda.at[aligned(f, piece)], n.wd_t.l.at[0]
            )
        ]

    for copy in cut_qkv():
        copy.start()
    for which in range(2):
        for m in range(MB):
            token_copy(which, m).start()
    for cut in (cut_up, cut_down):
        for copy in cut():
            copy.start()

    def remote(src, dst, ss, rs, rep, fsdp):
        return pltpu.make_async_remote_copy(
            src_ref=src,
            dst_ref=dst,
            send_sem=ss,
            recv_sem=rs,
            device_id={"rep": rep, "fsdp": fsdp},
            device_id_type=MESH,
        )

    def send(src, dst, ss, rs, rep, fsdp, cond=None, tag=None):
        def start():
            remote(src, dst, ss, rs, rep, fsdp).start()

        def done():
            remote(src, dst, ss, rs, rep, fsdp).wait_send()

        if cond is None:
            start()
            pending.setdefault(tag, []).append(done)
        else:
            pl.when(cond)(start)
            pending.setdefault(tag, []).append(lambda: pl.when(cond)(done))

    def drain(tag):
        for done in pending.pop(tag, []):
            done()

    def got(dst, rs):
        remote(dst, dst, rs, rs, sib, f).wait_recv()

    def xpeer(step):
        return lax.rem(x + 1 + step, X)

    def xfrom(step):
        return lax.rem(x + X - 1 - step, X)

    def outer(step):
        return lax.rem(a + step, A)

    def outer_from(step):
        return lax.rem(a + A - step, A)

    home_rep = (r // S) * S + b

    def home_fsdp(m):
        return m * S + lax.rem(r, S)

    barrier = pltpu.get_barrier_semaphore()

    def greet(rep, fsdp):
        pl.semaphore_signal(
            barrier, inc=1, device_id={"rep": rep, "fsdp": fsdp}, device_id_type=MESH
        )

    for step in range(1, A):
        greet(r, outer(step) * S + b)
    greet(r, a * S + other_b)
    greet(sib, f)
    for step in range(X - 1):
        greet(xpeer(step) * 2 + c, f)
    mine = [(home_fsdp(m) == f) & (home_rep == r) for m in range(MB)]
    for m in range(MB):

        @pl.when(jnp.logical_not(mine[m]))
        def _(m=m):
            greet(home_rep, home_fsdp(m))

    stays = (home_rep == r) & (lax.rem(r, S) == b)
    pl.semaphore_wait(barrier, (A - 1) + 1 + 1 + (X - 1) + MB - stays.astype(jnp.int32))

    def swap_start(which, src_of, dst_of):
        for m in range(MB):
            src, dst = src_of(m), dst_of(a)
            ss, rs = n.a2a_s.at[which, m], n.a2a_r.at[which, a]

            @pl.when(jnp.logical_not(mine[m]))
            def _():
                remote(src, dst, ss, rs, home_rep, home_fsdp(m)).start()

            @pl.when(mine[m])
            def _():
                pltpu.make_async_copy(src, dst, rs).start()

    def swap_end(which, src_of, dst_of):
        for m in range(MB):
            src, dst = src_of(m), dst_of(m)
            ss, rs = n.a2a_s.at[which, m], n.a2a_r.at[which, m]

            @pl.when(jnp.logical_not(mine[m]))
            def _():
                remote(src, dst, ss, rs, home_rep, home_fsdp(m)).wait()

            @pl.when(mine[m])
            def _():
                pltpu.make_async_copy(src, dst, rs).wait()

    def gather_start(t, buf, height):
        at = aligned(f, height)
        src = buf.at[at]
        for step in range(1, A):
            send(
                src,
                buf.at[at],
                t.os.at[step - 1],
                t.ors.at[step - 1],
                r,
                outer(step) * S + b,
            )
        send(src, buf.at[at], t.ins.at[0], t.inr.at[0], r, a * S + other_b)

    def gather_forward(t, buf, height):
        for step in range(1, A):
            at = buf.at[aligned(outer_from(step) * S + b, height)]
            got(at, t.ors.at[step - 1])
            send(at, at, t.ins.at[step], t.inr.at[step], r, a * S + other_b)

    def gather_end(t, buf, height):
        for step in range(A):
            at = buf.at[aligned(outer_from(step) * S + other_b, height)]
            got(at, t.inr.at[step])

    def hop(step):
        return lax.rem(a + A + step, A)

    def chain_start(t, buf, height):
        at = buf.at[aligned(f, height)]
        send(at, at, t.ups.at[0], t.upr.at[0], r, hop(1) * S + b, a < A - 1)
        send(at, at, t.dns.at[0], t.dnr.at[0], r, hop(-1) * S + b, a > 0)

    def chain_across(t, buf, height):
        at = buf.at[aligned(f, height)]
        send(at, at, t.ins.at[0], t.inr.at[0], r, a * S + other_b)

    def chain_forward(t, buf, height, step):
        for sends, takes, has, on, to, index in (
            (t.ups, t.upr, a >= step, a < A - 1, 1, step),
            (t.dns, t.dnr, a + step < A, a > 0, -1, A - 1 + step),
        ):
            at = buf.at[aligned(hop(-to * step) * S + b, height)]

            @pl.when(has)
            def _():
                got(at, takes.at[step - 1])

            if step < A - 1:
                send(
                    at,
                    at,
                    sends.at[step],
                    takes.at[step],
                    r,
                    hop(to) * S + b,
                    has & on,
                )
            send(
                at,
                at,
                t.ins.at[index],
                t.inr.at[index],
                r,
                a * S + other_b,
                has,
            )

    def chain_end(t, buf, height):
        got(buf.at[aligned(a * S + other_b, height)], t.inr.at[0])
        for step in range(1, A):
            for has, to, index in ((a >= step, 1, step), (a + step < A, -1, A - 1 + step)):
                at = buf.at[aligned(hop(-to * step) * S + other_b, height)]

                @pl.when(has)
                def _():
                    got(at, t.inr.at[index])

    is_source = a == r

    def out_start(src, buf):
        at = buf.at[aligned(b, piece)]

        @pl.when(is_source)
        def _():
            pltpu.make_async_copy(src, at, n.wo_t.l.at[0]).start()

        for step in range(1, A):
            send(
                src, at, n.wo_t.os.at[step - 1], n.wo_t.ors.at[0], r, outer(step) * S + b, is_source
            )
        send(src, at, n.wo_t.ins.at[0], n.wo_t.inr.at[0], r, a * S + other_b, is_source)

    def out_forward(buf):
        at = buf.at[aligned(b, piece)]

        @pl.when(jnp.logical_not(is_source))
        def _():
            got(at, n.wo_t.ors.at[0])

        send(
            at, at, n.wo_t.ins.at[1], n.wo_t.inr.at[0], r, a * S + other_b, jnp.logical_not(is_source)
        )

    def out_end(src, buf):
        @pl.when(is_source)
        def _():
            pltpu.make_async_copy(src, buf.at[aligned(b, piece)], n.wo_t.l.at[0]).wait()

        got(buf.at[aligned(other_b, piece)], n.wo_t.inr.at[0])

    def part_of(block, height, part):
        if part is None:
            return aligned(block, height)
        half = height // 2
        return pl.ds(pl.multiple_of(block * height + part * half, half), half)

    def share_start(t, buf, height, part=None):
        at = buf.at[part_of(r, height, part)]
        for step in range(X - 1):
            send(at, at, t.xs.at[step], t.xr.at[step], xpeer(step) * 2 + c, f)
        send(at, at, t.ss.at[0], t.sr.at[0], sib, f)

    def share_forward(t, buf, height, part=None):
        for step in range(X - 1):
            at = buf.at[part_of(xfrom(step) * 2 + c, height, part)]
            got(at, t.xr.at[step])
            send(at, at, t.ss.at[1 + step], t.sr.at[1 + step], sib, f)

    def share_near(t, buf, height, part=None):
        got(buf.at[part_of(sib, height, part)], t.sr.at[0])

    def share_far(t, buf, height, part=None):
        for step in range(X - 1):
            at = buf.at[part_of(xfrom(step) * 2 + 1 - c, height, part)]
            got(at, t.sr.at[1 + step])

    def share_end(t, buf, height):
        share_near(t, buf, height)
        share_far(t, buf, height)

    def rows_do(what, t, buf):
        what(t[0], buf, own)

    wide = 256

    def sum_owner(step):
        return xpeer(step) if step < X - 1 else x

    half_tiles = d // wide // 2

    def sum_near(index, slot, partial, step):
        to_sib, at = n.to_sib.at[slot], pl.ds(step * own, own)
        owner = sum_owner(step) * 2 + 1 - c
        if step == 0:
            drain(slot)
        for part in range(2):
            t, across = n.sums[index][part], pl.ds(part * d // 2, d // 2)

            def one(tile, part=part):
                cols = aligned(part * half_tiles + tile, wide)
                to_sib[at, cols] = partial(owner, cols).astype(BF)

            loop(half_tiles, one)
            send(
                to_sib.at[at, across],
                n.of_sib.at[slot, at, across],
                t.ss.at[step],
                t.sr.at[step],
                sib,
                f,
                tag=slot,
            )

    def sum_mine(index, slot, partial, step, acc):
        of_sib, to_x, at = n.of_sib.at[slot], n.to_x.at[slot], pl.ds(step * own, own)
        owner = sum_owner(step) * 2 + c
        last = step == X - 1
        for part in range(2):
            t, across = n.sums[index][part], pl.ds(part * d // 2, d // 2)
            got(of_sib.at[at, across], t.sr.at[step])

            def one(tile, part=part):
                cols = aligned(part * half_tiles + tile, wide)
                total = partial(owner, cols) + of_sib[at, cols].astype(F32)
                if last:
                    acc[:, cols] = total
                else:
                    to_x[at, cols] = total.astype(BF)

            loop(half_tiles, one)
            if not last:
                send(
                    n.to_x.at[slot, at, across],
                    n.of_x.at[slot, at, across],
                    t.xs.at[step],
                    t.xr.at[step],
                    sum_owner(step) * 2 + c,
                    f,
                    tag=slot,
                )

    def sum_end(index, slot):
        of_x = n.of_x.at[slot]
        for step in range(X - 1):
            for part in range(2):
                across = pl.ds(part * d // 2, d // 2)
                got(of_x.at[pl.ds(step * own, own), across], n.sums[index][part].xr.at[step])

    def came(slot, at):
        total = None
        for step in range(X - 1):
            part = n.of_x[slot, pl.ds(step * own + at, tall), :].astype(F32)
            total = part if total is None else total + part
        return total

    tall = 32

    def by_own(body):
        def one(index):
            at = pl.multiple_of(index * tall, tall)
            body(at, pl.ds(at, tall))

        loop(own // tall, one)

    def grad_start(t, buf, height):
        out = t is n.o
        inbox = t.inbox
        for step in range(1 if out else A):
            to_a = r if out else outer(step + 1)
            src = buf.at[aligned((0 if out else to_a * S) + other_b, height)]
            send(
                src,
                inbox.at[pl.ds(step * height, height)],
                t.ins.at[step],
                t.inr.at[step],
                r,
                a * S + other_b,
            )

    def add_into(dst, base, inbox, start, height):
        small = min(height, 32)

        def one(index):
            at = pl.ds(pl.multiple_of(base + index * small, small), small)
            of = pl.ds(pl.multiple_of(start + index * small, small), small)
            dst[at, :] = (dst[at, :].astype(F32) + inbox[of, :].astype(F32)).astype(dst.dtype)

        loop(height // small, one)

    def grad_forward(t, buf, height):
        out = t is n.o
        inbox, outbox = t.inbox, t.outbox
        for step in range(1 if out else A):
            to_a = r if out else outer(step + 1)
            base = ((0 if out else to_a * S) + b) * height
            got(inbox.at[pl.ds(step * height, height)], t.inr.at[step])
            add_into(buf, base, inbox, step * height, height)
            if out:
                slot = lax.rem(r + A - a - 1, A)
                slot = jnp.where(is_source, 0, slot)
                send(
                    buf.at[pl.ds(pl.multiple_of(base, height), height)],
                    outbox.at[aligned(slot, height)],
                    n.o.os.at[0],
                    n.o.ors.at[slot],
                    r,
                    r * S + b,
                    jnp.logical_not(is_source),
                )
            elif step < A - 1:
                send(
                    buf.at[pl.ds(pl.multiple_of(base, height), height)],
                    outbox.at[pl.ds(step * height, height)],
                    t.os.at[step],
                    t.ors.at[step],
                    r,
                    to_a * S + b,
                )

    def grad_wait(t, height):
        for step in range(A - 1):
            got(
                t.outbox.at[pl.ds(step * height, height)],
                t.ors.at[step],
            )

    def grad_total(t, buf, base, height, target, target_base, boxes):
        outbox = t.outbox
        small = min(height, 32)

        def one(index):
            off = index * small
            total = buf[pl.ds(pl.multiple_of(base + off, small), small), :].astype(F32)
            for box in boxes:
                at = pl.ds(pl.multiple_of(box * height + off, small), small)
                total = total + outbox[at, :].astype(F32)
            at = pl.ds(pl.multiple_of(target_base + off, small), small)
            target[at, :] = total.astype(target.dtype)

        loop(height // small, one)

    side = a // 2
    mate = a + 1 - 2 * lax.rem(a, 2)
    is_end = (a == 0) | (a == A - 1)
    passes_on = jnp.logical_not(is_end)
    piece_owner = (2 - side, 3 * (1 - side), mate, a)

    def piece_start(t, step):
        height, inbox = piece, t.inbox
        send(
            t.grad.at[aligned(piece_owner[step] * S + other_b, height)],
            inbox.at[pl.ds(step * height, height)],
            t.ins.at[step],
            t.inr.at[step],
            r,
            a * S + other_b,
        )

    def piece_take(t, step):
        buf, inbox, outbox = t.grad, t.inbox, t.outbox
        base = (piece_owner[step] * S + b) * piece
        got(inbox.at[pl.ds(step * piece, piece)], t.inr.at[step])
        add_into(buf, base, inbox, step * piece, piece)
        if step < 3:
            send(
                buf.at[pl.ds(pl.multiple_of(base, piece), piece)],
                outbox.at[pl.ds(step * piece, piece)],
                t.os.at[step],
                t.ors.at[step],
                r,
                mate * S + b,
                is_end if step < 2 else None,
            )

    def piece_pass(t, step):
        buf, outbox = t.grad, t.outbox
        base = (piece_owner[step] * S + b) * piece

        @pl.when(passes_on)
        def _():
            got(outbox.at[pl.ds(step * piece, piece)], t.ors.at[step])
            add_into(buf, base, outbox, step * piece, piece)

        send(
            buf.at[pl.ds(pl.multiple_of(base, piece), piece)],
            outbox.at[pl.ds(3 * piece, piece)],
            t.os.at[step],
            t.ors.at[3],
            r,
            piece_owner[step] * S + b,
            passes_on,
        )

    def piece_own(t):
        for box in (2, 3):
            got(
                t.outbox.at[pl.ds(box * piece, piece)], t.ors.at[box]
            )
        grad_total(t, t.grad, f * piece, piece, t.whole, r * piece, (2, 3))
        share_start(t.share, t.whole, piece)

    def hid_at(i):
        return n.hid.at[aligned(i, cap)]

    def ct_at(i):
        return n.ct.at[aligned(i, cap)]

    def info_src(i):
        return n.info.at[i]

    def info_own(i):
        return n.infos.at[aligned(r * MB + i, 8)]

    def info_home(i):
        return n.infos.at[aligned(home_rep * MB + i, 8)]

    odd = lax.rem(a, 2)
    lane_token = lax.broadcasted_iota(jnp.int32, (tok_count, 128), 0)
    lane = lax.broadcasted_iota(jnp.int32, (1, 128), 1)
    lane_used = (lane // cap) == odd
    def at_of(m):
        row = n.chosen[m : m + 1, :]
        return jnp.where(lane_used, jnp.concatenate([row, row], axis=1), -1)

    def hot_of(m):
        return (lane_token == at_of(m)).astype(F32).astype(BF)

    def tok_at(m):
        return n.picked.at[pl.ds(pl.multiple_of(m * 128 + odd * cap, cap), cap)]

    def cot_at(m):
        return n.picked_ct.at[pl.ds(pl.multiple_of(m * 128 + odd * cap, cap), cap)]

    mine_sm = pl.ds(pl.multiple_of(f * 8, 8), 8)
    def first_norm(at, rows_at):
        h = n.hid[rows_at, :].astype(F32)
        scale = lax.rsqrt(jnp.mean(h * h, axis=-1, keepdims=True) + eps)
        n.normed[pl.ds(pl.multiple_of(r * own + at, tall), tall), :] = (
            h * scale * n.vec[1:2, :]
        ).astype(BF)
        logit = jnp.sum(h * n.vec[0:1, :], axis=-1, keepdims=True)
        n.gate[rows_at, :] = jnp.broadcast_to(1.0 / (1.0 + jnp.exp(-logit)), (tall, 128))

    def mlp_cotangent(at, rows_at):
        gc = n.gate[rows_at, 0:1] * n.ct[rows_at, :].astype(F32)
        n.gmlp[pl.ds(pl.multiple_of(r * own + at, tall), tall), :] = gc.astype(BF)

    far = xpeer(0)
    near_blocks, far_blocks = (r, sib), (far * 2 + c, far * 2 + 1 - c)
    def project(block):
        at = aligned(block, own)
        half = g.qc // 3

        def one(part):
            cols = aligned(part, half)
            n.proj[at, cols] = dot(n.normed[at, :], n.wqa[:, cols], (1, 0)).astype(BF)

        loop(3, one)

    tree, pairs = g.tree, g.heads // 2
    scale = 64 ** (-0.5)
    low_lane = lax.broadcasted_iota(jnp.int32, (tree, 128), 1) < 64
    def half_of(value, half):
        keep = low_lane if half == 0 else jnp.logical_not(low_lane)
        return jnp.where(keep, value, jnp.zeros_like(value))

    def join(first, second):
        return jnp.where(low_lane, first, second)

    def make_bias(t):
        blocks = []
        for index in range(S * MB // 2):
            at = pl.multiple_of((t * S * MB + index * 2) * 8, 8)
            blocks.append(n.infos[pl.ds(at, 8), :] + n.infos[pl.ds(at + 8, 8), :])
        keys = jnp.concatenate(blocks, axis=1)
        asked = jnp.transpose(keys)
        near = keys[0:1, :] == asked[:, 0:1]
        near = near | (keys[0:1, :] == asked[:, 1:2])
        near = near | (keys[0:1, :] == asked[:, 2:3])
        near = near & (keys[3:4, :] <= asked[:, 3:4])
        n.bias[...] = jnp.where(near, 0.0, -1e30)

    def columns(part, pair):
        return pl.ds(part * g.ac + pair * 128, 128)

    def attend(t):
        make_bias(t)
        at = aligned(t, tree)
        for pair in range(pairs):
            q = n.proj[at, columns(0, pair)]
            k = n.proj[at, columns(1, pair)]
            v = n.proj[at, columns(2, pair)]
            made = []
            for half in range(2):
                s = dot(half_of(q, half), k, (1, 1)) * scale + n.bias[...]
                top = jnp.max(s, axis=-1, keepdims=True)
                e = jnp.exp(s - top)
                total = jnp.sum(e, axis=-1, keepdims=True)
                made.append(dot((e * (1.0 / total)).astype(BF), v, (1, 0)))
                head = pair * 2 + half
                n.lse[at, head : head + 1] = top + jnp.log(total)
            n.att[at, pl.ds(pair * 128, 128)] = join(*made).astype(BF)

    def branch_part(owner, cols):
        return dot(n.att[aligned(owner, own), :], n.woa[:, cols], (1, 0))

    def second_norm(at, rows_at):
        br = n.branch[rows_at, :] + came(0, at)
        n.branch[rows_at, :] = br
        mid = n.hid[rows_at, :].astype(F32) + br
        inv = lax.rsqrt(jnp.mean(mid * mid, axis=-1, keepdims=True) + eps)
        n.norm2[pl.ds(pl.multiple_of(r * own + at, tall), tall), :] = (
            mid * inv * n.vec[2:3, :]
        ).astype(BF)

    tiles = g.fc // wide
    def mlp_up(block):
        at = aligned(block, own)

        def one(tile):
            cols = aligned(tile, wide)
            u = dot(n.norm2[at, :], n.wua[:, cols], (1, 0))
            square = u * u
            t = jnp.tanh(GELU_A * (u + GELU_B * square * u))
            n.act[at, cols] = (0.5 * u * (1.0 + t)).astype(BF)
            n.dact[at, cols] = 0.5 * (1.0 + t) + (0.5 * GELU_A) * u * (1.0 - t * t) * (
                1.0 + (3.0 * GELU_B) * square
            )

        loop(tiles, one)

    def mlp_back(block):
        at = aligned(block, own)

        def one(tile):
            cols = aligned(tile, wide)
            ga = dot(n.gmlp[at, :], n.wda[cols, :], (1, 1))
            n.gup[at, cols] = (ga * n.dact[at, cols]).astype(BF)

        loop(tiles, one)

    def norm2_part(owner, cols):
        return dot(n.gup[aligned(owner, own), :], n.wua[cols, :], (1, 1))

    def weight_grad(left, right, target, count):
        def one(index):
            cols = aligned(index, 256)
            target[cols, :] = dot(left[:, cols], right[...], (0, 0)).astype(BF)

        loop(count // 256, one)

    def second_back(at, rows_at):
        dy = n.gmid[rows_at, :] + came(1, at)
        mid = n.hid[rows_at, :].astype(F32) + n.branch[rows_at, :]
        inv = lax.rsqrt(jnp.mean(mid * mid, axis=-1, keepdims=True) + eps)
        n.gsum[2:3, :] = n.gsum[2:3, :] + jnp.sum(dy * mid * inv, axis=0, keepdims=True)
        t = dy * n.vec[2:3, :]
        along = jnp.sum(mid * t, axis=-1, keepdims=True) * (inv * inv * inv * (1.0 / d))
        gm = inv * t - mid * along
        n.gmid[rows_at, :] = gm
        gc = n.gate[rows_at, 0:1] * n.ct[rows_at, :].astype(F32)
        n.gbr[pl.ds(pl.multiple_of(r * own + at, tall), tall), :] = (gc + gm).astype(BF)

    def attention_cotangent(block):
        at = aligned(block, own)
        n.gatt[at, :] = dot(n.gbr[at, :], n.woa[...], (1, 1)).astype(BF)

    def attend_back(t):
        make_bias(t)
        at = aligned(t, tree)
        for pair in range(pairs):
            q = n.proj[at, columns(0, pair)]
            k = n.proj[at, columns(1, pair)]
            v = n.proj[at, columns(2, pair)]
            da = n.gatt[at, pl.ds(pair * 128, 128)]
            dq, dk, dv = [], [], []
            for half in range(2):
                head = pair * 2 + half
                s = dot(half_of(q, half), k, (1, 1)) * scale + n.bias[...]
                p = jnp.exp(s - n.lse[at, head : head + 1])
                dp = dot(half_of(da, half), v, (1, 1))
                delta = jnp.sum(p * dp, axis=-1, keepdims=True)
                ds = (p * (dp - delta)).astype(BF)
                dq.append(dot(ds, k, (1, 0)))
                dk.append(dot(ds, q, (0, 0)))
                dv.append(dot(p.astype(BF), da, (0, 0)))
            n.gproj[at, columns(0, pair)] = (join(*dq) * scale).astype(BF)
            n.gproj[at, columns(1, pair)] = (join(*dk) * scale).astype(BF)
            n.gproj[at, columns(2, pair)] = join(*dv).astype(BF)

    def change_part(owner, cols):
        return dot(n.act[aligned(owner, own), :], n.wda[:, cols], (1, 0))

    def normed_part(owner, cols):
        return dot(n.gproj[aligned(owner, own), :], n.wqa[cols, :], (1, 1))

    def new_rows(at, rows_at):
        change = n.branch[rows_at, :] + n.acc[rows_at, :] + came(0, at)
        h = n.hid[rows_at, :].astype(F32)
        gate = n.gate[rows_at, 0:1]
        n.nrow[rows_at, :] = (h + gate * change).astype(BF)
        logit = jnp.sum(n.ct[rows_at, :].astype(F32) * change, axis=-1, keepdims=True)
        logit = logit * gate * (1.0 - gate)
        n.gsum[0:1, :] = n.gsum[0:1, :] + jnp.sum(logit * h, axis=0, keepdims=True)
        n.gmid[rows_at, :] = n.gmid[rows_at, :] + logit * n.vec[0:1, :]

    def new_at(i):
        return n.nrow.at[aligned(i, cap)]

    def grow_at(i):
        return n.grow.at[aligned(i, cap)]

    def first_back(at, rows_at):
        dy = n.gfirst[rows_at, :] + came(1, at)
        h = n.hid[rows_at, :].astype(F32)
        inv = lax.rsqrt(jnp.mean(h * h, axis=-1, keepdims=True) + eps)
        n.gsum[1:2, :] = n.gsum[1:2, :] + jnp.sum(dy * h * inv, axis=0, keepdims=True)
        t = dy * n.vec[1:2, :]
        along = jnp.sum(h * t, axis=-1, keepdims=True) * (inv * inv * inv * (1.0 / d))
        total = n.ct[rows_at, :].astype(F32) + n.gmid[rows_at, :] + (inv * t - h * along)
        n.grow[rows_at, :] = total.astype(BF)

    ax, ac = a // 2, lax.rem(a, 2)
    off_x = (c == ac) & (x != ax)
    def out_copies(t, target):
        return [
            pltpu.make_async_copy(
                t.whole.at[pl.ds(index * piece, piece)], target.at[index], t.out.at[index]
            )
            for index in range(R)
        ]

    last = pltpu.make_async_copy(n.o.whole, n.ro_out, n.o.out.at[0])
    n.sm[mine_sm, :] = jnp.concatenate(
        [n.router[...].astype(F32), n.gains[...].astype(F32), jnp.zeros((5, 128), F32)], axis=0
    )
    gather_start(n.small_t, n.sm, 8)
    for copy in cut_qkv():
        copy.wait()
    chain_start(n.wq_t, n.wqa, piece)
    chain_across(n.wq_t, n.wqa, piece)
    for m in range(MB):
        hot = hot_of(m)
        token_copy(0, m).wait()
        n.picked[m * 128 : (m + 1) * 128, :] = dot(
            hot, n.pair_a[m * tok_count : (m + 1) * tok_count, :], (0, 0)
        ).astype(BF)
        lines = jnp.concatenate([n.path[line, m : m + 1, :] for line in range(3)], axis=0)
        n.info[m, 0:3, :] = dot(lines.astype(F32).astype(BF), hot, (1, 0))
        at = at_of(m)
        n.info[m, 3:4, :] = jnp.where(at >= 0, at + f * tok_count, 0).astype(F32)
        n.info[m, 4:8, :] = jnp.zeros((4, 128), F32)
    swap_start(0, tok_at, hid_at)
    for m in range(MB):
        ss, rs = n.a2a_s.at[1, m], n.a2a_r.at[1, a]

        @pl.when(jnp.logical_not(mine[m]))
        def _():
            remote(info_src(m), info_home(a), ss, rs, home_rep, home_fsdp(m)).start()

        @pl.when(mine[m])
        def _():
            pltpu.make_async_copy(info_src(m), info_own(a), rs).start()
    gather_forward(n.small_t, n.sm, 8)
    chain_forward(n.wq_t, n.wqa, piece, 1)
    for m in range(MB):
        token_copy(1, m).wait()
        n.picked_ct[m * 128 : (m + 1) * 128, :] = dot(
            hot_of(m), n.pair_b[m * tok_count : (m + 1) * tok_count, :], (0, 0)
        ).astype(BF)
    gather_end(n.small_t, n.sm, 8)
    for index in range(F):
        n.vec[:, index * 128 : (index + 1) * 128] = n.sm[index * 8 : (index + 1) * 8, :]
    swap_end(1, info_src, info_own)
    share_start(n.info_t, n.infos, MB * 8)
    swap_end(0, tok_at, hid_at)
    by_own(first_norm)
    rows_do(share_start, n.normed_t, n.normed)
    chain_forward(n.wq_t, n.wqa, piece, 2)
    swap_start(2, cot_at, ct_at)
    share_forward(n.info_t, n.infos, MB * 8)
    out_start(n.w_out, n.woa)
    rows_do(share_forward, n.normed_t, n.normed)
    chain_forward(n.wq_t, n.wqa, piece, 3)
    for copy in cut_up():
        copy.wait()
    chain_start(n.wu_t, n.wua, piece)
    for copy in cut_down():
        copy.wait()
    share_end(n.info_t, n.infos, MB * 8)
    rows_do(share_near, n.normed_t, n.normed)
    rows_do(share_far, n.normed_t, n.normed)
    chain_end(n.wq_t, n.wqa, piece)
    swap_end(2, cot_at, ct_at)
    by_own(mlp_cotangent)
    share_start(n.gmlp_t[0], n.gmlp, own)
    chain_across(n.wu_t, n.wua, piece)
    for block in far_blocks:
        project(block)
    out_forward(n.woa)
    chain_forward(n.wu_t, n.wua, piece, 1)
    chain_start(n.wd_t, n.wda, piece)
    chain_across(n.wd_t, n.wda, piece)
    attend(far)
    out_end(n.w_out, n.woa)
    sum_near(0, 0, branch_part, 0)
    for block in near_blocks:
        project(block)
    sum_mine(0, 0, branch_part, 0, n.branch)
    chain_forward(n.wu_t, n.wua, piece, 2)
    chain_forward(n.wd_t, n.wda, piece, 1)
    attend(x)
    sum_near(0, 0, branch_part, 1)
    chain_forward(n.wu_t, n.wua, piece, 3)
    sum_mine(0, 0, branch_part, 1, n.branch)
    chain_forward(n.wd_t, n.wda, piece, 2)
    share_forward(n.gmlp_t[0], n.gmlp, own)
    sum_end(0, 0)
    by_own(second_norm)
    rows_do(share_start, n.norm2_t, n.norm2)
    chain_end(n.wu_t, n.wua, piece)
    chain_forward(n.wd_t, n.wda, piece, 3)
    mlp_up(r)
    rows_do(share_near, n.norm2_t, n.norm2)
    mlp_up(sib)
    rows_do(share_forward, n.norm2_t, n.norm2)
    mlp_up(far_blocks[0])
    rows_do(share_far, n.norm2_t, n.norm2)
    mlp_up(far_blocks[1])
    rows_do(share_near, n.gmlp_t, n.gmlp)
    rows_do(share_far, n.gmlp_t, n.gmlp)
    weight_grad(n.act, n.gmlp, n.d.grad, g.fc)
    piece_start(n.d, 0)
    piece_start(n.d, 1)
    piece_start(n.d, 2)
    chain_end(n.wd_t, n.wda, piece)
    mlp_back(far_blocks[1])
    sum_near(1, 1, norm2_part, 0)
    mlp_back(far_blocks[0])
    sum_mine(1, 1, norm2_part, 0, n.gmid)
    mlp_back(sib)
    sum_near(1, 1, norm2_part, 1)
    mlp_back(r)
    sum_mine(1, 1, norm2_part, 1, n.gmid)
    weight_grad(n.norm2, n.gup, n.u.grad, d)
    n.gsum[...] = jnp.zeros_like(n.gsum)
    sum_end(1, 1)
    by_own(second_back)
    rows_do(share_start, n.gbr_t, n.gbr)
    piece_take(n.d, 0)
    piece_start(n.d, 3)
    piece_take(n.d, 1)
    piece_start(n.u, 0)
    attention_cotangent(r)
    rows_do(share_near, n.gbr_t, n.gbr)
    attention_cotangent(sib)
    attend_back(x)
    piece_take(n.d, 2)
    piece_start(n.u, 1)
    piece_take(n.d, 3)
    piece_start(n.u, 2)
    piece_pass(n.d, 0)
    sum_near(2, 0, change_part, 0)
    sum_near(2, 0, change_part, 1)
    sum_mine(2, 0, change_part, 0, n.acc)
    rows_do(share_forward, n.gbr_t, n.gbr)
    piece_pass(n.d, 1)
    attention_cotangent(far_blocks[0])
    rows_do(share_far, n.gbr_t, n.gbr)
    attention_cotangent(far_blocks[1])
    weight_grad(n.att, n.gbr, n.o.grad, g.ac)
    grad_start(n.o, n.o.grad, piece)
    piece_take(n.u, 0)
    piece_start(n.u, 3)
    piece_take(n.u, 1)
    attend_back(far)
    sum_near(3, 1, normed_part, 0)
    sum_mine(3, 1, normed_part, 0, n.gfirst)
    sum_near(3, 1, normed_part, 1)
    sum_mine(2, 0, change_part, 1, n.acc)
    sum_end(2, 0)
    by_own(new_rows)
    swap_start(4, new_at, lambda m: n.new_out.at[m])
    grad_forward(n.o, n.o.grad, piece)
    piece_take(n.u, 2)
    weight_grad(n.normed, n.gproj, n.q.grad, d)
    piece_start(n.q, 0)
    piece_start(n.q, 1)
    piece_take(n.u, 3)
    piece_start(n.q, 2)
    sum_mine(3, 1, normed_part, 1, n.gfirst)
    piece_pass(n.u, 0)
    piece_pass(n.u, 1)
    piece_take(n.q, 0)
    piece_start(n.q, 3)
    piece_own(n.d)
    sum_end(3, 1)
    by_own(first_back)
    swap_start(3, grow_at, lambda m: n.grad_out.at[m])
    for index in range(F):
        n.gsp[index * 8 : (index + 1) * 8, :] = n.gsum[:, index * 128 : (index + 1) * 128]
    grad_start(n.s, n.gsp, 8)
    piece_take(n.q, 1)
    piece_take(n.q, 2)
    piece_pass(n.q, 0)
    piece_take(n.q, 3)
    piece_pass(n.q, 1)
    grad_forward(n.s, n.gsp, 8)
    share_forward(n.d.share, n.d.whole, piece)
    piece_own(n.u)
    @pl.when(is_source)
    def _():
        grad_wait(n.o, piece)
        grad_total(n.o, n.o.grad, b * piece, piece, n.o.whole, 0, range(A - 1))
    for step in range(X - 1):
        send(n.o.whole, n.o.whole, n.o.share.xs.at[step], n.o.share.xr.at[0], xpeer(step) * 2 + c, f, is_source)
    send(n.o.whole, n.o.whole, n.o.share.ss.at[0], n.o.share.sr.at[0], sib, f, is_source)
    grad_wait(n.s, 8)
    grad_total(n.s, n.gsp, f * 8, 8, n.gs_mine.at[0], 0, range(A - 1))
    send(n.gs_mine.at[0], n.gs_pair.at[0], n.pair_s.at[0], n.pair_r.at[0], sib, f)
    piece_own(n.q)
    share_end(n.d.share, n.d.whole, piece)
    @pl.when(off_x)
    def _():
        got(n.o.whole, n.o.share.xr.at[0])
    send(n.o.whole, n.o.whole, n.o.share.ss.at[1], n.o.share.sr.at[0], sib, f, off_x)
    for copy in out_copies(n.d, n.rd_out):
        copy.start()
    share_forward(n.u.share, n.u.whole, piece)
    share_end(n.u.share, n.u.whole, piece)
    for copy in out_copies(n.u, n.ru_out):
        copy.start()
    @pl.when(c != ac)
    def _():
        got(n.o.whole, n.o.share.sr.at[0])
    last.start()
    got(n.gs_pair.at[0], n.pair_r.at[0])
    n.gs_mine[1] = n.gs_mine[0] + n.gs_pair[0]
    send(n.gs_mine.at[1], n.gs_pair.at[1], n.pair_s.at[1], n.pair_r.at[1], xpeer(0) * 2 + c, f)
    share_forward(n.q.share, n.q.whole, piece)
    share_end(n.q.share, n.q.whole, piece)
    for copy in out_copies(n.q, n.rq_out):
        copy.start()
    got(n.gs_pair.at[1], n.pair_r.at[1])
    n.gs_out[...] = n.gs_mine[1] + n.gs_pair[1]
    swap_end(4, new_at, lambda m: n.new_out.at[m])
    swap_end(3, grow_at, lambda m: n.grad_out.at[m])
    for t, target in ((n.d, n.rd_out), (n.u, n.ru_out), (n.q, n.rq_out)):
        for copy in out_copies(t, target):
            copy.wait()
    last.wait()
    for tag in list(pending):
        drain(tag)


def place_kernel(g, at_ref, tok_ref, cot_ref, new_ref, grad_ref, rq_ref, ru_ref, rd_ref, ro_ref, gs_ref, *outs):
    mixed_ref, gt_ref, gq_ref, gu_ref, gd_ref, go_ref, grouter_ref, ggains_ref = outs
    grouter_ref[...] = gs_ref[0:1, :]
    ggains_ref[...] = gs_ref[1:3, :]
    tall = tok_ref.shape[1]
    first = pl.program_id(1) * tall
    token = lax.broadcasted_iota(jnp.int32, (tall, g.cap), 0) + first
    hot = token == at_ref[0]
    routed = jnp.max(hot.astype(F32), axis=-1, keepdims=True) > 0.0
    hot = hot.astype(BF)
    new = dot(hot, new_ref[0], (1, 0))
    mixed_ref[0] = jnp.where(routed, new, tok_ref[0].astype(F32)).astype(BF)
    grad = dot(hot, grad_ref[0], (1, 0))
    gt_ref[0] = jnp.where(routed, grad, cot_ref[0].astype(F32))
    for index in range(g.R):
        for part in range(3):
            gq_ref[:, pl.ds(part * g.d + index * g.ac, g.ac)] = rq_ref[
                index, :, pl.ds(part * g.ac, g.ac)
            ].astype(F32)
        for block in range(g.F):
            gu_ref[:, pl.ds((block * g.R + index) * 128, 128)] = ru_ref[
                index, :, pl.ds(block * 128, 128)
            ].astype(F32)
        gd_ref[index] = rd_ref[index].astype(F32)
    go_ref[...] = ro_ref[...].astype(F32)


def place(g, chosen, tokens, cotangent, new_rows, grad_rows, rq, ru, rd, ro, gs):
    halves = 1
    steps = g.MB * halves
    tok_count = tokens.shape[1]
    tall = tok_count // halves
    piece = g.d // g.F
    low = piece // steps
    hidden = g.F * g.R * 128

    def block(*shape):
        return pl.BlockSpec((1,) + shape, lambda m, h: (m, h, 0))

    def micro(*shape):
        return pl.BlockSpec((1,) + shape, lambda m, h: (m, 0, 0))

    def slab(*lead, cols):
        return pl.BlockSpec(
            lead + (low, cols), lambda m, h: (0,) * len(lead) + (m * halves + h, 0)
        )

    return pl.pallas_call(
        functools.partial(place_kernel, g),
        grid=(g.MB, halves),
        in_specs=[
            micro(1, g.cap),
            block(tall, g.d),
            block(tall, g.d),
            micro(g.cap, g.d),
            micro(g.cap, g.d),
            slab(g.R, cols=g.qc),
            slab(g.R, cols=g.fc),
            slab(g.R, cols=g.d),
            slab(cols=g.d),
            pl.BlockSpec((8, 128), lambda m, h: (0, 0)),
        ],
        out_specs=[
            block(tall, g.d),
            block(tall, g.d),
            slab(cols=3 * g.d),
            slab(cols=hidden),
            slab(g.R, cols=g.d),
            slab(cols=g.d),
            pl.BlockSpec((1, 128), lambda m, h: (0, 0)),
            pl.BlockSpec((2, 128), lambda m, h: (0, 0)),
        ],
        out_shape=[
            jax.ShapeDtypeStruct(tokens.shape, BF),
            jax.ShapeDtypeStruct(tokens.shape, F32),
            jax.ShapeDtypeStruct((piece, 3 * g.d), F32),
            jax.ShapeDtypeStruct((piece, hidden), F32),
            jax.ShapeDtypeStruct((g.R, piece, g.d), F32),
            jax.ShapeDtypeStruct((piece, g.d), F32),
            jax.ShapeDtypeStruct((1, 128), F32),
            jax.ShapeDtypeStruct((2, 128), F32),
        ],
        compiler_params=pltpu.CompilerParams(vmem_limit_bytes=60 * 1024 * 1024),
        name="place_rows",
    )(chosen[:, None, :], tokens, cotangent, new_rows, grad_rows, rq, ru, rd, ro, gs)


def group_shards(tokens, cotangent, path, chosen, router, gains, w_qkv, w_out, w_up, w_down):
    R, F = lax.axis_size("rep"), lax.axis_size("fsdp")
    MB, tok_count, d = tokens.shape
    cap = chosen.shape[1]
    S = F // MB
    hidden = w_up.shape[1]
    g = types.SimpleNamespace(
        R=R,
        F=F,
        S=S,
        A=MB,
        X=R // 2,
        MB=MB,
        cap=cap,
        d=d,
        own=MB * cap,
        rows=R * MB * cap,
        tree=S * MB * cap,
        trees=R // S,
        heads=HEADS // R,
        qc=3 * d // R,
        ac=d // R,
        fc=hidden // R,
    )
    piece = d // F

    anywhere, inside = pl.BlockSpec(memory_space=pl.ANY), pl.BlockSpec(memory_space=pltpu.VMEM)
    operands = dict(
        tokens=(tokens, anywhere),
        cotangent=(cotangent, anywhere),
        w_qkv=(w_qkv, anywhere),
        w_out=(w_out, anywhere),
        w_up=(w_up, anywhere),
        w_down=(w_down, anywhere),
        path=(jnp.transpose(path, (2, 0, 1)), inside),
        chosen=(chosen, inside),
        router=(router[None], inside),
        gains=(gains.T, inside),
    )
    results = dict(
        new_out=((MB, cap, d), BF, anywhere),
        grad_out=((MB, cap, d), BF, anywhere),
        rq_out=((R, piece, g.qc), BF, anywhere),
        ru_out=((R, piece, g.fc), BF, anywhere),
        rd_out=((R, piece, d), BF, anywhere),
        ro_out=((piece, d), BF, anywhere),
        gs_out=((8, 128), F32, inside),
    )
    scratch = scratch_shapes(g)
    flat, _ = jax.tree.flatten(scratch)
    order = list(operands) + list(results)
    made = pl.pallas_call(
        functools.partial(block_kernel, g, order, jax.tree.structure(scratch)),
        out_shape=[jax.ShapeDtypeStruct(*kind[:2]) for kind in results.values()],
        in_specs=[spec for _, spec in operands.values()],
        out_specs=[kind[2] for kind in results.values()],
        scratch_shapes=flat,
        compiler_params=pltpu.CompilerParams(
            collective_id=0, has_side_effects=True, vmem_limit_bytes=60 * 1024 * 1024
        ),
        name="routed_block",
    )(*[value for value, _ in operands.values()])
    new_rows, grad_rows, rq, ru, rd, ro, gs = made
    mixed, grad_tokens, grad_qkv, grad_up, grad_down, grad_out, grad_router, grad_gains = place(
        g, chosen, tokens, cotangent, new_rows, grad_rows, rq, ru, rd, ro, gs
    )
    return (
        mixed,
        grad_tokens,
        grad_router[0],
        grad_gains.T,
        grad_qkv,
        grad_out,
        grad_up,
        grad_down.reshape(R * piece, d),
    )


def plain_norm(matrix, gain_row):
    return matrix * lax.rsqrt(jnp.mean(matrix * matrix, axis=-1, keepdims=True) + eps) * gain_row


def inner(left, right):
    return lax.dot_general(
        left, right, (((0,), (0,)), ((), ())), preferred_element_type=jnp.float32
    )


def by_rows(left, right):
    return lax.dot_general(
        left, right, (((1,), (1,)), ((), ())), preferred_element_type=jnp.float32
    )


def gather_rows(arrays):
    return lax.all_gather(arrays, "fsdp", axis=0, tiled=True)


def scatter_sum(array):
    return lax.psum_scatter(
        array.astype(jnp.bfloat16), "fsdp", scatter_dimension=0, tiled=True
    ).astype(jnp.float32)


def plain_shards(tokens, cotangent, path, chosen, router, gains, w_qkv, w_out, w_up, w_down):
    micro_count, tok_count, model_width = tokens.shape
    slot_count = chosen.shape[1]
    row_count = micro_count * slot_count
    head_dim = model_width // HEADS
    score_scale = head_dim ** (-0.5)
    offset = lax.axis_index("fsdp") * tok_count
    fsdp = lax.axis_size("fsdp")

    def pick(array):
        return jax.vmap(lambda rows, at: rows[at])(array, chosen)

    small = jnp.concatenate([router[:, None], gains], axis=1)
    small_all = gather_rows(small)
    qkv_all = gather_rows(w_qkv)
    out_all = gather_rows(w_out)
    up_all = gather_rows(w_up)
    down_all = gather_rows(w_down)
    router_float = small_all[:, 0].astype(jnp.float32)
    gain_one = small_all[:, 1].astype(jnp.float32)
    gain_two = small_all[:, 2].astype(jnp.float32)

    routed = pick(tokens).reshape(row_count, model_width)
    hidden = routed.astype(jnp.float32)
    gate_rate = jax.nn.sigmoid(
        jnp.dot(routed, small_all[:, 0], preferred_element_type=jnp.float32)
    )
    normed = plain_norm(hidden, gain_one).astype(jnp.bfloat16)
    projected = jnp.dot(normed, qkv_all, preferred_element_type=jnp.float32).astype(jnp.bfloat16)
    queries = projected[:, :model_width].reshape(micro_count, slot_count, HEADS, head_dim)
    own_path = pick(path)
    own_place = offset + chosen
    key_info = jnp.concatenate([own_path[:, :, :1], own_place[:, :, None]], axis=2)
    gathered = lax.all_gather(
        projected[:, model_width:].reshape(micro_count, slot_count, 2 * model_width), "fsdp"
    )
    info_all = lax.all_gather(key_info, "fsdp")
    key_count = fsdp * slot_count
    gathered = jnp.swapaxes(gathered, 0, 1).reshape(micro_count, key_count, 2, HEADS, head_dim)
    info_all = jnp.swapaxes(info_all, 0, 1).reshape(micro_count, key_count, 2)
    key_rows = gathered[:, :, 0]
    value_rows = gathered[:, :, 1]
    key_seg = info_all[:, None, :, 0]
    visible = (
        (key_seg == own_path[:, :, 0:1])
        | (key_seg == own_path[:, :, 1:2])
        | (key_seg == own_path[:, :, 2:3])
    ) & (info_all[:, None, :, 1] <= own_place[:, :, None])
    visible = visible[:, None]

    def product(form, left, right):
        return jnp.einsum(form, left, right, preferred_element_type=jnp.float32)

    scores = product("mqhd,mkhd->mhqk", queries, key_rows) * score_scale
    scores = jnp.where(visible, scores, -1e30)
    row_max = jnp.max(scores, axis=-1, keepdims=True)
    exponent = jnp.where(visible, jnp.exp(scores - row_max), 0.0)
    row_total = jnp.sum(exponent, axis=-1, keepdims=True)
    soft_prob = exponent / row_total
    probs = soft_prob.astype(jnp.bfloat16)
    attention = product("mhqk,mkhd->mqhd", probs, value_rows)
    attention = attention.reshape(row_count, model_width).astype(jnp.bfloat16)
    branch = jnp.dot(attention, out_all, preferred_element_type=jnp.float32)
    middle = hidden + branch
    normed_two = plain_norm(middle, gain_two).astype(jnp.bfloat16)
    up_proj = jnp.dot(normed_two, up_all, preferred_element_type=jnp.float32)
    activated = jax.nn.gelu(up_proj).astype(jnp.bfloat16)
    change = branch + jnp.dot(activated, down_all, preferred_element_type=jnp.float32)
    new_rows = hidden + gate_rate[:, None] * change

    def put(array, rows):
        rows = rows.reshape(micro_count, slot_count, model_width).astype(array.dtype)
        return jax.vmap(lambda whole, at, new: whole.at[at].set(new))(array, chosen, rows)

    mixed = put(tokens, new_rows)

    grad_rows = pick(cotangent).reshape(row_count, model_width).astype(jnp.float32)
    grad_change = gate_rate[:, None] * grad_rows
    grad_logit = jnp.sum(grad_rows * change, axis=-1) * gate_rate * (1.0 - gate_rate)
    grad_mlp = grad_change.astype(jnp.bfloat16)
    grad_down = scatter_sum(inner(activated, grad_mlp))
    grad_act = by_rows(grad_mlp, down_all)
    gelu_value, gelu_back = jax.vjp(jax.nn.gelu, up_proj)
    grad_up_proj = gelu_back(grad_act)[0].astype(jnp.bfloat16)
    grad_up = scatter_sum(inner(normed_two, grad_up_proj))
    grad_normed_two = by_rows(grad_up_proj, up_all)
    norm_value, norm_back_two = jax.vjp(plain_norm, middle, gain_two)
    grad_middle, grad_gain_two = norm_back_two(grad_normed_two)
    grad_branch = (grad_change + grad_middle).astype(jnp.bfloat16)
    grad_outw = scatter_sum(inner(attention, grad_branch))
    grad_attention = by_rows(grad_branch, out_all).astype(jnp.bfloat16)
    grad_heads = grad_attention.reshape(micro_count, slot_count, HEADS, head_dim)
    prob_grad = product("mqhd,mkhd->mhqk", grad_heads, value_rows)
    delta = jnp.sum(soft_prob * prob_grad, axis=-1, keepdims=True)
    grad_scores = (soft_prob * (prob_grad - delta)).astype(jnp.bfloat16)
    grad_query = product("mhqk,mkhd->mqhd", grad_scores, key_rows) * score_scale
    grad_key = product("mhqk,mqhd->mkhd", grad_scores, queries) * score_scale
    grad_value = product("mhqk,mqhd->mkhd", probs, grad_heads)
    grad_kv = jnp.stack([grad_key, grad_value], axis=2).reshape(
        micro_count, fsdp, slot_count, 2 * model_width
    )
    grad_kv = lax.psum_scatter(
        jnp.swapaxes(grad_kv, 0, 1).astype(jnp.bfloat16).reshape(-1, 2 * model_width),
        "fsdp",
        scatter_dimension=0,
        tiled=True,
    )
    grad_projected = jnp.concatenate(
        [
            grad_query.reshape(row_count, model_width).astype(jnp.bfloat16),
            grad_kv.reshape(row_count, 2 * model_width),
        ],
        axis=1,
    )
    grad_qkvw = scatter_sum(inner(normed, grad_projected))
    grad_normed = by_rows(grad_projected, qkv_all)
    norm_value_one, norm_back_one = jax.vjp(plain_norm, hidden, gain_one)
    grad_hidden_norm, grad_gain_one = norm_back_one(grad_normed)
    grad_hidden = (
        grad_rows + grad_middle + grad_hidden_norm + grad_logit[:, None] * router_float[None, :]
    )
    grad_tokens = put(cotangent.astype(jnp.float32), grad_hidden)
    grad_routerw = jnp.sum(grad_logit[:, None] * hidden, axis=0)
    grad_small = jnp.stack([grad_routerw, grad_gain_one, grad_gain_two], axis=1)
    grad_small = lax.psum_scatter(grad_small, "fsdp", scatter_dimension=0, tiled=True)
    summed = lax.psum((grad_small, grad_qkvw, grad_outw, grad_up, grad_down), "rep")
    return (mixed, grad_tokens, summed[0][:, 0], summed[0][:, 1:]) + tuple(summed[1:])


def solution(mesh):
    rows = P(None, ("rep", "fsdp"), None)
    weight = P("fsdp", None)

    def whole(*args):
        grouped = fits(mesh, args[0], args[3], args[8])
        return jax.shard_map(
            group_shards if grouped else plain_shards,
            mesh=mesh,
            in_specs=(
                rows,
                rows,
                rows,
                P(None, ("rep", "fsdp")),
                P("fsdp"),
                weight,
                weight,
                weight,
                weight,
                weight,
            ),
            out_specs=(rows, rows, P("fsdp"), weight, weight, weight, weight, weight),
            check_vma=False,
        )(*args)

    return whole
```

```python
import functools
import math
import types

import jax
import jax.numpy as jnp
from jax import lax
from jax.experimental import pallas as pl
from jax.experimental.pallas import tpu as pltpu
from jax.sharding import PartitionSpec as P

HEADS = 16


eps = 1e-05
MESH = pl.DeviceIdType.MESH
BF = jnp.bfloat16
F32 = jnp.float32
GELU_A = math.sqrt(2.0 / math.pi)
GELU_B = 0.044715


def dot(left, right, contract):
    return lax.dot_general(
        left, right, (((contract[0],), (contract[1],)), ((), ())), preferred_element_type=F32
    )


def aligned(index, size):
    return pl.ds(pl.multiple_of(index * size, size), size)


def loop(count, body):
    def step(index, carry):
        body(index)
        return carry

    lax.fori_loop(0, count, step, 0)


def fits(mesh, tokens, chosen, w_up):
    rep, fsdp = mesh.shape["rep"], mesh.shape["fsdp"]
    micro, width, hidden = tokens.shape[0], tokens.shape[2], w_up.shape[1]
    if fsdp % micro or rep % 2:
        return False
    inner_count = fsdp // micro
    return (
        rep % inner_count == 0
        and rep == micro
        and fsdp == rep * inner_count
        and width == fsdp * 128
        and hidden == fsdp * rep * 128
        and HEADS % (2 * rep) == 0
        and width // HEADS == 64
        and chosen.shape[1] // (rep * fsdp) == 64
        and rep == 4
        and hidden == rep * width
        and tokens.shape[1] * micro // (rep * fsdp) == 2 * rep * micro * 64
    )


def scratch_shapes(g):
    own, rows, d, piece = g.own, g.rows, g.d, g.d // g.F

    def vmem(height, width, kind=BF):
        return pltpu.VMEM((height, width), kind)

    def dma(*shape):
        return pltpu.SemaphoreType.DMA(shape)

    def shared():
        return dict(xs=dma(g.X - 1), xr=dma(g.X - 1), ss=dma(g.X), sr=dma(g.X))

    def halves():
        return [shared(), shared()]

    def direct():
        return dict(l=dma(1), os=dma(g.A - 1), ors=dma(g.A - 1), ins=dma(g.A), inr=dma(g.A))

    def chained():
        ends = dict(ups=dma(g.A - 1), upr=dma(g.A - 1), dns=dma(g.A - 1), dnr=dma(g.A - 1))
        return dict(l=dma(g.F), ins=dma(2 * g.A - 1), inr=dma(2 * g.A - 1), **ends)

    def pieces(count, cols, kind, height, full):
        made = dict(
            inbox=vmem(count // g.S * height, cols, kind),
            outbox=vmem(g.A * height, cols, kind),
            ins=dma(g.A),
            inr=dma(g.A),
            os=dma(g.A),
            ors=dma(g.A),
        )
        if full:
            made.update(grad=vmem(count * height, cols), share=shared(), out=dma(g.R))
            made.update(whole=vmem(full * height, cols))
        return made

    return dict(
        hid=vmem(own, d),
        ct=vmem(own, d),
        infos=vmem(g.R * g.MB * 8, 128, F32),
        sm=vmem(g.F * 8, 128, F32),
        info=pltpu.VMEM((g.MB, 8, 128), F32),
        vec=vmem(8, d, F32),
        wqa=vmem(d, g.qc),
        woa=vmem(g.ac, d),
        wua=vmem(d, g.fc),
        wda=vmem(g.fc, d),
        normed=vmem(rows, d),
        norm2=vmem(rows, d),
        proj=vmem(rows, g.qc),
        att=vmem(rows, g.ac),
        gatt=vmem(rows, g.ac),
        gproj=vmem(rows, g.qc),
        lse=vmem(rows, 128, F32),
        bias=vmem(g.tree, g.tree, F32),
        pair_a=vmem(2 * rows, g.fc),
        pair_b=vmem(2 * rows, d),
        dact=vmem(rows, g.fc, F32),
        gate=vmem(own, 128, F32),
        branch=vmem(own, d, F32),
        gmid=vmem(own, d, F32),
        ends=vmem(2 * own, d),
        to_sib=pltpu.VMEM((2, g.X * own, d), BF),
        of_sib=pltpu.VMEM((2, g.X * own, d), BF),
        to_x=pltpu.VMEM((2, (g.X - 1) * own, d), BF),
        of_x=pltpu.VMEM((2, (g.X - 1) * own, d), BF),
        gsum=vmem(8, d, F32),
        gsp=vmem(g.F * 8, 128, F32),
        gs_pair=pltpu.VMEM((2, 8, 128), F32),
        gs_mine=pltpu.VMEM((2, 8, 128), F32),
        a2a_s=dma(5, g.MB),
        a2a_r=dma(5, g.MB),
        tok_l=dma(2, g.MB),
        pair_s=dma(2),
        pair_r=dma(2),
        small_t=direct(),
        wo_t=direct(),
        wq_t=chained(),
        wu_t=chained(),
        wd_t=chained(),
        info_t=shared(),
        normed_t=halves(),
        gmlp_t=halves(),
        norm2_t=halves(),
        gbr_t=halves(),
        sums=[halves() for _ in range(4)],
        q=pieces(g.F, g.qc, BF, piece, g.R),
        u=pieces(g.F, g.fc, BF, piece, g.R),
        d=pieces(g.F, d, BF, piece, g.R),
        o=pieces(g.S, d, BF, piece, 1),
        s=pieces(g.F, 128, F32, 8, 0),
    )


def spaces(tree):
    if isinstance(tree, dict):
        return types.SimpleNamespace(**{name: spaces(value) for name, value in tree.items()})
    return [spaces(value) for value in tree] if isinstance(tree, list) else tree


def block_kernel(g, order, form, *refs):
    split = len(order)
    n = spaces(dict(zip(order, refs[:split]), **jax.tree.unflatten(form, refs[split:])))
    R, F, S, A, X, MB = g.R, g.F, g.S, g.A, g.X, g.MB
    own, rows, d, cap = g.own, g.rows, g.d, g.cap
    piece = d // F
    r = lax.axis_index("rep")
    f = lax.axis_index("fsdp")
    x, c = r // 2, lax.rem(r, 2)
    a, b = f // S, lax.rem(f, S)
    other_b = lax.rem(b + 1, S)
    sib = x * 2 + 1 - c
    pending = {}
    n.act, n.gup = n.pair_a.at[pl.ds(0, rows)], n.pair_a.at[pl.ds(rows, rows)]
    n.gmlp, n.gbr = n.pair_b.at[pl.ds(0, rows)], n.pair_b.at[pl.ds(rows, rows)]
    n.nrow, n.grow = n.ends.at[pl.ds(0, own)], n.ends.at[pl.ds(own, own)]
    n.picked, n.picked_ct = n.ends, n.norm2
    n.acc, n.gfirst = n.dact.at[pl.ds(0, own)], n.dact.at[pl.ds(own, own)]
    tok_count = n.tokens.shape[1]

    def token_copy(which, m):
        source, target = (n.tokens, n.pair_a) if which == 0 else (n.cotangent, n.pair_b)
        return pltpu.make_async_copy(
            source.at[m], target.at[pl.ds(m * tok_count, tok_count)], n.tok_l.at[which, m]
        )

    def cut_qkv():
        return [
            pltpu.make_async_copy(
                n.w_qkv.at[:, pl.ds(pl.multiple_of(part * d + r * g.ac, g.ac), g.ac)],
                n.wqa.at[aligned(f, piece), pl.ds(part * g.ac, g.ac)],
                n.wq_t.l.at[part],
            )
            for part in range(3)
        ]

    def cut_up():
        return [
            pltpu.make_async_copy(
                n.w_up.at[:, pl.ds(pl.multiple_of((block * R + r) * 128, 128), 128)],
                n.wua.at[aligned(f, piece), pl.ds(block * 128, 128)],
                n.wu_t.l.at[block],
            )
            for block in range(F)
        ]

    def cut_down():
        return [
            pltpu.make_async_copy(
                n.w_down.at[aligned(r, piece)], n.wda.at[aligned(f, piece)], n.wd_t.l.at[0]
            )
        ]

    for copy in cut_qkv():
        copy.start()
    for which in range(2):
        for m in range(MB):
            token_copy(which, m).start()
    for cut in (cut_up, cut_down):
        for copy in cut():
            copy.start()

    def remote(src, dst, ss, rs, rep, fsdp):
        return pltpu.make_async_remote_copy(
            src_ref=src,
            dst_ref=dst,
            send_sem=ss,
            recv_sem=rs,
            device_id={"rep": rep, "fsdp": fsdp},
            device_id_type=MESH,
        )

    def send(src, dst, ss, rs, rep, fsdp, cond=None, tag=None):
        def start():
            remote(src, dst, ss, rs, rep, fsdp).start()

        def done():
            remote(src, dst, ss, rs, rep, fsdp).wait_send()

        if cond is None:
            start()
            pending.setdefault(tag, []).append(done)
        else:
            pl.when(cond)(start)
            pending.setdefault(tag, []).append(lambda: pl.when(cond)(done))

    def drain(tag):
        for done in pending.pop(tag, []):
            done()

    def got(dst, rs):
        remote(dst, dst, rs, rs, sib, f).wait_recv()

    def xpeer(step):
        return lax.rem(x + 1 + step, X)

    def xfrom(step):
        return lax.rem(x + X - 1 - step, X)

    def outer(step):
        return lax.rem(a + step, A)

    def outer_from(step):
        return lax.rem(a + A - step, A)

    home_rep = (r // S) * S + b

    def home_fsdp(m):
        return m * S + lax.rem(r, S)

    barrier = pltpu.get_barrier_semaphore()

    def greet(rep, fsdp):
        pl.semaphore_signal(
            barrier, inc=1, device_id={"rep": rep, "fsdp": fsdp}, device_id_type=MESH
        )

    for step in range(1, A):
        greet(r, outer(step) * S + b)
    greet(r, a * S + other_b)
    greet(sib, f)
    for step in range(X - 1):
        greet(xpeer(step) * 2 + c, f)
    mine = [(home_fsdp(m) == f) & (home_rep == r) for m in range(MB)]
    for m in range(MB):

        @pl.when(jnp.logical_not(mine[m]))
        def _(m=m):
            greet(home_rep, home_fsdp(m))

    stays = (home_rep == r) & (lax.rem(r, S) == b)
    pl.semaphore_wait(barrier, (A - 1) + 1 + 1 + (X - 1) + MB - stays.astype(jnp.int32))

    def swap_start(which, src_of, dst_of):
        for m in range(MB):
            src, dst = src_of(m), dst_of(a)
            ss, rs = n.a2a_s.at[which, m], n.a2a_r.at[which, a]

            @pl.when(jnp.logical_not(mine[m]))
            def _():
                remote(src, dst, ss, rs, home_rep, home_fsdp(m)).start()

            @pl.when(mine[m])
            def _():
                pltpu.make_async_copy(src, dst, rs).start()

    def swap_end(which, src_of, dst_of):
        for m in range(MB):
            src, dst = src_of(m), dst_of(m)
            ss, rs = n.a2a_s.at[which, m], n.a2a_r.at[which, m]

            @pl.when(jnp.logical_not(mine[m]))
            def _():
                remote(src, dst, ss, rs, home_rep, home_fsdp(m)).wait()

            @pl.when(mine[m])
            def _():
                pltpu.make_async_copy(src, dst, rs).wait()

    def gather_start(t, buf, height):
        at = aligned(f, height)
        src = buf.at[at]
        for step in range(1, A):
            send(
                src,
                buf.at[at],
                t.os.at[step - 1],
                t.ors.at[step - 1],
                r,
                outer(step) * S + b,
            )
        send(src, buf.at[at], t.ins.at[0], t.inr.at[0], r, a * S + other_b)

    def gather_forward(t, buf, height):
        for step in range(1, A):
            at = buf.at[aligned(outer_from(step) * S + b, height)]
            got(at, t.ors.at[step - 1])
            send(at, at, t.ins.at[step], t.inr.at[step], r, a * S + other_b)

    def gather_end(t, buf, height):
        for step in range(A):
            at = buf.at[aligned(outer_from(step) * S + other_b, height)]
            got(at, t.inr.at[step])

    def hop(step):
        return lax.rem(a + A + step, A)

    def chain_start(t, buf, height):
        at = buf.at[aligned(f, height)]
        send(at, at, t.ups.at[0], t.upr.at[0], r, hop(1) * S + b, a < A - 1)
        send(at, at, t.dns.at[0], t.dnr.at[0], r, hop(-1) * S + b, a > 0)

    def chain_across(t, buf, height):
        at = buf.at[aligned(f, height)]
        send(at, at, t.ins.at[0], t.inr.at[0], r, a * S + other_b)

    def chain_forward(t, buf, height, step):
        for sends, takes, has, on, to, index in (
            (t.ups, t.upr, a >= step, a < A - 1, 1, step),
            (t.dns, t.dnr, a + step < A, a > 0, -1, A - 1 + step),
        ):
            at = buf.at[aligned(hop(-to * step) * S + b, height)]

            @pl.when(has)
            def _():
                got(at, takes.at[step - 1])

            if step < A - 1:
                send(
                    at,
                    at,
                    sends.at[step],
                    takes.at[step],
                    r,
                    hop(to) * S + b,
                    has & on,
                )
            send(
                at,
                at,
                t.ins.at[index],
                t.inr.at[index],
                r,
                a * S + other_b,
                has,
            )

    def chain_end(t, buf, height):
        got(buf.at[aligned(a * S + other_b, height)], t.inr.at[0])
        for step in range(1, A):
            for has, to, index in ((a >= step, 1, step), (a + step < A, -1, A - 1 + step)):
                at = buf.at[aligned(hop(-to * step) * S + other_b, height)]

                @pl.when(has)
                def _():
                    got(at, t.inr.at[index])

    is_source = a == r

    def out_start(src, buf):
        at = buf.at[aligned(b, piece)]

        @pl.when(is_source)
        def _():
            pltpu.make_async_copy(src, at, n.wo_t.l.at[0]).start()

        for step in range(1, A):
            send(
                src, at, n.wo_t.os.at[step - 1], n.wo_t.ors.at[0], r, outer(step) * S + b, is_source
            )
        send(src, at, n.wo_t.ins.at[0], n.wo_t.inr.at[0], r, a * S + other_b, is_source)

    def out_forward(buf):
        at = buf.at[aligned(b, piece)]

        @pl.when(jnp.logical_not(is_source))
        def _():
            got(at, n.wo_t.ors.at[0])

        send(
            at, at, n.wo_t.ins.at[1], n.wo_t.inr.at[0], r, a * S + other_b, jnp.logical_not(is_source)
        )

    def out_end(src, buf):
        @pl.when(is_source)
        def _():
            pltpu.make_async_copy(src, buf.at[aligned(b, piece)], n.wo_t.l.at[0]).wait()

        got(buf.at[aligned(other_b, piece)], n.wo_t.inr.at[0])

    def part_of(block, height, part):
        if part is None:
            return aligned(block, height)
        half = height // 2
        return pl.ds(pl.multiple_of(block * height + part * half, half), half)

    def share_start(t, buf, height, part=None):
        at = buf.at[part_of(r, height, part)]
        for step in range(X - 1):
            send(at, at, t.xs.at[step], t.xr.at[step], xpeer(step) * 2 + c, f)
        send(at, at, t.ss.at[0], t.sr.at[0], sib, f)

    def share_forward(t, buf, height, part=None):
        for step in range(X - 1):
            at = buf.at[part_of(xfrom(step) * 2 + c, height, part)]
            got(at, t.xr.at[step])
            send(at, at, t.ss.at[1 + step], t.sr.at[1 + step], sib, f)

    def share_near(t, buf, height, part=None):
        got(buf.at[part_of(sib, height, part)], t.sr.at[0])

    def share_far(t, buf, height, part=None):
        for step in range(X - 1):
            at = buf.at[part_of(xfrom(step) * 2 + 1 - c, height, part)]
            got(at, t.sr.at[1 + step])

    def share_end(t, buf, height):
        share_near(t, buf, height)
        share_far(t, buf, height)

    def rows_do(what, t, buf):
        what(t[0], buf, own)

    wide = 256

    def sum_owner(step):
        return xpeer(step) if step < X - 1 else x

    half_tiles = d // wide // 2

    def sum_near(index, slot, partial, step):
        to_sib, at = n.to_sib.at[slot], pl.ds(step * own, own)
        owner = sum_owner(step) * 2 + 1 - c
        if step == 0:
            drain(slot)
        for part in range(2):
            t, across = n.sums[index][part], pl.ds(part * d // 2, d // 2)

            def one(tile, part=part):
                cols = aligned(part * half_tiles + tile, wide)
                to_sib[at, cols] = partial(owner, cols).astype(BF)

            loop(half_tiles, one)
            send(
                to_sib.at[at, across],
                n.of_sib.at[slot, at, across],
                t.ss.at[step],
                t.sr.at[step],
                sib,
                f,
                tag=slot,
            )

    def sum_mine(index, slot, partial, step, acc, post=True):
        of_sib, to_x, at = n.of_sib.at[slot], n.to_x.at[slot], pl.ds(step * own, own)
        owner = sum_owner(step) * 2 + c
        last = step == X - 1
        for part in range(2):
            t, across = n.sums[index][part], pl.ds(part * d // 2, d // 2)
            got(of_sib.at[at, across], t.sr.at[step])

            def one(tile, part=part):
                cols = aligned(part * half_tiles + tile, wide)
                total = partial(owner, cols) + of_sib[at, cols].astype(F32)
                if last:
                    acc[:, cols] = total
                else:
                    to_x[at, cols] = total.astype(BF)

            loop(half_tiles, one)
            if not last and post:
                sum_post(index, slot, step, part)

    def sum_post(index, slot, step, part):
        at, across = pl.ds(step * own, own), pl.ds(part * d // 2, d // 2)
        t = n.sums[index][part]
        send(
            n.to_x.at[slot, at, across],
            n.of_x.at[slot, at, across],
            t.xs.at[step],
            t.xr.at[step],
            sum_owner(step) * 2 + c,
            f,
            tag=slot,
        )

    def sum_end(index, slot):
        of_x = n.of_x.at[slot]
        for step in range(X - 1):
            for part in range(2):
                across = pl.ds(part * d // 2, d // 2)
                got(of_x.at[pl.ds(step * own, own), across], n.sums[index][part].xr.at[step])

    def came(slot, at):
        total = None
        for step in range(X - 1):
            part = n.of_x[slot, pl.ds(step * own + at, tall), :].astype(F32)
            total = part if total is None else total + part
        return total

    tall = 32

    def by_own(body):
        def one(index):
            at = pl.multiple_of(index * tall, tall)
            body(at, pl.ds(at, tall))

        loop(own // tall, one)

    def grad_start(t, buf, height):
        out = t is n.o
        inbox = t.inbox
        for step in range(1 if out else A):
            to_a = r if out else outer(step + 1)
            src = buf.at[aligned((0 if out else to_a * S) + other_b, height)]
            send(
                src,
                inbox.at[pl.ds(step * height, height)],
                t.ins.at[step],
                t.inr.at[step],
                r,
                a * S + other_b,
            )

    def add_into(dst, base, inbox, start, height):
        small = min(height, 32)

        def one(index):
            at = pl.ds(pl.multiple_of(base + index * small, small), small)
            of = pl.ds(pl.multiple_of(start + index * small, small), small)
            dst[at, :] = (dst[at, :].astype(F32) + inbox[of, :].astype(F32)).astype(dst.dtype)

        loop(height // small, one)

    def grad_forward(t, buf, height):
        out = t is n.o
        inbox, outbox = t.inbox, t.outbox
        for step in range(1 if out else A):
            to_a = r if out else outer(step + 1)
            base = ((0 if out else to_a * S) + b) * height
            got(inbox.at[pl.ds(step * height, height)], t.inr.at[step])
            add_into(buf, base, inbox, step * height, height)
            if out:
                slot = lax.rem(r + A - a - 1, A)
                slot = jnp.where(is_source, 0, slot)
                send(
                    buf.at[pl.ds(pl.multiple_of(base, height), height)],
                    outbox.at[aligned(slot, height)],
                    n.o.os.at[0],
                    n.o.ors.at[slot],
                    r,
                    r * S + b,
                    jnp.logical_not(is_source),
                )
            elif step < A - 1:
                send(
                    buf.at[pl.ds(pl.multiple_of(base, height), height)],
                    outbox.at[pl.ds(step * height, height)],
                    t.os.at[step],
                    t.ors.at[step],
                    r,
                    to_a * S + b,
                )

    def grad_wait(t, height):
        for step in range(A - 1):
            got(
                t.outbox.at[pl.ds(step * height, height)],
                t.ors.at[step],
            )

    def grad_total(t, buf, base, height, target, target_base, boxes):
        outbox = t.outbox
        small = min(height, 32)

        def one(index):
            off = index * small
            total = buf[pl.ds(pl.multiple_of(base + off, small), small), :].astype(F32)
            for box in boxes:
                at = pl.ds(pl.multiple_of(box * height + off, small), small)
                total = total + outbox[at, :].astype(F32)
            at = pl.ds(pl.multiple_of(target_base + off, small), small)
            target[at, :] = total.astype(target.dtype)

        loop(height // small, one)

    side = a // 2
    mate = a + 1 - 2 * lax.rem(a, 2)
    is_end = (a == 0) | (a == A - 1)
    passes_on = jnp.logical_not(is_end)
    piece_owner = (2 - side, 3 * (1 - side), mate, a)

    def piece_start(t, step):
        height, inbox = piece, t.inbox
        send(
            t.grad.at[aligned(piece_owner[step] * S + other_b, height)],
            inbox.at[pl.ds(step * height, height)],
            t.ins.at[step],
            t.inr.at[step],
            r,
            a * S + other_b,
        )

    def piece_take(t, step):
        buf, inbox, outbox = t.grad, t.inbox, t.outbox
        base = (piece_owner[step] * S + b) * piece
        got(inbox.at[pl.ds(step * piece, piece)], t.inr.at[step])
        add_into(buf, base, inbox, step * piece, piece)
        if step < 3:
            send(
                buf.at[pl.ds(pl.multiple_of(base, piece), piece)],
                outbox.at[pl.ds(step * piece, piece)],
                t.os.at[step],
                t.ors.at[step],
                r,
                mate * S + b,
                is_end if step < 2 else None,
            )

    def piece_pass(t, step):
        buf, outbox = t.grad, t.outbox
        base = (piece_owner[step] * S + b) * piece

        @pl.when(passes_on)
        def _():
            got(outbox.at[pl.ds(step * piece, piece)], t.ors.at[step])
            add_into(buf, base, outbox, step * piece, piece)

        send(
            buf.at[pl.ds(pl.multiple_of(base, piece), piece)],
            outbox.at[pl.ds(3 * piece, piece)],
            t.os.at[step],
            t.ors.at[3],
            r,
            piece_owner[step] * S + b,
            passes_on,
        )

    def piece_own(t):
        for box in (2, 3):
            got(
                t.outbox.at[pl.ds(box * piece, piece)], t.ors.at[box]
            )
        grad_total(t, t.grad, f * piece, piece, t.whole, r * piece, (2, 3))
        share_start(t.share, t.whole, piece)

    def hid_at(i):
        return n.hid.at[aligned(i, cap)]

    def ct_at(i):
        return n.ct.at[aligned(i, cap)]

    def info_src(i):
        return n.info.at[i]

    def info_own(i):
        return n.infos.at[aligned(r * MB + i, 8)]

    def info_home(i):
        return n.infos.at[aligned(home_rep * MB + i, 8)]

    odd = lax.rem(a, 2)
    lane_token = lax.broadcasted_iota(jnp.int32, (tok_count, 128), 0)
    lane = lax.broadcasted_iota(jnp.int32, (1, 128), 1)
    lane_used = (lane // cap) == odd
    def at_of(m):
        row = n.chosen[m : m + 1, :]
        return jnp.where(lane_used, jnp.concatenate([row, row], axis=1), -1)

    def hot_of(m):
        return (lane_token == at_of(m)).astype(F32).astype(BF)

    def tok_at(m):
        return n.picked.at[pl.ds(pl.multiple_of(m * 128 + odd * cap, cap), cap)]

    def cot_at(m):
        return n.picked_ct.at[pl.ds(pl.multiple_of(m * 128 + odd * cap, cap), cap)]

    mine_sm = pl.ds(pl.multiple_of(f * 8, 8), 8)
    def first_norm(at, rows_at):
        h = n.hid[rows_at, :].astype(F32)
        scale = lax.rsqrt(jnp.mean(h * h, axis=-1, keepdims=True) + eps)
        n.normed[pl.ds(pl.multiple_of(r * own + at, tall), tall), :] = (
            h * scale * n.vec[1:2, :]
        ).astype(BF)
        logit = jnp.sum(h * n.vec[0:1, :], axis=-1, keepdims=True)
        n.gate[rows_at, :] = jnp.broadcast_to(1.0 / (1.0 + jnp.exp(-logit)), (tall, 128))

    def mlp_cotangent(at, rows_at):
        gc = n.gate[rows_at, 0:1] * n.ct[rows_at, :].astype(F32)
        n.gmlp[pl.ds(pl.multiple_of(r * own + at, tall), tall), :] = gc.astype(BF)

    far = xpeer(0)
    near_blocks, far_blocks = (r, sib), (far * 2 + c, far * 2 + 1 - c)
    def project(block):
        at = aligned(block, own)
        half = g.qc // 3

        def one(part):
            cols = aligned(part, half)
            n.proj[at, cols] = dot(n.normed[at, :], n.wqa[:, cols], (1, 0)).astype(BF)

        loop(3, one)

    tree, pairs = g.tree, g.heads // 2
    scale = 64 ** (-0.5)
    low_lane = lax.broadcasted_iota(jnp.int32, (tree, 128), 1) < 64
    def half_of(value, half):
        keep = low_lane if half == 0 else jnp.logical_not(low_lane)
        return jnp.where(keep, value, jnp.zeros_like(value))

    def join(first, second):
        return jnp.where(low_lane, first, second)

    def make_bias(t):
        blocks = []
        for index in range(S * MB // 2):
            at = pl.multiple_of((t * S * MB + index * 2) * 8, 8)
            blocks.append(n.infos[pl.ds(at, 8), :] + n.infos[pl.ds(at + 8, 8), :])
        keys = jnp.concatenate(blocks, axis=1)
        asked = jnp.transpose(keys)
        near = keys[0:1, :] == asked[:, 0:1]
        near = near | (keys[0:1, :] == asked[:, 1:2])
        near = near | (keys[0:1, :] == asked[:, 2:3])
        near = near & (keys[3:4, :] <= asked[:, 3:4])
        n.bias[...] = jnp.where(near, 0.0, -1e30)

    def columns(part, pair):
        return pl.ds(part * g.ac + pair * 128, 128)

    def attend(t):
        make_bias(t)
        at = aligned(t, tree)
        for pair in range(pairs):
            q = n.proj[at, columns(0, pair)]
            k = n.proj[at, columns(1, pair)]
            v = n.proj[at, columns(2, pair)]
            made = []
            for half in range(2):
                s = dot(half_of(q, half), k, (1, 1)) * scale + n.bias[...]
                top = jnp.max(s, axis=-1, keepdims=True)
                e = jnp.exp(s - top)
                total = jnp.sum(e, axis=-1, keepdims=True)
                made.append(dot((e * (1.0 / total)).astype(BF), v, (1, 0)))
                head = pair * 2 + half
                n.lse[at, head : head + 1] = top + jnp.log(total)
            n.att[at, pl.ds(pair * 128, 128)] = join(*made).astype(BF)

    def branch_part(owner, cols):
        return dot(n.att[aligned(owner, own), :], n.woa[:, cols], (1, 0))

    def second_norm(at, rows_at):
        br = n.branch[rows_at, :] + came(0, at)
        n.branch[rows_at, :] = br
        mid = n.hid[rows_at, :].astype(F32) + br
        inv = lax.rsqrt(jnp.mean(mid * mid, axis=-1, keepdims=True) + eps)
        n.norm2[pl.ds(pl.multiple_of(r * own + at, tall), tall), :] = (
            mid * inv * n.vec[2:3, :]
        ).astype(BF)

    tiles = g.fc // wide
    def mlp_up(block):
        at = aligned(block, own)

        def one(tile):
            cols = aligned(tile, wide)
            u = dot(n.norm2[at, :], n.wua[:, cols], (1, 0))
            square = u * u
            t = jnp.tanh(GELU_A * (u + GELU_B * square * u))
            n.act[at, cols] = (0.5 * u * (1.0 + t)).astype(BF)
            n.dact[at, cols] = 0.5 * (1.0 + t) + (0.5 * GELU_A) * u * (1.0 - t * t) * (
                1.0 + (3.0 * GELU_B) * square
            )

        loop(tiles, one)

    def mlp_back(block):
        at = aligned(block, own)

        def one(tile):
            cols = aligned(tile, wide)
            ga = dot(n.gmlp[at, :], n.wda[cols, :], (1, 1))
            n.gup[at, cols] = (ga * n.dact[at, cols]).astype(BF)

        loop(tiles, one)

    def norm2_part(owner, cols):
        return dot(n.gup[aligned(owner, own), :], n.wua[cols, :], (1, 1))

    def weight_grad(left, right, target, count):
        def one(index):
            cols = aligned(index, 256)
            target[cols, :] = dot(left[:, cols], right[...], (0, 0)).astype(BF)

        loop(count // 256, one)

    def second_back(at, rows_at):
        dy = n.gmid[rows_at, :] + came(1, at)
        mid = n.hid[rows_at, :].astype(F32) + n.branch[rows_at, :]
        inv = lax.rsqrt(jnp.mean(mid * mid, axis=-1, keepdims=True) + eps)
        n.gsum[2:3, :] = n.gsum[2:3, :] + jnp.sum(dy * mid * inv, axis=0, keepdims=True)
        t = dy * n.vec[2:3, :]
        along = jnp.sum(mid * t, axis=-1, keepdims=True) * (inv * inv * inv * (1.0 / d))
        gm = inv * t - mid * along
        n.gmid[rows_at, :] = gm
        gc = n.gate[rows_at, 0:1] * n.ct[rows_at, :].astype(F32)
        n.gbr[pl.ds(pl.multiple_of(r * own + at, tall), tall), :] = (gc + gm).astype(BF)

    def attention_cotangent(block):
        at = aligned(block, own)
        n.gatt[at, :] = dot(n.gbr[at, :], n.woa[...], (1, 1)).astype(BF)

    def attend_back(t):
        make_bias(t)
        at = aligned(t, tree)
        for pair in range(pairs):
            q = n.proj[at, columns(0, pair)]
            k = n.proj[at, columns(1, pair)]
            v = n.proj[at, columns(2, pair)]
            da = n.gatt[at, pl.ds(pair * 128, 128)]
            dq, dk, dv = [], [], []
            for half in range(2):
                head = pair * 2 + half
                s = dot(half_of(q, half), k, (1, 1)) * scale + n.bias[...]
                p = jnp.exp(s - n.lse[at, head : head + 1])
                dp = dot(half_of(da, half), v, (1, 1))
                delta = jnp.sum(p * dp, axis=-1, keepdims=True)
                ds = (p * (dp - delta)).astype(BF)
                dq.append(dot(ds, k, (1, 0)))
                dk.append(dot(ds, q, (0, 0)))
                dv.append(dot(p.astype(BF), da, (0, 0)))
            n.gproj[at, columns(0, pair)] = (join(*dq) * scale).astype(BF)
            n.gproj[at, columns(1, pair)] = (join(*dk) * scale).astype(BF)
            n.gproj[at, columns(2, pair)] = join(*dv).astype(BF)

    def change_part(owner, cols):
        return dot(n.act[aligned(owner, own), :], n.wda[:, cols], (1, 0))

    def normed_part(owner, cols):
        return dot(n.gproj[aligned(owner, own), :], n.wqa[cols, :], (1, 1))

    def new_rows(at, rows_at):
        change = n.branch[rows_at, :] + n.acc[rows_at, :] + came(0, at)
        h = n.hid[rows_at, :].astype(F32)
        gate = n.gate[rows_at, 0:1]
        n.nrow[rows_at, :] = (h + gate * change).astype(BF)
        logit = jnp.sum(n.ct[rows_at, :].astype(F32) * change, axis=-1, keepdims=True)
        logit = logit * gate * (1.0 - gate)
        n.gsum[0:1, :] = n.gsum[0:1, :] + jnp.sum(logit * h, axis=0, keepdims=True)
        n.gmid[rows_at, :] = n.gmid[rows_at, :] + logit * n.vec[0:1, :]

    def new_at(i):
        return n.nrow.at[aligned(i, cap)]

    def grow_at(i):
        return n.grow.at[aligned(i, cap)]

    def first_back(at, rows_at):
        dy = n.gfirst[rows_at, :] + came(1, at)
        h = n.hid[rows_at, :].astype(F32)
        inv = lax.rsqrt(jnp.mean(h * h, axis=-1, keepdims=True) + eps)
        n.gsum[1:2, :] = n.gsum[1:2, :] + jnp.sum(dy * h * inv, axis=0, keepdims=True)
        t = dy * n.vec[1:2, :]
        along = jnp.sum(h * t, axis=-1, keepdims=True) * (inv * inv * inv * (1.0 / d))
        total = n.ct[rows_at, :].astype(F32) + n.gmid[rows_at, :] + (inv * t - h * along)
        n.grow[rows_at, :] = total.astype(BF)

    ax, ac = a // 2, lax.rem(a, 2)
    off_x = (c == ac) & (x != ax)
    def out_copies(t, target):
        return [
            pltpu.make_async_copy(
                t.whole.at[pl.ds(index * piece, piece)], target.at[index], t.out.at[index]
            )
            for index in range(R)
        ]

    last = pltpu.make_async_copy(n.o.whole, n.ro_out, n.o.out.at[0])
    n.sm[mine_sm, :] = jnp.concatenate(
        [n.router[...].astype(F32), n.gains[...].astype(F32), jnp.zeros((5, 128), F32)], axis=0
    )
    gather_start(n.small_t, n.sm, 8)
    for copy in cut_qkv():
        copy.wait()
    chain_start(n.wq_t, n.wqa, piece)
    chain_across(n.wq_t, n.wqa, piece)
    for m in range(MB):
        hot = hot_of(m)
        token_copy(0, m).wait()
        n.picked[m * 128 : (m + 1) * 128, :] = dot(
            hot, n.pair_a[m * tok_count : (m + 1) * tok_count, :], (0, 0)
        ).astype(BF)
        lines = jnp.concatenate([n.path[line, m : m + 1, :] for line in range(3)], axis=0)
        n.info[m, 0:3, :] = dot(lines.astype(F32).astype(BF), hot, (1, 0))
        at = at_of(m)
        n.info[m, 3:4, :] = jnp.where(at >= 0, at + f * tok_count, 0).astype(F32)
        n.info[m, 4:8, :] = jnp.zeros((4, 128), F32)
    swap_start(0, tok_at, hid_at)
    for m in range(MB):
        ss, rs = n.a2a_s.at[1, m], n.a2a_r.at[1, a]

        @pl.when(jnp.logical_not(mine[m]))
        def _():
            remote(info_src(m), info_home(a), ss, rs, home_rep, home_fsdp(m)).start()

        @pl.when(mine[m])
        def _():
            pltpu.make_async_copy(info_src(m), info_own(a), rs).start()
    gather_forward(n.small_t, n.sm, 8)
    chain_forward(n.wq_t, n.wqa, piece, 1)
    for m in range(MB):
        token_copy(1, m).wait()
        n.picked_ct[m * 128 : (m + 1) * 128, :] = dot(
            hot_of(m), n.pair_b[m * tok_count : (m + 1) * tok_count, :], (0, 0)
        ).astype(BF)
    gather_end(n.small_t, n.sm, 8)
    for index in range(F):
        n.vec[:, index * 128 : (index + 1) * 128] = n.sm[index * 8 : (index + 1) * 8, :]
    swap_end(1, info_src, info_own)
    share_start(n.info_t, n.infos, MB * 8)
    swap_end(0, tok_at, hid_at)
    by_own(first_norm)
    rows_do(share_start, n.normed_t, n.normed)
    chain_forward(n.wq_t, n.wqa, piece, 2)
    swap_start(2, cot_at, ct_at)
    share_forward(n.info_t, n.infos, MB * 8)
    out_start(n.w_out, n.woa)
    rows_do(share_forward, n.normed_t, n.normed)
    chain_forward(n.wq_t, n.wqa, piece, 3)
    for copy in cut_up():
        copy.wait()
    chain_start(n.wu_t, n.wua, piece)
    chain_across(n.wu_t, n.wua, piece)
    for copy in cut_down():
        copy.wait()
    share_end(n.info_t, n.infos, MB * 8)
    rows_do(share_near, n.normed_t, n.normed)
    rows_do(share_far, n.normed_t, n.normed)
    chain_end(n.wq_t, n.wqa, piece)
    swap_end(2, cot_at, ct_at)
    by_own(mlp_cotangent)
    share_start(n.gmlp_t[0], n.gmlp, own)
    for block in far_blocks:
        project(block)
    out_forward(n.woa)
    chain_forward(n.wu_t, n.wua, piece, 1)
    chain_start(n.wd_t, n.wda, piece)
    chain_across(n.wd_t, n.wda, piece)
    attend(far)
    out_end(n.w_out, n.woa)
    sum_near(0, 0, branch_part, 0)
    for block in near_blocks:
        project(block)
    sum_mine(0, 0, branch_part, 0, n.branch)
    chain_forward(n.wu_t, n.wua, piece, 2)
    chain_forward(n.wd_t, n.wda, piece, 1)
    attend(x)
    sum_near(0, 0, branch_part, 1)
    chain_forward(n.wu_t, n.wua, piece, 3)
    sum_mine(0, 0, branch_part, 1, n.branch)
    chain_forward(n.wd_t, n.wda, piece, 2)
    share_forward(n.gmlp_t[0], n.gmlp, own)
    sum_end(0, 0)
    by_own(second_norm)
    rows_do(share_start, n.norm2_t, n.norm2)
    chain_end(n.wu_t, n.wua, piece)
    chain_forward(n.wd_t, n.wda, piece, 3)
    mlp_up(r)
    rows_do(share_near, n.norm2_t, n.norm2)
    mlp_up(sib)
    rows_do(share_forward, n.norm2_t, n.norm2)
    mlp_up(far_blocks[0])
    rows_do(share_far, n.norm2_t, n.norm2)
    mlp_up(far_blocks[1])
    rows_do(share_near, n.gmlp_t, n.gmlp)
    rows_do(share_far, n.gmlp_t, n.gmlp)
    weight_grad(n.act, n.gmlp, n.d.grad, g.fc)
    piece_start(n.d, 0)
    piece_start(n.d, 1)
    chain_end(n.wd_t, n.wda, piece)
    mlp_back(far_blocks[1])
    sum_near(1, 1, norm2_part, 0)
    mlp_back(far_blocks[0])
    sum_mine(1, 1, norm2_part, 0, n.gmid)
    mlp_back(sib)
    sum_near(1, 1, norm2_part, 1)
    mlp_back(r)
    sum_mine(1, 1, norm2_part, 1, n.gmid)
    piece_start(n.d, 2)
    weight_grad(n.norm2, n.gup, n.u.grad, d)
    n.gsum[...] = jnp.zeros_like(n.gsum)
    sum_end(1, 1)
    by_own(second_back)
    rows_do(share_start, n.gbr_t, n.gbr)
    piece_start(n.d, 3)
    piece_take(n.d, 0)
    piece_take(n.d, 1)
    piece_start(n.u, 0)
    attention_cotangent(r)
    rows_do(share_near, n.gbr_t, n.gbr)
    attention_cotangent(sib)
    attend_back(x)
    sum_near(2, 0, change_part, 0)
    piece_start(n.u, 1)
    sum_near(2, 0, change_part, 1)
    piece_take(n.d, 3)
    piece_start(n.u, 2)
    piece_pass(n.d, 0)
    sum_mine(2, 0, change_part, 0, n.acc, False)
    rows_do(share_forward, n.gbr_t, n.gbr)
    for part in range(2):
        sum_post(2, 0, 0, part)
    piece_take(n.d, 2)
    piece_take(n.u, 0)
    piece_pass(n.d, 1)
    attention_cotangent(far_blocks[0])
    rows_do(share_far, n.gbr_t, n.gbr)
    attention_cotangent(far_blocks[1])
    weight_grad(n.att, n.gbr, n.o.grad, g.ac)
    grad_start(n.o, n.o.grad, piece)
    piece_start(n.u, 3)
    attend_back(far)
    piece_take(n.u, 1)
    sum_near(3, 1, normed_part, 0)
    piece_pass(n.u, 0)
    sum_mine(3, 1, normed_part, 0, n.gfirst)
    sum_near(3, 1, normed_part, 1)
    sum_mine(2, 0, change_part, 1, n.acc)
    piece_take(n.u, 2)
    sum_end(2, 0)
    by_own(new_rows)
    swap_start(4, new_at, lambda m: n.new_out.at[m])
    grad_forward(n.o, n.o.grad, piece)
    weight_grad(n.normed, n.gproj, n.q.grad, d)
    piece_start(n.q, 3)
    piece_start(n.q, 1)
    piece_take(n.q, 1)
    sum_mine(3, 1, normed_part, 1, n.gfirst)
    piece_pass(n.u, 1)
    piece_start(n.q, 0)
    piece_take(n.q, 0)
    piece_start(n.q, 2)
    piece_own(n.d)
    sum_end(3, 1)
    by_own(first_back)
    swap_start(3, grow_at, lambda m: n.grad_out.at[m])
    piece_take(n.u, 3)
    for index in range(F):
        n.gsp[index * 8 : (index + 1) * 8, :] = n.gsum[:, index * 128 : (index + 1) * 128]
    piece_take(n.q, 2)
    piece_pass(n.q, 1)
    grad_start(n.s, n.gsp, 8)
    grad_forward(n.s, n.gsp, 8)
    piece_pass(n.q, 0)
    piece_take(n.q, 3)
    piece_own(n.u)
    @pl.when(is_source)
    def _():
        grad_wait(n.o, piece)
        grad_total(n.o, n.o.grad, b * piece, piece, n.o.whole, 0, range(A - 1))
    for step in range(X - 1):
        send(n.o.whole, n.o.whole, n.o.share.xs.at[step], n.o.share.xr.at[0], xpeer(step) * 2 + c, f, is_source)
    send(n.o.whole, n.o.whole, n.o.share.ss.at[0], n.o.share.sr.at[0], sib, f, is_source)
    grad_wait(n.s, 8)
    grad_total(n.s, n.gsp, f * 8, 8, n.gs_mine.at[0], 0, range(A - 1))
    send(n.gs_mine.at[0], n.gs_pair.at[0], n.pair_s.at[0], n.pair_r.at[0], sib, f)
    piece_own(n.q)
    share_forward(n.d.share, n.d.whole, piece)
    share_end(n.d.share, n.d.whole, piece)
    @pl.when(off_x)
    def _():
        got(n.o.whole, n.o.share.xr.at[0])
    send(n.o.whole, n.o.whole, n.o.share.ss.at[1], n.o.share.sr.at[0], sib, f, off_x)
    share_forward(n.u.share, n.u.whole, piece)
    share_end(n.u.share, n.u.whole, piece)
    for copy in out_copies(n.d, n.rd_out):
        copy.start()
    @pl.when(c != ac)
    def _():
        got(n.o.whole, n.o.share.sr.at[0])
    last.start()
    got(n.gs_pair.at[0], n.pair_r.at[0])
    n.gs_mine[1] = n.gs_mine[0] + n.gs_pair[0]
    send(n.gs_mine.at[1], n.gs_pair.at[1], n.pair_s.at[1], n.pair_r.at[1], xpeer(0) * 2 + c, f)
    share_forward(n.q.share, n.q.whole, piece)
    for copy in out_copies(n.u, n.ru_out):
        copy.start()
    share_end(n.q.share, n.q.whole, piece)
    for copy in out_copies(n.q, n.rq_out):
        copy.start()
    got(n.gs_pair.at[1], n.pair_r.at[1])
    n.gs_out[...] = n.gs_mine[1] + n.gs_pair[1]
    swap_end(4, new_at, lambda m: n.new_out.at[m])
    swap_end(3, grow_at, lambda m: n.grad_out.at[m])
    for t, target in ((n.d, n.rd_out), (n.u, n.ru_out), (n.q, n.rq_out)):
        for copy in out_copies(t, target):
            copy.wait()
    last.wait()
    for tag in list(pending):
        drain(tag)


def place_kernel(g, at_ref, tok_ref, cot_ref, new_ref, grad_ref, rq_ref, ru_ref, rd_ref, ro_ref, gs_ref, *outs):
    mixed_ref, gt_ref, gq_ref, gu_ref, gd_ref, go_ref, grouter_ref, ggains_ref = outs
    grouter_ref[...] = gs_ref[0:1, :]
    ggains_ref[...] = gs_ref[1:3, :]
    tall = tok_ref.shape[1]
    first = pl.program_id(1) * tall
    for k in range(2):
        token = lax.broadcasted_iota(jnp.int32, (tall, g.cap), 0) + first
        hot = token == at_ref[k]
        routed = jnp.max(hot.astype(F32), axis=-1, keepdims=True) > 0.0
        hot = hot.astype(BF)
        new = dot(hot, new_ref[k], (1, 0))
        mixed_ref[k] = jnp.where(routed, new, tok_ref[k].astype(F32)).astype(BF)
        grad = dot(hot, grad_ref[k], (1, 0))
        gt_ref[k] = jnp.where(routed, grad, cot_ref[k].astype(F32))
    for index in range(g.R):
        for part in range(3):
            gq_ref[:, pl.ds(part * g.d + index * g.ac, g.ac)] = rq_ref[
                index, :, pl.ds(part * g.ac, g.ac)
            ].astype(F32)
        for block in range(g.F):
            gu_ref[:, pl.ds((block * g.R + index) * 128, 128)] = ru_ref[
                index, :, pl.ds(block * 128, 128)
            ].astype(F32)
        gd_ref[index] = rd_ref[index].astype(F32)
    go_ref[...] = ro_ref[...].astype(F32)


def place(g, chosen, tokens, cotangent, new_rows, grad_rows, rq, ru, rd, ro, gs):
    halves = 1
    steps = g.MB // 2 * halves
    tok_count = tokens.shape[1]
    tall = tok_count // halves
    piece = g.d // g.F
    low = piece // steps
    hidden = g.F * g.R * 128

    def block(*shape):
        return pl.BlockSpec((2,) + shape, lambda m, h: (m, h, 0))

    def micro(*shape):
        return pl.BlockSpec((2,) + shape, lambda m, h: (m, 0, 0))

    def slab(*lead, cols):
        return pl.BlockSpec(
            lead + (low, cols), lambda m, h: (0,) * len(lead) + (m * halves + h, 0)
        )

    return pl.pallas_call(
        functools.partial(place_kernel, g),
        grid=(g.MB // 2, halves),
        in_specs=[
            micro(1, g.cap),
            block(tall, g.d),
            block(tall, g.d),
            micro(g.cap, g.d),
            micro(g.cap, g.d),
            slab(g.R, cols=g.qc),
            slab(g.R, cols=g.fc),
            slab(g.R, cols=g.d),
            slab(cols=g.d),
            pl.BlockSpec((8, 128), lambda m, h: (0, 0)),
        ],
        out_specs=[
            block(tall, g.d),
            block(tall, g.d),
            slab(cols=3 * g.d),
            slab(cols=hidden),
            slab(g.R, cols=g.d),
            slab(cols=g.d),
            pl.BlockSpec((1, 128), lambda m, h: (0, 0)),
            pl.BlockSpec((2, 128), lambda m, h: (0, 0)),
        ],
        out_shape=[
            jax.ShapeDtypeStruct(tokens.shape, BF),
            jax.ShapeDtypeStruct(tokens.shape, F32),
            jax.ShapeDtypeStruct((piece, 3 * g.d), F32),
            jax.ShapeDtypeStruct((piece, hidden), F32),
            jax.ShapeDtypeStruct((g.R, piece, g.d), F32),
            jax.ShapeDtypeStruct((piece, g.d), F32),
            jax.ShapeDtypeStruct((1, 128), F32),
            jax.ShapeDtypeStruct((2, 128), F32),
        ],
        compiler_params=pltpu.CompilerParams(vmem_limit_bytes=60 * 1024 * 1024),
        name="place_rows",
    )(chosen[:, None, :], tokens, cotangent, new_rows, grad_rows, rq, ru, rd, ro, gs)


def group_shards(tokens, cotangent, path, chosen, router, gains, w_qkv, w_out, w_up, w_down):
    R, F = lax.axis_size("rep"), lax.axis_size("fsdp")
    MB, tok_count, d = tokens.shape
    cap = chosen.shape[1]
    S = F // MB
    hidden = w_up.shape[1]
    g = types.SimpleNamespace(
        R=R,
        F=F,
        S=S,
        A=MB,
        X=R // 2,
        MB=MB,
        cap=cap,
        d=d,
        own=MB * cap,
        rows=R * MB * cap,
        tree=S * MB * cap,
        trees=R // S,
        heads=HEADS // R,
        qc=3 * d // R,
        ac=d // R,
        fc=hidden // R,
    )
    piece = d // F

    anywhere, inside = pl.BlockSpec(memory_space=pl.ANY), pl.BlockSpec(memory_space=pltpu.VMEM)
    operands = dict(
        tokens=(tokens, anywhere),
        cotangent=(cotangent, anywhere),
        w_qkv=(w_qkv, anywhere),
        w_out=(w_out, anywhere),
        w_up=(w_up, anywhere),
        w_down=(w_down, anywhere),
        path=(jnp.transpose(path, (2, 0, 1)), inside),
        chosen=(chosen, inside),
        router=(router[None], inside),
        gains=(gains.T, inside),
    )
    results = dict(
        new_out=((MB, cap, d), BF, anywhere),
        grad_out=((MB, cap, d), BF, anywhere),
        rq_out=((R, piece, g.qc), BF, anywhere),
        ru_out=((R, piece, g.fc), BF, anywhere),
        rd_out=((R, piece, d), BF, anywhere),
        ro_out=((piece, d), BF, anywhere),
        gs_out=((8, 128), F32, inside),
    )
    scratch = scratch_shapes(g)
    flat, _ = jax.tree.flatten(scratch)
    order = list(operands) + list(results)
    made = pl.pallas_call(
        functools.partial(block_kernel, g, order, jax.tree.structure(scratch)),
        out_shape=[jax.ShapeDtypeStruct(*kind[:2]) for kind in results.values()],
        in_specs=[spec for _, spec in operands.values()],
        out_specs=[kind[2] for kind in results.values()],
        scratch_shapes=flat,
        compiler_params=pltpu.CompilerParams(
            collective_id=0, has_side_effects=True, vmem_limit_bytes=60 * 1024 * 1024
        ),
        name="routed_block",
    )(*[value for value, _ in operands.values()])
    new_rows, grad_rows, rq, ru, rd, ro, gs = made
    mixed, grad_tokens, grad_qkv, grad_up, grad_down, grad_out, grad_router, grad_gains = place(
        g, chosen, tokens, cotangent, new_rows, grad_rows, rq, ru, rd, ro, gs
    )
    return (
        mixed,
        grad_tokens,
        grad_router[0],
        grad_gains.T,
        grad_qkv,
        grad_out,
        grad_up,
        grad_down.reshape(R * piece, d),
    )


def plain_norm(matrix, gain_row):
    return matrix * lax.rsqrt(jnp.mean(matrix * matrix, axis=-1, keepdims=True) + eps) * gain_row


def inner(left, right):
    return lax.dot_general(
        left, right, (((0,), (0,)), ((), ())), preferred_element_type=jnp.float32
    )


def by_rows(left, right):
    return lax.dot_general(
        left, right, (((1,), (1,)), ((), ())), preferred_element_type=jnp.float32
    )


def gather_rows(arrays):
    return lax.all_gather(arrays, "fsdp", axis=0, tiled=True)


def scatter_sum(array):
    return lax.psum_scatter(
        array.astype(jnp.bfloat16), "fsdp", scatter_dimension=0, tiled=True
    ).astype(jnp.float32)


def plain_shards(tokens, cotangent, path, chosen, router, gains, w_qkv, w_out, w_up, w_down):
    micro_count, tok_count, model_width = tokens.shape
    slot_count = chosen.shape[1]
    row_count = micro_count * slot_count
    head_dim = model_width // HEADS
    score_scale = head_dim ** (-0.5)
    offset = lax.axis_index("fsdp") * tok_count
    fsdp = lax.axis_size("fsdp")

    def pick(array):
        return jax.vmap(lambda rows, at: rows[at])(array, chosen)

    small = jnp.concatenate([router[:, None], gains], axis=1)
    small_all = gather_rows(small)
    qkv_all = gather_rows(w_qkv)
    out_all = gather_rows(w_out)
    up_all = gather_rows(w_up)
    down_all = gather_rows(w_down)
    router_float = small_all[:, 0].astype(jnp.float32)
    gain_one = small_all[:, 1].astype(jnp.float32)
    gain_two = small_all[:, 2].astype(jnp.float32)

    routed = pick(tokens).reshape(row_count, model_width)
    hidden = routed.astype(jnp.float32)
    gate_rate = jax.nn.sigmoid(
        jnp.dot(routed, small_all[:, 0], preferred_element_type=jnp.float32)
    )
    normed = plain_norm(hidden, gain_one).astype(jnp.bfloat16)
    projected = jnp.dot(normed, qkv_all, preferred_element_type=jnp.float32).astype(jnp.bfloat16)
    queries = projected[:, :model_width].reshape(micro_count, slot_count, HEADS, head_dim)
    own_path = pick(path)
    own_place = offset + chosen
    key_info = jnp.concatenate([own_path[:, :, :1], own_place[:, :, None]], axis=2)
    gathered = lax.all_gather(
        projected[:, model_width:].reshape(micro_count, slot_count, 2 * model_width), "fsdp"
    )
    info_all = lax.all_gather(key_info, "fsdp")
    key_count = fsdp * slot_count
    gathered = jnp.swapaxes(gathered, 0, 1).reshape(micro_count, key_count, 2, HEADS, head_dim)
    info_all = jnp.swapaxes(info_all, 0, 1).reshape(micro_count, key_count, 2)
    key_rows = gathered[:, :, 0]
    value_rows = gathered[:, :, 1]
    key_seg = info_all[:, None, :, 0]
    visible = (
        (key_seg == own_path[:, :, 0:1])
        | (key_seg == own_path[:, :, 1:2])
        | (key_seg == own_path[:, :, 2:3])
    ) & (info_all[:, None, :, 1] <= own_place[:, :, None])
    visible = visible[:, None]

    def product(form, left, right):
        return jnp.einsum(form, left, right, preferred_element_type=jnp.float32)

    scores = product("mqhd,mkhd->mhqk", queries, key_rows) * score_scale
    scores = jnp.where(visible, scores, -1e30)
    row_max = jnp.max(scores, axis=-1, keepdims=True)
    exponent = jnp.where(visible, jnp.exp(scores - row_max), 0.0)
    row_total = jnp.sum(exponent, axis=-1, keepdims=True)
    soft_prob = exponent / row_total
    probs = soft_prob.astype(jnp.bfloat16)
    attention = product("mhqk,mkhd->mqhd", probs, value_rows)
    attention = attention.reshape(row_count, model_width).astype(jnp.bfloat16)
    branch = jnp.dot(attention, out_all, preferred_element_type=jnp.float32)
    middle = hidden + branch
    normed_two = plain_norm(middle, gain_two).astype(jnp.bfloat16)
    up_proj = jnp.dot(normed_two, up_all, preferred_element_type=jnp.float32)
    activated = jax.nn.gelu(up_proj).astype(jnp.bfloat16)
    change = branch + jnp.dot(activated, down_all, preferred_element_type=jnp.float32)
    new_rows = hidden + gate_rate[:, None] * change

    def put(array, rows):
        rows = rows.reshape(micro_count, slot_count, model_width).astype(array.dtype)
        return jax.vmap(lambda whole, at, new: whole.at[at].set(new))(array, chosen, rows)

    mixed = put(tokens, new_rows)

    grad_rows = pick(cotangent).reshape(row_count, model_width).astype(jnp.float32)
    grad_change = gate_rate[:, None] * grad_rows
    grad_logit = jnp.sum(grad_rows * change, axis=-1) * gate_rate * (1.0 - gate_rate)
    grad_mlp = grad_change.astype(jnp.bfloat16)
    grad_down = scatter_sum(inner(activated, grad_mlp))
    grad_act = by_rows(grad_mlp, down_all)
    gelu_value, gelu_back = jax.vjp(jax.nn.gelu, up_proj)
    grad_up_proj = gelu_back(grad_act)[0].astype(jnp.bfloat16)
    grad_up = scatter_sum(inner(normed_two, grad_up_proj))
    grad_normed_two = by_rows(grad_up_proj, up_all)
    norm_value, norm_back_two = jax.vjp(plain_norm, middle, gain_two)
    grad_middle, grad_gain_two = norm_back_two(grad_normed_two)
    grad_branch = (grad_change + grad_middle).astype(jnp.bfloat16)
    grad_outw = scatter_sum(inner(attention, grad_branch))
    grad_attention = by_rows(grad_branch, out_all).astype(jnp.bfloat16)
    grad_heads = grad_attention.reshape(micro_count, slot_count, HEADS, head_dim)
    prob_grad = product("mqhd,mkhd->mhqk", grad_heads, value_rows)
    delta = jnp.sum(soft_prob * prob_grad, axis=-1, keepdims=True)
    grad_scores = (soft_prob * (prob_grad - delta)).astype(jnp.bfloat16)
    grad_query = product("mhqk,mkhd->mqhd", grad_scores, key_rows) * score_scale
    grad_key = product("mhqk,mqhd->mkhd", grad_scores, queries) * score_scale
    grad_value = product("mhqk,mqhd->mkhd", probs, grad_heads)
    grad_kv = jnp.stack([grad_key, grad_value], axis=2).reshape(
        micro_count, fsdp, slot_count, 2 * model_width
    )
    grad_kv = lax.psum_scatter(
        jnp.swapaxes(grad_kv, 0, 1).astype(jnp.bfloat16).reshape(-1, 2 * model_width),
        "fsdp",
        scatter_dimension=0,
        tiled=True,
    )
    grad_projected = jnp.concatenate(
        [
            grad_query.reshape(row_count, model_width).astype(jnp.bfloat16),
            grad_kv.reshape(row_count, 2 * model_width),
        ],
        axis=1,
    )
    grad_qkvw = scatter_sum(inner(normed, grad_projected))
    grad_normed = by_rows(grad_projected, qkv_all)
    norm_value_one, norm_back_one = jax.vjp(plain_norm, hidden, gain_one)
    grad_hidden_norm, grad_gain_one = norm_back_one(grad_normed)
    grad_hidden = (
        grad_rows + grad_middle + grad_hidden_norm + grad_logit[:, None] * router_float[None, :]
    )
    grad_tokens = put(cotangent.astype(jnp.float32), grad_hidden)
    grad_routerw = jnp.sum(grad_logit[:, None] * hidden, axis=0)
    grad_small = jnp.stack([grad_routerw, grad_gain_one, grad_gain_two], axis=1)
    grad_small = lax.psum_scatter(grad_small, "fsdp", scatter_dimension=0, tiled=True)
    summed = lax.psum((grad_small, grad_qkvw, grad_outw, grad_up, grad_down), "rep")
    return (mixed, grad_tokens, summed[0][:, 0], summed[0][:, 1:]) + tuple(summed[1:])


def solution(mesh):
    rows = P(None, ("rep", "fsdp"), None)
    weight = P("fsdp", None)

    def whole(*args):
        grouped = fits(mesh, args[0], args[3], args[8])
        return jax.shard_map(
            group_shards if grouped else plain_shards,
            mesh=mesh,
            in_specs=(
                rows,
                rows,
                rows,
                P(None, ("rep", "fsdp")),
                P("fsdp"),
                weight,
                weight,
                weight,
                weight,
                weight,
            ),
            out_specs=(rows, rows, P("fsdp"), weight, weight, weight, weight, weight),
            check_vma=False,
        )(*args)

    return whole
```

```python
import functools
import math
import types

import jax
import jax.numpy as jnp
from jax import lax
from jax.experimental import pallas as pl
from jax.experimental.pallas import tpu as pltpu
from jax.sharding import PartitionSpec as P

HEADS = 16


eps = 1e-05
MESH = pl.DeviceIdType.MESH
BF = jnp.bfloat16
F32 = jnp.float32
GELU_A = math.sqrt(2.0 / math.pi)
GELU_B = 0.044715


def dot(left, right, contract):
    return lax.dot_general(
        left, right, (((contract[0],), (contract[1],)), ((), ())), preferred_element_type=F32
    )


def aligned(index, size):
    return pl.ds(pl.multiple_of(index * size, size), size)


def loop(count, body):
    def step(index, carry):
        body(index)
        return carry

    lax.fori_loop(0, count, step, 0)


def fits(mesh, tokens, chosen, w_up):
    rep, fsdp = mesh.shape["rep"], mesh.shape["fsdp"]
    micro, width, hidden = tokens.shape[0], tokens.shape[2], w_up.shape[1]
    if fsdp % micro or rep % 2:
        return False
    inner_count = fsdp // micro
    return (
        rep % inner_count == 0
        and rep == micro
        and fsdp == rep * inner_count
        and width == fsdp * 128
        and hidden == fsdp * rep * 128
        and HEADS % (2 * rep) == 0
        and width // HEADS == 64
        and chosen.shape[1] // (rep * fsdp) == 64
        and rep == 4
        and hidden == rep * width
        and tokens.shape[1] * micro // (rep * fsdp) == 2 * rep * micro * 64
    )


def scratch_shapes(g):
    own, rows, d, piece = g.own, g.rows, g.d, g.d // g.F

    def vmem(height, width, kind=BF):
        return pltpu.VMEM((height, width), kind)

    def dma(*shape):
        return pltpu.SemaphoreType.DMA(shape)

    def shared():
        return dict(xs=dma(g.X - 1), xr=dma(g.X - 1), ss=dma(g.X), sr=dma(g.X))

    def halves():
        return [shared(), shared()]

    def direct():
        return dict(l=dma(1), os=dma(g.A - 1), ors=dma(g.A - 1), ins=dma(g.A), inr=dma(g.A))

    def chained():
        ends = dict(ups=dma(g.A - 1), upr=dma(g.A - 1), dns=dma(g.A - 1), dnr=dma(g.A - 1))
        return dict(l=dma(g.F), ins=dma(2 * g.A - 1), inr=dma(2 * g.A - 1), **ends)

    def pieces(count, cols, kind, height, full):
        made = dict(
            inbox=vmem(count // g.S * height, cols, kind),
            outbox=vmem(g.A * height, cols, kind),
            ins=dma(g.A),
            inr=dma(g.A),
            os=dma(g.A),
            ors=dma(g.A),
        )
        if full:
            made.update(grad=vmem(count * height, cols), share=shared(), out=dma(g.R))
            made.update(whole=vmem(full * height, cols))
        return made

    return dict(
        hid=vmem(own, d),
        ct=vmem(own, d),
        infos=vmem(g.R * g.MB * 8, 128, F32),
        sm=vmem(g.F * 8, 128, F32),
        info=pltpu.VMEM((g.MB, 8, 128), F32),
        vec=vmem(8, d, F32),
        wqa=vmem(d, g.qc),
        woa=vmem(g.ac, d),
        wua=vmem(d, g.fc),
        wda=vmem(g.fc, d),
        normed=vmem(rows, d),
        norm2=vmem(rows, d),
        proj=vmem(rows, g.qc),
        att=vmem(rows, g.ac),
        gatt=vmem(rows, g.ac),
        gproj=vmem(rows, g.qc),
        lse=vmem(rows, 128, F32),
        bias=vmem(g.tree, g.tree, F32),
        pair_a=vmem(2 * rows, g.fc),
        pair_b=vmem(2 * rows, d),
        dact=vmem(rows, g.fc, F32),
        gate=vmem(own, 128, F32),
        branch=vmem(own, d, F32),
        gmid=vmem(own, d, F32),
        ends=vmem(2 * own, d),
        to_sib=pltpu.VMEM((2, g.X * own, d), BF),
        of_sib=pltpu.VMEM((2, g.X * own, d), BF),
        to_x=pltpu.VMEM((2, (g.X - 1) * own, d), BF),
        of_x=pltpu.VMEM((2, (g.X - 1) * own, d), BF),
        gsum=vmem(8, d, F32),
        gsp=vmem(g.F * 8, 128, F32),
        gs_pair=pltpu.VMEM((2, 8, 128), F32),
        gs_mine=pltpu.VMEM((2, 8, 128), F32),
        a2a_s=dma(5, g.MB),
        a2a_r=dma(5, g.MB),
        tok_l=dma(2, g.MB),
        pair_s=dma(2),
        pair_r=dma(2),
        small_t=direct(),
        wo_t=direct(),
        wq_t=chained(),
        wu_t=chained(),
        wd_t=chained(),
        info_t=shared(),
        normed_t=halves(),
        gmlp_t=halves(),
        norm2_t=halves(),
        gbr_t=halves(),
        sums=[halves() for _ in range(4)],
        q=pieces(g.F, g.qc, BF, piece, g.R),
        u=pieces(g.F, g.fc, BF, piece, g.R),
        d=pieces(g.F, d, BF, piece, g.R),
        o=pieces(g.S, d, BF, piece, 1),
        s=pieces(g.F, 128, F32, 8, 0),
    )


def spaces(tree):
    if isinstance(tree, dict):
        return types.SimpleNamespace(**{name: spaces(value) for name, value in tree.items()})
    return [spaces(value) for value in tree] if isinstance(tree, list) else tree


def block_kernel(g, order, form, *refs):
    split = len(order)
    n = spaces(dict(zip(order, refs[:split]), **jax.tree.unflatten(form, refs[split:])))
    R, F, S, A, X, MB = g.R, g.F, g.S, g.A, g.X, g.MB
    own, rows, d, cap = g.own, g.rows, g.d, g.cap
    piece = d // F
    r = lax.axis_index("rep")
    f = lax.axis_index("fsdp")
    x, c = r // 2, lax.rem(r, 2)
    a, b = f // S, lax.rem(f, S)
    other_b = lax.rem(b + 1, S)
    sib = x * 2 + 1 - c
    pending = {}
    n.act, n.gup = n.pair_a.at[pl.ds(0, rows)], n.pair_a.at[pl.ds(rows, rows)]
    n.gmlp, n.gbr = n.pair_b.at[pl.ds(0, rows)], n.pair_b.at[pl.ds(rows, rows)]
    n.nrow, n.grow = n.ends.at[pl.ds(0, own)], n.ends.at[pl.ds(own, own)]
    n.picked, n.picked_ct = n.ends, n.norm2
    n.acc, n.gfirst = n.dact.at[pl.ds(0, own)], n.dact.at[pl.ds(own, own)]
    tok_count = n.tokens.shape[1]

    def token_copy(which, m):
        source, target = (n.tokens, n.pair_a) if which == 0 else (n.cotangent, n.pair_b)
        return pltpu.make_async_copy(
            source.at[m], target.at[pl.ds(m * tok_count, tok_count)], n.tok_l.at[which, m]
        )

    def cut_qkv():
        return [
            pltpu.make_async_copy(
                n.w_qkv.at[:, pl.ds(pl.multiple_of(part * d + r * g.ac, g.ac), g.ac)],
                n.wqa.at[aligned(f, piece), pl.ds(part * g.ac, g.ac)],
                n.wq_t.l.at[part],
            )
            for part in range(3)
        ]

    def cut_up():
        return [
            pltpu.make_async_copy(
                n.w_up.at[:, pl.ds(pl.multiple_of((block * R + r) * 128, 128), 128)],
                n.wua.at[aligned(f, piece), pl.ds(block * 128, 128)],
                n.wu_t.l.at[block],
            )
            for block in range(F)
        ]

    def cut_down():
        return [
            pltpu.make_async_copy(
                n.w_down.at[aligned(r, piece)], n.wda.at[aligned(f, piece)], n.wd_t.l.at[0]
            )
        ]

    for copy in cut_qkv():
        copy.start()
    for which in range(2):
        for m in range(MB):
            token_copy(which, m).start()
    for cut in (cut_up, cut_down):
        for copy in cut():
            copy.start()

    def remote(src, dst, ss, rs, rep, fsdp):
        return pltpu.make_async_remote_copy(
            src_ref=src,
            dst_ref=dst,
            send_sem=ss,
            recv_sem=rs,
            device_id={"rep": rep, "fsdp": fsdp},
            device_id_type=MESH,
        )

    def send(src, dst, ss, rs, rep, fsdp, cond=None, tag=None):
        def start():
            remote(src, dst, ss, rs, rep, fsdp).start()

        def done():
            remote(src, dst, ss, rs, rep, fsdp).wait_send()

        if cond is None:
            start()
            pending.setdefault(tag, []).append(done)
        else:
            pl.when(cond)(start)
            pending.setdefault(tag, []).append(lambda: pl.when(cond)(done))

    def drain(tag):
        for done in pending.pop(tag, []):
            done()

    def got(dst, rs):
        remote(dst, dst, rs, rs, sib, f).wait_recv()

    def xpeer(step):
        return lax.rem(x + 1 + step, X)

    def xfrom(step):
        return lax.rem(x + X - 1 - step, X)

    def outer(step):
        return lax.rem(a + step, A)

    def outer_from(step):
        return lax.rem(a + A - step, A)

    home_rep = (r // S) * S + b

    def home_fsdp(m):
        return m * S + lax.rem(r, S)

    barrier = pltpu.get_barrier_semaphore()

    def greet(rep, fsdp):
        pl.semaphore_signal(
            barrier, inc=1, device_id={"rep": rep, "fsdp": fsdp}, device_id_type=MESH
        )

    for step in range(1, A):
        greet(r, outer(step) * S + b)
    greet(r, a * S + other_b)
    greet(sib, f)
    for step in range(X - 1):
        greet(xpeer(step) * 2 + c, f)
    mine = [(home_fsdp(m) == f) & (home_rep == r) for m in range(MB)]
    for m in range(MB):

        @pl.when(jnp.logical_not(mine[m]))
        def _(m=m):
            greet(home_rep, home_fsdp(m))

    stays = (home_rep == r) & (lax.rem(r, S) == b)
    pl.semaphore_wait(barrier, (A - 1) + 1 + 1 + (X - 1) + MB - stays.astype(jnp.int32))

    def swap_start(which, src_of, dst_of):
        for m in range(MB):
            src, dst = src_of(m), dst_of(a)
            ss, rs = n.a2a_s.at[which, m], n.a2a_r.at[which, a]

            @pl.when(jnp.logical_not(mine[m]))
            def _():
                remote(src, dst, ss, rs, home_rep, home_fsdp(m)).start()

            @pl.when(mine[m])
            def _():
                pltpu.make_async_copy(src, dst, rs).start()

    def swap_end(which, src_of, dst_of):
        for m in range(MB):
            src, dst = src_of(m), dst_of(m)
            ss, rs = n.a2a_s.at[which, m], n.a2a_r.at[which, m]

            @pl.when(jnp.logical_not(mine[m]))
            def _():
                remote(src, dst, ss, rs, home_rep, home_fsdp(m)).wait()

            @pl.when(mine[m])
            def _():
                pltpu.make_async_copy(src, dst, rs).wait()

    def gather_start(t, buf, height):
        at = aligned(f, height)
        src = buf.at[at]
        for step in range(1, A):
            send(
                src,
                buf.at[at],
                t.os.at[step - 1],
                t.ors.at[step - 1],
                r,
                outer(step) * S + b,
            )
        send(src, buf.at[at], t.ins.at[0], t.inr.at[0], r, a * S + other_b)

    def gather_forward(t, buf, height):
        for step in range(1, A):
            at = buf.at[aligned(outer_from(step) * S + b, height)]
            got(at, t.ors.at[step - 1])
            send(at, at, t.ins.at[step], t.inr.at[step], r, a * S + other_b)

    def gather_end(t, buf, height):
        for step in range(A):
            at = buf.at[aligned(outer_from(step) * S + other_b, height)]
            got(at, t.inr.at[step])

    def hop(step):
        return lax.rem(a + A + step, A)

    def chain_start(t, buf, height):
        at = buf.at[aligned(f, height)]
        send(at, at, t.ups.at[0], t.upr.at[0], r, hop(1) * S + b, a < A - 1)
        send(at, at, t.dns.at[0], t.dnr.at[0], r, hop(-1) * S + b, a > 0)

    def chain_across(t, buf, height):
        at = buf.at[aligned(f, height)]
        send(at, at, t.ins.at[0], t.inr.at[0], r, a * S + other_b)

    def chain_forward(t, buf, height, step):
        for sends, takes, has, on, to, index in (
            (t.ups, t.upr, a >= step, a < A - 1, 1, step),
            (t.dns, t.dnr, a + step < A, a > 0, -1, A - 1 + step),
        ):
            at = buf.at[aligned(hop(-to * step) * S + b, height)]

            @pl.when(has)
            def _():
                got(at, takes.at[step - 1])

            if step < A - 1:
                send(
                    at,
                    at,
                    sends.at[step],
                    takes.at[step],
                    r,
                    hop(to) * S + b,
                    has & on,
                )
            send(
                at,
                at,
                t.ins.at[index],
                t.inr.at[index],
                r,
                a * S + other_b,
                has,
            )

    def chain_end(t, buf, height):
        got(buf.at[aligned(a * S + other_b, height)], t.inr.at[0])
        for step in range(1, A):
            for has, to, index in ((a >= step, 1, step), (a + step < A, -1, A - 1 + step)):
                at = buf.at[aligned(hop(-to * step) * S + other_b, height)]

                @pl.when(has)
                def _():
                    got(at, t.inr.at[index])

    is_source = a == r

    def out_start(src, buf):
        at = buf.at[aligned(b, piece)]

        @pl.when(is_source)
        def _():
            pltpu.make_async_copy(src, at, n.wo_t.l.at[0]).start()

        for step in range(1, A):
            send(
                src, at, n.wo_t.os.at[step - 1], n.wo_t.ors.at[0], r, outer(step) * S + b, is_source
            )
        send(src, at, n.wo_t.ins.at[0], n.wo_t.inr.at[0], r, a * S + other_b, is_source)

    def out_forward(buf):
        at = buf.at[aligned(b, piece)]

        @pl.when(jnp.logical_not(is_source))
        def _():
            got(at, n.wo_t.ors.at[0])

        send(
            at, at, n.wo_t.ins.at[1], n.wo_t.inr.at[0], r, a * S + other_b, jnp.logical_not(is_source)
        )

    def out_end(src, buf):
        @pl.when(is_source)
        def _():
            pltpu.make_async_copy(src, buf.at[aligned(b, piece)], n.wo_t.l.at[0]).wait()

        got(buf.at[aligned(other_b, piece)], n.wo_t.inr.at[0])

    def part_of(block, height, part):
        if part is None:
            return aligned(block, height)
        half = height // 2
        return pl.ds(pl.multiple_of(block * height + part * half, half), half)

    def share_start(t, buf, height, part=None):
        at = buf.at[part_of(r, height, part)]
        for step in range(X - 1):
            send(at, at, t.xs.at[step], t.xr.at[step], xpeer(step) * 2 + c, f)
        send(at, at, t.ss.at[0], t.sr.at[0], sib, f)

    def share_forward(t, buf, height, part=None):
        for step in range(X - 1):
            at = buf.at[part_of(xfrom(step) * 2 + c, height, part)]
            got(at, t.xr.at[step])
            send(at, at, t.ss.at[1 + step], t.sr.at[1 + step], sib, f)

    def share_near(t, buf, height, part=None):
        got(buf.at[part_of(sib, height, part)], t.sr.at[0])

    def share_far(t, buf, height, part=None):
        for step in range(X - 1):
            at = buf.at[part_of(xfrom(step) * 2 + 1 - c, height, part)]
            got(at, t.sr.at[1 + step])

    def share_end(t, buf, height):
        share_near(t, buf, height)
        share_far(t, buf, height)

    def rows_do(what, t, buf):
        what(t[0], buf, own)

    wide = 256

    def sum_owner(step):
        return xpeer(step) if step < X - 1 else x

    half_tiles = d // wide // 2

    def sum_near(index, slot, partial, step):
        to_sib, at = n.to_sib.at[slot], pl.ds(step * own, own)
        owner = sum_owner(step) * 2 + 1 - c
        if step == 0:
            drain(slot)
        for part in range(2):
            t, across = n.sums[index][part], pl.ds(part * d // 2, d // 2)

            def one(tile, part=part):
                cols = aligned(part * half_tiles + tile, wide)
                to_sib[at, cols] = partial(owner, cols).astype(BF)

            loop(half_tiles, one)
            send(
                to_sib.at[at, across],
                n.of_sib.at[slot, at, across],
                t.ss.at[step],
                t.sr.at[step],
                sib,
                f,
                tag=slot,
            )

    def sum_mine(index, slot, partial, step, acc, post=True):
        of_sib, to_x, at = n.of_sib.at[slot], n.to_x.at[slot], pl.ds(step * own, own)
        owner = sum_owner(step) * 2 + c
        last = step == X - 1
        for part in range(2):
            t, across = n.sums[index][part], pl.ds(part * d // 2, d // 2)
            got(of_sib.at[at, across], t.sr.at[step])

            def one(tile, part=part):
                cols = aligned(part * half_tiles + tile, wide)
                total = partial(owner, cols) + of_sib[at, cols].astype(F32)
                if last:
                    acc[:, cols] = total
                else:
                    to_x[at, cols] = total.astype(BF)

            loop(half_tiles, one)
            if not last and post:
                sum_post(index, slot, step, part)

    def sum_post(index, slot, step, part):
        at, across = pl.ds(step * own, own), pl.ds(part * d // 2, d // 2)
        t = n.sums[index][part]
        send(
            n.to_x.at[slot, at, across],
            n.of_x.at[slot, at, across],
            t.xs.at[step],
            t.xr.at[step],
            sum_owner(step) * 2 + c,
            f,
            tag=slot,
        )

    def sum_end(index, slot):
        of_x = n.of_x.at[slot]
        for step in range(X - 1):
            for part in range(2):
                across = pl.ds(part * d // 2, d // 2)
                got(of_x.at[pl.ds(step * own, own), across], n.sums[index][part].xr.at[step])

    def came(slot, at):
        total = None
        for step in range(X - 1):
            part = n.of_x[slot, pl.ds(step * own + at, tall), :].astype(F32)
            total = part if total is None else total + part
        return total

    tall = 32

    def by_own(body):
        def one(index):
            at = pl.multiple_of(index * tall, tall)
            body(at, pl.ds(at, tall))

        loop(own // tall, one)

    def grad_start(t, buf, height):
        out = t is n.o
        inbox = t.inbox
        for step in range(1 if out else A):
            to_a = r if out else outer(step + 1)
            src = buf.at[aligned((0 if out else to_a * S) + other_b, height)]
            send(
                src,
                inbox.at[pl.ds(step * height, height)],
                t.ins.at[step],
                t.inr.at[step],
                r,
                a * S + other_b,
            )

    def add_into(dst, base, inbox, start, height):
        small = min(height, 32)

        def one(index):
            at = pl.ds(pl.multiple_of(base + index * small, small), small)
            of = pl.ds(pl.multiple_of(start + index * small, small), small)
            dst[at, :] = (dst[at, :].astype(F32) + inbox[of, :].astype(F32)).astype(dst.dtype)

        loop(height // small, one)

    def grad_forward(t, buf, height):
        out = t is n.o
        inbox, outbox = t.inbox, t.outbox
        for step in range(1 if out else A):
            to_a = r if out else outer(step + 1)
            base = ((0 if out else to_a * S) + b) * height
            got(inbox.at[pl.ds(step * height, height)], t.inr.at[step])
            add_into(buf, base, inbox, step * height, height)
            if out:
                slot = lax.rem(r + A - a - 1, A)
                slot = jnp.where(is_source, 0, slot)
                send(
                    buf.at[pl.ds(pl.multiple_of(base, height), height)],
                    outbox.at[aligned(slot, height)],
                    n.o.os.at[0],
                    n.o.ors.at[slot],
                    r,
                    r * S + b,
                    jnp.logical_not(is_source),
                )
            elif step < A - 1:
                send(
                    buf.at[pl.ds(pl.multiple_of(base, height), height)],
                    outbox.at[pl.ds(step * height, height)],
                    t.os.at[step],
                    t.ors.at[step],
                    r,
                    to_a * S + b,
                )

    def grad_wait(t, height):
        for step in range(A - 1):
            got(
                t.outbox.at[pl.ds(step * height, height)],
                t.ors.at[step],
            )

    def grad_total(t, buf, base, height, target, target_base, boxes):
        outbox = t.outbox
        small = min(height, 32)

        def one(index):
            off = index * small
            total = buf[pl.ds(pl.multiple_of(base + off, small), small), :].astype(F32)
            for box in boxes:
                at = pl.ds(pl.multiple_of(box * height + off, small), small)
                total = total + outbox[at, :].astype(F32)
            at = pl.ds(pl.multiple_of(target_base + off, small), small)
            target[at, :] = total.astype(target.dtype)

        loop(height // small, one)

    side = a // 2
    mate = a + 1 - 2 * lax.rem(a, 2)
    is_end = (a == 0) | (a == A - 1)
    passes_on = jnp.logical_not(is_end)
    piece_owner = (2 - side, 3 * (1 - side), mate, a)

    def piece_start(t, step):
        height, inbox = piece, t.inbox
        send(
            t.grad.at[aligned(piece_owner[step] * S + other_b, height)],
            inbox.at[pl.ds(step * height, height)],
            t.ins.at[step],
            t.inr.at[step],
            r,
            a * S + other_b,
        )

    def piece_take(t, step):
        buf, inbox, outbox = t.grad, t.inbox, t.outbox
        base = (piece_owner[step] * S + b) * piece
        got(inbox.at[pl.ds(step * piece, piece)], t.inr.at[step])
        add_into(buf, base, inbox, step * piece, piece)
        if step < 3:
            send(
                buf.at[pl.ds(pl.multiple_of(base, piece), piece)],
                outbox.at[pl.ds(step * piece, piece)],
                t.os.at[step],
                t.ors.at[step],
                r,
                mate * S + b,
                is_end if step < 2 else None,
            )

    def piece_pass(t, step):
        buf, outbox = t.grad, t.outbox
        base = (piece_owner[step] * S + b) * piece

        @pl.when(passes_on)
        def _():
            got(outbox.at[pl.ds(step * piece, piece)], t.ors.at[step])
            add_into(buf, base, outbox, step * piece, piece)

        send(
            buf.at[pl.ds(pl.multiple_of(base, piece), piece)],
            outbox.at[pl.ds(3 * piece, piece)],
            t.os.at[step],
            t.ors.at[3],
            r,
            piece_owner[step] * S + b,
            passes_on,
        )

    def piece_own(t):
        for box in (2, 3):
            got(
                t.outbox.at[pl.ds(box * piece, piece)], t.ors.at[box]
            )
        grad_total(t, t.grad, f * piece, piece, t.whole, r * piece, (2, 3))
        share_start(t.share, t.whole, piece)

    def hid_at(i):
        return n.hid.at[aligned(i, cap)]

    def ct_at(i):
        return n.ct.at[aligned(i, cap)]

    def info_src(i):
        return n.info.at[i]

    def info_own(i):
        return n.infos.at[aligned(r * MB + i, 8)]

    def info_home(i):
        return n.infos.at[aligned(home_rep * MB + i, 8)]

    odd = lax.rem(a, 2)
    lane_token = lax.broadcasted_iota(jnp.int32, (tok_count, 128), 0)
    lane = lax.broadcasted_iota(jnp.int32, (1, 128), 1)
    lane_used = (lane // cap) == odd
    def at_of(m):
        row = n.chosen[m : m + 1, :]
        return jnp.where(lane_used, jnp.concatenate([row, row], axis=1), -1)

    def hot_of(m):
        return (lane_token == at_of(m)).astype(F32).astype(BF)

    def tok_at(m):
        return n.picked.at[pl.ds(pl.multiple_of(m * 128 + odd * cap, cap), cap)]

    def cot_at(m):
        return n.picked_ct.at[pl.ds(pl.multiple_of(m * 128 + odd * cap, cap), cap)]

    mine_sm = pl.ds(pl.multiple_of(f * 8, 8), 8)
    def first_norm(at, rows_at):
        h = n.hid[rows_at, :].astype(F32)
        scale = lax.rsqrt(jnp.mean(h * h, axis=-1, keepdims=True) + eps)
        n.normed[pl.ds(pl.multiple_of(r * own + at, tall), tall), :] = (
            h * scale * n.vec[1:2, :]
        ).astype(BF)
        logit = jnp.sum(h * n.vec[0:1, :], axis=-1, keepdims=True)
        n.gate[rows_at, :] = jnp.broadcast_to(1.0 / (1.0 + jnp.exp(-logit)), (tall, 128))

    def mlp_cotangent(at, rows_at):
        gc = n.gate[rows_at, 0:1] * n.ct[rows_at, :].astype(F32)
        n.gmlp[pl.ds(pl.multiple_of(r * own + at, tall), tall), :] = gc.astype(BF)

    far = xpeer(0)
    near_blocks, far_blocks = (r, sib), (far * 2 + c, far * 2 + 1 - c)
    def project(block):
        at = aligned(block, own)
        half = g.qc // 3

        def one(part):
            cols = aligned(part, half)
            n.proj[at, cols] = dot(n.normed[at, :], n.wqa[:, cols], (1, 0)).astype(BF)

        loop(3, one)

    tree, pairs = g.tree, g.heads // 2
    scale = 64 ** (-0.5)
    low_lane = lax.broadcasted_iota(jnp.int32, (tree, 128), 1) < 64
    def half_of(value, half):
        keep = low_lane if half == 0 else jnp.logical_not(low_lane)
        return jnp.where(keep, value, jnp.zeros_like(value))

    def join(first, second):
        return jnp.where(low_lane, first, second)

    def make_bias(t):
        blocks = []
        for index in range(S * MB // 2):
            at = pl.multiple_of((t * S * MB + index * 2) * 8, 8)
            blocks.append(n.infos[pl.ds(at, 8), :] + n.infos[pl.ds(at + 8, 8), :])
        keys = jnp.concatenate(blocks, axis=1)
        asked = jnp.transpose(keys)
        near = keys[0:1, :] == asked[:, 0:1]
        near = near | (keys[0:1, :] == asked[:, 1:2])
        near = near | (keys[0:1, :] == asked[:, 2:3])
        near = near & (keys[3:4, :] <= asked[:, 3:4])
        n.bias[...] = jnp.where(near, 0.0, -1e30)

    def columns(part, pair):
        return pl.ds(part * g.ac + pair * 128, 128)

    def attend(t):
        make_bias(t)
        at = aligned(t, tree)
        for pair in range(pairs):
            q = n.proj[at, columns(0, pair)]
            k = n.proj[at, columns(1, pair)]
            v = n.proj[at, columns(2, pair)]
            made = []
            for half in range(2):
                s = dot(half_of(q, half), k, (1, 1)) * scale + n.bias[...]
                top = jnp.max(s, axis=-1, keepdims=True)
                e = jnp.exp(s - top)
                total = jnp.sum(e, axis=-1, keepdims=True)
                made.append(dot((e * (1.0 / total)).astype(BF), v, (1, 0)))
                head = pair * 2 + half
                n.lse[at, head : head + 1] = top + jnp.log(total)
            n.att[at, pl.ds(pair * 128, 128)] = join(*made).astype(BF)

    def branch_part(owner, cols):
        return dot(n.att[aligned(owner, own), :], n.woa[:, cols], (1, 0))

    def second_norm(at, rows_at):
        br = n.branch[rows_at, :] + came(0, at)
        n.branch[rows_at, :] = br
        mid = n.hid[rows_at, :].astype(F32) + br
        inv = lax.rsqrt(jnp.mean(mid * mid, axis=-1, keepdims=True) + eps)
        n.norm2[pl.ds(pl.multiple_of(r * own + at, tall), tall), :] = (
            mid * inv * n.vec[2:3, :]
        ).astype(BF)

    tiles = g.fc // wide
    def mlp_up(block):
        at = aligned(block, own)

        def one(tile):
            cols = aligned(tile, wide)
            u = dot(n.norm2[at, :], n.wua[:, cols], (1, 0))
            square = u * u
            t = jnp.tanh(GELU_A * (u + GELU_B * square * u))
            n.act[at, cols] = (0.5 * u * (1.0 + t)).astype(BF)
            n.dact[at, cols] = 0.5 * (1.0 + t) + (0.5 * GELU_A) * u * (1.0 - t * t) * (
                1.0 + (3.0 * GELU_B) * square
            )

        loop(tiles, one)

    def mlp_back(block):
        at = aligned(block, own)

        def one(tile):
            cols = aligned(tile, wide)
            ga = dot(n.gmlp[at, :], n.wda[cols, :], (1, 1))
            n.gup[at, cols] = (ga * n.dact[at, cols]).astype(BF)

        loop(tiles, one)

    def norm2_part(owner, cols):
        return dot(n.gup[aligned(owner, own), :], n.wua[cols, :], (1, 1))

    def weight_grad(left, right, target, count):
        def one(index):
            cols = aligned(index, 256)
            target[cols, :] = dot(left[:, cols], right[...], (0, 0)).astype(BF)

        loop(count // 256, one)

    def second_back(at, rows_at):
        dy = n.gmid[rows_at, :] + came(1, at)
        mid = n.hid[rows_at, :].astype(F32) + n.branch[rows_at, :]
        inv = lax.rsqrt(jnp.mean(mid * mid, axis=-1, keepdims=True) + eps)
        n.gsum[2:3, :] = n.gsum[2:3, :] + jnp.sum(dy * mid * inv, axis=0, keepdims=True)
        t = dy * n.vec[2:3, :]
        along = jnp.sum(mid * t, axis=-1, keepdims=True) * (inv * inv * inv * (1.0 / d))
        gm = inv * t - mid * along
        n.gmid[rows_at, :] = gm
        gc = n.gate[rows_at, 0:1] * n.ct[rows_at, :].astype(F32)
        n.gbr[pl.ds(pl.multiple_of(r * own + at, tall), tall), :] = (gc + gm).astype(BF)

    def attention_cotangent(block):
        at = aligned(block, own)
        n.gatt[at, :] = dot(n.gbr[at, :], n.woa[...], (1, 1)).astype(BF)

    def attend_back(t):
        make_bias(t)
        at = aligned(t, tree)
        for pair in range(pairs):
            q = n.proj[at, columns(0, pair)]
            k = n.proj[at, columns(1, pair)]
            v = n.proj[at, columns(2, pair)]
            da = n.gatt[at, pl.ds(pair * 128, 128)]
            dq, dk, dv = [], [], []
            for half in range(2):
                head = pair * 2 + half
                s = dot(half_of(q, half), k, (1, 1)) * scale + n.bias[...]
                p = jnp.exp(s - n.lse[at, head : head + 1])
                dp = dot(half_of(da, half), v, (1, 1))
                delta = jnp.sum(p * dp, axis=-1, keepdims=True)
                ds = (p * (dp - delta)).astype(BF)
                dq.append(dot(ds, k, (1, 0)))
                dk.append(dot(ds, q, (0, 0)))
                dv.append(dot(p.astype(BF), da, (0, 0)))
            n.gproj[at, columns(0, pair)] = (join(*dq) * scale).astype(BF)
            n.gproj[at, columns(1, pair)] = (join(*dk) * scale).astype(BF)
            n.gproj[at, columns(2, pair)] = join(*dv).astype(BF)

    def change_part(owner, cols):
        return dot(n.act[aligned(owner, own), :], n.wda[:, cols], (1, 0))

    def normed_part(owner, cols):
        return dot(n.gproj[aligned(owner, own), :], n.wqa[cols, :], (1, 1))

    def new_rows(at, rows_at):
        change = n.branch[rows_at, :] + n.acc[rows_at, :] + came(0, at)
        h = n.hid[rows_at, :].astype(F32)
        gate = n.gate[rows_at, 0:1]
        n.nrow[rows_at, :] = (h + gate * change).astype(BF)
        logit = jnp.sum(n.ct[rows_at, :].astype(F32) * change, axis=-1, keepdims=True)
        logit = logit * gate * (1.0 - gate)
        n.gsum[0:1, :] = n.gsum[0:1, :] + jnp.sum(logit * h, axis=0, keepdims=True)
        n.gmid[rows_at, :] = n.gmid[rows_at, :] + logit * n.vec[0:1, :]

    def new_at(i):
        return n.nrow.at[aligned(i, cap)]

    def grow_at(i):
        return n.grow.at[aligned(i, cap)]

    def first_back(at, rows_at):
        dy = n.gfirst[rows_at, :] + came(1, at)
        h = n.hid[rows_at, :].astype(F32)
        inv = lax.rsqrt(jnp.mean(h * h, axis=-1, keepdims=True) + eps)
        n.gsum[1:2, :] = n.gsum[1:2, :] + jnp.sum(dy * h * inv, axis=0, keepdims=True)
        t = dy * n.vec[1:2, :]
        along = jnp.sum(h * t, axis=-1, keepdims=True) * (inv * inv * inv * (1.0 / d))
        total = n.ct[rows_at, :].astype(F32) + n.gmid[rows_at, :] + (inv * t - h * along)
        n.grow[rows_at, :] = total.astype(BF)

    ax, ac = a // 2, lax.rem(a, 2)
    off_x = (c == ac) & (x != ax)
    def out_copies(t, target):
        return [
            pltpu.make_async_copy(
                t.whole.at[pl.ds(index * piece, piece)], target.at[index], t.out.at[index]
            )
            for index in range(R)
        ]

    last = pltpu.make_async_copy(n.o.whole, n.ro_out, n.o.out.at[0])
    n.sm[mine_sm, :] = jnp.concatenate(
        [n.router[...].astype(F32), n.gains[...].astype(F32), jnp.zeros((5, 128), F32)], axis=0
    )
    gather_start(n.small_t, n.sm, 8)
    for copy in cut_qkv():
        copy.wait()
    chain_start(n.wq_t, n.wqa, piece)
    chain_across(n.wq_t, n.wqa, piece)
    for m in range(MB):
        hot = hot_of(m)
        token_copy(0, m).wait()
        n.picked[m * 128 : (m + 1) * 128, :] = dot(
            hot, n.pair_a[m * tok_count : (m + 1) * tok_count, :], (0, 0)
        ).astype(BF)
        lines = jnp.concatenate([n.path[line, m : m + 1, :] for line in range(3)], axis=0)
        n.info[m, 0:3, :] = dot(lines.astype(F32).astype(BF), hot, (1, 0))
        at = at_of(m)
        n.info[m, 3:4, :] = jnp.where(at >= 0, at + f * tok_count, 0).astype(F32)
        n.info[m, 4:8, :] = jnp.zeros((4, 128), F32)
    swap_start(0, tok_at, hid_at)
    for m in range(MB):
        ss, rs = n.a2a_s.at[1, m], n.a2a_r.at[1, a]

        @pl.when(jnp.logical_not(mine[m]))
        def _():
            remote(info_src(m), info_home(a), ss, rs, home_rep, home_fsdp(m)).start()

        @pl.when(mine[m])
        def _():
            pltpu.make_async_copy(info_src(m), info_own(a), rs).start()
    gather_forward(n.small_t, n.sm, 8)
    chain_forward(n.wq_t, n.wqa, piece, 1)
    for m in range(MB):
        token_copy(1, m).wait()
        n.picked_ct[m * 128 : (m + 1) * 128, :] = dot(
            hot_of(m), n.pair_b[m * tok_count : (m + 1) * tok_count, :], (0, 0)
        ).astype(BF)
    gather_end(n.small_t, n.sm, 8)
    for index in range(F):
        n.vec[:, index * 128 : (index + 1) * 128] = n.sm[index * 8 : (index + 1) * 8, :]
    swap_end(1, info_src, info_own)
    share_start(n.info_t, n.infos, MB * 8)
    swap_end(0, tok_at, hid_at)
    by_own(first_norm)
    rows_do(share_start, n.normed_t, n.normed)
    chain_forward(n.wq_t, n.wqa, piece, 2)
    swap_start(2, cot_at, ct_at)
    share_forward(n.info_t, n.infos, MB * 8)
    out_start(n.w_out, n.woa)
    rows_do(share_forward, n.normed_t, n.normed)
    chain_forward(n.wq_t, n.wqa, piece, 3)
    for copy in cut_up():
        copy.wait()
    chain_start(n.wu_t, n.wua, piece)
    chain_across(n.wu_t, n.wua, piece)
    for copy in cut_down():
        copy.wait()
    share_end(n.info_t, n.infos, MB * 8)
    rows_do(share_near, n.normed_t, n.normed)
    rows_do(share_far, n.normed_t, n.normed)
    chain_end(n.wq_t, n.wqa, piece)
    swap_end(2, cot_at, ct_at)
    by_own(mlp_cotangent)
    share_start(n.gmlp_t[0], n.gmlp, own)
    for block in far_blocks:
        project(block)
    out_forward(n.woa)
    chain_forward(n.wu_t, n.wua, piece, 1)
    chain_start(n.wd_t, n.wda, piece)
    chain_across(n.wd_t, n.wda, piece)
    attend(far)
    out_end(n.w_out, n.woa)
    sum_near(0, 0, branch_part, 0)
    for block in near_blocks:
        project(block)
    sum_mine(0, 0, branch_part, 0, n.branch)
    chain_forward(n.wu_t, n.wua, piece, 2)
    chain_forward(n.wd_t, n.wda, piece, 1)
    attend(x)
    sum_near(0, 0, branch_part, 1)
    chain_forward(n.wu_t, n.wua, piece, 3)
    sum_mine(0, 0, branch_part, 1, n.branch)
    chain_forward(n.wd_t, n.wda, piece, 2)
    share_forward(n.gmlp_t[0], n.gmlp, own)
    sum_end(0, 0)
    by_own(second_norm)
    rows_do(share_start, n.norm2_t, n.norm2)
    chain_end(n.wu_t, n.wua, piece)
    chain_forward(n.wd_t, n.wda, piece, 3)
    mlp_up(r)
    rows_do(share_near, n.norm2_t, n.norm2)
    mlp_up(sib)
    rows_do(share_forward, n.norm2_t, n.norm2)
    mlp_up(far_blocks[0])
    rows_do(share_far, n.norm2_t, n.norm2)
    mlp_up(far_blocks[1])
    rows_do(share_near, n.gmlp_t, n.gmlp)
    rows_do(share_far, n.gmlp_t, n.gmlp)
    weight_grad(n.act, n.gmlp, n.d.grad, g.fc)
    piece_start(n.d, 1)
    chain_end(n.wd_t, n.wda, piece)
    mlp_back(far_blocks[1])
    sum_near(1, 1, norm2_part, 0)
    mlp_back(far_blocks[0])
    sum_mine(1, 1, norm2_part, 0, n.gmid)
    mlp_back(sib)
    piece_start(n.d, 0)
    sum_near(1, 1, norm2_part, 1)
    mlp_back(r)
    sum_mine(1, 1, norm2_part, 1, n.gmid)
    piece_start(n.d, 2)
    weight_grad(n.norm2, n.gup, n.u.grad, d)
    piece_take(n.d, 0)
    n.gsum[...] = jnp.zeros_like(n.gsum)
    sum_end(1, 1)
    by_own(second_back)
    rows_do(share_start, n.gbr_t, n.gbr)
    piece_start(n.d, 3)
    piece_start(n.u, 0)
    piece_take(n.d, 1)
    attention_cotangent(r)
    sum_near(2, 0, change_part, 0)
    rows_do(share_near, n.gbr_t, n.gbr)
    attention_cotangent(sib)
    attend_back(x)
    piece_start(n.u, 1)
    sum_near(2, 0, change_part, 1)
    sum_mine(2, 0, change_part, 0, n.acc, False)
    piece_take(n.d, 2)
    for part in range(2):
        sum_post(2, 0, 0, part)
    piece_pass(n.d, 0)
    rows_do(share_forward, n.gbr_t, n.gbr)
    piece_take(n.d, 3)
    piece_take(n.u, 0)
    piece_pass(n.d, 1)
    attention_cotangent(far_blocks[0])
    rows_do(share_far, n.gbr_t, n.gbr)
    attention_cotangent(far_blocks[1])
    weight_grad(n.att, n.gbr, n.o.grad, g.ac)
    grad_start(n.o, n.o.grad, piece)
    attend_back(far)
    piece_take(n.u, 1)
    sum_near(3, 1, normed_part, 0)
    piece_pass(n.u, 0)
    piece_start(n.u, 2)
    sum_mine(2, 0, change_part, 1, n.acc)
    piece_start(n.u, 3)
    piece_take(n.u, 2)
    sum_mine(3, 1, normed_part, 0, n.gfirst)
    sum_near(3, 1, normed_part, 1)
    sum_end(2, 0)
    by_own(new_rows)
    swap_start(4, new_at, lambda m: n.new_out.at[m])
    grad_forward(n.o, n.o.grad, piece)
    weight_grad(n.normed, n.gproj, n.q.grad, d)
    piece_start(n.q, 1)
    piece_start(n.q, 3)
    piece_take(n.q, 1)
    sum_mine(3, 1, normed_part, 1, n.gfirst)
    piece_pass(n.u, 1)
    piece_start(n.q, 0)
    piece_take(n.q, 3)
    piece_start(n.q, 2)
    piece_own(n.d)
    sum_end(3, 1)
    by_own(first_back)
    swap_start(3, grow_at, lambda m: n.grad_out.at[m])
    piece_take(n.u, 3)
    piece_pass(n.q, 1)
    for index in range(F):
        n.gsp[index * 8 : (index + 1) * 8, :] = n.gsum[:, index * 128 : (index + 1) * 128]
    piece_take(n.q, 2)
    @pl.when(is_source)
    def _():
        grad_wait(n.o, piece)
        grad_total(n.o, n.o.grad, b * piece, piece, n.o.whole, 0, range(A - 1))
    piece_own(n.u)
    piece_take(n.q, 0)
    grad_start(n.s, n.gsp, 8)
    grad_forward(n.s, n.gsp, 8)
    piece_pass(n.q, 0)
    for step in range(X - 1):
        send(n.o.whole, n.o.whole, n.o.share.xs.at[step], n.o.share.xr.at[0], xpeer(step) * 2 + c, f, is_source)
    send(n.o.whole, n.o.whole, n.o.share.ss.at[0], n.o.share.sr.at[0], sib, f, is_source)
    grad_wait(n.s, 8)
    grad_total(n.s, n.gsp, f * 8, 8, n.gs_mine.at[0], 0, range(A - 1))
    send(n.gs_mine.at[0], n.gs_pair.at[0], n.pair_s.at[0], n.pair_r.at[0], sib, f)
    piece_own(n.q)
    share_forward(n.d.share, n.d.whole, piece)
    @pl.when(off_x)
    def _():
        got(n.o.whole, n.o.share.xr.at[0])
    send(n.o.whole, n.o.whole, n.o.share.ss.at[1], n.o.share.sr.at[0], sib, f, off_x)
    share_forward(n.u.share, n.u.whole, piece)
    share_end(n.u.share, n.u.whole, piece)
    share_forward(n.q.share, n.q.whole, piece)
    @pl.when(c != ac)
    def _():
        got(n.o.whole, n.o.share.sr.at[0])
    last.start()
    got(n.gs_pair.at[0], n.pair_r.at[0])
    share_end(n.d.share, n.d.whole, piece)
    n.gs_mine[1] = n.gs_mine[0] + n.gs_pair[0]
    for copy in out_copies(n.d, n.rd_out):
        copy.start()
    send(n.gs_mine.at[1], n.gs_pair.at[1], n.pair_s.at[1], n.pair_r.at[1], xpeer(0) * 2 + c, f)
    for copy in out_copies(n.u, n.ru_out):
        copy.start()
    share_end(n.q.share, n.q.whole, piece)
    for copy in out_copies(n.q, n.rq_out):
        copy.start()
    got(n.gs_pair.at[1], n.pair_r.at[1])
    n.gs_out[...] = n.gs_mine[1] + n.gs_pair[1]
    swap_end(4, new_at, lambda m: n.new_out.at[m])
    swap_end(3, grow_at, lambda m: n.grad_out.at[m])
    for t, target in ((n.d, n.rd_out), (n.u, n.ru_out), (n.q, n.rq_out)):
        for copy in out_copies(t, target):
            copy.wait()
    last.wait()
    for tag in list(pending):
        drain(tag)


def place_kernel(g, at_ref, tok_ref, cot_ref, new_ref, grad_ref, rq_ref, ru_ref, rd_ref, ro_ref, gs_ref, *outs):
    mixed_ref, gt_ref, gq_ref, gu_ref, gd_ref, go_ref, grouter_ref, ggains_ref = outs
    grouter_ref[...] = gs_ref[0:1, :]
    ggains_ref[...] = gs_ref[1:3, :]
    tall = tok_ref.shape[1]
    first = pl.program_id(1) * tall
    for k in range(2):
        token = lax.broadcasted_iota(jnp.int32, (tall, g.cap), 0) + first
        hot = token == at_ref[k]
        routed = jnp.max(hot.astype(F32), axis=-1, keepdims=True) > 0.0
        hot = hot.astype(BF)
        new = dot(hot, new_ref[k], (1, 0))
        mixed_ref[k] = jnp.where(routed, new, tok_ref[k].astype(F32)).astype(BF)
        grad = dot(hot, grad_ref[k], (1, 0))
        gt_ref[k] = jnp.where(routed, grad, cot_ref[k].astype(F32))
    for index in range(g.R):
        for part in range(3):
            gq_ref[:, pl.ds(part * g.d + index * g.ac, g.ac)] = rq_ref[
                index, :, pl.ds(part * g.ac, g.ac)
            ].astype(F32)
        for block in range(g.F):
            gu_ref[:, pl.ds((block * g.R + index) * 128, 128)] = ru_ref[
                index, :, pl.ds(block * 128, 128)
            ].astype(F32)
        gd_ref[index] = rd_ref[index].astype(F32)
    go_ref[...] = ro_ref[...].astype(F32)


def place(g, chosen, tokens, cotangent, new_rows, grad_rows, rq, ru, rd, ro, gs):
    halves = 1
    steps = g.MB // 2 * halves
    tok_count = tokens.shape[1]
    tall = tok_count // halves
    piece = g.d // g.F
    low = piece // steps
    hidden = g.F * g.R * 128

    def block(*shape):
        return pl.BlockSpec((2,) + shape, lambda m, h: (m, h, 0))

    def micro(*shape):
        return pl.BlockSpec((2,) + shape, lambda m, h: (m, 0, 0))

    def slab(*lead, cols):
        return pl.BlockSpec(
            lead + (low, cols), lambda m, h: (0,) * len(lead) + (m * halves + h, 0)
        )

    return pl.pallas_call(
        functools.partial(place_kernel, g),
        grid=(g.MB // 2, halves),
        in_specs=[
            micro(1, g.cap),
            block(tall, g.d),
            block(tall, g.d),
            micro(g.cap, g.d),
            micro(g.cap, g.d),
            slab(g.R, cols=g.qc),
            slab(g.R, cols=g.fc),
            slab(g.R, cols=g.d),
            slab(cols=g.d),
            pl.BlockSpec((8, 128), lambda m, h: (0, 0)),
        ],
        out_specs=[
            block(tall, g.d),
            block(tall, g.d),
            slab(cols=3 * g.d),
            slab(cols=hidden),
            slab(g.R, cols=g.d),
            slab(cols=g.d),
            pl.BlockSpec((1, 128), lambda m, h: (0, 0)),
            pl.BlockSpec((2, 128), lambda m, h: (0, 0)),
        ],
        out_shape=[
            jax.ShapeDtypeStruct(tokens.shape, BF),
            jax.ShapeDtypeStruct(tokens.shape, F32),
            jax.ShapeDtypeStruct((piece, 3 * g.d), F32),
            jax.ShapeDtypeStruct((piece, hidden), F32),
            jax.ShapeDtypeStruct((g.R, piece, g.d), F32),
            jax.ShapeDtypeStruct((piece, g.d), F32),
            jax.ShapeDtypeStruct((1, 128), F32),
            jax.ShapeDtypeStruct((2, 128), F32),
        ],
        compiler_params=pltpu.CompilerParams(vmem_limit_bytes=60 * 1024 * 1024),
        name="place_rows",
    )(chosen[:, None, :], tokens, cotangent, new_rows, grad_rows, rq, ru, rd, ro, gs)


def group_shards(tokens, cotangent, path, chosen, router, gains, w_qkv, w_out, w_up, w_down):
    R, F = lax.axis_size("rep"), lax.axis_size("fsdp")
    MB, tok_count, d = tokens.shape
    cap = chosen.shape[1]
    S = F // MB
    hidden = w_up.shape[1]
    g = types.SimpleNamespace(
        R=R,
        F=F,
        S=S,
        A=MB,
        X=R // 2,
        MB=MB,
        cap=cap,
        d=d,
        own=MB * cap,
        rows=R * MB * cap,
        tree=S * MB * cap,
        trees=R // S,
        heads=HEADS // R,
        qc=3 * d // R,
        ac=d // R,
        fc=hidden // R,
    )
    piece = d // F

    anywhere, inside = pl.BlockSpec(memory_space=pl.ANY), pl.BlockSpec(memory_space=pltpu.VMEM)
    operands = dict(
        tokens=(tokens, anywhere),
        cotangent=(cotangent, anywhere),
        w_qkv=(w_qkv, anywhere),
        w_out=(w_out, anywhere),
        w_up=(w_up, anywhere),
        w_down=(w_down, anywhere),
        path=(jnp.transpose(path, (2, 0, 1)), inside),
        chosen=(chosen, inside),
        router=(router[None], inside),
        gains=(gains.T, inside),
    )
    results = dict(
        new_out=((MB, cap, d), BF, anywhere),
        grad_out=((MB, cap, d), BF, anywhere),
        rq_out=((R, piece, g.qc), BF, anywhere),
        ru_out=((R, piece, g.fc), BF, anywhere),
        rd_out=((R, piece, d), BF, anywhere),
        ro_out=((piece, d), BF, anywhere),
        gs_out=((8, 128), F32, inside),
    )
    scratch = scratch_shapes(g)
    flat, _ = jax.tree.flatten(scratch)
    order = list(operands) + list(results)
    made = pl.pallas_call(
        functools.partial(block_kernel, g, order, jax.tree.structure(scratch)),
        out_shape=[jax.ShapeDtypeStruct(*kind[:2]) for kind in results.values()],
        in_specs=[spec for _, spec in operands.values()],
        out_specs=[kind[2] for kind in results.values()],
        scratch_shapes=flat,
        compiler_params=pltpu.CompilerParams(
            collective_id=0, has_side_effects=True, vmem_limit_bytes=60 * 1024 * 1024
        ),
        name="routed_block",
    )(*[value for value, _ in operands.values()])
    new_rows, grad_rows, rq, ru, rd, ro, gs = made
    mixed, grad_tokens, grad_qkv, grad_up, grad_down, grad_out, grad_router, grad_gains = place(
        g, chosen, tokens, cotangent, new_rows, grad_rows, rq, ru, rd, ro, gs
    )
    return (
        mixed,
        grad_tokens,
        grad_router[0],
        grad_gains.T,
        grad_qkv,
        grad_out,
        grad_up,
        grad_down.reshape(R * piece, d),
    )


def plain_norm(matrix, gain_row):
    return matrix * lax.rsqrt(jnp.mean(matrix * matrix, axis=-1, keepdims=True) + eps) * gain_row


def inner(left, right):
    return lax.dot_general(
        left, right, (((0,), (0,)), ((), ())), preferred_element_type=jnp.float32
    )


def by_rows(left, right):
    return lax.dot_general(
        left, right, (((1,), (1,)), ((), ())), preferred_element_type=jnp.float32
    )


def gather_rows(arrays):
    return lax.all_gather(arrays, "fsdp", axis=0, tiled=True)


def scatter_sum(array):
    return lax.psum_scatter(
        array.astype(jnp.bfloat16), "fsdp", scatter_dimension=0, tiled=True
    ).astype(jnp.float32)


def plain_shards(tokens, cotangent, path, chosen, router, gains, w_qkv, w_out, w_up, w_down):
    micro_count, tok_count, model_width = tokens.shape
    slot_count = chosen.shape[1]
    row_count = micro_count * slot_count
    head_dim = model_width // HEADS
    score_scale = head_dim ** (-0.5)
    offset = lax.axis_index("fsdp") * tok_count
    fsdp = lax.axis_size("fsdp")

    def pick(array):
        return jax.vmap(lambda rows, at: rows[at])(array, chosen)

    small = jnp.concatenate([router[:, None], gains], axis=1)
    small_all = gather_rows(small)
    qkv_all = gather_rows(w_qkv)
    out_all = gather_rows(w_out)
    up_all = gather_rows(w_up)
    down_all = gather_rows(w_down)
    router_float = small_all[:, 0].astype(jnp.float32)
    gain_one = small_all[:, 1].astype(jnp.float32)
    gain_two = small_all[:, 2].astype(jnp.float32)

    routed = pick(tokens).reshape(row_count, model_width)
    hidden = routed.astype(jnp.float32)
    gate_rate = jax.nn.sigmoid(
        jnp.dot(routed, small_all[:, 0], preferred_element_type=jnp.float32)
    )
    normed = plain_norm(hidden, gain_one).astype(jnp.bfloat16)
    projected = jnp.dot(normed, qkv_all, preferred_element_type=jnp.float32).astype(jnp.bfloat16)
    queries = projected[:, :model_width].reshape(micro_count, slot_count, HEADS, head_dim)
    own_path = pick(path)
    own_place = offset + chosen
    key_info = jnp.concatenate([own_path[:, :, :1], own_place[:, :, None]], axis=2)
    gathered = lax.all_gather(
        projected[:, model_width:].reshape(micro_count, slot_count, 2 * model_width), "fsdp"
    )
    info_all = lax.all_gather(key_info, "fsdp")
    key_count = fsdp * slot_count
    gathered = jnp.swapaxes(gathered, 0, 1).reshape(micro_count, key_count, 2, HEADS, head_dim)
    info_all = jnp.swapaxes(info_all, 0, 1).reshape(micro_count, key_count, 2)
    key_rows = gathered[:, :, 0]
    value_rows = gathered[:, :, 1]
    key_seg = info_all[:, None, :, 0]
    visible = (
        (key_seg == own_path[:, :, 0:1])
        | (key_seg == own_path[:, :, 1:2])
        | (key_seg == own_path[:, :, 2:3])
    ) & (info_all[:, None, :, 1] <= own_place[:, :, None])
    visible = visible[:, None]

    def product(form, left, right):
        return jnp.einsum(form, left, right, preferred_element_type=jnp.float32)

    scores = product("mqhd,mkhd->mhqk", queries, key_rows) * score_scale
    scores = jnp.where(visible, scores, -1e30)
    row_max = jnp.max(scores, axis=-1, keepdims=True)
    exponent = jnp.where(visible, jnp.exp(scores - row_max), 0.0)
    row_total = jnp.sum(exponent, axis=-1, keepdims=True)
    soft_prob = exponent / row_total
    probs = soft_prob.astype(jnp.bfloat16)
    attention = product("mhqk,mkhd->mqhd", probs, value_rows)
    attention = attention.reshape(row_count, model_width).astype(jnp.bfloat16)
    branch = jnp.dot(attention, out_all, preferred_element_type=jnp.float32)
    middle = hidden + branch
    normed_two = plain_norm(middle, gain_two).astype(jnp.bfloat16)
    up_proj = jnp.dot(normed_two, up_all, preferred_element_type=jnp.float32)
    activated = jax.nn.gelu(up_proj).astype(jnp.bfloat16)
    change = branch + jnp.dot(activated, down_all, preferred_element_type=jnp.float32)
    new_rows = hidden + gate_rate[:, None] * change

    def put(array, rows):
        rows = rows.reshape(micro_count, slot_count, model_width).astype(array.dtype)
        return jax.vmap(lambda whole, at, new: whole.at[at].set(new))(array, chosen, rows)

    mixed = put(tokens, new_rows)

    grad_rows = pick(cotangent).reshape(row_count, model_width).astype(jnp.float32)
    grad_change = gate_rate[:, None] * grad_rows
    grad_logit = jnp.sum(grad_rows * change, axis=-1) * gate_rate * (1.0 - gate_rate)
    grad_mlp = grad_change.astype(jnp.bfloat16)
    grad_down = scatter_sum(inner(activated, grad_mlp))
    grad_act = by_rows(grad_mlp, down_all)
    gelu_value, gelu_back = jax.vjp(jax.nn.gelu, up_proj)
    grad_up_proj = gelu_back(grad_act)[0].astype(jnp.bfloat16)
    grad_up = scatter_sum(inner(normed_two, grad_up_proj))
    grad_normed_two = by_rows(grad_up_proj, up_all)
    norm_value, norm_back_two = jax.vjp(plain_norm, middle, gain_two)
    grad_middle, grad_gain_two = norm_back_two(grad_normed_two)
    grad_branch = (grad_change + grad_middle).astype(jnp.bfloat16)
    grad_outw = scatter_sum(inner(attention, grad_branch))
    grad_attention = by_rows(grad_branch, out_all).astype(jnp.bfloat16)
    grad_heads = grad_attention.reshape(micro_count, slot_count, HEADS, head_dim)
    prob_grad = product("mqhd,mkhd->mhqk", grad_heads, value_rows)
    delta = jnp.sum(soft_prob * prob_grad, axis=-1, keepdims=True)
    grad_scores = (soft_prob * (prob_grad - delta)).astype(jnp.bfloat16)
    grad_query = product("mhqk,mkhd->mqhd", grad_scores, key_rows) * score_scale
    grad_key = product("mhqk,mqhd->mkhd", grad_scores, queries) * score_scale
    grad_value = product("mhqk,mqhd->mkhd", probs, grad_heads)
    grad_kv = jnp.stack([grad_key, grad_value], axis=2).reshape(
        micro_count, fsdp, slot_count, 2 * model_width
    )
    grad_kv = lax.psum_scatter(
        jnp.swapaxes(grad_kv, 0, 1).astype(jnp.bfloat16).reshape(-1, 2 * model_width),
        "fsdp",
        scatter_dimension=0,
        tiled=True,
    )
    grad_projected = jnp.concatenate(
        [
            grad_query.reshape(row_count, model_width).astype(jnp.bfloat16),
            grad_kv.reshape(row_count, 2 * model_width),
        ],
        axis=1,
    )
    grad_qkvw = scatter_sum(inner(normed, grad_projected))
    grad_normed = by_rows(grad_projected, qkv_all)
    norm_value_one, norm_back_one = jax.vjp(plain_norm, hidden, gain_one)
    grad_hidden_norm, grad_gain_one = norm_back_one(grad_normed)
    grad_hidden = (
        grad_rows + grad_middle + grad_hidden_norm + grad_logit[:, None] * router_float[None, :]
    )
    grad_tokens = put(cotangent.astype(jnp.float32), grad_hidden)
    grad_routerw = jnp.sum(grad_logit[:, None] * hidden, axis=0)
    grad_small = jnp.stack([grad_routerw, grad_gain_one, grad_gain_two], axis=1)
    grad_small = lax.psum_scatter(grad_small, "fsdp", scatter_dimension=0, tiled=True)
    summed = lax.psum((grad_small, grad_qkvw, grad_outw, grad_up, grad_down), "rep")
    return (mixed, grad_tokens, summed[0][:, 0], summed[0][:, 1:]) + tuple(summed[1:])


def solution(mesh):
    rows = P(None, ("rep", "fsdp"), None)
    weight = P("fsdp", None)

    def whole(*args):
        grouped = fits(mesh, args[0], args[3], args[8])
        return jax.shard_map(
            group_shards if grouped else plain_shards,
            mesh=mesh,
            in_specs=(
                rows,
                rows,
                rows,
                P(None, ("rep", "fsdp")),
                P("fsdp"),
                weight,
                weight,
                weight,
                weight,
                weight,
            ),
            out_specs=(rows, rows, P("fsdp"), weight, weight, weight, weight, weight),
            check_vma=False,
        )(*args)

    return whole
```

```python
import functools
import math
import types

import jax
import jax.numpy as jnp
from jax import lax
from jax.experimental import pallas as pl
from jax.experimental.pallas import tpu as pltpu
from jax.sharding import PartitionSpec as P

HEADS = 16


eps = 1e-05
MESH = pl.DeviceIdType.MESH
BF = jnp.bfloat16
F32 = jnp.float32
GELU_A = math.sqrt(2.0 / math.pi)
GELU_B = 0.044715


def dot(left, right, contract):
    return lax.dot_general(
        left, right, (((contract[0],), (contract[1],)), ((), ())), preferred_element_type=F32
    )


def aligned(index, size):
    return pl.ds(pl.multiple_of(index * size, size), size)


def loop(count, body):
    def step(index, carry):
        body(index)
        return carry

    lax.fori_loop(0, count, step, 0)


def fits(mesh, tokens, chosen, w_up):
    rep, fsdp = mesh.shape["rep"], mesh.shape["fsdp"]
    micro, width, hidden = tokens.shape[0], tokens.shape[2], w_up.shape[1]
    if fsdp % micro or rep % 2:
        return False
    inner_count = fsdp // micro
    return (
        rep % inner_count == 0
        and rep == micro
        and fsdp == rep * inner_count
        and width == fsdp * 128
        and hidden == fsdp * rep * 128
        and HEADS % (2 * rep) == 0
        and width // HEADS == 64
        and chosen.shape[1] // (rep * fsdp) == 64
        and rep == 4
        and hidden == rep * width
        and tokens.shape[1] * micro // (rep * fsdp) == 2 * rep * micro * 64
    )


def scratch_shapes(g):
    own, rows, d, piece = g.own, g.rows, g.d, g.d // g.F

    def vmem(height, width, kind=BF):
        return pltpu.VMEM((height, width), kind)

    def dma(*shape):
        return pltpu.SemaphoreType.DMA(shape)

    def shared():
        return dict(xs=dma(g.X - 1), xr=dma(g.X - 1), ss=dma(g.X), sr=dma(g.X))

    def halves():
        return [shared(), shared()]

    def direct():
        return dict(l=dma(1), os=dma(g.A - 1), ors=dma(g.A - 1), ins=dma(g.A), inr=dma(g.A))

    def chained():
        ends = dict(ups=dma(g.A - 1), upr=dma(g.A - 1), dns=dma(g.A - 1), dnr=dma(g.A - 1))
        return dict(l=dma(g.F), ins=dma(2 * g.A - 1), inr=dma(2 * g.A - 1), **ends)

    def pieces(count, cols, kind, height, full):
        made = dict(
            inbox=vmem(count // g.S * height, cols, kind),
            outbox=vmem(g.A * height, cols, kind),
            ins=dma(g.A),
            inr=dma(g.A),
            os=dma(g.A),
            ors=dma(g.A),
        )
        if full:
            made.update(grad=vmem(count * height, cols), share=shared(), out=dma(g.R))
            made.update(whole=vmem(full * height, cols))
        return made

    return dict(
        hid=vmem(own, d),
        ct=vmem(own, d),
        infos=vmem(g.R * g.MB * 8, 128, F32),
        sm=vmem(g.F * 8, 128, F32),
        info=pltpu.VMEM((g.MB, 8, 128), F32),
        vec=vmem(8, d, F32),
        wqa=vmem(d, g.qc),
        woa=vmem(g.ac, d),
        wua=vmem(d, g.fc),
        wda=vmem(g.fc, d),
        normed=vmem(rows, d),
        norm2=vmem(rows, d),
        proj=vmem(rows, g.qc),
        att=vmem(rows, g.ac),
        gatt=vmem(rows, g.ac),
        gproj=vmem(rows, g.qc),
        lse=vmem(rows, 128, F32),
        bias=vmem(g.tree, g.tree, F32),
        pair_a=vmem(2 * rows, g.fc),
        pair_b=vmem(2 * rows, d),
        dact=vmem(rows, g.fc, F32),
        gate=vmem(own, 128, F32),
        branch=vmem(own, d, F32),
        gmid=vmem(own, d, F32),
        ends=vmem(2 * own, d),
        to_sib=pltpu.VMEM((2, g.X * own, d), BF),
        of_sib=pltpu.VMEM((2, g.X * own, d), BF),
        to_x=pltpu.VMEM((2, (g.X - 1) * own, d), BF),
        of_x=pltpu.VMEM((2, (g.X - 1) * own, d), BF),
        gsum=vmem(8, d, F32),
        gsp=vmem(g.F * 8, 128, F32),
        gs_pair=pltpu.VMEM((2, 8, 128), F32),
        gs_mine=pltpu.VMEM((2, 8, 128), F32),
        a2a_s=dma(5, g.MB),
        a2a_r=dma(5, g.MB),
        tok_l=dma(2, g.MB),
        pair_s=dma(2),
        pair_r=dma(2),
        small_t=direct(),
        wo_t=direct(),
        wq_t=chained(),
        wu_t=chained(),
        wd_t=chained(),
        info_t=shared(),
        normed_t=halves(),
        gmlp_t=halves(),
        norm2_t=halves(),
        gbr_t=halves(),
        sums=[halves() for _ in range(4)],
        q=pieces(g.F, g.qc, BF, piece, g.R),
        u=pieces(g.F, g.fc, BF, piece, g.R),
        d=pieces(g.F, d, BF, piece, g.R),
        o=pieces(g.S, d, BF, piece, 1),
        s=pieces(g.F, 128, F32, 8, 0),
    )


def spaces(tree):
    if isinstance(tree, dict):
        return types.SimpleNamespace(**{name: spaces(value) for name, value in tree.items()})
    return [spaces(value) for value in tree] if isinstance(tree, list) else tree


def block_kernel(g, order, form, *refs):
    split = len(order)
    n = spaces(dict(zip(order, refs[:split]), **jax.tree.unflatten(form, refs[split:])))
    R, F, S, A, X, MB = g.R, g.F, g.S, g.A, g.X, g.MB
    own, rows, d, cap = g.own, g.rows, g.d, g.cap
    piece = d // F
    r = lax.axis_index("rep")
    f = lax.axis_index("fsdp")
    x, c = r // 2, lax.rem(r, 2)
    a, b = f // S, lax.rem(f, S)
    other_b = lax.rem(b + 1, S)
    sib = x * 2 + 1 - c
    pending = {}
    n.act, n.gup = n.pair_a.at[pl.ds(0, rows)], n.pair_a.at[pl.ds(rows, rows)]
    n.gmlp, n.gbr = n.pair_b.at[pl.ds(0, rows)], n.pair_b.at[pl.ds(rows, rows)]
    n.nrow, n.grow = n.ends.at[pl.ds(0, own)], n.ends.at[pl.ds(own, own)]
    n.picked, n.picked_ct = n.ends, n.norm2
    n.acc, n.gfirst = n.dact.at[pl.ds(0, own)], n.dact.at[pl.ds(own, own)]
    tok_count = n.tokens.shape[1]

    def token_copy(which, m):
        source, target = (n.tokens, n.pair_a) if which == 0 else (n.cotangent, n.pair_b)
        return pltpu.make_async_copy(
            source.at[m], target.at[pl.ds(m * tok_count, tok_count)], n.tok_l.at[which, m]
        )

    def cut_qkv():
        return [
            pltpu.make_async_copy(
                n.w_qkv.at[:, pl.ds(pl.multiple_of(part * d + r * g.ac, g.ac), g.ac)],
                n.wqa.at[aligned(f, piece), pl.ds(part * g.ac, g.ac)],
                n.wq_t.l.at[part],
            )
            for part in range(3)
        ]

    def cut_up():
        return [
            pltpu.make_async_copy(
                n.w_up.at[:, pl.ds(pl.multiple_of((block * R + r) * 128, 128), 128)],
                n.wua.at[aligned(f, piece), pl.ds(block * 128, 128)],
                n.wu_t.l.at[block],
            )
            for block in range(F)
        ]

    def cut_down():
        return [
            pltpu.make_async_copy(
                n.w_down.at[aligned(r, piece)], n.wda.at[aligned(f, piece)], n.wd_t.l.at[0]
            )
        ]

    for copy in cut_qkv():
        copy.start()
    for which in range(2):
        for m in range(MB):
            token_copy(which, m).start()
    for cut in (cut_up, cut_down):
        for copy in cut():
            copy.start()

    def remote(src, dst, ss, rs, rep, fsdp):
        return pltpu.make_async_remote_copy(
            src_ref=src,
            dst_ref=dst,
            send_sem=ss,
            recv_sem=rs,
            device_id={"rep": rep, "fsdp": fsdp},
            device_id_type=MESH,
        )

    def send(src, dst, ss, rs, rep, fsdp, cond=None, tag=None):
        def start():
            remote(src, dst, ss, rs, rep, fsdp).start()

        def done():
            remote(src, dst, ss, rs, rep, fsdp).wait_send()

        if cond is None:
            start()
            pending.setdefault(tag, []).append(done)
        else:
            pl.when(cond)(start)
            pending.setdefault(tag, []).append(lambda: pl.when(cond)(done))

    def drain(tag):
        for done in pending.pop(tag, []):
            done()

    def got(dst, rs):
        remote(dst, dst, rs, rs, sib, f).wait_recv()

    def xpeer(step):
        return lax.rem(x + 1 + step, X)

    def xfrom(step):
        return lax.rem(x + X - 1 - step, X)

    def outer(step):
        return lax.rem(a + step, A)

    def outer_from(step):
        return lax.rem(a + A - step, A)

    home_rep = (r // S) * S + b

    def home_fsdp(m):
        return m * S + lax.rem(r, S)

    barrier = pltpu.get_barrier_semaphore()

    def greet(rep, fsdp):
        pl.semaphore_signal(
            barrier, inc=1, device_id={"rep": rep, "fsdp": fsdp}, device_id_type=MESH
        )

    for step in range(1, A):
        greet(r, outer(step) * S + b)
    greet(r, a * S + other_b)
    greet(sib, f)
    for step in range(X - 1):
        greet(xpeer(step) * 2 + c, f)
    mine = [(home_fsdp(m) == f) & (home_rep == r) for m in range(MB)]
    for m in range(MB):

        @pl.when(jnp.logical_not(mine[m]))
        def _(m=m):
            greet(home_rep, home_fsdp(m))

    stays = (home_rep == r) & (lax.rem(r, S) == b)
    pl.semaphore_wait(barrier, (A - 1) + 1 + 1 + (X - 1) + MB - stays.astype(jnp.int32))

    def swap_start(which, src_of, dst_of):
        for m in range(MB):
            src, dst = src_of(m), dst_of(a)
            ss, rs = n.a2a_s.at[which, m], n.a2a_r.at[which, a]

            @pl.when(jnp.logical_not(mine[m]))
            def _():
                remote(src, dst, ss, rs, home_rep, home_fsdp(m)).start()

            @pl.when(mine[m])
            def _():
                pltpu.make_async_copy(src, dst, rs).start()

    def swap_end(which, src_of, dst_of):
        for m in range(MB):
            src, dst = src_of(m), dst_of(m)
            ss, rs = n.a2a_s.at[which, m], n.a2a_r.at[which, m]

            @pl.when(jnp.logical_not(mine[m]))
            def _():
                remote(src, dst, ss, rs, home_rep, home_fsdp(m)).wait()

            @pl.when(mine[m])
            def _():
                pltpu.make_async_copy(src, dst, rs).wait()

    def gather_start(t, buf, height):
        at = aligned(f, height)
        src = buf.at[at]
        for step in range(1, A):
            send(
                src,
                buf.at[at],
                t.os.at[step - 1],
                t.ors.at[step - 1],
                r,
                outer(step) * S + b,
            )
        send(src, buf.at[at], t.ins.at[0], t.inr.at[0], r, a * S + other_b)

    def gather_forward(t, buf, height):
        for step in range(1, A):
            at = buf.at[aligned(outer_from(step) * S + b, height)]
            got(at, t.ors.at[step - 1])
            send(at, at, t.ins.at[step], t.inr.at[step], r, a * S + other_b)

    def gather_end(t, buf, height):
        for step in range(A):
            at = buf.at[aligned(outer_from(step) * S + other_b, height)]
            got(at, t.inr.at[step])

    def hop(step):
        return lax.rem(a + A + step, A)

    def chain_start(t, buf, height):
        at = buf.at[aligned(f, height)]
        send(at, at, t.ups.at[0], t.upr.at[0], r, hop(1) * S + b, a < A - 1)
        send(at, at, t.dns.at[0], t.dnr.at[0], r, hop(-1) * S + b, a > 0)

    def chain_across(t, buf, height):
        at = buf.at[aligned(f, height)]
        send(at, at, t.ins.at[0], t.inr.at[0], r, a * S + other_b)

    def chain_forward(t, buf, height, step):
        for sends, takes, has, on, to, index in (
            (t.ups, t.upr, a >= step, a < A - 1, 1, step),
            (t.dns, t.dnr, a + step < A, a > 0, -1, A - 1 + step),
        ):
            at = buf.at[aligned(hop(-to * step) * S + b, height)]

            @pl.when(has)
            def _():
                got(at, takes.at[step - 1])

            if step < A - 1:
                send(
                    at,
                    at,
                    sends.at[step],
                    takes.at[step],
                    r,
                    hop(to) * S + b,
                    has & on,
                )
            send(
                at,
                at,
                t.ins.at[index],
                t.inr.at[index],
                r,
                a * S + other_b,
                has,
            )

    def chain_end(t, buf, height):
        got(buf.at[aligned(a * S + other_b, height)], t.inr.at[0])
        for step in range(1, A):
            for has, to, index in ((a >= step, 1, step), (a + step < A, -1, A - 1 + step)):
                at = buf.at[aligned(hop(-to * step) * S + other_b, height)]

                @pl.when(has)
                def _():
                    got(at, t.inr.at[index])

    is_source = a == r

    def out_start(src, buf):
        at = buf.at[aligned(b, piece)]

        @pl.when(is_source)
        def _():
            pltpu.make_async_copy(src, at, n.wo_t.l.at[0]).start()

        for step in range(1, A):
            send(
                src, at, n.wo_t.os.at[step - 1], n.wo_t.ors.at[0], r, outer(step) * S + b, is_source
            )
        send(src, at, n.wo_t.ins.at[0], n.wo_t.inr.at[0], r, a * S + other_b, is_source)

    def out_forward(buf):
        at = buf.at[aligned(b, piece)]

        @pl.when(jnp.logical_not(is_source))
        def _():
            got(at, n.wo_t.ors.at[0])

        send(
            at, at, n.wo_t.ins.at[1], n.wo_t.inr.at[0], r, a * S + other_b, jnp.logical_not(is_source)
        )

    def out_end(src, buf):
        @pl.when(is_source)
        def _():
            pltpu.make_async_copy(src, buf.at[aligned(b, piece)], n.wo_t.l.at[0]).wait()

        got(buf.at[aligned(other_b, piece)], n.wo_t.inr.at[0])

    def part_of(block, height, part):
        if part is None:
            return aligned(block, height)
        half = height // 2
        return pl.ds(pl.multiple_of(block * height + part * half, half), half)

    def share_start(t, buf, height, part=None):
        at = buf.at[part_of(r, height, part)]
        for step in range(X - 1):
            send(at, at, t.xs.at[step], t.xr.at[step], xpeer(step) * 2 + c, f)
        send(at, at, t.ss.at[0], t.sr.at[0], sib, f)

    def share_forward(t, buf, height, part=None):
        for step in range(X - 1):
            at = buf.at[part_of(xfrom(step) * 2 + c, height, part)]
            got(at, t.xr.at[step])
            send(at, at, t.ss.at[1 + step], t.sr.at[1 + step], sib, f)

    def share_near(t, buf, height, part=None):
        got(buf.at[part_of(sib, height, part)], t.sr.at[0])

    def share_far(t, buf, height, part=None):
        for step in range(X - 1):
            at = buf.at[part_of(xfrom(step) * 2 + 1 - c, height, part)]
            got(at, t.sr.at[1 + step])

    def share_end(t, buf, height):
        share_near(t, buf, height)
        share_far(t, buf, height)

    def rows_do(what, t, buf):
        what(t[0], buf, own)

    wide = 256

    def sum_owner(step):
        return xpeer(step) if step < X - 1 else x

    half_tiles = d // wide // 2

    def sum_near(index, slot, partial, step):
        to_sib, at = n.to_sib.at[slot], pl.ds(step * own, own)
        owner = sum_owner(step) * 2 + 1 - c
        if step == 0:
            drain(slot)
        for part in range(2):
            t, across = n.sums[index][part], pl.ds(part * d // 2, d // 2)

            def one(tile, part=part):
                cols = aligned(part * half_tiles + tile, wide)
                to_sib[at, cols] = partial(owner, cols).astype(BF)

            loop(half_tiles, one)
            send(
                to_sib.at[at, across],
                n.of_sib.at[slot, at, across],
                t.ss.at[step],
                t.sr.at[step],
                sib,
                f,
                tag=slot,
            )

    def sum_mine(index, slot, partial, step, acc, post=True):
        of_sib, to_x, at = n.of_sib.at[slot], n.to_x.at[slot], pl.ds(step * own, own)
        owner = sum_owner(step) * 2 + c
        last = step == X - 1
        for part in range(2):
            t, across = n.sums[index][part], pl.ds(part * d // 2, d // 2)
            got(of_sib.at[at, across], t.sr.at[step])

            def one(tile, part=part):
                cols = aligned(part * half_tiles + tile, wide)
                total = partial(owner, cols) + of_sib[at, cols].astype(F32)
                if last:
                    acc[:, cols] = total
                else:
                    to_x[at, cols] = total.astype(BF)

            loop(half_tiles, one)
            if not last and post:
                sum_post(index, slot, step, part)

    def sum_post(index, slot, step, part):
        at, across = pl.ds(step * own, own), pl.ds(part * d // 2, d // 2)
        t = n.sums[index][part]
        send(
            n.to_x.at[slot, at, across],
            n.of_x.at[slot, at, across],
            t.xs.at[step],
            t.xr.at[step],
            sum_owner(step) * 2 + c,
            f,
            tag=slot,
        )

    def sum_end(index, slot):
        of_x = n.of_x.at[slot]
        for step in range(X - 1):
            for part in range(2):
                across = pl.ds(part * d // 2, d // 2)
                got(of_x.at[pl.ds(step * own, own), across], n.sums[index][part].xr.at[step])

    def came(slot, at):
        total = None
        for step in range(X - 1):
            part = n.of_x[slot, pl.ds(step * own + at, tall), :].astype(F32)
            total = part if total is None else total + part
        return total

    tall = 32

    def by_own(body):
        def one(index):
            at = pl.multiple_of(index * tall, tall)
            body(at, pl.ds(at, tall))

        loop(own // tall, one)

    def grad_start(t, buf, height):
        out = t is n.o
        inbox = t.inbox
        for step in range(1 if out else A):
            to_a = r if out else outer(step + 1)
            src = buf.at[aligned((0 if out else to_a * S) + other_b, height)]
            send(
                src,
                inbox.at[pl.ds(step * height, height)],
                t.ins.at[step],
                t.inr.at[step],
                r,
                a * S + other_b,
            )

    def add_into(dst, base, inbox, start, height):
        small = min(height, 32)

        def one(index):
            at = pl.ds(pl.multiple_of(base + index * small, small), small)
            of = pl.ds(pl.multiple_of(start + index * small, small), small)
            dst[at, :] = (dst[at, :].astype(F32) + inbox[of, :].astype(F32)).astype(dst.dtype)

        loop(height // small, one)

    def grad_forward(t, buf, height):
        out = t is n.o
        inbox, outbox = t.inbox, t.outbox
        for step in range(1 if out else A):
            to_a = r if out else outer(step + 1)
            base = ((0 if out else to_a * S) + b) * height
            got(inbox.at[pl.ds(step * height, height)], t.inr.at[step])
            add_into(buf, base, inbox, step * height, height)
            if out:
                slot = lax.rem(r + A - a - 1, A)
                slot = jnp.where(is_source, 0, slot)
                send(
                    buf.at[pl.ds(pl.multiple_of(base, height), height)],
                    outbox.at[aligned(slot, height)],
                    n.o.os.at[0],
                    n.o.ors.at[slot],
                    r,
                    r * S + b,
                    jnp.logical_not(is_source),
                )
            elif step < A - 1:
                send(
                    buf.at[pl.ds(pl.multiple_of(base, height), height)],
                    outbox.at[pl.ds(step * height, height)],
                    t.os.at[step],
                    t.ors.at[step],
                    r,
                    to_a * S + b,
                )

    def grad_wait(t, height):
        for step in range(A - 1):
            got(
                t.outbox.at[pl.ds(step * height, height)],
                t.ors.at[step],
            )

    def grad_total(t, buf, base, height, target, target_base, boxes):
        outbox = t.outbox
        small = min(height, 32)

        def one(index):
            off = index * small
            total = buf[pl.ds(pl.multiple_of(base + off, small), small), :].astype(F32)
            for box in boxes:
                at = pl.ds(pl.multiple_of(box * height + off, small), small)
                total = total + outbox[at, :].astype(F32)
            at = pl.ds(pl.multiple_of(target_base + off, small), small)
            target[at, :] = total.astype(target.dtype)

        loop(height // small, one)

    side = a // 2
    mate = a + 1 - 2 * lax.rem(a, 2)
    is_end = (a == 0) | (a == A - 1)
    passes_on = jnp.logical_not(is_end)
    piece_owner = (2 - side, 3 * (1 - side), mate, a)

    def piece_start(t, step):
        height, inbox = piece, t.inbox
        send(
            t.grad.at[aligned(piece_owner[step] * S + other_b, height)],
            inbox.at[pl.ds(step * height, height)],
            t.ins.at[step],
            t.inr.at[step],
            r,
            a * S + other_b,
        )

    def piece_take(t, step):
        buf, inbox, outbox = t.grad, t.inbox, t.outbox
        base = (piece_owner[step] * S + b) * piece
        got(inbox.at[pl.ds(step * piece, piece)], t.inr.at[step])
        add_into(buf, base, inbox, step * piece, piece)
        if step < 3:
            send(
                buf.at[pl.ds(pl.multiple_of(base, piece), piece)],
                outbox.at[pl.ds(step * piece, piece)],
                t.os.at[step],
                t.ors.at[step],
                r,
                mate * S + b,
                is_end if step < 2 else None,
            )

    def piece_pass(t, step):
        buf, outbox = t.grad, t.outbox
        base = (piece_owner[step] * S + b) * piece

        @pl.when(passes_on)
        def _():
            got(outbox.at[pl.ds(step * piece, piece)], t.ors.at[step])
            add_into(buf, base, outbox, step * piece, piece)

        send(
            buf.at[pl.ds(pl.multiple_of(base, piece), piece)],
            outbox.at[pl.ds(3 * piece, piece)],
            t.os.at[step],
            t.ors.at[3],
            r,
            piece_owner[step] * S + b,
            passes_on,
        )

    def piece_own(t):
        for box in (2, 3):
            got(
                t.outbox.at[pl.ds(box * piece, piece)], t.ors.at[box]
            )
        grad_total(t, t.grad, f * piece, piece, t.whole, r * piece, (2, 3))
        share_start(t.share, t.whole, piece)

    def hid_at(i):
        return n.hid.at[aligned(i, cap)]

    def ct_at(i):
        return n.ct.at[aligned(i, cap)]

    def info_src(i):
        return n.info.at[i]

    def info_own(i):
        return n.infos.at[aligned(r * MB + i, 8)]

    def info_home(i):
        return n.infos.at[aligned(home_rep * MB + i, 8)]

    odd = lax.rem(a, 2)
    lane_token = lax.broadcasted_iota(jnp.int32, (tok_count, 128), 0)
    lane = lax.broadcasted_iota(jnp.int32, (1, 128), 1)
    lane_used = (lane // cap) == odd
    def at_of(m):
        row = n.chosen[m : m + 1, :]
        return jnp.where(lane_used, jnp.concatenate([row, row], axis=1), -1)

    def hot_of(m):
        return (lane_token == at_of(m)).astype(F32).astype(BF)

    def tok_at(m):
        return n.picked.at[pl.ds(pl.multiple_of(m * 128 + odd * cap, cap), cap)]

    def cot_at(m):
        return n.picked_ct.at[pl.ds(pl.multiple_of(m * 128 + odd * cap, cap), cap)]

    mine_sm = pl.ds(pl.multiple_of(f * 8, 8), 8)
    def first_norm(at, rows_at):
        h = n.hid[rows_at, :].astype(F32)
        scale = lax.rsqrt(jnp.mean(h * h, axis=-1, keepdims=True) + eps)
        n.normed[pl.ds(pl.multiple_of(r * own + at, tall), tall), :] = (
            h * scale * n.vec[1:2, :]
        ).astype(BF)
        logit = jnp.sum(h * n.vec[0:1, :], axis=-1, keepdims=True)
        n.gate[rows_at, :] = jnp.broadcast_to(1.0 / (1.0 + jnp.exp(-logit)), (tall, 128))

    def mlp_cotangent(at, rows_at):
        gc = n.gate[rows_at, 0:1] * n.ct[rows_at, :].astype(F32)
        n.gmlp[pl.ds(pl.multiple_of(r * own + at, tall), tall), :] = gc.astype(BF)

    far = xpeer(0)
    near_blocks, far_blocks = (r, sib), (far * 2 + c, far * 2 + 1 - c)
    def project(block):
        at = aligned(block, own)
        half = g.qc // 3

        def one(part):
            cols = aligned(part, half)
            n.proj[at, cols] = dot(n.normed[at, :], n.wqa[:, cols], (1, 0)).astype(BF)

        loop(3, one)

    tree, pairs = g.tree, g.heads // 2
    scale = 64 ** (-0.5)
    low_lane = lax.broadcasted_iota(jnp.int32, (tree, 128), 1) < 64
    def half_of(value, half):
        keep = low_lane if half == 0 else jnp.logical_not(low_lane)
        return jnp.where(keep, value, jnp.zeros_like(value))

    def join(first, second):
        return jnp.where(low_lane, first, second)

    def make_bias(t):
        blocks = []
        for index in range(S * MB // 2):
            at = pl.multiple_of((t * S * MB + index * 2) * 8, 8)
            blocks.append(n.infos[pl.ds(at, 8), :] + n.infos[pl.ds(at + 8, 8), :])
        keys = jnp.concatenate(blocks, axis=1)
        asked = jnp.transpose(keys)
        near = keys[0:1, :] == asked[:, 0:1]
        near = near | (keys[0:1, :] == asked[:, 1:2])
        near = near | (keys[0:1, :] == asked[:, 2:3])
        near = near & (keys[3:4, :] <= asked[:, 3:4])
        n.bias[...] = jnp.where(near, 0.0, -1e30)

    def columns(part, pair):
        return pl.ds(part * g.ac + pair * 128, 128)

    def attend(t):
        make_bias(t)
        at = aligned(t, tree)
        for pair in range(pairs):
            q = n.proj[at, columns(0, pair)]
            k = n.proj[at, columns(1, pair)]
            v = n.proj[at, columns(2, pair)]
            made = []
            for half in range(2):
                s = dot(half_of(q, half), k, (1, 1)) * scale + n.bias[...]
                top = jnp.max(s, axis=-1, keepdims=True)
                e = jnp.exp(s - top)
                total = jnp.sum(e, axis=-1, keepdims=True)
                made.append(dot((e * (1.0 / total)).astype(BF), v, (1, 0)))
                head = pair * 2 + half
                n.lse[at, head : head + 1] = top + jnp.log(total)
            n.att[at, pl.ds(pair * 128, 128)] = join(*made).astype(BF)

    def branch_part(owner, cols):
        return dot(n.att[aligned(owner, own), :], n.woa[:, cols], (1, 0))

    def second_norm(at, rows_at):
        br = n.branch[rows_at, :] + came(0, at)
        n.branch[rows_at, :] = br
        mid = n.hid[rows_at, :].astype(F32) + br
        inv = lax.rsqrt(jnp.mean(mid * mid, axis=-1, keepdims=True) + eps)
        n.norm2[pl.ds(pl.multiple_of(r * own + at, tall), tall), :] = (
            mid * inv * n.vec[2:3, :]
        ).astype(BF)

    tiles = g.fc // wide
    def mlp_up(block):
        at = aligned(block, own)

        def one(tile):
            cols = aligned(tile, wide)
            u = dot(n.norm2[at, :], n.wua[:, cols], (1, 0))
            square = u * u
            t = jnp.tanh(GELU_A * (u + GELU_B * square * u))
            n.act[at, cols] = (0.5 * u * (1.0 + t)).astype(BF)
            n.dact[at, cols] = 0.5 * (1.0 + t) + (0.5 * GELU_A) * u * (1.0 - t * t) * (
                1.0 + (3.0 * GELU_B) * square
            )

        loop(tiles, one)

    def mlp_back(block):
        at = aligned(block, own)

        def one(tile):
            cols = aligned(tile, wide)
            ga = dot(n.gmlp[at, :], n.wda[cols, :], (1, 1))
            n.gup[at, cols] = (ga * n.dact[at, cols]).astype(BF)

        loop(tiles, one)

    def norm2_part(owner, cols):
        return dot(n.gup[aligned(owner, own), :], n.wua[cols, :], (1, 1))

    def weight_grad(left, right, target, count):
        def one(index):
            cols = aligned(index, 256)
            target[cols, :] = dot(left[:, cols], right[...], (0, 0)).astype(BF)

        loop(count // 256, one)

    def second_back(at, rows_at):
        dy = n.gmid[rows_at, :] + came(1, at)
        mid = n.hid[rows_at, :].astype(F32) + n.branch[rows_at, :]
        inv = lax.rsqrt(jnp.mean(mid * mid, axis=-1, keepdims=True) + eps)
        n.gsum[2:3, :] = n.gsum[2:3, :] + jnp.sum(dy * mid * inv, axis=0, keepdims=True)
        t = dy * n.vec[2:3, :]
        along = jnp.sum(mid * t, axis=-1, keepdims=True) * (inv * inv * inv * (1.0 / d))
        gm = inv * t - mid * along
        n.gmid[rows_at, :] = gm
        gc = n.gate[rows_at, 0:1] * n.ct[rows_at, :].astype(F32)
        n.gbr[pl.ds(pl.multiple_of(r * own + at, tall), tall), :] = (gc + gm).astype(BF)

    def attention_cotangent(block):
        at = aligned(block, own)
        n.gatt[at, :] = dot(n.gbr[at, :], n.woa[...], (1, 1)).astype(BF)

    def attend_back(t):
        make_bias(t)
        at = aligned(t, tree)
        for pair in range(pairs):
            q = n.proj[at, columns(0, pair)]
            k = n.proj[at, columns(1, pair)]
            v = n.proj[at, columns(2, pair)]
            da = n.gatt[at, pl.ds(pair * 128, 128)]
            dq, dk, dv = [], [], []
            for half in range(2):
                head = pair * 2 + half
                s = dot(half_of(q, half), k, (1, 1)) * scale + n.bias[...]
                p = jnp.exp(s - n.lse[at, head : head + 1])
                dp = dot(half_of(da, half), v, (1, 1))
                delta = jnp.sum(p * dp, axis=-1, keepdims=True)
                ds = (p * (dp - delta)).astype(BF)
                dq.append(dot(ds, k, (1, 0)))
                dk.append(dot(ds, q, (0, 0)))
                dv.append(dot(p.astype(BF), da, (0, 0)))
            n.gproj[at, columns(0, pair)] = (join(*dq) * scale).astype(BF)
            n.gproj[at, columns(1, pair)] = (join(*dk) * scale).astype(BF)
            n.gproj[at, columns(2, pair)] = join(*dv).astype(BF)

    def change_part(owner, cols):
        return dot(n.act[aligned(owner, own), :], n.wda[:, cols], (1, 0))

    def normed_part(owner, cols):
        return dot(n.gproj[aligned(owner, own), :], n.wqa[cols, :], (1, 1))

    def new_rows(at, rows_at):
        change = n.branch[rows_at, :] + n.acc[rows_at, :] + came(0, at)
        h = n.hid[rows_at, :].astype(F32)
        gate = n.gate[rows_at, 0:1]
        n.nrow[rows_at, :] = (h + gate * change).astype(BF)
        logit = jnp.sum(n.ct[rows_at, :].astype(F32) * change, axis=-1, keepdims=True)
        logit = logit * gate * (1.0 - gate)
        n.gsum[0:1, :] = n.gsum[0:1, :] + jnp.sum(logit * h, axis=0, keepdims=True)
        n.gmid[rows_at, :] = n.gmid[rows_at, :] + logit * n.vec[0:1, :]

    def new_at(i):
        return n.nrow.at[aligned(i, cap)]

    def grow_at(i):
        return n.grow.at[aligned(i, cap)]

    def first_back(at, rows_at):
        dy = n.gfirst[rows_at, :] + came(1, at)
        h = n.hid[rows_at, :].astype(F32)
        inv = lax.rsqrt(jnp.mean(h * h, axis=-1, keepdims=True) + eps)
        n.gsum[1:2, :] = n.gsum[1:2, :] + jnp.sum(dy * h * inv, axis=0, keepdims=True)
        t = dy * n.vec[1:2, :]
        along = jnp.sum(h * t, axis=-1, keepdims=True) * (inv * inv * inv * (1.0 / d))
        total = n.ct[rows_at, :].astype(F32) + n.gmid[rows_at, :] + (inv * t - h * along)
        n.grow[rows_at, :] = total.astype(BF)

    ax, ac = a // 2, lax.rem(a, 2)
    off_x = (c == ac) & (x != ax)
    def out_copies(t, target):
        return [
            pltpu.make_async_copy(
                t.whole.at[pl.ds(index * piece, piece)], target.at[index], t.out.at[index]
            )
            for index in range(R)
        ]

    last = pltpu.make_async_copy(n.o.whole, n.ro_out, n.o.out.at[0])
    n.sm[mine_sm, :] = jnp.concatenate(
        [n.router[...].astype(F32), n.gains[...].astype(F32), jnp.zeros((5, 128), F32)], axis=0
    )
    gather_start(n.small_t, n.sm, 8)
    for copy in cut_qkv():
        copy.wait()
    chain_start(n.wq_t, n.wqa, piece)
    chain_across(n.wq_t, n.wqa, piece)
    for m in range(MB):
        hot = hot_of(m)
        token_copy(0, m).wait()
        n.picked[m * 128 : (m + 1) * 128, :] = dot(
            hot, n.pair_a[m * tok_count : (m + 1) * tok_count, :], (0, 0)
        ).astype(BF)
        lines = jnp.concatenate([n.path[line, m : m + 1, :] for line in range(3)], axis=0)
        n.info[m, 0:3, :] = dot(lines.astype(F32).astype(BF), hot, (1, 0))
        at = at_of(m)
        n.info[m, 3:4, :] = jnp.where(at >= 0, at + f * tok_count, 0).astype(F32)
        n.info[m, 4:8, :] = jnp.zeros((4, 128), F32)
    swap_start(0, tok_at, hid_at)
    for m in range(MB):
        ss, rs = n.a2a_s.at[1, m], n.a2a_r.at[1, a]

        @pl.when(jnp.logical_not(mine[m]))
        def _():
            remote(info_src(m), info_home(a), ss, rs, home_rep, home_fsdp(m)).start()

        @pl.when(mine[m])
        def _():
            pltpu.make_async_copy(info_src(m), info_own(a), rs).start()
    gather_forward(n.small_t, n.sm, 8)
    chain_forward(n.wq_t, n.wqa, piece, 1)
    for m in range(MB):
        token_copy(1, m).wait()
        n.picked_ct[m * 128 : (m + 1) * 128, :] = dot(
            hot_of(m), n.pair_b[m * tok_count : (m + 1) * tok_count, :], (0, 0)
        ).astype(BF)
    gather_end(n.small_t, n.sm, 8)
    for index in range(F):
        n.vec[:, index * 128 : (index + 1) * 128] = n.sm[index * 8 : (index + 1) * 8, :]
    swap_end(1, info_src, info_own)
    share_start(n.info_t, n.infos, MB * 8)
    swap_end(0, tok_at, hid_at)
    by_own(first_norm)
    rows_do(share_start, n.normed_t, n.normed)
    chain_forward(n.wq_t, n.wqa, piece, 2)
    swap_start(2, cot_at, ct_at)
    share_forward(n.info_t, n.infos, MB * 8)
    out_start(n.w_out, n.woa)
    rows_do(share_forward, n.normed_t, n.normed)
    chain_forward(n.wq_t, n.wqa, piece, 3)
    for copy in cut_up():
        copy.wait()
    chain_start(n.wu_t, n.wua, piece)
    chain_across(n.wu_t, n.wua, piece)
    for copy in cut_down():
        copy.wait()
    share_end(n.info_t, n.infos, MB * 8)
    rows_do(share_near, n.normed_t, n.normed)
    rows_do(share_far, n.normed_t, n.normed)
    chain_end(n.wq_t, n.wqa, piece)
    swap_end(2, cot_at, ct_at)
    by_own(mlp_cotangent)
    share_start(n.gmlp_t[0], n.gmlp, own)
    for block in far_blocks:
        project(block)
    out_forward(n.woa)
    chain_forward(n.wu_t, n.wua, piece, 1)
    chain_start(n.wd_t, n.wda, piece)
    chain_across(n.wd_t, n.wda, piece)
    attend(far)
    out_end(n.w_out, n.woa)
    sum_near(0, 0, branch_part, 0)
    for block in near_blocks:
        project(block)
    sum_mine(0, 0, branch_part, 0, n.branch)
    chain_forward(n.wu_t, n.wua, piece, 2)
    chain_forward(n.wd_t, n.wda, piece, 1)
    attend(x)
    sum_near(0, 0, branch_part, 1)
    chain_forward(n.wu_t, n.wua, piece, 3)
    sum_mine(0, 0, branch_part, 1, n.branch)
    chain_forward(n.wd_t, n.wda, piece, 2)
    share_forward(n.gmlp_t[0], n.gmlp, own)
    sum_end(0, 0)
    by_own(second_norm)
    rows_do(share_start, n.norm2_t, n.norm2)
    chain_end(n.wu_t, n.wua, piece)
    chain_forward(n.wd_t, n.wda, piece, 3)
    mlp_up(r)
    rows_do(share_near, n.norm2_t, n.norm2)
    mlp_up(sib)
    rows_do(share_forward, n.norm2_t, n.norm2)
    mlp_up(far_blocks[0])
    rows_do(share_far, n.norm2_t, n.norm2)
    mlp_up(far_blocks[1])
    rows_do(share_near, n.gmlp_t, n.gmlp)
    rows_do(share_far, n.gmlp_t, n.gmlp)
    weight_grad(n.act, n.gmlp, n.d.grad, g.fc)
    piece_start(n.d, 1)
    chain_end(n.wd_t, n.wda, piece)
    mlp_back(far_blocks[1])
    sum_near(1, 1, norm2_part, 0)
    mlp_back(far_blocks[0])
    sum_mine(1, 1, norm2_part, 0, n.gmid)
    mlp_back(sib)
    piece_start(n.d, 0)
    sum_near(1, 1, norm2_part, 1)
    mlp_back(r)
    sum_mine(1, 1, norm2_part, 1, n.gmid)
    piece_start(n.d, 2)
    weight_grad(n.norm2, n.gup, n.u.grad, d)
    piece_take(n.d, 0)
    n.gsum[...] = jnp.zeros_like(n.gsum)
    sum_end(1, 1)
    by_own(second_back)
    rows_do(share_start, n.gbr_t, n.gbr)
    piece_start(n.d, 3)
    piece_start(n.u, 0)
    piece_take(n.d, 1)
    attention_cotangent(r)
    sum_near(2, 0, change_part, 0)
    rows_do(share_near, n.gbr_t, n.gbr)
    attention_cotangent(sib)
    attend_back(x)
    piece_start(n.u, 1)
    sum_near(2, 0, change_part, 1)
    sum_mine(2, 0, change_part, 0, n.acc, False)
    piece_take(n.d, 2)
    for part in range(2):
        sum_post(2, 0, 0, part)
    piece_pass(n.d, 0)
    rows_do(share_forward, n.gbr_t, n.gbr)
    piece_take(n.d, 3)
    piece_take(n.u, 0)
    piece_pass(n.d, 1)
    attention_cotangent(far_blocks[0])
    rows_do(share_far, n.gbr_t, n.gbr)
    piece_start(n.u, 2)
    attention_cotangent(far_blocks[1])
    weight_grad(n.att, n.gbr, n.o.grad, g.ac)
    grad_start(n.o, n.o.grad, piece)
    attend_back(far)
    piece_take(n.u, 1)
    sum_near(3, 1, normed_part, 0)
    piece_pass(n.u, 0)
    sum_mine(2, 0, change_part, 1, n.acc)
    piece_start(n.u, 3)
    piece_take(n.u, 2)
    sum_mine(3, 1, normed_part, 0, n.gfirst)
    sum_near(3, 1, normed_part, 1)
    sum_end(2, 0)
    by_own(new_rows)
    swap_start(4, new_at, lambda m: n.new_out.at[m])
    grad_forward(n.o, n.o.grad, piece)
    weight_grad(n.normed, n.gproj, n.q.grad, d)
    piece_start(n.q, 1)
    piece_start(n.q, 3)
    piece_take(n.q, 1)
    sum_mine(3, 1, normed_part, 1, n.gfirst)
    piece_pass(n.u, 1)
    piece_start(n.q, 0)
    piece_take(n.q, 0)
    piece_take(n.q, 3)
    piece_start(n.q, 2)
    piece_own(n.d)
    sum_end(3, 1)
    by_own(first_back)
    swap_start(3, grow_at, lambda m: n.grad_out.at[m])
    piece_take(n.u, 3)
    piece_pass(n.q, 1)
    for index in range(F):
        n.gsp[index * 8 : (index + 1) * 8, :] = n.gsum[:, index * 128 : (index + 1) * 128]
    piece_take(n.q, 2)
    @pl.when(is_source)
    def _():
        grad_wait(n.o, piece)
        grad_total(n.o, n.o.grad, b * piece, piece, n.o.whole, 0, range(A - 1))
    grad_start(n.s, n.gsp, 8)
    piece_own(n.u)
    grad_forward(n.s, n.gsp, 8)
    piece_pass(n.q, 0)
    for step in range(X - 1):
        send(n.o.whole, n.o.whole, n.o.share.xs.at[step], n.o.share.xr.at[0], xpeer(step) * 2 + c, f, is_source)
    send(n.o.whole, n.o.whole, n.o.share.ss.at[0], n.o.share.sr.at[0], sib, f, is_source)
    grad_wait(n.s, 8)
    grad_total(n.s, n.gsp, f * 8, 8, n.gs_mine.at[0], 0, range(A - 1))
    send(n.gs_mine.at[0], n.gs_pair.at[0], n.pair_s.at[0], n.pair_r.at[0], sib, f)
    piece_own(n.q)
    share_forward(n.d.share, n.d.whole, piece)
    @pl.when(off_x)
    def _():
        got(n.o.whole, n.o.share.xr.at[0])
    send(n.o.whole, n.o.whole, n.o.share.ss.at[1], n.o.share.sr.at[0], sib, f, off_x)
    share_forward(n.u.share, n.u.whole, piece)
    share_end(n.u.share, n.u.whole, piece)
    share_forward(n.q.share, n.q.whole, piece)
    @pl.when(c != ac)
    def _():
        got(n.o.whole, n.o.share.sr.at[0])
    last.start()
    got(n.gs_pair.at[0], n.pair_r.at[0])
    share_end(n.d.share, n.d.whole, piece)
    n.gs_mine[1] = n.gs_mine[0] + n.gs_pair[0]
    for copy in out_copies(n.d, n.rd_out):
        copy.start()
    send(n.gs_mine.at[1], n.gs_pair.at[1], n.pair_s.at[1], n.pair_r.at[1], xpeer(0) * 2 + c, f)
    for copy in out_copies(n.u, n.ru_out):
        copy.start()
    share_end(n.q.share, n.q.whole, piece)
    for copy in out_copies(n.q, n.rq_out):
        copy.start()
    got(n.gs_pair.at[1], n.pair_r.at[1])
    n.gs_out[...] = n.gs_mine[1] + n.gs_pair[1]
    swap_end(4, new_at, lambda m: n.new_out.at[m])
    swap_end(3, grow_at, lambda m: n.grad_out.at[m])
    for t, target in ((n.d, n.rd_out), (n.u, n.ru_out), (n.q, n.rq_out)):
        for copy in out_copies(t, target):
            copy.wait()
    last.wait()
    for tag in list(pending):
        drain(tag)


def place_kernel(g, at_ref, tok_ref, cot_ref, new_ref, grad_ref, rq_ref, ru_ref, rd_ref, ro_ref, gs_ref, *outs):
    mixed_ref, gt_ref, gq_ref, gu_ref, gd_ref, go_ref, grouter_ref, ggains_ref = outs
    grouter_ref[...] = gs_ref[0:1, :]
    ggains_ref[...] = gs_ref[1:3, :]
    tall = tok_ref.shape[1]
    first = pl.program_id(1) * tall
    for k in range(2):
        token = lax.broadcasted_iota(jnp.int32, (tall, g.cap), 0) + first
        hot = token == at_ref[k]
        routed = jnp.max(hot.astype(F32), axis=-1, keepdims=True) > 0.0
        hot = hot.astype(BF)
        new = dot(hot, new_ref[k], (1, 0))
        mixed_ref[k] = jnp.where(routed, new, tok_ref[k].astype(F32)).astype(BF)
        grad = dot(hot, grad_ref[k], (1, 0))
        gt_ref[k] = jnp.where(routed, grad, cot_ref[k].astype(F32))
    for index in range(g.R):
        for part in range(3):
            gq_ref[:, pl.ds(part * g.d + index * g.ac, g.ac)] = rq_ref[
                index, :, pl.ds(part * g.ac, g.ac)
            ].astype(F32)
        for block in range(g.F):
            gu_ref[:, pl.ds((block * g.R + index) * 128, 128)] = ru_ref[
                index, :, pl.ds(block * 128, 128)
            ].astype(F32)
        gd_ref[index] = rd_ref[index].astype(F32)
    go_ref[...] = ro_ref[...].astype(F32)


def place(g, chosen, tokens, cotangent, new_rows, grad_rows, rq, ru, rd, ro, gs):
    halves = 1
    steps = g.MB // 2 * halves
    tok_count = tokens.shape[1]
    tall = tok_count // halves
    piece = g.d // g.F
    low = piece // steps
    hidden = g.F * g.R * 128

    def block(*shape):
        return pl.BlockSpec((2,) + shape, lambda m, h: (m, h, 0))

    def micro(*shape):
        return pl.BlockSpec((2,) + shape, lambda m, h: (m, 0, 0))

    def slab(*lead, cols):
        return pl.BlockSpec(
            lead + (low, cols), lambda m, h: (0,) * len(lead) + (m * halves + h, 0)
        )

    return pl.pallas_call(
        functools.partial(place_kernel, g),
        grid=(g.MB // 2, halves),
        in_specs=[
            micro(1, g.cap),
            block(tall, g.d),
            block(tall, g.d),
            micro(g.cap, g.d),
            micro(g.cap, g.d),
            slab(g.R, cols=g.qc),
            slab(g.R, cols=g.fc),
            slab(g.R, cols=g.d),
            slab(cols=g.d),
            pl.BlockSpec((8, 128), lambda m, h: (0, 0)),
        ],
        out_specs=[
            block(tall, g.d),
            block(tall, g.d),
            slab(cols=3 * g.d),
            slab(cols=hidden),
            slab(g.R, cols=g.d),
            slab(cols=g.d),
            pl.BlockSpec((1, 128), lambda m, h: (0, 0)),
            pl.BlockSpec((2, 128), lambda m, h: (0, 0)),
        ],
        out_shape=[
            jax.ShapeDtypeStruct(tokens.shape, BF),
            jax.ShapeDtypeStruct(tokens.shape, F32),
            jax.ShapeDtypeStruct((piece, 3 * g.d), F32),
            jax.ShapeDtypeStruct((piece, hidden), F32),
            jax.ShapeDtypeStruct((g.R, piece, g.d), F32),
            jax.ShapeDtypeStruct((piece, g.d), F32),
            jax.ShapeDtypeStruct((1, 128), F32),
            jax.ShapeDtypeStruct((2, 128), F32),
        ],
        compiler_params=pltpu.CompilerParams(vmem_limit_bytes=60 * 1024 * 1024),
        name="place_rows",
    )(chosen[:, None, :], tokens, cotangent, new_rows, grad_rows, rq, ru, rd, ro, gs)


def group_shards(tokens, cotangent, path, chosen, router, gains, w_qkv, w_out, w_up, w_down):
    R, F = lax.axis_size("rep"), lax.axis_size("fsdp")
    MB, tok_count, d = tokens.shape
    cap = chosen.shape[1]
    S = F // MB
    hidden = w_up.shape[1]
    g = types.SimpleNamespace(
        R=R,
        F=F,
        S=S,
        A=MB,
        X=R // 2,
        MB=MB,
        cap=cap,
        d=d,
        own=MB * cap,
        rows=R * MB * cap,
        tree=S * MB * cap,
        trees=R // S,
        heads=HEADS // R,
        qc=3 * d // R,
        ac=d // R,
        fc=hidden // R,
    )
    piece = d // F

    anywhere, inside = pl.BlockSpec(memory_space=pl.ANY), pl.BlockSpec(memory_space=pltpu.VMEM)
    operands = dict(
        tokens=(tokens, anywhere),
        cotangent=(cotangent, anywhere),
        w_qkv=(w_qkv, anywhere),
        w_out=(w_out, anywhere),
        w_up=(w_up, anywhere),
        w_down=(w_down, anywhere),
        path=(jnp.transpose(path, (2, 0, 1)), inside),
        chosen=(chosen, inside),
        router=(router[None], inside),
        gains=(gains.T, inside),
    )
    results = dict(
        new_out=((MB, cap, d), BF, anywhere),
        grad_out=((MB, cap, d), BF, anywhere),
        rq_out=((R, piece, g.qc), BF, anywhere),
        ru_out=((R, piece, g.fc), BF, anywhere),
        rd_out=((R, piece, d), BF, anywhere),
        ro_out=((piece, d), BF, anywhere),
        gs_out=((8, 128), F32, inside),
    )
    scratch = scratch_shapes(g)
    flat, _ = jax.tree.flatten(scratch)
    order = list(operands) + list(results)
    made = pl.pallas_call(
        functools.partial(block_kernel, g, order, jax.tree.structure(scratch)),
        out_shape=[jax.ShapeDtypeStruct(*kind[:2]) for kind in results.values()],
        in_specs=[spec for _, spec in operands.values()],
        out_specs=[kind[2] for kind in results.values()],
        scratch_shapes=flat,
        compiler_params=pltpu.CompilerParams(
            collective_id=0, has_side_effects=True, vmem_limit_bytes=60 * 1024 * 1024
        ),
        name="routed_block",
    )(*[value for value, _ in operands.values()])
    new_rows, grad_rows, rq, ru, rd, ro, gs = made
    mixed, grad_tokens, grad_qkv, grad_up, grad_down, grad_out, grad_router, grad_gains = place(
        g, chosen, tokens, cotangent, new_rows, grad_rows, rq, ru, rd, ro, gs
    )
    return (
        mixed,
        grad_tokens,
        grad_router[0],
        grad_gains.T,
        grad_qkv,
        grad_out,
        grad_up,
        grad_down.reshape(R * piece, d),
    )


def plain_norm(matrix, gain_row):
    return matrix * lax.rsqrt(jnp.mean(matrix * matrix, axis=-1, keepdims=True) + eps) * gain_row


def inner(left, right):
    return lax.dot_general(
        left, right, (((0,), (0,)), ((), ())), preferred_element_type=jnp.float32
    )


def by_rows(left, right):
    return lax.dot_general(
        left, right, (((1,), (1,)), ((), ())), preferred_element_type=jnp.float32
    )


def gather_rows(arrays):
    return lax.all_gather(arrays, "fsdp", axis=0, tiled=True)


def scatter_sum(array):
    return lax.psum_scatter(
        array.astype(jnp.bfloat16), "fsdp", scatter_dimension=0, tiled=True
    ).astype(jnp.float32)


def plain_shards(tokens, cotangent, path, chosen, router, gains, w_qkv, w_out, w_up, w_down):
    micro_count, tok_count, model_width = tokens.shape
    slot_count = chosen.shape[1]
    row_count = micro_count * slot_count
    head_dim = model_width // HEADS
    score_scale = head_dim ** (-0.5)
    offset = lax.axis_index("fsdp") * tok_count
    fsdp = lax.axis_size("fsdp")

    def pick(array):
        return jax.vmap(lambda rows, at: rows[at])(array, chosen)

    small = jnp.concatenate([router[:, None], gains], axis=1)
    small_all = gather_rows(small)
    qkv_all = gather_rows(w_qkv)
    out_all = gather_rows(w_out)
    up_all = gather_rows(w_up)
    down_all = gather_rows(w_down)
    router_float = small_all[:, 0].astype(jnp.float32)
    gain_one = small_all[:, 1].astype(jnp.float32)
    gain_two = small_all[:, 2].astype(jnp.float32)

    routed = pick(tokens).reshape(row_count, model_width)
    hidden = routed.astype(jnp.float32)
    gate_rate = jax.nn.sigmoid(
        jnp.dot(routed, small_all[:, 0], preferred_element_type=jnp.float32)
    )
    normed = plain_norm(hidden, gain_one).astype(jnp.bfloat16)
    projected = jnp.dot(normed, qkv_all, preferred_element_type=jnp.float32).astype(jnp.bfloat16)
    queries = projected[:, :model_width].reshape(micro_count, slot_count, HEADS, head_dim)
    own_path = pick(path)
    own_place = offset + chosen
    key_info = jnp.concatenate([own_path[:, :, :1], own_place[:, :, None]], axis=2)
    gathered = lax.all_gather(
        projected[:, model_width:].reshape(micro_count, slot_count, 2 * model_width), "fsdp"
    )
    info_all = lax.all_gather(key_info, "fsdp")
    key_count = fsdp * slot_count
    gathered = jnp.swapaxes(gathered, 0, 1).reshape(micro_count, key_count, 2, HEADS, head_dim)
    info_all = jnp.swapaxes(info_all, 0, 1).reshape(micro_count, key_count, 2)
    key_rows = gathered[:, :, 0]
    value_rows = gathered[:, :, 1]
    key_seg = info_all[:, None, :, 0]
    visible = (
        (key_seg == own_path[:, :, 0:1])
        | (key_seg == own_path[:, :, 1:2])
        | (key_seg == own_path[:, :, 2:3])
    ) & (info_all[:, None, :, 1] <= own_place[:, :, None])
    visible = visible[:, None]

    def product(form, left, right):
        return jnp.einsum(form, left, right, preferred_element_type=jnp.float32)

    scores = product("mqhd,mkhd->mhqk", queries, key_rows) * score_scale
    scores = jnp.where(visible, scores, -1e30)
    row_max = jnp.max(scores, axis=-1, keepdims=True)
    exponent = jnp.where(visible, jnp.exp(scores - row_max), 0.0)
    row_total = jnp.sum(exponent, axis=-1, keepdims=True)
    soft_prob = exponent / row_total
    probs = soft_prob.astype(jnp.bfloat16)
    attention = product("mhqk,mkhd->mqhd", probs, value_rows)
    attention = attention.reshape(row_count, model_width).astype(jnp.bfloat16)
    branch = jnp.dot(attention, out_all, preferred_element_type=jnp.float32)
    middle = hidden + branch
    normed_two = plain_norm(middle, gain_two).astype(jnp.bfloat16)
    up_proj = jnp.dot(normed_two, up_all, preferred_element_type=jnp.float32)
    activated = jax.nn.gelu(up_proj).astype(jnp.bfloat16)
    change = branch + jnp.dot(activated, down_all, preferred_element_type=jnp.float32)
    new_rows = hidden + gate_rate[:, None] * change

    def put(array, rows):
        rows = rows.reshape(micro_count, slot_count, model_width).astype(array.dtype)
        return jax.vmap(lambda whole, at, new: whole.at[at].set(new))(array, chosen, rows)

    mixed = put(tokens, new_rows)

    grad_rows = pick(cotangent).reshape(row_count, model_width).astype(jnp.float32)
    grad_change = gate_rate[:, None] * grad_rows
    grad_logit = jnp.sum(grad_rows * change, axis=-1) * gate_rate * (1.0 - gate_rate)
    grad_mlp = grad_change.astype(jnp.bfloat16)
    grad_down = scatter_sum(inner(activated, grad_mlp))
    grad_act = by_rows(grad_mlp, down_all)
    gelu_value, gelu_back = jax.vjp(jax.nn.gelu, up_proj)
    grad_up_proj = gelu_back(grad_act)[0].astype(jnp.bfloat16)
    grad_up = scatter_sum(inner(normed_two, grad_up_proj))
    grad_normed_two = by_rows(grad_up_proj, up_all)
    norm_value, norm_back_two = jax.vjp(plain_norm, middle, gain_two)
    grad_middle, grad_gain_two = norm_back_two(grad_normed_two)
    grad_branch = (grad_change + grad_middle).astype(jnp.bfloat16)
    grad_outw = scatter_sum(inner(attention, grad_branch))
    grad_attention = by_rows(grad_branch, out_all).astype(jnp.bfloat16)
    grad_heads = grad_attention.reshape(micro_count, slot_count, HEADS, head_dim)
    prob_grad = product("mqhd,mkhd->mhqk", grad_heads, value_rows)
    delta = jnp.sum(soft_prob * prob_grad, axis=-1, keepdims=True)
    grad_scores = (soft_prob * (prob_grad - delta)).astype(jnp.bfloat16)
    grad_query = product("mhqk,mkhd->mqhd", grad_scores, key_rows) * score_scale
    grad_key = product("mhqk,mqhd->mkhd", grad_scores, queries) * score_scale
    grad_value = product("mhqk,mqhd->mkhd", probs, grad_heads)
    grad_kv = jnp.stack([grad_key, grad_value], axis=2).reshape(
        micro_count, fsdp, slot_count, 2 * model_width
    )
    grad_kv = lax.psum_scatter(
        jnp.swapaxes(grad_kv, 0, 1).astype(jnp.bfloat16).reshape(-1, 2 * model_width),
        "fsdp",
        scatter_dimension=0,
        tiled=True,
    )
    grad_projected = jnp.concatenate(
        [
            grad_query.reshape(row_count, model_width).astype(jnp.bfloat16),
            grad_kv.reshape(row_count, 2 * model_width),
        ],
        axis=1,
    )
    grad_qkvw = scatter_sum(inner(normed, grad_projected))
    grad_normed = by_rows(grad_projected, qkv_all)
    norm_value_one, norm_back_one = jax.vjp(plain_norm, hidden, gain_one)
    grad_hidden_norm, grad_gain_one = norm_back_one(grad_normed)
    grad_hidden = (
        grad_rows + grad_middle + grad_hidden_norm + grad_logit[:, None] * router_float[None, :]
    )
    grad_tokens = put(cotangent.astype(jnp.float32), grad_hidden)
    grad_routerw = jnp.sum(grad_logit[:, None] * hidden, axis=0)
    grad_small = jnp.stack([grad_routerw, grad_gain_one, grad_gain_two], axis=1)
    grad_small = lax.psum_scatter(grad_small, "fsdp", scatter_dimension=0, tiled=True)
    summed = lax.psum((grad_small, grad_qkvw, grad_outw, grad_up, grad_down), "rep")
    return (mixed, grad_tokens, summed[0][:, 0], summed[0][:, 1:]) + tuple(summed[1:])


def solution(mesh):
    rows = P(None, ("rep", "fsdp"), None)
    weight = P("fsdp", None)

    def whole(*args):
        grouped = fits(mesh, args[0], args[3], args[8])
        return jax.shard_map(
            group_shards if grouped else plain_shards,
            mesh=mesh,
            in_specs=(
                rows,
                rows,
                rows,
                P(None, ("rep", "fsdp")),
                P("fsdp"),
                weight,
                weight,
                weight,
                weight,
                weight,
            ),
            out_specs=(rows, rows, P("fsdp"), weight, weight, weight, weight, weight),
            check_vma=False,
        )(*args)

    return whole
```
